32 devices in a mesh: dp: 8 (over z, y), expert: 4 (over x, core).
Axes of the slice: x: 2, y: 2, z: 4, core: 2. Of those that a mesh axis runs over, the one named last changes fastest.
Arguments:
- tokens: bfloat16 [32768, 768], P(('dp', 'expert')), may hold values from -6 to 6
- prev_logits: float32 [32768, 12], P(('dp', 'expert')), may hold values from -4 to 4
- routes: int32 [32768, 2], P(('dp', 'expert')), may hold values from 0 to 11, all different within a row
- priority: int32 [32768], P(('dp', 'expert')), may hold values from 0 to 1023, as said below
- norm_attn: float32 [768], replicated, may hold values from 0.5 to 1.5
- w_query: bfloat16 [768, 768], replicated, may hold values from -0.21875 to 0.21875
- w_key: bfloat16 [768, 768], replicated, may hold values from -0.21875 to 0.21875
- w_value: bfloat16 [768, 768], replicated, may hold values from -0.21875 to 0.21875
- w_out: bfloat16 [768, 768], replicated, may hold values from -6 to 6
- norm_ffn: float32 [768], replicated, may hold values from 0.5 to 1.5
- router: bfloat16 [768, 12], replicated, may hold values from -0.109375 to 0.109375
- const_w: bfloat16 [2, 768, 2], replicated, may hold values from -0.21875 to 0.21875
- const_v: float32 [2, 768], replicated, may hold values from -6 to 6
- w_gate: bfloat16 [8, 768, 2048], P('expert'), may hold values from -0.21875 to 0.21875
- w_up: bfloat16 [8, 768, 2048], P('expert'), may hold values from -0.21875 to 0.21875
- w_down: bfloat16 [8, 2048, 768], P('expert'), may hold values from -0.125 to 0.125
- cotangent: bfloat16 [32768, 768], P(('dp', 'expert')), may hold values from -6 to 6
Outputs:
- mixed_out: bfloat16 [32768, 768], P(('dp', 'expert'))
- grad_tokens: float32 [32768, 768], P(('dp', 'expert'))
- grad_prev: float32 [32768, 12], P(('dp', 'expert'))
- grad_norm_attn: float32 [768], replicated
- grad_query: float32 [768, 768], replicated
- grad_key: float32 [768, 768], replicated
- grad_value: float32 [768, 768], replicated
- grad_out_proj: float32 [768, 768], replicated
- grad_norm_ffn: float32 [768], replicated
- grad_router: float32 [768, 12], replicated
- grad_const_w: float32 [2, 768, 2], replicated
- grad_const_v: float32 [2, 768], replicated
- grad_w_gate: float32 [8, 768, 2048], P('expert', None, 'dp')
- grad_w_up: float32 [8, 768, 2048], P('expert', None, 'dp')
- grad_w_down: float32 [8, 2048, 768], P('expert', 'dp')
The draws below stay inside these ranges and needn't reach their ends.
Inputs may be any that keep to these rules, and one draw needn't show every extreme that they name: `routes`: each row names two different experts; every expert is named somewhere. `priority`: in each aligned block of 1024 rows the values are a permutation of 0 to 1023.
All inputs are finite; a program needn't handle non-finite values.
Results may differ from the reference program's by a relative error of at most 0.015.
Values may be sent and summed in bfloat16 or wider, within the bound.
A program may use at most 384 MiB of HBM per device.

```python
import jax
import jax.numpy as jnp
from jax import lax

D = 768
HEADS = 12
HEAD_DIM = 64
FF = 2048
FFN_EXP = 8
CONST_EXP = 2
ALL_EXPERTS = 12
TOPK = 2
PROMPT = 2048
NCONT = 8
CONT = 256
TOK_DEV = 1024
TOKENS = 32768
CAP = 192
N_DP = 8
N_EXPERT = 4


def draw_priority(key, part):
    block_count = TOKENS // TOK_DEV
    keys_list = jax.random.split(key, block_count)
    orders = jax.vmap(lambda one_key: jax.random.permutation(one_key, TOK_DEV))(keys_list)
    return orders.reshape(-1).astype(jnp.int32)


def level_of(key, shape, cuts, low, top_value):
    loudness, own = 1.0, jax.random.fold_in(key, 6)
    for axis_at, shards_of in cuts:
        heights = jnp.exp(jax.random.uniform(jax.random.fold_in(own, axis_at), (shards_of,), jnp.float32, low / len(cuts), top_value / len(cuts)))
        loudness = loudness * jnp.repeat(heights, shape[axis_at] // shards_of).reshape([-1 if axis == axis_at else 1 for axis in range(len(shape))])
    return loudness


def choose_distinct(key, rows, count, top, lift):
    ranking = jax.random.permutation(jax.random.fold_in(key, 1), count)
    pull = ranking
    for power in range(3):
        pull = pull * pull // count
    pull = pull * lift // count
    chance = jax.random.randint(jax.random.fold_in(key, 2), (rows, count), 0, 4096) + pull
    fixed_rows = jax.random.permutation(jax.random.fold_in(key, 3), rows)[jnp.arange(count) % rows]
    chance = jnp.where(jnp.arange(rows)[:, None] == fixed_rows[None, :], 1 << 14, chance)
    score = chance * count + jnp.arange(count)
    return lax.top_k(score.astype(jnp.int32), top)[1].astype(jnp.int32)


def scatter_about(own_key, dims, spread, most, pieces=(), held_as=jnp.bfloat16):
    loudness = level_of(own_key, dims, pieces, -0.22, 0.18) if pieces else 1.0
    array = jax.random.normal(own_key, dims, jnp.float32) * spread * loudness
    return jnp.minimum(jnp.maximum(array, -most), most).astype(held_as)


def setup_inputs(seed: int = 0) -> dict:
    streams_of = jax.random.split(jax.random.key(seed), 18)
    return {
        "tokens": scatter_about(streams_of[0], (TOKENS, D), 1.0, 6.0, ((0, 32),)),
        "prev_logits": scatter_about(streams_of[1], (TOKENS, ALL_EXPERTS), 0.5, 4.0, ((0, 32),), jnp.float32),
        "routes": choose_distinct(streams_of[2], TOKENS, ALL_EXPERTS, TOPK, 1365),
        "priority": draw_priority(jax.random.fold_in(streams_of[17], 71), 0),
        "norm_attn": jnp.clip(1.0 + 0.1 * jax.random.normal(streams_of[4], (D,), jnp.float32), 0.5, 1.5),
        "w_query": scatter_about(streams_of[5], (D, D), D ** -0.5, 0.21875),
        "w_key": scatter_about(streams_of[6], (D, D), D ** -0.5, 0.21875),
        "w_value": scatter_about(streams_of[7], (D, D), D ** -0.5, 0.21875),
        "w_out": scatter_about(streams_of[8], (D, D), (max(1, D // 512)) ** -0.5, 6.0),
        "norm_ffn": jnp.clip(1.0 + 0.1 * jax.random.normal(streams_of[9], (D,), jnp.float32), 0.5, 1.5),
        "router": scatter_about(streams_of[10], (D, ALL_EXPERTS), (4 * D) ** -0.5, 0.109375),
        "const_w": scatter_about(streams_of[11], (CONST_EXP, D, 2), D ** -0.5, 0.21875),
        "const_v": scatter_about(streams_of[12], (CONST_EXP, D), 1.0, 6.0, (), jnp.float32),
        "w_gate": scatter_about(streams_of[13], (FFN_EXP, D, FF), D ** -0.5, 0.21875, ((0, 4),)),
        "w_up": scatter_about(streams_of[14], (FFN_EXP, D, FF), D ** -0.5, 0.21875, ((0, 4),)),
        "w_down": scatter_about(streams_of[15], (FFN_EXP, FF, D), FF ** -0.5, 0.125, ((0, 4),)),
        "cotangent": scatter_about(streams_of[16], (TOKENS, D), 1.0, 6.0, ((0, 32),)),
    }


epsilon = 1e-06
neg_fill = -1000000000.0
highest = lax.Precision.HIGHEST

@jax.custom_vjp
def low(v):
    return lax.optimization_barrier(v.astype(jnp.bfloat16)).astype(jnp.float32)

@jax.custom_vjp
def low_back(v):
    return v

def low_keep(v):
    return (low(v), None)

def low_pass(kept, grad):
    return (grad,)

def back_keep(v):
    return (v, None)

def back_low(kept, grad):
    return (low(grad),)
low.defvjp(low_keep, low_pass)
low_back.defvjp(back_keep, back_low)

def rms_scale(values_in):
    return lax.rsqrt(lax.optimization_barrier(jnp.mean(values_in * values_in, axis=-1, keepdims=True)) + epsilon)

def rotate(values_in, positions, turn_sign):
    head_width = values_in.shape[-1]
    half_width = head_width // 2
    frequency = jnp.exp(-jnp.log(10000.0) * jnp.arange(half_width, dtype=jnp.float32) * 2.0 / head_width)
    angle = positions.astype(jnp.float32)[:, None] * frequency[None, :]
    cosine = jnp.cos(angle)[:, None, :]
    sine_part = turn_sign * jnp.sin(angle)[:, None, :]
    first_half = values_in[..., :half_width]
    second_half = values_in[..., half_width:]
    return jnp.concatenate([first_half * cosine - second_half * sine_part, second_half * cosine + first_half * sine_part], axis=-1)

def block_layout(device, row_count, prompt_dev, cont_dev):
    row_index = jnp.arange(row_count, dtype=jnp.int32)
    offset = jnp.maximum(row_index - prompt_dev, 0)
    in_prompt = row_index < prompt_dev
    positions = jnp.where(in_prompt, device * prompt_dev + row_index, PROMPT + offset % CONT)
    segments = jnp.where(in_prompt, 0, 1 + device * cont_dev + offset // CONT)
    return (positions.astype(jnp.int32), segments.astype(jnp.int32))

def slot_table(route_ids, priority, expert_count, capacity):
    row_count, pick_count = route_ids.shape
    expert_ids = jnp.arange(expert_count, dtype=jnp.int32)
    picked = route_ids[:, :, None] == expert_ids[None, None, :]
    assigned = jnp.any(picked, axis=1).astype(jnp.int32)
    row_index = jnp.arange(row_count, dtype=jnp.int32)
    by_priority = jnp.zeros((row_count,), jnp.int32).at[priority].set(row_index)
    ordered = assigned[by_priority]
    before = (jnp.cumsum(ordered, axis=0) - ordered).astype(jnp.int32)
    rank_table = before[priority]
    pick_rank = lax.optimization_barrier(jnp.sum(jnp.where(picked, rank_table[:, None, :], 0), axis=-1)).astype(jnp.int32)
    kept_pick = (route_ids < expert_count) & (pick_rank < capacity)
    slot_index = jnp.where(kept_pick, route_ids * capacity + pick_rank, -1).astype(jnp.int32)
    slot_ids = jnp.arange(expert_count * capacity, dtype=jnp.int32)
    matched = slot_index.reshape(-1)[None, :] == slot_ids[:, None]
    flat_index = jnp.arange(row_count * pick_count, dtype=jnp.int32)
    owner_pick = lax.optimization_barrier(jnp.sum(jnp.where(matched, flat_index[None, :], 0), axis=1)).astype(jnp.int32)
    filled = jnp.any(matched, axis=1)
    return (slot_index, kept_pick, owner_pick, filled)

def group_forward(tokens_g, prev_g, tables, weights):
    routes_g, slot_index, kept_pick, owner_pick, filled = tables
    norm_attn, w_query, w_key, w_value, w_out, norm_ffn, router, const_w, const_v, w_gate, w_up, w_down = weights
    row_total = tokens_g.shape[0]
    prompt_dev = PROMPT // N_EXPERT
    cont_dev = NCONT // N_EXPERT
    score_scale = HEAD_DIM ** (-0.5)
    normed_one = low(tokens_g * rms_scale(tokens_g) * norm_attn)
    query_proj = low_back(jnp.dot(normed_one, w_query, precision=highest)).reshape(row_total, HEADS, HEAD_DIM)
    key_proj = low_back(jnp.dot(normed_one, w_key, precision=highest)).reshape(row_total, HEADS, HEAD_DIM)
    value_proj = low_back(low(jnp.dot(normed_one, w_value, precision=highest)))
    layouts = [block_layout(device, TOK_DEV, prompt_dev, cont_dev) for device in range(N_EXPERT)]
    positions = jnp.concatenate([entry[0] for entry in layouts])
    segments = jnp.concatenate([entry[1] for entry in layouts])
    queries = low(rotate(query_proj, positions, 1.0))
    key_rows = low(rotate(key_proj, positions, 1.0))
    value_rows = value_proj.reshape(row_total, HEADS, HEAD_DIM)
    query_blocks = queries.reshape(N_EXPERT, TOK_DEV, HEADS, HEAD_DIM)
    key_blocks = key_rows.reshape(N_EXPERT, TOK_DEV, HEADS, HEAD_DIM)
    value_blocks = value_rows.reshape(N_EXPERT, TOK_DEV, HEADS, HEAD_DIM)
    prompt_keys = key_blocks[:, :prompt_dev].reshape(PROMPT, HEADS, HEAD_DIM)
    prompt_values = value_blocks[:, :prompt_dev].reshape(PROMPT, HEADS, HEAD_DIM)

    def one_device(inputs):
        query_block, cont_keys, cont_values, query_pos, query_seg = inputs
        keys_all = jnp.concatenate([prompt_keys, cont_keys], axis=0)
        values_all = jnp.concatenate([prompt_values, cont_values], axis=0)
        key_pos = jnp.concatenate([jnp.arange(PROMPT, dtype=jnp.int32), query_pos[prompt_dev:]])
        key_seg = jnp.concatenate([jnp.zeros((PROMPT,), jnp.int32), query_seg[prompt_dev:]])
        raw_scores = low_back(jnp.einsum('qhd,khd->hqk', query_block, keys_all, precision=highest))
        allowed = ((key_seg[None, :] == 0) | (key_seg[None, :] == query_seg[:, None])) & (key_pos[None, :] <= query_pos[:, None])
        scores = jnp.where(allowed[None], raw_scores * score_scale, neg_fill)
        prob_rows = jax.nn.softmax(scores, axis=-1)
        return jnp.einsum('hqk,khd->qhd', low(prob_rows), values_all, precision=highest)
    attended = lax.map(jax.checkpoint(one_device), (query_blocks, key_blocks[:, prompt_dev:], value_blocks[:, prompt_dev:], positions.reshape(N_EXPERT, TOK_DEV), segments.reshape(N_EXPERT, TOK_DEV)))
    attn_low = low_back(low(attended.reshape(row_total, HEADS * HEAD_DIM)))
    residual_two = tokens_g + low_back(jnp.dot(attn_low, w_out, precision=highest))
    normed_two = low(residual_two * rms_scale(residual_two) * norm_ffn)
    logits = low_back(jnp.dot(normed_two, router, precision=highest)) + prev_g
    pick_hot = (routes_g[:, :, None] == jnp.arange(ALL_EXPERTS, dtype=jnp.int32)[None, None, :]).astype(jnp.float32)
    picked_logits = lax.optimization_barrier(jnp.sum(logits[:, None, :] * pick_hot, axis=-1))
    gate_probs = jax.nn.softmax(picked_logits, axis=-1)
    const_mix = low_back(jnp.einsum('td,cdk->tck', normed_two, const_w, precision=highest))
    mix_weight = jax.nn.softmax(const_mix, axis=-1)
    const_out = mix_weight[..., 0:1] * normed_two[:, None, :] + mix_weight[..., 1:2] * const_v[None]
    const_ids = FFN_EXP + 2 + jnp.arange(CONST_EXP, dtype=jnp.int32)
    const_pick = (routes_g[:, :, None] == const_ids[None, None, :]).astype(jnp.float32)
    copy_pick = (routes_g == FFN_EXP + 1).astype(jnp.float32)
    normed_blocks = normed_two.reshape(N_EXPERT, TOK_DEV, D)
    send_rows = jax.vmap(lambda block_rows, owners: jnp.take(block_rows, owners // TOPK, axis=0))(normed_blocks, owner_pick)
    send_rows = low_back(jnp.where(filled[..., None], send_rows, 0.0)).reshape(N_EXPERT, FFN_EXP, CAP, D)
    gate_pre = low_back(jnp.einsum('secd,edf->secf', send_rows, w_gate, precision=highest))
    up_pre = low_back(jnp.einsum('secd,edf->secf', send_rows, w_up, precision=highest))
    hidden = low(jax.nn.silu(gate_pre) * up_pre)
    produced = low_back(low(jnp.einsum('secf,efd->secd', hidden, w_down, precision=highest))).reshape(N_EXPERT, FFN_EXP * CAP, D)
    ffn_branch = jax.vmap(lambda made, slot_rows: jnp.take(made, jnp.maximum(slot_rows, 0), axis=0))(produced, slot_index)
    ffn_branch = jnp.where(kept_pick[..., None], ffn_branch, 0.0).reshape(row_total, TOPK, D)
    branch = ffn_branch + copy_pick[:, :, None] * normed_two[:, None, :] + lax.optimization_barrier(jnp.sum(const_pick[:, :, :, None] * const_out[:, None, :, :], axis=2))
    return residual_two + lax.optimization_barrier(jnp.sum(gate_probs[:, :, None] * branch, axis=1))

def reference(tokens, prev_logits, routes, priority, norm_attn, w_query, w_key, w_value, w_out, norm_ffn, router, const_w, const_v, w_gate, w_up, w_down, cotangent):
    weights = tuple((entry.astype(jnp.float32) for entry in (norm_attn, w_query, w_key, w_value, w_out, norm_ffn, router, const_w, const_v, w_gate, w_up, w_down)))
    group_rows = N_EXPERT * TOK_DEV
    block_routes = routes.reshape(N_DP * N_EXPERT, TOK_DEV, TOPK)
    block_priority = priority.reshape(N_DP * N_EXPERT, TOK_DEV)
    tables = lax.map(lambda pair: slot_table(pair[0], pair[1], FFN_EXP, CAP), (block_routes, block_priority))
    tables = tuple((entry.reshape((N_DP, N_EXPERT) + entry.shape[1:]) for entry in tables))
    stacked = (tokens.astype(jnp.float32).reshape(N_DP, group_rows, D), prev_logits.reshape(N_DP, group_rows, ALL_EXPERTS), routes.reshape(N_DP, group_rows, TOPK)) + tables + (cotangent.astype(jnp.float32).reshape(N_DP, group_rows, D),)

    def group_step(running, group_item):
        tokens_g, prev_g, routes_g, slot_index, kept_pick, owner_pick, filled, cot_g = group_item

        def forward(tokens_in, prev_in, *params):
            return group_forward(tokens_in, prev_in, (routes_g, slot_index, kept_pick, owner_pick, filled), params)
        result, pullback = jax.vjp(forward, tokens_g, prev_g, *weights)
        gradients = pullback(cot_g)
        running = tuple((acc_sum + new_part for acc_sum, new_part in zip(running, gradients[2:])))
        return (running, (result.astype(jnp.bfloat16), gradients[0], gradients[1]))
    zero_sums = tuple((jnp.zeros_like(entry) for entry in weights))
    running, (mixed_out, grad_tokens, grad_prev) = lax.scan(group_step, zero_sums, stacked)
    return (mixed_out.reshape(TOKENS, D), grad_tokens.reshape(TOKENS, D), grad_prev.reshape(TOKENS, ALL_EXPERTS), running[0], running[1], running[2], running[3], running[4], running[5], running[6], running[7], running[8], running[9], running[10], running[11])
```

```python
import functools

import jax
import jax.numpy as jnp
import numpy as np
from jax import lax
from jax.experimental import pallas as pl
from jax.experimental.pallas import tpu as pltpu
from jax.sharding import PartitionSpec as P

HEADS = 12
FFN_EXP = 8
PROMPT = 2048
NCONT = 8
CONT = 256

epsilon = 1e-06
LOG2E = 1.4426950408889634
F32 = jnp.float32
BF = jnp.bfloat16
NN = (((1,), (0,)), ((), ()))
NT = (((1,), (1,)), ((), ()))
VMEM_LIMIT = 56 << 20


def dot(a, b, dims=NN):
    return lax.dot_general(a, b, dims, preferred_element_type=F32)


def params(**kw):
    return pltpu.CompilerParams(vmem_limit_bytes=VMEM_LIMIT, **kw)


def whole(shape):
    return pl.BlockSpec(shape, lambda *_: (0,) * len(shape))


def rms_scale(x):
    return lax.rsqrt(jnp.mean(x * x, axis=-1, keepdims=True) + epsilon)


def angle_tables():
    positions = np.arange(PROMPT + CONT, dtype=np.float32)
    frequency = np.exp(
        np.float32(-np.log(10000.0)) * np.arange(32, dtype=np.float32) * np.float32(2.0) / np.float32(64)
    ).astype(np.float32)
    angle = (positions[:, None] * frequency[None, :]).astype(np.float64)
    cosine = np.cos(angle).astype(np.float32)
    sine = np.sin(angle).astype(np.float32)
    return (
        np.concatenate([cosine] * 4, axis=1),
        np.concatenate([-sine, sine, -sine, sine], axis=1),
    )


def lane_iota(width=128):
    return lax.broadcasted_iota(jnp.int32, (1, width), 1)


def swap_halves(x):
    return jnp.where(lane_iota() % 64 < 32, pltpu.roll(x, 96, 1), pltpu.roll(x, 32, 1))


def project_kernel(e_ref, x_ref, gain_ref, *refs, count):
    weights, (cos_ref, sin_ref), (h_ref, *outs) = refs[:count], refs[count:count + 2], refs[count + 2:]
    x = x_ref[...].astype(F32)
    h = (x * rms_scale(x) * gain_ref[...]).astype(BF)
    h_ref[...] = h
    cosine, sine = cos_ref[...], sin_ref[...]
    for n, (w_ref, out_ref) in enumerate(zip(weights, outs)):
        full = dot(h, w_ref[...])
        if n == count - 1:
            out_ref[...] = full.astype(BF)
            continue
        for i in range(full.shape[1] // 128):
            part = full[:, i * 128:(i + 1) * 128]
            out_ref[:, i * 128:(i + 1) * 128] = (part * cosine + swap_halves(part) * sine).astype(BF)


def project(e, x, gain, weights, cos, sin, own, tile=256):
    rows, width = x.shape
    block = pl.BlockSpec((tile, width), lambda i, *_: (i, 0))
    half = rows // 2 // tile

    def position(i, e_ref):
        if not own:
            return (i, 0)
        return (jnp.where(i < half, e_ref[0] * half + i, PROMPT // tile), 0)

    table = pl.BlockSpec((tile, 128), position)
    return pl.pallas_call(
        functools.partial(project_kernel, count=len(weights)),
        grid_spec=pltpu.PrefetchScalarGridSpec(
            num_scalar_prefetch=1,
            grid=(rows // tile,),
            in_specs=[block, whole((1, width))] + [whole(weights[0].shape)] * len(weights) + [table, table],
            out_specs=[block] * (len(weights) + 1),
        ),
        out_shape=[jax.ShapeDtypeStruct((rows, width), BF)] * (len(weights) + 1),
        compiler_params=params(),
        cost_estimate=pl.CostEstimate(
            flops=2 * rows * width * width * len(weights), bytes_accessed=2 * rows * width * 6, transcendentals=0
        ),
        name="project_own" if own else "project_prompt",
    )(e, x, gain, *weights, cos, sin)


def attn_fwd_kernel(e_ref, q_ref, ko_ref, vo_ref, kp_ref, vp_ref, o_ref, lse_ref, vt_ref, qm_ref, m_ref, acc_ref, *, chunk, tile, scale):
    e = e_ref[0]
    rows = q_ref.shape[0]
    half = rows // 2
    npr = kp_ref.shape[0]
    nchunk = npr // chunk
    lane = lax.broadcasted_iota(jnp.int32, (1, 128), 1)
    low = lane < 64
    c = scale * LOG2E
    zero = jnp.zeros((), BF)
    q = q_ref[...]
    qm_ref[0] = jnp.where(low, q, zero)
    qm_ref[1] = jnp.where(low, zero, q)
    ones = jnp.ones((16, npr + rows), BF)
    for r, n, ref in ((0, npr, vp_ref), (npr, rows, vo_ref)):
        vt = ref[...].T
        vt_ref[0, :64, r:r + n] = vt[:64]
        vt_ref[1, :64, r:r + n] = vt[64:]
    vt_ref[0, 64:, :] = ones
    vt_ref[1, 64:, :] = ones
    tri = lax.broadcasted_iota(jnp.int32, (tile, tile), 0) <= lax.broadcasted_iota(jnp.int32, (tile, tile), 1)

    def first(q0, qn, k, vts):
        for h in range(2):
            s = dot(k, qm_ref[h, q0:q0 + qn, :], NT)
            s = s * c
            s = jnp.where(tri, s, -1e30)
            mx = jnp.max(s, axis=0, keepdims=True)
            p = jnp.exp2(s - mx).astype(BF)
            m_ref[h, 0:1, q0:q0 + qn] = mx
            acc_ref[h, :, q0:q0 + qn] = dot(vts[h], p)

    def step(blocks, k, vts):
        ss = [[dot(k, qm_ref[h, q0:q0 + qn, :], NT) for h in range(2)] for q0, qn in blocks]
        for (q0, qn), sb in zip(blocks, ss):
            for h in range(2):
                s = sb[h] * c
                mx = jnp.max(s, axis=0, keepdims=True)
                m = m_ref[h, 0:1, q0:q0 + qn]
                mn = jnp.maximum(m, mx)
                p = jnp.exp2(s - mn).astype(BF)
                m_ref[h, 0:1, q0:q0 + qn] = mn
                acc_ref[h, :, q0:q0 + qn] = acc_ref[h, :, q0:q0 + qn] * jnp.exp2(m - mn) + dot(vts[h], p)

    for j in range(rows // tile):
        r0 = j * tile
        first(r0, tile, ko_ref[r0:r0 + tile, :], [vt_ref[h, :, npr + r0:npr + r0 + tile] for h in range(2)])
    for j in range(1, half // tile):
        for i in range(j):
            r0 = i * tile
            step([(j * tile, tile)], ko_ref[r0:r0 + tile, :], [vt_ref[h, :, npr + r0:npr + r0 + tile] for h in range(2)])

    def body(ci, blocks):
        r0 = pl.multiple_of(ci * chunk, chunk)
        step(blocks, kp_ref[pl.ds(r0, chunk), :], [vt_ref[h, :, pl.ds(r0, chunk)] for h in range(2)])

    ne = e * half // chunk

    @pl.loop(0, ne)
    def _(ci):
        body(ci, [(0, half), (half, half)])

    @pl.loop(ne, nchunk)
    def _(ci):
        body(ci, [(half, half)])

    outs = []
    for h in range(2):
        l = acc_ref[h, 64:65, :]
        outs.append(acc_ref[h, :64, :] / l)
        lse_ref[0, h:h + 1, :] = m_ref[h, 0:1, :] + jnp.log2(l)
    o_ref[...] = jnp.concatenate(outs, axis=0).T.astype(BF)


def attn_fwd(e, q, ko, vo, kp, vp, *, chunk=512, tile=256):
    rows, width = q.shape
    npr = kp.shape[0]
    pairs = width // 128
    own = pl.BlockSpec((rows, 128), lambda i, *_: (0, i))
    pr = pl.BlockSpec((npr, 128), lambda i, *_: (0, i))
    return pl.pallas_call(
        functools.partial(attn_fwd_kernel, chunk=chunk, tile=tile, scale=0.125),
        grid_spec=pltpu.PrefetchScalarGridSpec(
            num_scalar_prefetch=1, grid=(pairs,),
            in_specs=[own, own, own, pr, pr],
            out_specs=[own, pl.BlockSpec((1, 2, rows), lambda i, *_: (i, 0, 0))],
            scratch_shapes=[pltpu.VMEM((2, 80, npr + rows), BF), pltpu.VMEM((2, rows, 128), BF),
            pltpu.VMEM((2, 8, rows), F32), pltpu.VMEM((2, 80, rows), F32)]),
        out_shape=[jax.ShapeDtypeStruct((rows, width), BF), jax.ShapeDtypeStruct((pairs, 2, rows), F32)],
        compiler_params=params(),
        cost_estimate=pl.CostEstimate(flops=4 * rows * npr * width * 2, bytes_accessed=2 * npr * width * 4, transcendentals=rows * npr * 12),
        name="attn_fwd",
    )(e, q, ko, vo, kp, vp)


def attn_bwd_kernel(e_ref, q_ref, do_ref, o_ref, lse_ref, ko_ref, vo_ref, kp_ref, vp_ref, cos_ref, sin_ref,
               dq_ref, dk_ref, dv_ref,
               kt_ref, dqt_ref, qm_ref, dom_ref, dl_ref, dks_ref, dvs_ref, *, tile, scale):
    e = e_ref[0]
    rows = q_ref.shape[0]
    half = rows // 2
    chunk = half
    npr = kp_ref.shape[0]
    nchunk = npr // chunk
    cont = cos_ref.shape[0] - npr
    lane = lax.broadcasted_iota(jnp.int32, (1, 128), 1)
    low = lane < 64
    c = scale * LOG2E
    zero = jnp.zeros((), BF)
    q = q_ref[...]
    do = do_ref[...]
    qm_ref[0] = jnp.where(low, q, zero)
    qm_ref[1] = jnp.where(low, zero, q)
    dom_ref[0] = jnp.where(low, do, zero)
    dom_ref[1] = jnp.where(low, zero, do)
    prod = (do.astype(F32) * o_ref[...].astype(F32)).T
    dl_ref[0:1, :] = jnp.sum(prod[:64], axis=0, keepdims=True)
    dl_ref[1:2, :] = jnp.sum(prod[64:], axis=0, keepdims=True)
    kt_ref[:, :npr] = kp_ref[...].T
    kt_ref[:, npr:] = ko_ref[...].T
    tri = lax.broadcasted_iota(jnp.int32, (tile, tile), 0) <= lax.broadcasted_iota(jnp.int32, (tile, tile), 1)

    def unrope(x, pos, n):
        first = (lane % 64) < 32
        sw = jnp.where(first, pltpu.roll(x, 96, 1), pltpu.roll(x, 32, 1))
        return x * cos_ref[pl.ds(pos, n), :] - sw * sin_ref[pl.ds(pos, n), :]

    def block(k, v, kt, q0, qn, mask):
        dk = dv = None
        dqs = []
        qs = [qm_ref[h, q0:q0 + qn, :] for h in range(2)]
        dos = [dom_ref[h, q0:q0 + qn, :] for h in range(2)]
        sts = [dot(k, qs[h], NT) for h in range(2)]
        dps = [dot(v, dos[h], NT) for h in range(2)]
        for h in range(2):
            p = jnp.exp2(sts[h] * c - lse_ref[0, h:h + 1, q0:q0 + qn])
            if mask is not None:
                p = jnp.where(mask, p, 0.0)
            ds = (p * (dps[h] - dl_ref[h:h + 1, q0:q0 + qn])).astype(BF)
            dvh = dot(p.astype(BF), dos[h])
            dkh = dot(ds, qs[h])
            dk, dv = (dkh, dvh) if dk is None else (dk + dkh, dv + dvh)
            dqs.append(dot(kt[h * 64:(h + 1) * 64], ds))
        return dk, dv, jnp.concatenate(dqs, axis=0)

    nt = rows // tile
    for i in range(nt):
        r0 = i * tile
        k = ko_ref[r0:r0 + tile, :]
        v = vo_ref[r0:r0 + tile, :]
        kt = kt_ref[:, npr + r0:npr + r0 + tile]
        prompt = r0 < half
        dk = dv = None
        for j in (range(i, nt // 2) if prompt else [i]):
            a, b, dq = block(k, v, kt, j * tile, tile, tri if i == j else None)
            dk, dv = (a, b) if dk is None else (dk + a, dv + b)
            sl = slice(j * tile, (j + 1) * tile)
            if i == 0 or not prompt:
                dqt_ref[:, sl] = dq
            else:
                dqt_ref[:, sl] += dq
        if prompt:
            dks_ref[r0:r0 + tile, :] = dk
            dvs_ref[r0:r0 + tile, :] = dv
        else:
            o0 = npr + r0 - half
            dk_ref[o0:o0 + tile, :] = (unrope(dk, npr, tile) * scale).astype(BF)
            dv_ref[o0:o0 + tile, :] = dv.astype(BF)

    def chunk_step(ci, kind):
        r0 = pl.multiple_of(ci * chunk, chunk)
        k = kp_ref[pl.ds(r0, chunk), :]
        v = vp_ref[pl.ds(r0, chunk), :]
        kt = kt_ref[:, pl.ds(r0, chunk)]
        dk, dv, dq = block(k, v, kt, half, half, None)
        dqt_ref[:, half:] += dq
        if kind == 0:
            a, b, dq = block(k, v, kt, 0, half, None)
            dk, dv = dk + a, dv + b
            dqt_ref[:, :half] += dq
        elif kind == 1:
            dk, dv = dk + dks_ref[...], dv + dvs_ref[...]
        dk_ref[pl.ds(r0, chunk), :] = (unrope(dk, r0, chunk) * scale).astype(BF)
        dv_ref[pl.ds(r0, chunk), :] = dv.astype(BF)

    @pl.loop(0, e)
    def _(ci):
        chunk_step(ci, 0)

    chunk_step(e, 1)

    @pl.loop(e + 1, nchunk)
    def _(ci):
        chunk_step(ci, 2)

    dq = dqt_ref[...].T
    base = pl.multiple_of(e * half, half)
    dq_ref[:half, :] = (unrope(dq[:half], base, half) * scale).astype(BF)
    for r in range(half, rows, cont):
        dq_ref[r:r + cont, :] = (unrope(dq[r:r + cont], npr, cont) * scale).astype(BF)


def attn_bwd(e, q, do, o, lse, ko, vo, kp, vp, cos, sin, *, tile=256):
    rows, width = q.shape
    npr = kp.shape[0]
    keys = npr + rows // 2
    pairs = width // 128
    own = pl.BlockSpec((rows, 128), lambda i, *_: (0, i))
    pr = pl.BlockSpec((npr, 128), lambda i, *_: (0, i))
    al = pl.BlockSpec((keys, 128), lambda i, *_: (0, i))
    tab = pl.BlockSpec(cos.shape, lambda i, *_: (0, 0))
    return pl.pallas_call(
        functools.partial(attn_bwd_kernel, tile=tile, scale=0.125),
        grid_spec=pltpu.PrefetchScalarGridSpec(
            num_scalar_prefetch=1, grid=(pairs,),
            in_specs=[own, own, own, pl.BlockSpec((1, 2, rows), lambda i, *_: (i, 0, 0)), own, own, pr, pr, tab, tab],
            out_specs=[own, al, al],
            scratch_shapes=[pltpu.VMEM((128, npr + rows), BF), pltpu.VMEM((128, rows), F32),
                            pltpu.VMEM((2, rows, 128), BF), pltpu.VMEM((2, rows, 128), BF),
                            pltpu.VMEM((8, rows), F32),
                            pltpu.VMEM((rows // 2, 128), F32), pltpu.VMEM((rows // 2, 128), F32)]),
        out_shape=[jax.ShapeDtypeStruct((rows, width), BF), jax.ShapeDtypeStruct((keys, width), BF),
                   jax.ShapeDtypeStruct((keys, width), BF)],
        compiler_params=params(),
        cost_estimate=pl.CostEstimate(flops=10 * rows * npr * width * 2, bytes_accessed=2 * npr * width * 8, transcendentals=rows * npr * 12),
        name="attn_bwd",
    )(e, q, do, o, lse, ko, vo, kp, vp, cos, sin)


def pick(values, lane, index):
    return jnp.sum(jnp.where(lane == index, values, 0.0), axis=1, keepdims=True)


def softmax_pair(a, b):
    top = jnp.maximum(a, b)
    ea, eb = jnp.exp(a - top), jnp.exp(b - top)
    total = ea + eb
    return ea / total, eb / total


def gate_kernel(x_ref, o_ref, w_ref, gain_ref, wcat_ref, prev_ref, routes_ref, x2_ref, h2_ref, aux_ref, ext_ref, *, experts):
    x2 = x_ref[...].astype(F32) + dot(o_ref[...], w_ref[...])
    x2_ref[...] = x2
    h2 = (x2 * rms_scale(x2) * gain_ref[...]).astype(BF)
    h2_ref[...] = h2
    logits = dot(h2, wcat_ref[...]) + prev_ref[...]
    lane = lane_iota()
    gates = softmax_pair(*[pick(logits, lane, routes_ref[:, k:k + 1]) for k in range(2)])
    aux = logits
    for k in range(2):
        aux = jnp.where(lane == experts + k, gates[k], aux)
    at = experts + 2
    for c in range(2):
        alpha = softmax_pair(*[pick(logits, lane, experts + 2 * c + k) for k in range(2)])
        for k in range(2):
            aux = jnp.where(lane == at + 2 * c + k, alpha[k], aux)
    aux_ref[...] = aux
    for k in range(2):
        parts, left = [], gates[k]
        for _ in range(3):
            part = left.astype(BF)
            parts.append(part.astype(F32))
            left = left - parts[-1]
        spread = jnp.where(lane == 0, parts[0], jnp.where(lane == 1, parts[1], jnp.where(lane == 2, parts[2], 0.0)))
        ext_ref[:, k * 128:(k + 1) * 128] = spread.astype(BF)


def gates(x, o, w_out, gain, wcat, prev, routes, experts, tile=256):
    rows, width = x.shape
    block = pl.BlockSpec((tile, width), lambda i: (i, 0))
    thin = pl.BlockSpec((tile, 128), lambda i: (i, 0))
    return pl.pallas_call(
        functools.partial(gate_kernel, experts=experts),
        grid=(rows // tile,),
        in_specs=[block, block, whole(w_out.shape), whole(gain.shape), whole(wcat.shape), thin,
                  pl.BlockSpec((tile, 2), lambda i: (i, 0))],
        out_specs=[block, block, thin, pl.BlockSpec((tile, 256), lambda i: (i, 0))],
        out_shape=[jax.ShapeDtypeStruct((rows, width), F32), jax.ShapeDtypeStruct((rows, width), BF),
                   jax.ShapeDtypeStruct((rows, 128), F32), jax.ShapeDtypeStruct((rows, 256), BF)],
        compiler_params=params(),
        cost_estimate=pl.CostEstimate(flops=2 * rows * width * width, bytes_accessed=12 * rows * width, transcendentals=0),
        name="gates",
    )(x, o, w_out, gain, wcat, prev, routes)


def dispatch_kernel(slot_ref, rows_ref, *refs, capacity):
    out_ref = refs[-1]
    width = rows_ref.shape[1]
    ids = pl.program_id(0) * capacity + lax.broadcasted_iota(jnp.int32, (capacity, 1), 0)
    hot = [jnp.where(ids == slot_ref[k:k + 1, :], 1.0, 0.0).astype(BF) for k in range(2)]
    out_ref[0, :, :width] = dot(hot[0] + hot[1], rows_ref[...]).astype(BF)
    if len(refs) > 1:
        out_ref[0, :, width:] = (dot(hot[0], refs[0][:, :128]) + dot(hot[1], refs[0][:, 128:])).astype(BF)


def dispatch(slots, rows, ext, destinations, capacity):
    count, width = rows.shape
    extra = () if ext is None else (ext,)
    out_width = width + (128 if extra else 0)
    return pl.pallas_call(
        functools.partial(dispatch_kernel, capacity=capacity),
        grid=(destinations,),
        in_specs=[whole(slots.shape), whole(rows.shape)] + [whole(a.shape) for a in extra],
        out_specs=pl.BlockSpec((1, capacity, out_width), lambda i: (i, 0, 0)),
        out_shape=jax.ShapeDtypeStruct((destinations, capacity, out_width), BF),
        compiler_params=params(),
        cost_estimate=pl.CostEstimate(flops=2 * destinations * capacity * count * width, bytes_accessed=4 * count * width,
                                      transcendentals=0),
        name="dispatch_rows" if extra else "dispatch_grads",
    )(slots, rows, *extra)


def ffn_fwd_kernel(j_ref, a_ref, wg_ref, wu_ref, wd_ref, hid_ref, act_ref, slope_ref, out_ref, acc_ref):
    width = wg_ref.shape[1]
    a = a_ref[:, :width]
    gate, up = dot(a, wg_ref[0]), dot(a, wu_ref[0])
    sig = jax.nn.sigmoid(gate)
    act = gate * sig
    hidden = (act * up).astype(BF)
    hid_ref[...] = hidden
    act_ref[...] = act.astype(BF)
    slope_ref[...] = (up * sig * (1.0 + gate * (1.0 - sig))).astype(BF)
    made = dot(hidden, wd_ref[0])
    step = pl.program_id(0)

    @pl.when(step == 0)
    def _():
        acc_ref[...] = made

    @pl.when(step > 0)
    def _():
        acc_ref[...] += made

    @pl.when(step == pl.num_programs(0) - 1)
    def _():
        out_ref[...] = acc_ref[...].astype(BF)


def ffn_fwd(j, a, w_gate, w_up, w_down, tile=256):
    rows = a.shape[0]
    _, width, ff = w_gate.shape
    col = pl.BlockSpec((1, width, tile), lambda i, j: (j[0], 0, i))
    row = pl.BlockSpec((1, tile, width), lambda i, j: (j[0], i, 0))
    mid = pl.BlockSpec((rows, tile), lambda i, j: (0, i))
    return pl.pallas_call(
        ffn_fwd_kernel,
        grid_spec=pltpu.PrefetchScalarGridSpec(
            num_scalar_prefetch=1, grid=(ff // tile,),
            in_specs=[whole(a.shape), col, col, row],
            out_specs=[mid, mid, mid, whole((rows, width))],
            scratch_shapes=[pltpu.VMEM((rows, width), F32)]),
        out_shape=[jax.ShapeDtypeStruct((rows, ff), BF)] * 3 + [jax.ShapeDtypeStruct((rows, width), BF)],
        compiler_params=params(),
        cost_estimate=pl.CostEstimate(flops=6 * rows * width * ff, bytes_accessed=6 * rows * ff + 6 * width * ff,
                                      transcendentals=rows * ff),
        name="ffn_fwd",
    )(j, a, w_gate, w_up, w_down)


def ffn_bwd_kernel(j_ref, g_ref, a_ref, act_ref, slope_ref, wg_ref, wu_ref, wd_ref, dg_ref, du_ref, dout_ref, drow_ref, acc_ref):
    width = g_ref.shape[1]
    step = pl.program_id(0)

    @pl.when(step == 0)
    def _():
        gate = jnp.sum(a_ref[...].astype(F32), axis=1, keepdims=True)
        dout_ref[...] = (g_ref[...].astype(F32) * gate).astype(BF)

    dh = dot(dout_ref[...], wd_ref[0], NT)
    du = (dh * act_ref[...].astype(F32)).astype(BF)
    dg = (dh * slope_ref[...].astype(F32)).astype(BF)
    du_ref[...] = du
    dg_ref[...] = dg
    back = dot(dg, wg_ref[0], NT) + dot(du, wu_ref[0], NT)

    @pl.when(step == 0)
    def _():
        acc_ref[...] = back

    @pl.when(step > 0)
    def _():
        acc_ref[...] += back

    @pl.when(step == pl.num_programs(0) - 1)
    def _():
        drow_ref[...] = acc_ref[...].astype(BF)


def ffn_bwd(j, g, a, act, slope, w_gate, w_up, w_down, tile=256):
    rows, width = g.shape
    ff = w_gate.shape[2]
    col = pl.BlockSpec((1, width, tile), lambda i, j: (j[0], 0, i))
    row = pl.BlockSpec((1, tile, width), lambda i, j: (j[0], i, 0))
    mid = pl.BlockSpec((rows, tile), lambda i, j: (0, i))
    gate = pl.BlockSpec((rows, 128), lambda i, j: (0, width // 128))
    return pl.pallas_call(
        ffn_bwd_kernel,
        grid_spec=pltpu.PrefetchScalarGridSpec(
            num_scalar_prefetch=1, grid=(ff // tile,),
            in_specs=[whole(g.shape), gate, mid, mid, col, col, row],
            out_specs=[mid, mid, whole((rows, width)), whole((rows, width))],
            scratch_shapes=[pltpu.VMEM((rows, width), F32)]),
        out_shape=[jax.ShapeDtypeStruct((rows, ff), BF)] * 2 + [jax.ShapeDtypeStruct((rows, width), BF)] * 2,
        compiler_params=params(),
        cost_estimate=pl.CostEstimate(flops=6 * rows * width * ff, bytes_accessed=8 * rows * ff + 6 * width * ff,
                                      transcendentals=0),
        name="ffn_bwd",
    )(j, g, a, act, slope, w_gate, w_up, w_down)


def ffn_grad_kernel(a_ref, dout_ref, hid_ref, dg_ref, du_ref, out_ref, at_ref, dt_ref):
    width = dout_ref.shape[1]

    @pl.when(pl.program_id(0) == 0)
    def _():
        at_ref[...] = a_ref[:, :width].T
        dt_ref[...] = dout_ref[...].T

    out_ref[0] = dot(at_ref[...], dg_ref[...]).astype(BF)
    out_ref[1] = dot(at_ref[...], du_ref[...]).astype(BF)
    out_ref[2] = dot(dt_ref[...], hid_ref[...]).astype(BF)


def ffn_grad(a, dout, hidden, dg, du, tile=256):
    rows, width = dout.shape
    ff = dg.shape[1]
    mid = pl.BlockSpec((rows, tile), lambda i: (0, i))
    return pl.pallas_call(
        ffn_grad_kernel,
        grid=(ff // tile,),
        in_specs=[whole(a.shape), whole(dout.shape), mid, mid, mid],
        out_specs=pl.BlockSpec((3, width, tile), lambda i: (0, 0, i)),
        out_shape=jax.ShapeDtypeStruct((3, width, ff), BF),
        scratch_shapes=[pltpu.VMEM((width, rows), BF)] * 2,
        compiler_params=params(),
        cost_estimate=pl.CostEstimate(flops=6 * rows * width * ff, bytes_accessed=6 * rows * ff + 6 * width * ff,
                                      transcendentals=0),
        name="ffn_grad",
    )(a, dout, hidden, dg, du)


def combine_kernel(made_ref, back_ref, slot_ref, routes_ref, aux_ref, x2_ref, h2_ref, g_ref, gain_ref, wcat_ref, v_ref, w_ref,
                   mixed_ref, prev_ref, dx2_ref, da_ref, do_ref, cat_ref, sums_ref, *, experts):
    step = pl.program_id(0)
    lane = lane_iota()
    aux = aux_ref[...]
    h2 = h2_ref[...].astype(F32)
    g = g_ref[...].astype(F32)
    x2 = x2_ref[...]
    r2 = rms_scale(x2)
    slot_total = made_ref.shape[0]
    slot_ids = lane_iota(slot_total)
    hot = [jnp.where(slot_ids == slot_ref[:, k:k + 1], 1.0, 0.0).astype(BF) for k in range(2)]
    gate = [pick(aux, lane, experts + k) for k in range(2)]
    alpha = [[pick(aux, lane, experts + 2 + 2 * c + k) for k in range(2)] for c in range(2)]
    route = [routes_ref[:, k:k + 1] for k in range(2)]
    one = lambda cond: jnp.where(cond, 1.0, 0.0)
    copy = [one(route[k] == FFN_EXP + 1) for k in range(2)]
    const = [[one(route[k] == FFN_EXP + 2 + c) for c in range(2)] for k in range(2)]
    dgate = []
    x3 = x2
    for k in range(2):
        on_h2 = copy[k] + const[k][0] * alpha[0][0] + const[k][1] * alpha[1][0]
        branch = dot(hot[k], made_ref[...]) + on_h2 * h2
        for c in range(2):
            branch = branch + (const[k][c] * alpha[c][1]) * v_ref[c:c + 1, :]
        x3 = x3 + gate[k] * branch
        dgate.append(jnp.sum(g * branch, axis=1, keepdims=True))
    mixed_ref[...] = x3.astype(BF)
    mean = gate[0] * dgate[0] + gate[1] * dgate[1]
    dl = [gate[k] * (dgate[k] - mean) for k in range(2)]
    grads = jnp.where(lane == route[0], dl[0], 0.0) + jnp.where(lane == route[1], dl[1], 0.0)
    prev_ref[...] = grads[:, :experts]
    weight = [gate[0] * const[0][c] + gate[1] * const[1][c] for c in range(2)]
    g_h2 = jnp.sum(g * h2, axis=1, keepdims=True)
    sums = []
    on_g = copy[0] * gate[0] + copy[1] * gate[1]
    for c in range(2):
        da0 = weight[c] * g_h2
        da1 = weight[c] * jnp.sum(g * v_ref[c:c + 1, :], axis=1, keepdims=True)
        mid = alpha[c][0] * da0 + alpha[c][1] * da1
        grads = jnp.where(lane == experts + 2 * c, alpha[c][0] * (da0 - mid), grads)
        grads = jnp.where(lane == experts + 2 * c + 1, alpha[c][1] * (da1 - mid), grads)
        on_g = on_g + alpha[c][0] * weight[c]
        sums.append(jnp.sum((alpha[c][1] * weight[c]) * g, axis=0, keepdims=True))
    low = grads.astype(BF)
    cat = dot(low.T, h2_ref[...])
    dh2 = dot(low, wcat_ref[...], NT) + on_g * g + dot(hot[0] + hot[1], back_ref[...])
    sums.append(jnp.sum(dh2 * x2 * r2, axis=0, keepdims=True))
    u = dh2 * gain_ref[...]
    dx2 = g + r2 * (u - x2 * (r2 * r2) * jnp.mean(u * x2, axis=-1, keepdims=True))
    dx2_ref[...] = dx2
    da = dx2.astype(BF)
    da_ref[...] = da
    do_ref[...] = dot(da, w_ref[...], NT).astype(BF)
    parts = jnp.concatenate(sums + [jnp.zeros((8 - len(sums), g.shape[1]), F32)], axis=0)

    @pl.when(step == 0)
    def _():
        cat_ref[...] = cat
        sums_ref[...] = parts

    @pl.when(step > 0)
    def _():
        cat_ref[...] += cat
        sums_ref[...] += parts


def combine(made, back, slots, routes, aux, x2, h2, g, gain, wcat, const_v, w_out, experts, tile=256):
    rows, width = x2.shape
    block = pl.BlockSpec((tile, width), lambda i: (i, 0))
    thin = pl.BlockSpec((tile, 128), lambda i: (i, 0))
    two = pl.BlockSpec((tile, 2), lambda i: (i, 0))
    sds = jax.ShapeDtypeStruct
    return pl.pallas_call(
        functools.partial(combine_kernel, experts=experts),
        grid=(rows // tile,),
        in_specs=[whole(made.shape), whole(back.shape), two, two, thin, block, block, block, whole(gain.shape),
                  whole(wcat.shape), whole(const_v.shape), whole(w_out.shape)],
        out_specs=[block, pl.BlockSpec((tile, experts), lambda i: (i, 0)), block, block, block, whole((128, width)),
                   whole((8, width))],
        out_shape=[sds((rows, width), BF), sds((rows, experts), F32), sds((rows, width), F32), sds((rows, width), BF),
                   sds((rows, width), BF), sds((128, width), F32), sds((8, width), F32)],
        compiler_params=params(),
        cost_estimate=pl.CostEstimate(flops=8 * rows * width * made.shape[0], bytes_accessed=30 * rows * width,
                                      transcendentals=0),
        name="combine",
    )(made, back, slots, routes, aux, x2, h2, g, gain, wcat, const_v, w_out)


def prompt_back_kernel(dk_ref, dv_ref, wk_ref, wv_ref, x_ref, out_ref, sum_ref):
    dh = dot(dk_ref[...], wk_ref[...], NT) + dot(dv_ref[...], wv_ref[...], NT)
    out_ref[...] = dh.astype(BF)
    x = x_ref[...].astype(F32)
    part = jnp.sum(dh * (x * rms_scale(x)), axis=0, keepdims=True)
    step = pl.program_id(0)

    @pl.when(step == 0)
    def _():
        sum_ref[...] = part

    @pl.when(step > 0)
    def _():
        sum_ref[...] += part


def prompt_back(dk, dv, w_key, w_value, x, tile=256):
    rows, width = x.shape
    block = pl.BlockSpec((tile, width), lambda i: (i, 0))
    return pl.pallas_call(
        prompt_back_kernel,
        grid=(rows // tile,),
        in_specs=[block, block, whole(w_key.shape), whole(w_value.shape), block],
        out_specs=[block, whole((1, width))],
        out_shape=[jax.ShapeDtypeStruct((rows, width), BF), jax.ShapeDtypeStruct((1, width), F32)],
        compiler_params=params(),
        cost_estimate=pl.CostEstimate(flops=4 * rows * width * width, bytes_accessed=8 * rows * width, transcendentals=0),
        name="prompt_back",
    )(dk, dv, w_key, w_value, x)


def own_back_kernel(dq_ref, dk_ref, dv_ref, wq_ref, wk_ref, wv_ref, x_ref, out_ref, sum_ref):
    step = pl.program_id(0)
    x = x_ref[...].astype(F32)
    xr = x * rms_scale(x)

    @pl.when(step == 0)
    def _():
        sum_ref[...] = jnp.zeros_like(sum_ref)

    def put(dh):
        out_ref[...] = dh
        sum_ref[...] += jnp.sum(dh * xr, axis=0, keepdims=True)

    @pl.when(step < pl.num_programs(0) // 2)
    def _():
        put(dot(dq_ref[...], wq_ref[...], NT))

    @pl.when(step >= pl.num_programs(0) // 2)
    def _():
        put(dot(dq_ref[...], wq_ref[...], NT) + dot(dk_ref[...], wk_ref[...], NT) + dot(dv_ref[...], wv_ref[...], NT))


def own_back(dq, dk, dv, w_query, w_key, w_value, x, tile=256):
    rows, width = x.shape
    block = pl.BlockSpec((tile, width), lambda i: (i, 0))
    half = rows // 2 // tile
    first = (dk.shape[0] - rows // 2) // tile
    key = pl.BlockSpec((tile, width), lambda i: (first + jnp.maximum(i - half, 0), 0))
    return pl.pallas_call(
        own_back_kernel,
        grid=(rows // tile,),
        in_specs=[block, key, key] + [whole(w_key.shape)] * 3 + [block],
        out_specs=[block, whole((1, width))],
        out_shape=[jax.ShapeDtypeStruct((rows, width), F32), jax.ShapeDtypeStruct((1, width), F32)],
        compiler_params=params(),
        cost_estimate=pl.CostEstimate(flops=4 * rows * width * width, bytes_accessed=8 * rows * width, transcendentals=0),
        name="own_back",
    )(dq, dk, dv, w_query, w_key, w_value, x)


def weight_back_kernel(hp_ref, ho_ref, dq_ref, dk_ref, dv_ref, out_ref, acc_ref, *, prompt_steps, own_steps):
    step = pl.program_id(0)
    half = own_steps // 2

    @pl.when(step == 0)
    def _():
        acc_ref[...] = jnp.zeros_like(acc_ref)

    @pl.when(step < prompt_steps)
    def _():
        ht = hp_ref[...].T
        acc_ref[1] += dot(ht, dk_ref[...])
        acc_ref[2] += dot(ht, dv_ref[...])

    @pl.when(step >= prompt_steps)
    def _():
        ht = ho_ref[...].T
        acc_ref[0] += dot(ht, dq_ref[...])

        @pl.when(step >= prompt_steps + half)
        def _():
            acc_ref[1] += dot(ht, dk_ref[...])
            acc_ref[2] += dot(ht, dv_ref[...])

    @pl.when(step == pl.num_programs(0) - 1)
    def _():
        out_ref[...] = acc_ref[...].astype(BF)


def weight_back(hp, ho, dq, dk, dv, tile=256):
    rows, width = ho.shape
    ps, os_ = hp.shape[0] // tile, rows // tile
    half = os_ // 2
    prompt = pl.BlockSpec((tile, width), lambda i: (jnp.minimum(i, ps - 1), 0))
    own = pl.BlockSpec((tile, width), lambda i: (jnp.maximum(i - ps, 0), 0))
    key = pl.BlockSpec((tile, width), lambda i: (jnp.where(i < ps + half, jnp.minimum(i, ps - 1), i - half), 0))
    return pl.pallas_call(
        functools.partial(weight_back_kernel, prompt_steps=ps, own_steps=os_),
        grid=(ps + os_,),
        in_specs=[prompt, own, own, key, key],
        out_specs=whole((3, width, width)),
        out_shape=jax.ShapeDtypeStruct((3, width, width), BF),
        scratch_shapes=[pltpu.VMEM((3, width, width), F32)],
        compiler_params=params(),
        cost_estimate=pl.CostEstimate(flops=12 * rows * width * width, bytes_accessed=12 * rows * width, transcendentals=0),
        name="weight_back",
    )(hp, ho, dq, dk, dv)


def token_back_kernel(own_ref, got_ref, x_ref, dx2_ref, gain_ref, out_ref):
    x = x_ref[...].astype(F32)
    r1 = rms_scale(x)

    def put(dh):
        u = dh * gain_ref[...]
        out_ref[...] = dx2_ref[...] + r1 * (u - x * (r1 * r1) * jnp.mean(u * x, axis=-1, keepdims=True))

    step = pl.program_id(0)

    @pl.when(step < pl.num_programs(0) // 2)
    def _():
        put(own_ref[...] + jnp.sum(got_ref[...].astype(F32), axis=0))

    @pl.when(step >= pl.num_programs(0) // 2)
    def _():
        put(own_ref[...])


def token_back(own, got, x, dx2, gain, tile=256):
    rows, width = x.shape
    block = pl.BlockSpec((tile, width), lambda i: (i, 0))
    half = rows // 2 // tile
    return pl.pallas_call(
        token_back_kernel,
        grid=(rows // tile,),
        in_specs=[block, pl.BlockSpec((got.shape[0], tile, width), lambda i: (0, jnp.minimum(i, half - 1), 0)), block, block,
                  whole(gain.shape)],
        out_specs=block,
        out_shape=jax.ShapeDtypeStruct((rows, width), F32),
        compiler_params=params(),
        cost_estimate=pl.CostEstimate(flops=10 * rows * width, bytes_accessed=14 * rows * width, transcendentals=0),
        name="token_back",
    )(own, got, x, dx2, gain)


def slot_table(routes_t, priority, groups, capacity):
    ids = jnp.arange(FFN_EXP, dtype=jnp.int32)
    picked = routes_t[:, None, :] == ids[None, :, None]
    assigned = jnp.any(picked, axis=0).astype(BF)
    earlier = (priority[:, None] < priority[None, :]).astype(BF)
    rank_table = jnp.dot(assigned, earlier, preferred_element_type=F32)
    rank = jnp.sum(jnp.where(picked, rank_table[None], 0.0), axis=1).astype(jnp.int32)
    place = (routes_t % groups) * (FFN_EXP // groups) + routes_t // groups
    return jnp.where((routes_t < FFN_EXP) & (rank < capacity), place * capacity + rank, -1)


def local(
    tokens, prev_logits, routes, priority, norm_attn, w_query, w_key, w_value, w_out, norm_ffn, router, const_w, const_v,
    w_gate, w_up, w_down, cotangent,
):
    rows, width = tokens.shape
    experts = prev_logits.shape[1]
    dp = lax.axis_size("dp")
    expert_devices = lax.axis_size("expert")
    pair = w_gate.shape[0]
    capacity = 9 * rows * routes.shape[1] // (8 * experts)
    prompt_dev = PROMPT // expert_devices
    ff = w_gate.shape[2]
    e = lax.axis_index("expert").astype(jnp.int32).reshape(1)
    j = (lax.axis_index("dp") % pair).astype(jnp.int32).reshape(1)
    members = pair * expert_devices
    everyone = ("dp", "expert")
    exchange = [list(range(p * members, (p + 1) * members)) for p in range(dp // pair)]
    alike = [list(range(q, dp, pair)) for q in range(pair)]
    pairs = [list(range(p * pair, (p + 1) * pair)) for p in range(dp // pair)]

    def swap(x):
        return lax.all_to_all(x, everyone, split_axis=0, concat_axis=0, axis_index_groups=exchange, tiled=True)

    cos, sin = (jnp.asarray(t) for t in angle_tables())
    gain1, gain2 = norm_attn[None, :], norm_ffn[None, :]

    prompt_x = lax.all_gather(tokens[:prompt_dev], "expert", axis=0, tiled=True)
    slots_t = slot_table(routes.T, priority, pair, capacity)
    slots = slots_t.T
    grads_in = swap(dispatch(slots_t, cotangent, None, members, capacity)).reshape(-1, width)
    h_own, q, k_own, v_own = project(e, tokens, gain1, (w_query, w_key, w_value), cos, sin, True)
    h_prompt, k_prompt, v_prompt = project(e, prompt_x, gain1, (w_key, w_value), cos, sin, False)
    o, lse = attn_fwd(e, q, k_own, v_own, k_prompt, v_prompt)

    wcat = jnp.concatenate(
        [router, const_w.transpose(1, 0, 2).reshape(width, -1), jnp.zeros((width, 128 - experts - 4), BF)], axis=1
    )
    prev = jnp.pad(prev_logits, ((0, 0), (0, 128 - experts)))
    x2, h2, aux, ext = gates(tokens, o, w_out, gain2, wcat, prev, routes, experts)
    arrived = swap(dispatch(slots_t, h2, ext, members, capacity)).reshape(-1, width + 128)
    hidden, act, slope, made = ffn_fwd(j, arrived, w_gate, w_up, w_down)
    made = swap(made.reshape(members, capacity, width)).reshape(-1, width)
    dg, du, dout, drow = ffn_bwd(j, grads_in, arrived, act, slope, w_gate, w_up, w_down)
    drow = swap(drow.reshape(members, capacity, width)).reshape(-1, width)
    ffn_sum = ffn_grad(arrived, dout, hidden, dg, du)
    ffn_sum = lax.psum_scatter(ffn_sum, "dp", scatter_dimension=2, axis_index_groups=alike, tiled=True)

    mixed, grad_prev, dx2, da, do, cat, sums = combine(
        made, drow, slots, routes, aux, x2, h2, cotangent, gain2, wcat, const_v, w_out, experts
    )
    grad_out = jnp.dot(o.T, da, preferred_element_type=F32).astype(BF)
    dq, dk, dv = attn_bwd(e, q, do, o, lse, k_own, v_own, k_prompt, v_prompt, cos, sin)
    dh_prompt, sum_p = prompt_back(dk, dv, w_key, w_value, prompt_x)
    got = lax.all_to_all(
        dh_prompt.reshape(expert_devices, prompt_dev, width), "expert", split_axis=0, concat_axis=0, tiled=True
    )
    dh_own, sum_o = own_back(dq, dk, dv, w_query, w_key, w_value, tokens)
    grad_w = weight_back(h_prompt, h_own, dq, dk, dv)
    small = jnp.concatenate([cat[:experts + 4], sums[:3], sum_p + sum_o], axis=0).astype(BF)
    grad_w, grad_out, small = lax.psum((grad_w, grad_out, small), everyone)
    grad_w, grad_out, small = grad_w.astype(F32), grad_out.astype(F32), small.astype(F32)
    grad_tokens = token_back(dh_own, got, tokens, dx2, gain1)

    ffn_sum = ffn_sum.reshape(3, width, pair, -1).transpose(2, 0, 1, 3)
    ffn_sum = lax.all_to_all(ffn_sum, "dp", split_axis=0, concat_axis=0, axis_index_groups=pairs, tiled=True)
    ffn_sum = ffn_sum.astype(F32)
    n = experts
    return (
        mixed,
        grad_tokens,
        grad_prev,
        small[n + 7],
        grad_w[0],
        grad_w[1],
        grad_w[2],
        grad_out,
        small[n + 6],
        small[:n].T,
        small[n:n + 4].reshape(2, 2, width).transpose(0, 2, 1),
        small[n + 4:n + 6],
        ffn_sum[:, 0],
        ffn_sum[:, 1],
        ffn_sum[:, 2].transpose(0, 2, 1),
    )


def solution(mesh):
    block = P(("dp", "expert"), None)
    in_specs = (block, block, block, P(("dp", "expert"))) + (P(),) * 9 + (P("expert", None, None),) * 3 + (block,)
    out_specs = (block, block, block) + (P(),) * 9 + (
        P("expert", None, "dp"), P("expert", None, "dp"), P("expert", "dp", None),
    )
    return jax.shard_map(local, mesh=mesh, in_specs=in_specs, out_specs=out_specs, check_vma=False)
```

```python
import functools

import jax
import jax.numpy as jnp
import numpy as np
from jax import lax
from jax.experimental import pallas as pl
from jax.experimental.pallas import tpu as pltpu
from jax.sharding import PartitionSpec as P

HEADS = 12
FFN_EXP = 8
PROMPT = 2048
NCONT = 8
CONT = 256

epsilon = 1e-06
LOG2E = 1.4426950408889634
F32 = jnp.float32
BF = jnp.bfloat16
NN = (((1,), (0,)), ((), ()))
NT = (((1,), (1,)), ((), ()))
VMEM_LIMIT = 56 << 20


def dot(a, b, dims=NN):
    return lax.dot_general(a, b, dims, preferred_element_type=F32)


def params(**kw):
    return pltpu.CompilerParams(vmem_limit_bytes=VMEM_LIMIT, **kw)


def whole(shape):
    return pl.BlockSpec(shape, lambda *_: (0,) * len(shape))


def rms_scale(x):
    return lax.rsqrt(jnp.mean(x * x, axis=-1, keepdims=True) + epsilon)


def angle_tables():
    positions = np.arange(PROMPT + CONT, dtype=np.float32)
    frequency = np.exp(
        np.float32(-np.log(10000.0)) * np.arange(32, dtype=np.float32) * np.float32(2.0) / np.float32(64)
    ).astype(np.float32)
    angle = (positions[:, None] * frequency[None, :]).astype(np.float64)
    cosine = np.cos(angle).astype(np.float32)
    sine = np.sin(angle).astype(np.float32)
    return (
        np.concatenate([cosine] * 4, axis=1),
        np.concatenate([-sine, sine, -sine, sine], axis=1),
    )


def lane_iota(width=128):
    return lax.broadcasted_iota(jnp.int32, (1, width), 1)


def swap_halves(x):
    return jnp.where(lane_iota() % 64 < 32, pltpu.roll(x, 96, 1), pltpu.roll(x, 32, 1))


def project_kernel(e_ref, x_ref, gain_ref, *refs, count):
    weights, (cos_ref, sin_ref), (h_ref, *outs) = refs[:count], refs[count:count + 2], refs[count + 2:]
    x = x_ref[...].astype(F32)
    h = (x * rms_scale(x) * gain_ref[...]).astype(BF)
    h_ref[...] = h
    cosine, sine = cos_ref[...], sin_ref[...]
    for n, (w_ref, out_ref) in enumerate(zip(weights, outs)):
        full = dot(h, w_ref[...])
        if n == count - 1:
            out_ref[...] = full.astype(BF)
            continue
        for i in range(full.shape[1] // 128):
            part = full[:, i * 128:(i + 1) * 128]
            out_ref[:, i * 128:(i + 1) * 128] = (part * cosine + swap_halves(part) * sine).astype(BF)


def project(e, x, gain, weights, cos, sin, own, tile=256):
    rows, width = x.shape
    block = pl.BlockSpec((tile, width), lambda i, *_: (i, 0))
    half = rows // 2 // tile

    def position(i, e_ref):
        if not own:
            return (i, 0)
        return (jnp.where(i < half, e_ref[0] * half + i, PROMPT // tile), 0)

    table = pl.BlockSpec((tile, 128), position)
    return pl.pallas_call(
        functools.partial(project_kernel, count=len(weights)),
        grid_spec=pltpu.PrefetchScalarGridSpec(
            num_scalar_prefetch=1,
            grid=(rows // tile,),
            in_specs=[block, whole((1, width))] + [whole(weights[0].shape)] * len(weights) + [table, table],
            out_specs=[block] * (len(weights) + 1),
        ),
        out_shape=[jax.ShapeDtypeStruct((rows, width), BF)] * (len(weights) + 1),
        compiler_params=params(),
        cost_estimate=pl.CostEstimate(
            flops=2 * rows * width * width * len(weights), bytes_accessed=2 * rows * width * 6, transcendentals=0
        ),
        name="project_own" if own else "project_prompt",
    )(e, x, gain, *weights, cos, sin)


def attn_fwd_kernel(e_ref, q_ref, ko_ref, vo_ref, kp_ref, vp_ref, o_ref, lse_ref, vt_ref, qm_ref, m_ref, acc_ref, *, chunk, tile, scale):
    e = e_ref[0]
    rows = q_ref.shape[0]
    half = rows // 2
    npr = kp_ref.shape[0]
    nchunk = npr // chunk
    lane = lax.broadcasted_iota(jnp.int32, (1, 128), 1)
    low = lane < 64
    c = scale * LOG2E
    zero = jnp.zeros((), BF)
    q = q_ref[...]
    qm_ref[0] = jnp.where(low, q, zero)
    qm_ref[1] = jnp.where(low, zero, q)
    ones = jnp.ones((16, npr + rows), BF)
    for r, n, ref in ((0, npr, vp_ref), (npr, rows, vo_ref)):
        vt = ref[...].T
        vt_ref[0, :64, r:r + n] = vt[:64]
        vt_ref[1, :64, r:r + n] = vt[64:]
    vt_ref[0, 64:, :] = ones
    vt_ref[1, 64:, :] = ones
    tri = lax.broadcasted_iota(jnp.int32, (tile, tile), 0) <= lax.broadcasted_iota(jnp.int32, (tile, tile), 1)

    def first(q0, qn, k, vts):
        for h in range(2):
            s = dot(k, qm_ref[h, q0:q0 + qn, :], NT)
            s = s * c
            s = jnp.where(tri, s, -1e30)
            mx = jnp.max(s, axis=0, keepdims=True)
            p = jnp.exp2(s - mx).astype(BF)
            m_ref[h, 0:1, q0:q0 + qn] = mx
            acc_ref[h, :, q0:q0 + qn] = dot(vts[h], p)

    def step(blocks, k, vts):
        ss = [[dot(k, qm_ref[h, q0:q0 + qn, :], NT) for h in range(2)] for q0, qn in blocks]
        for (q0, qn), sb in zip(blocks, ss):
            for h in range(2):
                s = sb[h] * c
                mx = jnp.max(s, axis=0, keepdims=True)
                m = m_ref[h, 0:1, q0:q0 + qn]
                mn = jnp.maximum(m, mx)
                p = jnp.exp2(s - mn).astype(BF)
                m_ref[h, 0:1, q0:q0 + qn] = mn
                acc_ref[h, :, q0:q0 + qn] = acc_ref[h, :, q0:q0 + qn] * jnp.exp2(m - mn) + dot(vts[h], p)

    for j in range(rows // tile):
        r0 = j * tile
        first(r0, tile, ko_ref[r0:r0 + tile, :], [vt_ref[h, :, npr + r0:npr + r0 + tile] for h in range(2)])
    for j in range(1, half // tile):
        for i in range(j):
            r0 = i * tile
            step([(j * tile, tile)], ko_ref[r0:r0 + tile, :], [vt_ref[h, :, npr + r0:npr + r0 + tile] for h in range(2)])

    def body(ci, blocks):
        r0 = pl.multiple_of(ci * chunk, chunk)
        step(blocks, kp_ref[pl.ds(r0, chunk), :], [vt_ref[h, :, pl.ds(r0, chunk)] for h in range(2)])

    ne = e * half // chunk

    @pl.loop(0, ne)
    def _(ci):
        body(ci, [(0, half), (half, half)])

    @pl.loop(ne, nchunk)
    def _(ci):
        body(ci, [(half, half)])

    outs = []
    for h in range(2):
        l = acc_ref[h, 64:65, :]
        outs.append(acc_ref[h, :64, :] / l)
        lse_ref[0, h:h + 1, :] = m_ref[h, 0:1, :] + jnp.log2(l)
    o_ref[...] = jnp.concatenate(outs, axis=0).T.astype(BF)


def attn_fwd(e, q, ko, vo, kp, vp, *, chunk=512, tile=256):
    rows, width = q.shape
    npr = kp.shape[0]
    pairs = width // 128
    own = pl.BlockSpec((rows, 128), lambda i, *_: (0, i))
    pr = pl.BlockSpec((npr, 128), lambda i, *_: (0, i))
    return pl.pallas_call(
        functools.partial(attn_fwd_kernel, chunk=chunk, tile=tile, scale=0.125),
        grid_spec=pltpu.PrefetchScalarGridSpec(
            num_scalar_prefetch=1, grid=(pairs,),
            in_specs=[own, own, own, pr, pr],
            out_specs=[own, pl.BlockSpec((1, 2, rows), lambda i, *_: (i, 0, 0))],
            scratch_shapes=[pltpu.VMEM((2, 80, npr + rows), BF), pltpu.VMEM((2, rows, 128), BF),
            pltpu.VMEM((2, 8, rows), F32), pltpu.VMEM((2, 80, rows), F32)]),
        out_shape=[jax.ShapeDtypeStruct((rows, width), BF), jax.ShapeDtypeStruct((pairs, 2, rows), F32)],
        compiler_params=params(),
        cost_estimate=pl.CostEstimate(flops=4 * rows * npr * width * 2, bytes_accessed=2 * npr * width * 4, transcendentals=rows * npr * 12),
        name="attn_fwd",
    )(e, q, ko, vo, kp, vp)


def attn_bwd_kernel(e_ref, q_ref, do_ref, o_ref, lse_ref, ko_ref, vo_ref, kp_ref, vp_ref, cos_ref, sin_ref,
               dq_ref, dk_ref, dv_ref,
               kt_ref, dqt_ref, qm_ref, dom_ref, dl_ref, dks_ref, dvs_ref, *, tile, scale):
    e = e_ref[0]
    rows = q_ref.shape[0]
    half = rows // 2
    chunk = half
    npr = kp_ref.shape[0]
    nchunk = npr // chunk
    cont = cos_ref.shape[0] - npr
    lane = lax.broadcasted_iota(jnp.int32, (1, 128), 1)
    low = lane < 64
    c = scale * LOG2E
    zero = jnp.zeros((), BF)
    q = q_ref[...]
    do = do_ref[...]
    qm_ref[0] = jnp.where(low, q, zero)
    qm_ref[1] = jnp.where(low, zero, q)
    dom_ref[0] = jnp.where(low, do, zero)
    dom_ref[1] = jnp.where(low, zero, do)
    prod = (do.astype(F32) * o_ref[...].astype(F32)).T
    dl_ref[0:1, :] = jnp.sum(prod[:64], axis=0, keepdims=True)
    dl_ref[1:2, :] = jnp.sum(prod[64:], axis=0, keepdims=True)
    kt_ref[:, :npr] = kp_ref[...].T
    kt_ref[:, npr:] = ko_ref[...].T
    tri = lax.broadcasted_iota(jnp.int32, (tile, tile), 0) <= lax.broadcasted_iota(jnp.int32, (tile, tile), 1)

    def unrope(x, pos, n):
        first = (lane % 64) < 32
        sw = jnp.where(first, pltpu.roll(x, 96, 1), pltpu.roll(x, 32, 1))
        return x * cos_ref[pl.ds(pos, n), :] - sw * sin_ref[pl.ds(pos, n), :]

    def block(k, v, kt, q0, qn, mask):
        dk = dv = None
        dqs = []
        qs = [qm_ref[h, q0:q0 + qn, :] for h in range(2)]
        dos = [dom_ref[h, q0:q0 + qn, :] for h in range(2)]
        sts = [dot(k, qs[h], NT) for h in range(2)]
        dps = [dot(v, dos[h], NT) for h in range(2)]
        for h in range(2):
            p = jnp.exp2(sts[h] * c - lse_ref[0, h:h + 1, q0:q0 + qn])
            if mask is not None:
                p = jnp.where(mask, p, 0.0)
            ds = (p * (dps[h] - dl_ref[h:h + 1, q0:q0 + qn])).astype(BF)
            dvh = dot(p.astype(BF), dos[h])
            dkh = dot(ds, qs[h])
            dk, dv = (dkh, dvh) if dk is None else (dk + dkh, dv + dvh)
            dqs.append(dot(kt[h * 64:(h + 1) * 64], ds))
        return dk, dv, jnp.concatenate(dqs, axis=0)

    nt = rows // tile
    for i in range(nt):
        r0 = i * tile
        k = ko_ref[r0:r0 + tile, :]
        v = vo_ref[r0:r0 + tile, :]
        kt = kt_ref[:, npr + r0:npr + r0 + tile]
        prompt = r0 < half
        dk = dv = None
        for j in (range(i, nt // 2) if prompt else [i]):
            a, b, dq = block(k, v, kt, j * tile, tile, tri if i == j else None)
            dk, dv = (a, b) if dk is None else (dk + a, dv + b)
            sl = slice(j * tile, (j + 1) * tile)
            if i == 0 or not prompt:
                dqt_ref[:, sl] = dq
            else:
                dqt_ref[:, sl] += dq
        if prompt:
            dks_ref[r0:r0 + tile, :] = dk
            dvs_ref[r0:r0 + tile, :] = dv
        else:
            o0 = npr + r0 - half
            dk_ref[o0:o0 + tile, :] = (unrope(dk, npr, tile) * scale).astype(BF)
            dv_ref[o0:o0 + tile, :] = dv.astype(BF)

    def chunk_step(ci, kind):
        r0 = pl.multiple_of(ci * chunk, chunk)
        k = kp_ref[pl.ds(r0, chunk), :]
        v = vp_ref[pl.ds(r0, chunk), :]
        kt = kt_ref[:, pl.ds(r0, chunk)]
        dk, dv, dq = block(k, v, kt, half, half, None)
        dqt_ref[:, half:] += dq
        if kind == 0:
            a, b, dq = block(k, v, kt, 0, half, None)
            dk, dv = dk + a, dv + b
            dqt_ref[:, :half] += dq
        elif kind == 1:
            dk, dv = dk + dks_ref[...], dv + dvs_ref[...]
        dk_ref[pl.ds(r0, chunk), :] = (unrope(dk, r0, chunk) * scale).astype(BF)
        dv_ref[pl.ds(r0, chunk), :] = dv.astype(BF)

    @pl.loop(0, e)
    def _(ci):
        chunk_step(ci, 0)

    chunk_step(e, 1)

    @pl.loop(e + 1, nchunk)
    def _(ci):
        chunk_step(ci, 2)

    dq = dqt_ref[...].T
    base = pl.multiple_of(e * half, half)
    dq_ref[:half, :] = (unrope(dq[:half], base, half) * scale).astype(BF)
    for r in range(half, rows, cont):
        dq_ref[r:r + cont, :] = (unrope(dq[r:r + cont], npr, cont) * scale).astype(BF)


def attn_bwd(e, q, do, o, lse, ko, vo, kp, vp, cos, sin, *, tile=256):
    rows, width = q.shape
    npr = kp.shape[0]
    keys = npr + rows // 2
    pairs = width // 128
    own = pl.BlockSpec((rows, 128), lambda i, *_: (0, i))
    pr = pl.BlockSpec((npr, 128), lambda i, *_: (0, i))
    al = pl.BlockSpec((keys, 128), lambda i, *_: (0, i))
    tab = pl.BlockSpec(cos.shape, lambda i, *_: (0, 0))
    return pl.pallas_call(
        functools.partial(attn_bwd_kernel, tile=tile, scale=0.125),
        grid_spec=pltpu.PrefetchScalarGridSpec(
            num_scalar_prefetch=1, grid=(pairs,),
            in_specs=[own, own, own, pl.BlockSpec((1, 2, rows), lambda i, *_: (i, 0, 0)), own, own, pr, pr, tab, tab],
            out_specs=[own, al, al],
            scratch_shapes=[pltpu.VMEM((128, npr + rows), BF), pltpu.VMEM((128, rows), F32),
                            pltpu.VMEM((2, rows, 128), BF), pltpu.VMEM((2, rows, 128), BF),
                            pltpu.VMEM((8, rows), F32),
                            pltpu.VMEM((rows // 2, 128), F32), pltpu.VMEM((rows // 2, 128), F32)]),
        out_shape=[jax.ShapeDtypeStruct((rows, width), BF), jax.ShapeDtypeStruct((keys, width), BF),
                   jax.ShapeDtypeStruct((keys, width), BF)],
        compiler_params=params(),
        cost_estimate=pl.CostEstimate(flops=10 * rows * npr * width * 2, bytes_accessed=2 * npr * width * 8, transcendentals=rows * npr * 12),
        name="attn_bwd",
    )(e, q, do, o, lse, ko, vo, kp, vp, cos, sin)


def pick(values, lane, index):
    return jnp.sum(jnp.where(lane == index, values, 0.0), axis=1, keepdims=True)


def softmax_pair(a, b):
    top = jnp.maximum(a, b)
    ea, eb = jnp.exp(a - top), jnp.exp(b - top)
    total = ea + eb
    return ea / total, eb / total


def gate_kernel(x_ref, o_ref, w_ref, gain_ref, wcat_ref, prev_ref, routes_ref, x2_ref, h2_ref, aux_ref, ext_ref, *, experts):
    x2 = x_ref[...].astype(F32) + dot(o_ref[...], w_ref[...])
    x2_ref[...] = x2
    h2 = (x2 * rms_scale(x2) * gain_ref[...]).astype(BF)
    h2_ref[...] = h2
    logits = dot(h2, wcat_ref[...]) + prev_ref[...]
    lane = lane_iota()
    gates = softmax_pair(*[pick(logits, lane, routes_ref[:, k:k + 1]) for k in range(2)])
    aux = logits
    for k in range(2):
        aux = jnp.where(lane == experts + k, gates[k], aux)
    at = experts + 2
    for c in range(2):
        alpha = softmax_pair(*[pick(logits, lane, experts + 2 * c + k) for k in range(2)])
        for k in range(2):
            aux = jnp.where(lane == at + 2 * c + k, alpha[k], aux)
    aux_ref[...] = aux
    for k in range(2):
        parts, left = [], gates[k]
        for _ in range(3):
            part = left.astype(BF)
            parts.append(part.astype(F32))
            left = left - parts[-1]
        spread = jnp.where(lane == 0, parts[0], jnp.where(lane == 1, parts[1], jnp.where(lane == 2, parts[2], 0.0)))
        ext_ref[:, k * 128:(k + 1) * 128] = spread.astype(BF)


def gates(x, o, w_out, gain, wcat, prev, routes, experts, tile=256):
    rows, width = x.shape
    block = pl.BlockSpec((tile, width), lambda i: (i, 0))
    thin = pl.BlockSpec((tile, 128), lambda i: (i, 0))
    return pl.pallas_call(
        functools.partial(gate_kernel, experts=experts),
        grid=(rows // tile,),
        in_specs=[block, block, whole(w_out.shape), whole(gain.shape), whole(wcat.shape), thin,
                  pl.BlockSpec((tile, 2), lambda i: (i, 0))],
        out_specs=[block, block, thin, pl.BlockSpec((tile, 256), lambda i: (i, 0))],
        out_shape=[jax.ShapeDtypeStruct((rows, width), F32), jax.ShapeDtypeStruct((rows, width), BF),
                   jax.ShapeDtypeStruct((rows, 128), F32), jax.ShapeDtypeStruct((rows, 256), BF)],
        compiler_params=params(),
        cost_estimate=pl.CostEstimate(flops=2 * rows * width * width, bytes_accessed=12 * rows * width, transcendentals=0),
        name="gates",
    )(x, o, w_out, gain, wcat, prev, routes)


def dispatch_kernel(slot_ref, rows_ref, *refs, capacity):
    out_ref = refs[-1]
    width = rows_ref.shape[1]
    ids = pl.program_id(0) * capacity + lax.broadcasted_iota(jnp.int32, (capacity, 1), 0)
    hot = [jnp.where(ids == slot_ref[k:k + 1, :], 1.0, 0.0).astype(BF) for k in range(2)]
    out_ref[0, :, :width] = dot(hot[0] + hot[1], rows_ref[...]).astype(BF)
    if len(refs) > 1:
        out_ref[0, :, width:] = (dot(hot[0], refs[0][:, :128]) + dot(hot[1], refs[0][:, 128:])).astype(BF)


def dispatch(slots, rows, ext, destinations, capacity):
    count, width = rows.shape
    extra = () if ext is None else (ext,)
    out_width = width + (128 if extra else 0)
    return pl.pallas_call(
        functools.partial(dispatch_kernel, capacity=capacity),
        grid=(destinations,),
        in_specs=[whole(slots.shape), whole(rows.shape)] + [whole(a.shape) for a in extra],
        out_specs=pl.BlockSpec((1, capacity, out_width), lambda i: (i, 0, 0)),
        out_shape=jax.ShapeDtypeStruct((destinations, capacity, out_width), BF),
        compiler_params=params(),
        cost_estimate=pl.CostEstimate(flops=2 * destinations * capacity * count * width, bytes_accessed=4 * count * width,
                                      transcendentals=0),
        name="dispatch_rows" if extra else "dispatch_grads",
    )(slots, rows, *extra)


def ffn_fwd_kernel(j_ref, a_ref, wg_ref, wu_ref, wd_ref, hid_ref, act_ref, slope_ref, out_ref, acc_ref):
    width = wg_ref.shape[1]
    a = a_ref[:, :width]
    gate, up = dot(a, wg_ref[0]), dot(a, wu_ref[0])
    sig = jax.nn.sigmoid(gate)
    act = gate * sig
    hidden = (act * up).astype(BF)
    hid_ref[...] = hidden
    act_ref[...] = act.astype(BF)
    slope_ref[...] = (up * sig * (1.0 + gate * (1.0 - sig))).astype(BF)
    made = dot(hidden, wd_ref[0])
    step = pl.program_id(0)

    @pl.when(step == 0)
    def _():
        acc_ref[...] = made

    @pl.when(step > 0)
    def _():
        acc_ref[...] += made

    @pl.when(step == pl.num_programs(0) - 1)
    def _():
        out_ref[...] = acc_ref[...].astype(BF)


def ffn_fwd(j, a, w_gate, w_up, w_down, tile=256):
    rows = a.shape[0]
    _, width, ff = w_gate.shape
    col = pl.BlockSpec((1, width, tile), lambda i, j: (j[0], 0, i))
    row = pl.BlockSpec((1, tile, width), lambda i, j: (j[0], i, 0))
    mid = pl.BlockSpec((rows, tile), lambda i, j: (0, i))
    return pl.pallas_call(
        ffn_fwd_kernel,
        grid_spec=pltpu.PrefetchScalarGridSpec(
            num_scalar_prefetch=1, grid=(ff // tile,),
            in_specs=[whole(a.shape), col, col, row],
            out_specs=[mid, mid, mid, whole((rows, width))],
            scratch_shapes=[pltpu.VMEM((rows, width), F32)]),
        out_shape=[jax.ShapeDtypeStruct((rows, ff), BF)] * 3 + [jax.ShapeDtypeStruct((rows, width), BF)],
        compiler_params=params(),
        cost_estimate=pl.CostEstimate(flops=6 * rows * width * ff, bytes_accessed=6 * rows * ff + 6 * width * ff,
                                      transcendentals=rows * ff),
        name="ffn_fwd",
    )(j, a, w_gate, w_up, w_down)


def ffn_bwd_kernel(j_ref, g_ref, a_ref, act_ref, slope_ref, wg_ref, wu_ref, wd_ref, dg_ref, du_ref, dout_ref, drow_ref, acc_ref):
    width = g_ref.shape[1]
    step = pl.program_id(0)

    @pl.when(step == 0)
    def _():
        gate = jnp.sum(a_ref[...].astype(F32), axis=1, keepdims=True)
        dout_ref[...] = (g_ref[...].astype(F32) * gate).astype(BF)

    dh = dot(dout_ref[...], wd_ref[0], NT)
    du = (dh * act_ref[...].astype(F32)).astype(BF)
    dg = (dh * slope_ref[...].astype(F32)).astype(BF)
    du_ref[...] = du
    dg_ref[...] = dg
    back = dot(dg, wg_ref[0], NT) + dot(du, wu_ref[0], NT)

    @pl.when(step == 0)
    def _():
        acc_ref[...] = back

    @pl.when(step > 0)
    def _():
        acc_ref[...] += back

    @pl.when(step == pl.num_programs(0) - 1)
    def _():
        drow_ref[...] = acc_ref[...].astype(BF)


def ffn_bwd(j, g, a, act, slope, w_gate, w_up, w_down, tile=256):
    rows, width = g.shape
    ff = w_gate.shape[2]
    col = pl.BlockSpec((1, width, tile), lambda i, j: (j[0], 0, i))
    row = pl.BlockSpec((1, tile, width), lambda i, j: (j[0], i, 0))
    mid = pl.BlockSpec((rows, tile), lambda i, j: (0, i))
    gate = pl.BlockSpec((rows, 128), lambda i, j: (0, width // 128))
    return pl.pallas_call(
        ffn_bwd_kernel,
        grid_spec=pltpu.PrefetchScalarGridSpec(
            num_scalar_prefetch=1, grid=(ff // tile,),
            in_specs=[whole(g.shape), gate, mid, mid, col, col, row],
            out_specs=[mid, mid, whole((rows, width)), whole((rows, width))],
            scratch_shapes=[pltpu.VMEM((rows, width), F32)]),
        out_shape=[jax.ShapeDtypeStruct((rows, ff), BF)] * 2 + [jax.ShapeDtypeStruct((rows, width), BF)] * 2,
        compiler_params=params(),
        cost_estimate=pl.CostEstimate(flops=6 * rows * width * ff, bytes_accessed=8 * rows * ff + 6 * width * ff,
                                      transcendentals=0),
        name="ffn_bwd",
    )(j, g, a, act, slope, w_gate, w_up, w_down)


def ffn_grad_kernel(a_ref, dout_ref, hid_ref, dg_ref, du_ref, out_ref, at_ref, dt_ref):
    width = dout_ref.shape[1]

    @pl.when(pl.program_id(0) == 0)
    def _():
        at_ref[...] = a_ref[:, :width].T
        dt_ref[...] = dout_ref[...].T

    out_ref[0] = dot(at_ref[...], dg_ref[...]).astype(BF)
    out_ref[1] = dot(at_ref[...], du_ref[...]).astype(BF)
    out_ref[2] = dot(dt_ref[...], hid_ref[...]).astype(BF)


def ffn_grad(a, dout, hidden, dg, du, tile=256):
    rows, width = dout.shape
    ff = dg.shape[1]
    mid = pl.BlockSpec((rows, tile), lambda i: (0, i))
    return pl.pallas_call(
        ffn_grad_kernel,
        grid=(ff // tile,),
        in_specs=[whole(a.shape), whole(dout.shape), mid, mid, mid],
        out_specs=pl.BlockSpec((3, width, tile), lambda i: (0, 0, i)),
        out_shape=jax.ShapeDtypeStruct((3, width, ff), BF),
        scratch_shapes=[pltpu.VMEM((width, rows), BF)] * 2,
        compiler_params=params(),
        cost_estimate=pl.CostEstimate(flops=6 * rows * width * ff, bytes_accessed=6 * rows * ff + 6 * width * ff,
                                      transcendentals=0),
        name="ffn_grad",
    )(a, dout, hidden, dg, du)


def combine_kernel(made_ref, back_ref, slot_ref, routes_ref, aux_ref, x2_ref, h2_ref, g_ref, gain_ref, wcat_ref, v_ref, w_ref,
                   mixed_ref, prev_ref, dx2_ref, da_ref, do_ref, cat_ref, sums_ref, *, experts):
    step = pl.program_id(0)
    lane = lane_iota()
    aux = aux_ref[...]
    h2 = h2_ref[...].astype(F32)
    g = g_ref[...].astype(F32)
    x2 = x2_ref[...]
    r2 = rms_scale(x2)
    slot_total = made_ref.shape[0]
    slot_ids = lane_iota(slot_total)
    hot = [jnp.where(slot_ids == slot_ref[:, k:k + 1], 1.0, 0.0).astype(BF) for k in range(2)]
    gate = [pick(aux, lane, experts + k) for k in range(2)]
    alpha = [[pick(aux, lane, experts + 2 + 2 * c + k) for k in range(2)] for c in range(2)]
    route = [routes_ref[:, k:k + 1] for k in range(2)]
    one = lambda cond: jnp.where(cond, 1.0, 0.0)
    copy = [one(route[k] == FFN_EXP + 1) for k in range(2)]
    const = [[one(route[k] == FFN_EXP + 2 + c) for c in range(2)] for k in range(2)]
    dgate = []
    x3 = x2
    for k in range(2):
        on_h2 = copy[k] + const[k][0] * alpha[0][0] + const[k][1] * alpha[1][0]
        branch = dot(hot[k], made_ref[...]) + on_h2 * h2
        for c in range(2):
            branch = branch + (const[k][c] * alpha[c][1]) * v_ref[c:c + 1, :]
        x3 = x3 + gate[k] * branch
        dgate.append(jnp.sum(g * branch, axis=1, keepdims=True))
    mixed_ref[...] = x3.astype(BF)
    mean = gate[0] * dgate[0] + gate[1] * dgate[1]
    dl = [gate[k] * (dgate[k] - mean) for k in range(2)]
    grads = jnp.where(lane == route[0], dl[0], 0.0) + jnp.where(lane == route[1], dl[1], 0.0)
    prev_ref[...] = grads[:, :experts]
    weight = [gate[0] * const[0][c] + gate[1] * const[1][c] for c in range(2)]
    g_h2 = jnp.sum(g * h2, axis=1, keepdims=True)
    sums = []
    on_g = copy[0] * gate[0] + copy[1] * gate[1]
    for c in range(2):
        da0 = weight[c] * g_h2
        da1 = weight[c] * jnp.sum(g * v_ref[c:c + 1, :], axis=1, keepdims=True)
        mid = alpha[c][0] * da0 + alpha[c][1] * da1
        grads = jnp.where(lane == experts + 2 * c, alpha[c][0] * (da0 - mid), grads)
        grads = jnp.where(lane == experts + 2 * c + 1, alpha[c][1] * (da1 - mid), grads)
        on_g = on_g + alpha[c][0] * weight[c]
        sums.append(jnp.sum((alpha[c][1] * weight[c]) * g, axis=0, keepdims=True))
    low = grads.astype(BF)
    cat = dot(low.T, h2_ref[...])
    dh2 = dot(low, wcat_ref[...], NT) + on_g * g + dot(hot[0] + hot[1], back_ref[...])
    sums.append(jnp.sum(dh2 * x2 * r2, axis=0, keepdims=True))
    u = dh2 * gain_ref[...]
    dx2 = g + r2 * (u - x2 * (r2 * r2) * jnp.mean(u * x2, axis=-1, keepdims=True))
    dx2_ref[...] = dx2
    da = dx2.astype(BF)
    da_ref[...] = da
    do_ref[...] = dot(da, w_ref[...], NT).astype(BF)
    parts = jnp.concatenate(sums + [jnp.zeros((8 - len(sums), g.shape[1]), F32)], axis=0)

    @pl.when(step == 0)
    def _():
        cat_ref[...] = cat
        sums_ref[...] = parts

    @pl.when(step > 0)
    def _():
        cat_ref[...] += cat
        sums_ref[...] += parts


def combine(made, back, slots, routes, aux, x2, h2, g, gain, wcat, const_v, w_out, experts, tile=256):
    rows, width = x2.shape
    block = pl.BlockSpec((tile, width), lambda i: (i, 0))
    thin = pl.BlockSpec((tile, 128), lambda i: (i, 0))
    two = pl.BlockSpec((tile, 2), lambda i: (i, 0))
    sds = jax.ShapeDtypeStruct
    return pl.pallas_call(
        functools.partial(combine_kernel, experts=experts),
        grid=(rows // tile,),
        in_specs=[whole(made.shape), whole(back.shape), two, two, thin, block, block, block, whole(gain.shape),
                  whole(wcat.shape), whole(const_v.shape), whole(w_out.shape)],
        out_specs=[block, pl.BlockSpec((tile, experts), lambda i: (i, 0)), block, block, block, whole((128, width)),
                   whole((8, width))],
        out_shape=[sds((rows, width), BF), sds((rows, experts), F32), sds((rows, width), F32), sds((rows, width), BF),
                   sds((rows, width), BF), sds((128, width), F32), sds((8, width), F32)],
        compiler_params=params(),
        cost_estimate=pl.CostEstimate(flops=8 * rows * width * made.shape[0], bytes_accessed=30 * rows * width,
                                      transcendentals=0),
        name="combine",
    )(made, back, slots, routes, aux, x2, h2, g, gain, wcat, const_v, w_out)


def prompt_back_kernel(dk_ref, dv_ref, wk_ref, wv_ref, x_ref, out_ref, sum_ref):
    dh = dot(dk_ref[...], wk_ref[...], NT) + dot(dv_ref[...], wv_ref[...], NT)
    out_ref[...] = dh.astype(BF)
    x = x_ref[...].astype(F32)
    part = jnp.sum(dh * (x * rms_scale(x)), axis=0, keepdims=True)
    step = pl.program_id(0)

    @pl.when(step == 0)
    def _():
        sum_ref[...] = part

    @pl.when(step > 0)
    def _():
        sum_ref[...] += part


def prompt_back(dk, dv, w_key, w_value, x, tile=256):
    rows, width = x.shape
    block = pl.BlockSpec((tile, width), lambda i: (i, 0))
    return pl.pallas_call(
        prompt_back_kernel,
        grid=(rows // tile,),
        in_specs=[block, block, whole(w_key.shape), whole(w_value.shape), block],
        out_specs=[block, whole((1, width))],
        out_shape=[jax.ShapeDtypeStruct((rows, width), BF), jax.ShapeDtypeStruct((1, width), F32)],
        compiler_params=params(),
        cost_estimate=pl.CostEstimate(flops=4 * rows * width * width, bytes_accessed=8 * rows * width, transcendentals=0),
        name="prompt_back",
    )(dk, dv, w_key, w_value, x)


def own_back_kernel(dq_ref, dk_ref, dv_ref, wq_ref, wk_ref, wv_ref, x_ref, out_ref, sum_ref):
    step = pl.program_id(0)
    x = x_ref[...].astype(F32)
    xr = x * rms_scale(x)

    @pl.when(step == 0)
    def _():
        sum_ref[...] = jnp.zeros_like(sum_ref)

    def put(dh):
        out_ref[...] = dh
        sum_ref[...] += jnp.sum(dh * xr, axis=0, keepdims=True)

    @pl.when(step < pl.num_programs(0) // 2)
    def _():
        put(dot(dq_ref[...], wq_ref[...], NT))

    @pl.when(step >= pl.num_programs(0) // 2)
    def _():
        put(dot(dq_ref[...], wq_ref[...], NT) + dot(dk_ref[...], wk_ref[...], NT) + dot(dv_ref[...], wv_ref[...], NT))


def own_back(dq, dk, dv, w_query, w_key, w_value, x, tile=256):
    rows, width = x.shape
    block = pl.BlockSpec((tile, width), lambda i: (i, 0))
    half = rows // 2 // tile
    first = (dk.shape[0] - rows // 2) // tile
    key = pl.BlockSpec((tile, width), lambda i: (first + jnp.maximum(i - half, 0), 0))
    return pl.pallas_call(
        own_back_kernel,
        grid=(rows // tile,),
        in_specs=[block, key, key] + [whole(w_key.shape)] * 3 + [block],
        out_specs=[block, whole((1, width))],
        out_shape=[jax.ShapeDtypeStruct((rows, width), F32), jax.ShapeDtypeStruct((1, width), F32)],
        compiler_params=params(),
        cost_estimate=pl.CostEstimate(flops=4 * rows * width * width, bytes_accessed=8 * rows * width, transcendentals=0),
        name="own_back",
    )(dq, dk, dv, w_query, w_key, w_value, x)


def weight_back_kernel(hp_ref, ho_ref, o_ref, da_ref, dq_ref, dk_ref, dv_ref, out_ref, acc_ref, *, prompt_steps, own_steps):
    step = pl.program_id(0)
    half = own_steps // 2

    @pl.when(step == 0)
    def _():
        acc_ref[...] = jnp.zeros_like(acc_ref)

    @pl.when(step < prompt_steps)
    def _():
        ht = hp_ref[...].T
        acc_ref[1] += dot(ht, dk_ref[...])
        acc_ref[2] += dot(ht, dv_ref[...])

    @pl.when(step >= prompt_steps)
    def _():
        ht = ho_ref[...].T
        acc_ref[0] += dot(ht, dq_ref[...])
        acc_ref[3] += dot(o_ref[...].T, da_ref[...])

        @pl.when(step >= prompt_steps + half)
        def _():
            acc_ref[1] += dot(ht, dk_ref[...])
            acc_ref[2] += dot(ht, dv_ref[...])

    @pl.when(step == pl.num_programs(0) - 1)
    def _():
        width = acc_ref.shape[1]
        for n in range(4):
            out_ref[n * width:(n + 1) * width, :] = acc_ref[n].astype(BF)
        if out_ref.shape[0] > 4 * width:
            out_ref[4 * width:, :] = jnp.zeros((out_ref.shape[0] - 4 * width, width), BF)


def weight_back(hp, ho, o, da, dq, dk, dv, out_rows, tile=256):
    rows, width = ho.shape
    ps, os_ = hp.shape[0] // tile, rows // tile
    half = os_ // 2
    prompt = pl.BlockSpec((tile, width), lambda i: (jnp.minimum(i, ps - 1), 0))
    own = pl.BlockSpec((tile, width), lambda i: (jnp.maximum(i - ps, 0), 0))
    key = pl.BlockSpec((tile, width), lambda i: (jnp.where(i < ps + half, jnp.minimum(i, ps - 1), i - half), 0))
    return pl.pallas_call(
        functools.partial(weight_back_kernel, prompt_steps=ps, own_steps=os_),
        grid=(ps + os_,),
        in_specs=[prompt, own, own, own, own, key, key],
        out_specs=whole((out_rows, width)),
        out_shape=jax.ShapeDtypeStruct((out_rows, width), BF),
        scratch_shapes=[pltpu.VMEM((4, width, width), F32)],
        compiler_params=params(),
        cost_estimate=pl.CostEstimate(flops=16 * rows * width * width, bytes_accessed=14 * rows * width, transcendentals=0),
        name="weight_back",
    )(hp, ho, o, da, dq, dk, dv)


def token_back_kernel(own_ref, got_ref, x_ref, dx2_ref, gain_ref, out_ref):
    x = x_ref[...].astype(F32)
    r1 = rms_scale(x)

    def put(dh):
        u = dh * gain_ref[...]
        out_ref[...] = dx2_ref[...] + r1 * (u - x * (r1 * r1) * jnp.mean(u * x, axis=-1, keepdims=True))

    step = pl.program_id(0)

    @pl.when(step < pl.num_programs(0) // 2)
    def _():
        put(own_ref[...] + got_ref[...])

    @pl.when(step >= pl.num_programs(0) // 2)
    def _():
        put(own_ref[...])


def token_back(own, got, x, dx2, gain, tile=256):
    rows, width = x.shape
    block = pl.BlockSpec((tile, width), lambda i: (i, 0))
    half = rows // 2 // tile
    return pl.pallas_call(
        token_back_kernel,
        grid=(rows // tile,),
        in_specs=[block, pl.BlockSpec((tile, width), lambda i: (jnp.minimum(i, half - 1), 0)), block, block,
                  whole(gain.shape)],
        out_specs=block,
        out_shape=jax.ShapeDtypeStruct((rows, width), F32),
        compiler_params=params(),
        cost_estimate=pl.CostEstimate(flops=10 * rows * width, bytes_accessed=14 * rows * width, transcendentals=0),
        name="token_back",
    )(own, got, x, dx2, gain)


MESH = pl.DeviceIdType.MESH


def padded_rows(rows, rest):
    unit = 8 * rest * 16
    return -(-rows // unit) * unit


def sum_kernel(g_ref, small_ref, dh_ref, out_ref, small_out_ref, got_ref, half_ref, r0_ref, t1_ref, r1_ref, t2_ref, r2_ref,
               r3_ref, sm_ref, rs_ref, rd0_ref, td_ref, rd1_ref, send_sem, recv_sem, *, rest, chunks):
    dp, ex = lax.axis_index("dp"), lax.axis_index("expert")
    c, x, y, z = ex % 2, ex // 2, dp % 2, dp // 2
    mate = (dp, x * 2 + 1 - c)
    across = (dp, (1 - x) * 2 + c)
    beside = (z * 2 + 1 - y, ex)
    ahead = [((z + d) % rest * 2 + y, ex) for d in range(1, rest)]

    barrier = pltpu.get_barrier_semaphore()
    for peer in [mate, across, beside] + ahead:
        pl.semaphore_signal(barrier, inc=1, device_id=peer, device_id_type=MESH)
    pl.semaphore_wait(barrier, 2 + rest)

    started = []

    def send(src, dst, peer):
        n = len(started)
        copy = pltpu.make_async_remote_copy(src_ref=src, dst_ref=dst, send_sem=send_sem.at[n], recv_sem=recv_sem.at[n],
                                            device_id=peer, device_id_type=MESH)
        copy.start()
        started.append(copy)
        return copy

    rows, width = g_ref.shape
    half = rows // 2
    size = half // chunks
    lanes = width // 2
    q1, q2, q3 = size // 2, size // 4, size // 4 // rest
    part = [pl.ds(0, lanes), pl.ds(lanes, lanes)]
    first, second = [across, beside], [beside, across]
    bit1, bit2 = [x, y], [y, x]

    def ds(at, n):
        return pl.ds(pl.multiple_of(at, 16), n)

    def at1(k, p, bit):
        return k * size + bit * q1

    def spot2(k, p, bit):
        return k * size + bit1[p] * q1 + bit * q2

    def stage0(k):
        return [send(g_ref.at[ds((1 - c) * half + k * size, size)], r0_ref.at[ds(k * size, size)], mate)]

    def stage1(k):
        sl = pl.ds(k * size, size)
        half_ref[sl] = (g_ref[ds(c * half + k * size, size)].astype(F32) + r0_ref[sl].astype(F32)).astype(BF)
        return [send(half_ref.at[ds(at1(k, p, 1 - bit1[p]), q1), part[p]], r1_ref.at[p, pl.ds(k * q1, q1)], first[p])
                for p in range(2)]

    def stage2(k):
        out = []
        for p in range(2):
            sl = pl.ds(k * q1, q1)
            t1_ref[p, sl] = (half_ref[ds(at1(k, p, bit1[p]), q1), part[p]].astype(F32) + r1_ref[p, sl].astype(F32)).astype(BF)
            out.append(send(t1_ref.at[p, ds(k * q1 + (1 - bit2[p]) * q2, q2)], r2_ref.at[p, pl.ds(k * q2, q2)], second[p]))
        return out

    def stage3(k):
        out = []
        for p in range(2):
            sl = pl.ds(k * q2, q2)
            t2_ref[p, sl] = (t1_ref[p, ds(k * q1 + bit2[p] * q2, q2)].astype(F32) + r2_ref[p, sl].astype(F32)).astype(BF)
            for d in range(1, rest):
                to = (z + d) % rest
                out.append(send(t2_ref.at[p, ds(k * q2 + to * q3, q3)], r3_ref.at[p, d - 1, pl.ds(k * q3, q3)], ahead[d - 1]))
        return out

    def stage4(k):
        out = []
        for p in range(2):
            total = t2_ref[p, ds(k * q2 + z * q3, q3)].astype(F32)
            for d in range(1, rest):
                total = total + r3_ref[p, d - 1, pl.ds(k * q3, q3)].astype(F32)
            mine = ds(c * half + spot2(k, p, bit2[p]) + z * q3, q3)
            out_ref[mine, part[p]] = total.astype(BF)
            for d in range(1, rest):
                out.append(send(out_ref.at[mine, part[p]], out_ref.at[mine, part[p]], ahead[d - 1]))
        return out

    def stage5(k):
        out = []
        for p in range(2):
            mine = ds(c * half + spot2(k, p, bit2[p]), q2)
            out.append(send(out_ref.at[mine, part[p]], out_ref.at[mine, part[p]], second[p]))
        return out

    def stage6(k):
        out = []
        for p in range(2):
            mine = ds(c * half + at1(k, p, bit1[p]), q1)
            out.append(send(out_ref.at[mine, part[p]], out_ref.at[mine, part[p]], first[p]))
        return out

    def stage7(k):
        mine = ds(c * half + k * size, size)
        return [send(out_ref.at[mine], out_ref.at[mine], mate)]

    block = got_ref.shape[0]

    def dh_rows(xx, cc):
        return ds((xx * 2 + cc) * block, block)

    def dh0():
        return [send(dh_ref.at[dh_rows(w, 1 - c)], rd0_ref.at[w], mate) for w in range(2)]

    def dh1():
        td_ref[...] = (dh_ref[dh_rows(1 - x, c)].astype(F32) + rd0_ref[1 - x].astype(F32)).astype(BF)
        return [send(td_ref, rd1_ref, across)]

    def dh2():
        got_ref[...] = dh_ref[dh_rows(x, c)].astype(F32) + rd0_ref[x].astype(F32) + rd1_ref[...].astype(F32)
        return []

    def small_pair(n, peer):
        def run():
            if n:
                sm_ref[n] = sm_ref[n - 1] + rs_ref[n - 1]
            else:
                sm_ref[0] = small_ref[...]
            return [send(sm_ref.at[n], rs_ref.at[n], peer)]
        return run

    def small_rest():
        sm_ref[3] = sm_ref[2] + rs_ref[2]
        return [send(sm_ref.at[3], rs_ref.at[2 + d], ahead[d - 1]) for d in range(1, rest)]

    def small_end():
        total = sm_ref[3]
        for d in range(1, rest):
            total = total + rs_ref[2 + d]
        small_out_ref[...] = total
        return []

    lines = [[functools.partial(f, k) for f in (stage0, stage1, stage2, stage3, stage4, stage5, stage6, stage7)]
             for k in range(chunks)]
    lines.insert(1, [dh0, dh1, dh2])
    lines.append([small_pair(0, mate), small_pair(1, across), small_pair(2, beside), small_rest, small_end])
    waiting = [[] for _ in lines]
    for t in range(max(n + len(line) for n, line in enumerate(lines)) + 1):
        for n, line in enumerate(lines):
            s = t - n
            if 0 <= s <= len(line):
                for copy in waiting[n]:
                    copy.wait_recv()
                waiting[n] = line[s]() if s < len(line) else []
    for copy in started:
        copy.wait_send()


def device_sums(g, small, dh, rest, block, chunks):
    rows, width = g.shape
    half, lanes = rows // 2, width // 2
    copies = chunks * (1 + 2 + 2 + 2 * (rest - 1) * 2 + 2 + 2 + 1) + 3 + 3 + rest - 1
    vm = pltpu.VMEM
    vmem = pl.BlockSpec(memory_space=pltpu.VMEM)
    return pl.pallas_call(
        functools.partial(sum_kernel, rest=rest, chunks=chunks),
        in_specs=[vmem] * 3,
        out_specs=[vmem] * 3,
        out_shape=[jax.ShapeDtypeStruct(g.shape, BF), jax.ShapeDtypeStruct(small.shape, F32),
                   jax.ShapeDtypeStruct((block, width), F32)],
        scratch_shapes=[
            vm((half, width), BF), vm((half, width), BF), vm((2, half // 2, lanes), BF), vm((2, half // 2, lanes), BF),
            vm((2, half // 4, lanes), BF), vm((2, half // 4, lanes), BF), vm((2, rest - 1, half // 4 // rest, lanes), BF),
            vm((4,) + small.shape, F32), vm((2 + rest,) + small.shape, F32), vm((2, block, width), BF), vm((block, width), BF),
            vm((block, width), BF), pltpu.SemaphoreType.DMA((copies,)), pltpu.SemaphoreType.DMA((copies,)),
        ],
        compiler_params=params(collective_id=0, has_side_effects=True),
        cost_estimate=pl.CostEstimate(flops=4 * rows * width, bytes_accessed=8 * rows * width, transcendentals=0),
        name="device_sums",
    )(g, small, dh)


def slot_table(routes_t, priority, groups, capacity):
    ids = jnp.arange(FFN_EXP, dtype=jnp.int32)
    picked = routes_t[:, None, :] == ids[None, :, None]
    assigned = jnp.any(picked, axis=0).astype(BF)
    earlier = (priority[:, None] < priority[None, :]).astype(BF)
    rank_table = jnp.dot(assigned, earlier, preferred_element_type=F32)
    rank = jnp.sum(jnp.where(picked, rank_table[None], 0.0), axis=1).astype(jnp.int32)
    place = (routes_t % groups) * (FFN_EXP // groups) + routes_t // groups
    return jnp.where((routes_t < FFN_EXP) & (rank < capacity), place * capacity + rank, -1)


def local(
    tokens, prev_logits, routes, priority, norm_attn, w_query, w_key, w_value, w_out, norm_ffn, router, const_w, const_v,
    w_gate, w_up, w_down, cotangent,
):
    rows, width = tokens.shape
    experts = prev_logits.shape[1]
    dp = lax.axis_size("dp")
    expert_devices = lax.axis_size("expert")
    pair = w_gate.shape[0]
    capacity = 9 * rows * routes.shape[1] // (8 * experts)
    prompt_dev = PROMPT // expert_devices
    ff = w_gate.shape[2]
    e = lax.axis_index("expert").astype(jnp.int32).reshape(1)
    j = (lax.axis_index("dp") % pair).astype(jnp.int32).reshape(1)
    members = pair * expert_devices
    everyone = ("dp", "expert")
    exchange = [list(range(p * members, (p + 1) * members)) for p in range(dp // pair)]
    alike = [list(range(q, dp, pair)) for q in range(pair)]
    pairs = [list(range(p * pair, (p + 1) * pair)) for p in range(dp // pair)]

    def swap(x):
        return lax.all_to_all(x, everyone, split_axis=0, concat_axis=0, axis_index_groups=exchange, tiled=True)

    cos, sin = (jnp.asarray(t) for t in angle_tables())
    gain1, gain2 = norm_attn[None, :], norm_ffn[None, :]

    prompt_x = lax.all_gather(tokens[:prompt_dev], "expert", axis=0, tiled=True)
    slots_t = slot_table(routes.T, priority, pair, capacity)
    slots = slots_t.T
    grads_in = swap(dispatch(slots_t, cotangent, None, members, capacity)).reshape(-1, width)
    h_own, q, k_own, v_own = project(e, tokens, gain1, (w_query, w_key, w_value), cos, sin, True)
    h_prompt, k_prompt, v_prompt = project(e, prompt_x, gain1, (w_key, w_value), cos, sin, False)
    o, lse = attn_fwd(e, q, k_own, v_own, k_prompt, v_prompt)

    wcat = jnp.concatenate(
        [router, const_w.transpose(1, 0, 2).reshape(width, -1), jnp.zeros((width, 128 - experts - 4), BF)], axis=1
    )
    prev = jnp.pad(prev_logits, ((0, 0), (0, 128 - experts)))
    x2, h2, aux, ext = gates(tokens, o, w_out, gain2, wcat, prev, routes, experts)
    arrived = swap(dispatch(slots_t, h2, ext, members, capacity)).reshape(-1, width + 128)
    hidden, act, slope, made = ffn_fwd(j, arrived, w_gate, w_up, w_down)
    made = swap(made.reshape(members, capacity, width)).reshape(-1, width)
    dg, du, dout, drow = ffn_bwd(j, grads_in, arrived, act, slope, w_gate, w_up, w_down)
    drow = swap(drow.reshape(members, capacity, width)).reshape(-1, width)
    ffn_sum = ffn_grad(arrived, dout, hidden, dg, du)
    ffn_sum = lax.psum_scatter(ffn_sum, "dp", scatter_dimension=2, axis_index_groups=alike, tiled=True)

    mixed, grad_prev, dx2, da, do, cat, sums = combine(
        made, drow, slots, routes, aux, x2, h2, cotangent, gain2, wcat, const_v, w_out, experts
    )
    dq, dk, dv = attn_bwd(e, q, do, o, lse, k_own, v_own, k_prompt, v_prompt, cos, sin)
    dh_prompt, sum_p = prompt_back(dk, dv, w_key, w_value, prompt_x)
    dh_own, sum_o = own_back(dq, dk, dv, w_query, w_key, w_value, tokens)
    rest = dp // 2
    out_rows = padded_rows(4 * width, rest)
    chunks = max(n for n in (1, 2, 3) if out_rows // 2 % (n * 4 * rest * 16) == 0)
    grad_w = weight_back(h_prompt, h_own, o, da, dq, dk, dv, out_rows)
    n = experts
    small = jnp.concatenate([cat[:n + 4], sums[:3], sum_p + sum_o, jnp.zeros((4, width), F32)], axis=0)
    grad_w, small, got = device_sums(grad_w, small, dh_prompt, rest, prompt_dev, chunks)
    grad_w = grad_w.astype(F32)
    grad_tokens = token_back(dh_own, got, tokens, dx2, gain1)

    ffn_sum = ffn_sum.reshape(3, width, pair, -1).transpose(2, 0, 1, 3)
    ffn_sum = lax.all_to_all(ffn_sum, "dp", split_axis=0, concat_axis=0, axis_index_groups=pairs, tiled=True)
    ffn_sum = ffn_sum.astype(F32)
    return (
        mixed,
        grad_tokens,
        grad_prev,
        small[n + 7],
        grad_w[:width],
        grad_w[width:2 * width],
        grad_w[2 * width:3 * width],
        grad_w[3 * width:4 * width],
        small[n + 6],
        small[:n].T,
        small[n:n + 4].reshape(2, 2, width).transpose(0, 2, 1),
        small[n + 4:n + 6],
        ffn_sum[:, 0],
        ffn_sum[:, 1],
        ffn_sum[:, 2].transpose(0, 2, 1),
    )


def solution(mesh):
    block = P(("dp", "expert"), None)
    in_specs = (block, block, block, P(("dp", "expert"))) + (P(),) * 9 + (P("expert", None, None),) * 3 + (block,)
    out_specs = (block, block, block) + (P(),) * 9 + (
        P("expert", None, "dp"), P("expert", None, "dp"), P("expert", "dp", None),
    )
    return jax.shard_map(local, mesh=mesh, in_specs=in_specs, out_specs=out_specs, check_vma=False)
```

```python
import functools

import jax
import jax.numpy as jnp
import numpy as np
from jax import lax
from jax.experimental import pallas as pl
from jax.experimental.pallas import tpu as pltpu
from jax.sharding import PartitionSpec as P

HEADS = 12
FFN_EXP = 8
PROMPT = 2048
NCONT = 8
CONT = 256

epsilon = 1e-06
LOG2E = 1.4426950408889634
F32 = jnp.float32
BF = jnp.bfloat16
NN = (((1,), (0,)), ((), ()))
NT = (((1,), (1,)), ((), ()))
VMEM_LIMIT = 56 << 20


def dot(a, b, dims=NN):
    return lax.dot_general(a, b, dims, preferred_element_type=F32)


def params(**kw):
    return pltpu.CompilerParams(vmem_limit_bytes=VMEM_LIMIT, **kw)


def whole(shape):
    return pl.BlockSpec(shape, lambda *_: (0,) * len(shape))


def rms_scale(x):
    return lax.rsqrt(jnp.mean(x * x, axis=-1, keepdims=True) + epsilon)


def angle_tables():
    positions = np.arange(PROMPT + CONT, dtype=np.float32)
    frequency = np.exp(
        np.float32(-np.log(10000.0)) * np.arange(32, dtype=np.float32) * np.float32(2.0) / np.float32(64)
    ).astype(np.float32)
    angle = (positions[:, None] * frequency[None, :]).astype(np.float64)
    cosine = np.cos(angle).astype(np.float32)
    sine = np.sin(angle).astype(np.float32)
    return (
        np.concatenate([cosine] * 4, axis=1),
        np.concatenate([-sine, sine, -sine, sine], axis=1),
    )


def lane_iota(width=128):
    return lax.broadcasted_iota(jnp.int32, (1, width), 1)


def swap_halves(x):
    return jnp.where(lane_iota() % 64 < 32, pltpu.roll(x, 96, 1), pltpu.roll(x, 32, 1))


def project_kernel(e_ref, x_ref, gain_ref, *refs, count):
    weights, (cos_ref, sin_ref), (h_ref, *outs) = refs[:count], refs[count:count + 2], refs[count + 2:]
    x = x_ref[...].astype(F32)
    h = (x * rms_scale(x) * gain_ref[...]).astype(BF)
    h_ref[...] = h
    cosine, sine = cos_ref[...], sin_ref[...]
    for n, (w_ref, out_ref) in enumerate(zip(weights, outs)):
        full = dot(h, w_ref[...])
        if n == count - 1:
            out_ref[...] = full.astype(BF)
            continue
        for i in range(full.shape[1] // 128):
            part = full[:, i * 128:(i + 1) * 128]
            out_ref[:, i * 128:(i + 1) * 128] = (part * cosine + swap_halves(part) * sine).astype(BF)


def project(e, x, gain, weights, cos, sin, own, tile=256):
    rows, width = x.shape
    block = pl.BlockSpec((tile, width), lambda i, *_: (i, 0))
    half = rows // 2 // tile

    def position(i, e_ref):
        if not own:
            return (i, 0)
        return (jnp.where(i < half, e_ref[0] * half + i, PROMPT // tile), 0)

    table = pl.BlockSpec((tile, 128), position)
    return pl.pallas_call(
        functools.partial(project_kernel, count=len(weights)),
        grid_spec=pltpu.PrefetchScalarGridSpec(
            num_scalar_prefetch=1,
            grid=(rows // tile,),
            in_specs=[block, whole((1, width))] + [whole(weights[0].shape)] * len(weights) + [table, table],
            out_specs=[block] * (len(weights) + 1),
        ),
        out_shape=[jax.ShapeDtypeStruct((rows, width), BF)] * (len(weights) + 1),
        compiler_params=params(),
        cost_estimate=pl.CostEstimate(
            flops=2 * rows * width * width * len(weights), bytes_accessed=2 * rows * width * 6, transcendentals=0
        ),
        name="project_own" if own else "project_prompt",
    )(e, x, gain, *weights, cos, sin)


def attn_fwd_kernel(e_ref, q_ref, ko_ref, vo_ref, kp_ref, vp_ref, o_ref, lse_ref, vt_ref, qm_ref, m_ref, acc_ref, *, chunk, tile, scale):
    e = e_ref[0]
    rows = q_ref.shape[0]
    half = rows // 2
    npr = kp_ref.shape[0]
    nchunk = npr // chunk
    lane = lax.broadcasted_iota(jnp.int32, (1, 128), 1)
    low = lane < 64
    c = scale * LOG2E
    zero = jnp.zeros((), BF)
    q = q_ref[...]
    qm_ref[0] = jnp.where(low, q, zero)
    qm_ref[1] = jnp.where(low, zero, q)
    ones = jnp.ones((16, npr + rows), BF)
    for r, n, ref in ((0, npr, vp_ref), (npr, rows, vo_ref)):
        vt = ref[...].T
        vt_ref[0, :64, r:r + n] = vt[:64]
        vt_ref[1, :64, r:r + n] = vt[64:]
    vt_ref[0, 64:, :] = ones
    vt_ref[1, 64:, :] = ones
    tri = lax.broadcasted_iota(jnp.int32, (tile, tile), 0) <= lax.broadcasted_iota(jnp.int32, (tile, tile), 1)

    def first(q0, qn, k, vts):
        for h in range(2):
            s = dot(k, qm_ref[h, q0:q0 + qn, :], NT)
            s = s * c
            s = jnp.where(tri, s, -1e30)
            mx = jnp.max(s, axis=0, keepdims=True)
            p = jnp.exp2(s - mx).astype(BF)
            m_ref[h, 0:1, q0:q0 + qn] = mx
            acc_ref[h, :, q0:q0 + qn] = dot(vts[h], p)

    def step(blocks, k, vts):
        ss = [[dot(k, qm_ref[h, q0:q0 + qn, :], NT) for h in range(2)] for q0, qn in blocks]
        for (q0, qn), sb in zip(blocks, ss):
            for h in range(2):
                s = sb[h] * c
                mx = jnp.max(s, axis=0, keepdims=True)
                m = m_ref[h, 0:1, q0:q0 + qn]
                mn = jnp.maximum(m, mx)
                p = jnp.exp2(s - mn).astype(BF)
                m_ref[h, 0:1, q0:q0 + qn] = mn
                acc_ref[h, :, q0:q0 + qn] = acc_ref[h, :, q0:q0 + qn] * jnp.exp2(m - mn) + dot(vts[h], p)

    for j in range(rows // tile):
        r0 = j * tile
        first(r0, tile, ko_ref[r0:r0 + tile, :], [vt_ref[h, :, npr + r0:npr + r0 + tile] for h in range(2)])
    for j in range(1, half // tile):
        for i in range(j):
            r0 = i * tile
            step([(j * tile, tile)], ko_ref[r0:r0 + tile, :], [vt_ref[h, :, npr + r0:npr + r0 + tile] for h in range(2)])

    def body(ci, blocks):
        r0 = pl.multiple_of(ci * chunk, chunk)
        step(blocks, kp_ref[pl.ds(r0, chunk), :], [vt_ref[h, :, pl.ds(r0, chunk)] for h in range(2)])

    ne = e * half // chunk

    @pl.loop(0, ne)
    def _(ci):
        body(ci, [(0, half), (half, half)])

    @pl.loop(ne, nchunk)
    def _(ci):
        body(ci, [(half, half)])

    outs = []
    for h in range(2):
        l = acc_ref[h, 64:65, :]
        outs.append(acc_ref[h, :64, :] / l)
        lse_ref[0, h:h + 1, :] = m_ref[h, 0:1, :] + jnp.log2(l)
    o_ref[...] = jnp.concatenate(outs, axis=0).T.astype(BF)


def attn_fwd(e, q, ko, vo, kp, vp, *, chunk=512, tile=256):
    rows, width = q.shape
    npr = kp.shape[0]
    pairs = width // 128
    own = pl.BlockSpec((rows, 128), lambda i, *_: (0, i))
    pr = pl.BlockSpec((npr, 128), lambda i, *_: (0, i))
    return pl.pallas_call(
        functools.partial(attn_fwd_kernel, chunk=chunk, tile=tile, scale=0.125),
        grid_spec=pltpu.PrefetchScalarGridSpec(
            num_scalar_prefetch=1, grid=(pairs,),
            in_specs=[own, own, own, pr, pr],
            out_specs=[own, pl.BlockSpec((1, 2, rows), lambda i, *_: (i, 0, 0))],
            scratch_shapes=[pltpu.VMEM((2, 80, npr + rows), BF), pltpu.VMEM((2, rows, 128), BF),
            pltpu.VMEM((2, 8, rows), F32), pltpu.VMEM((2, 80, rows), F32)]),
        out_shape=[jax.ShapeDtypeStruct((rows, width), BF), jax.ShapeDtypeStruct((pairs, 2, rows), F32)],
        compiler_params=params(),
        cost_estimate=pl.CostEstimate(flops=4 * rows * npr * width * 2, bytes_accessed=2 * npr * width * 4, transcendentals=rows * npr * 12),
        name="attn_fwd",
    )(e, q, ko, vo, kp, vp)


def attn_bwd_kernel(e_ref, q_ref, do_ref, o_ref, lse_ref, ko_ref, vo_ref, kp_ref, vp_ref, cos_ref, sin_ref,
               dq_ref, dk_ref, dv_ref,
               kt_ref, dqt_ref, qm_ref, dom_ref, dl_ref, dks_ref, dvs_ref, *, tile, scale):
    e = e_ref[0]
    rows = q_ref.shape[0]
    half = rows // 2
    chunk = half
    npr = kp_ref.shape[0]
    nchunk = npr // chunk
    cont = cos_ref.shape[0] - npr
    lane = lax.broadcasted_iota(jnp.int32, (1, 128), 1)
    low = lane < 64
    c = scale * LOG2E
    zero = jnp.zeros((), BF)
    q = q_ref[...]
    do = do_ref[...]
    qm_ref[0] = jnp.where(low, q, zero)
    qm_ref[1] = jnp.where(low, zero, q)
    dom_ref[0] = jnp.where(low, do, zero)
    dom_ref[1] = jnp.where(low, zero, do)
    prod = (do.astype(F32) * o_ref[...].astype(F32)).T
    dl_ref[0:1, :] = jnp.sum(prod[:64], axis=0, keepdims=True)
    dl_ref[1:2, :] = jnp.sum(prod[64:], axis=0, keepdims=True)
    kt_ref[:, :npr] = kp_ref[...].T
    kt_ref[:, npr:] = ko_ref[...].T
    tri = lax.broadcasted_iota(jnp.int32, (tile, tile), 0) <= lax.broadcasted_iota(jnp.int32, (tile, tile), 1)

    def unrope(x, pos, n):
        first = (lane % 64) < 32
        sw = jnp.where(first, pltpu.roll(x, 96, 1), pltpu.roll(x, 32, 1))
        return x * cos_ref[pl.ds(pos, n), :] - sw * sin_ref[pl.ds(pos, n), :]

    def block(k, v, kt, q0, qn, mask):
        dk = dv = None
        dqs = []
        qs = [qm_ref[h, q0:q0 + qn, :] for h in range(2)]
        dos = [dom_ref[h, q0:q0 + qn, :] for h in range(2)]
        sts = [dot(k, qs[h], NT) for h in range(2)]
        dps = [dot(v, dos[h], NT) for h in range(2)]
        for h in range(2):
            p = jnp.exp2(sts[h] * c - lse_ref[0, h:h + 1, q0:q0 + qn])
            if mask is not None:
                p = jnp.where(mask, p, 0.0)
            ds = (p * (dps[h] - dl_ref[h:h + 1, q0:q0 + qn])).astype(BF)
            dvh = dot(p.astype(BF), dos[h])
            dkh = dot(ds, qs[h])
            dk, dv = (dkh, dvh) if dk is None else (dk + dkh, dv + dvh)
            dqs.append(dot(kt[h * 64:(h + 1) * 64], ds))
        return dk, dv, jnp.concatenate(dqs, axis=0)

    nt = rows // tile
    for i in range(nt):
        r0 = i * tile
        k = ko_ref[r0:r0 + tile, :]
        v = vo_ref[r0:r0 + tile, :]
        kt = kt_ref[:, npr + r0:npr + r0 + tile]
        prompt = r0 < half
        dk = dv = None
        for j in (range(i, nt // 2) if prompt else [i]):
            a, b, dq = block(k, v, kt, j * tile, tile, tri if i == j else None)
            dk, dv = (a, b) if dk is None else (dk + a, dv + b)
            sl = slice(j * tile, (j + 1) * tile)
            if i == 0 or not prompt:
                dqt_ref[:, sl] = dq
            else:
                dqt_ref[:, sl] += dq
        if prompt:
            dks_ref[r0:r0 + tile, :] = dk
            dvs_ref[r0:r0 + tile, :] = dv
        else:
            o0 = npr + r0 - half
            dk_ref[o0:o0 + tile, :] = (unrope(dk, npr, tile) * scale).astype(BF)
            dv_ref[o0:o0 + tile, :] = dv.astype(BF)

    def chunk_step(ci, kind):
        r0 = pl.multiple_of(ci * chunk, chunk)
        k = kp_ref[pl.ds(r0, chunk), :]
        v = vp_ref[pl.ds(r0, chunk), :]
        kt = kt_ref[:, pl.ds(r0, chunk)]
        dk, dv, dq = block(k, v, kt, half, half, None)
        dqt_ref[:, half:] += dq
        if kind == 0:
            a, b, dq = block(k, v, kt, 0, half, None)
            dk, dv = dk + a, dv + b
            dqt_ref[:, :half] += dq
        elif kind == 1:
            dk, dv = dk + dks_ref[...], dv + dvs_ref[...]
        dk_ref[pl.ds(r0, chunk), :] = (unrope(dk, r0, chunk) * scale).astype(BF)
        dv_ref[pl.ds(r0, chunk), :] = dv.astype(BF)

    @pl.loop(0, e)
    def _(ci):
        chunk_step(ci, 0)

    chunk_step(e, 1)

    @pl.loop(e + 1, nchunk)
    def _(ci):
        chunk_step(ci, 2)

    dq = dqt_ref[...].T
    base = pl.multiple_of(e * half, half)
    dq_ref[:half, :] = (unrope(dq[:half], base, half) * scale).astype(BF)
    for r in range(half, rows, cont):
        dq_ref[r:r + cont, :] = (unrope(dq[r:r + cont], npr, cont) * scale).astype(BF)


def attn_bwd(e, q, do, o, lse, ko, vo, kp, vp, cos, sin, *, tile=256):
    rows, width = q.shape
    npr = kp.shape[0]
    keys = npr + rows // 2
    pairs = width // 128
    own = pl.BlockSpec((rows, 128), lambda i, *_: (0, i))
    pr = pl.BlockSpec((npr, 128), lambda i, *_: (0, i))
    al = pl.BlockSpec((keys, 128), lambda i, *_: (0, i))
    tab = pl.BlockSpec(cos.shape, lambda i, *_: (0, 0))
    return pl.pallas_call(
        functools.partial(attn_bwd_kernel, tile=tile, scale=0.125),
        grid_spec=pltpu.PrefetchScalarGridSpec(
            num_scalar_prefetch=1, grid=(pairs,),
            in_specs=[own, own, own, pl.BlockSpec((1, 2, rows), lambda i, *_: (i, 0, 0)), own, own, pr, pr, tab, tab],
            out_specs=[own, al, al],
            scratch_shapes=[pltpu.VMEM((128, npr + rows), BF), pltpu.VMEM((128, rows), F32),
                            pltpu.VMEM((2, rows, 128), BF), pltpu.VMEM((2, rows, 128), BF),
                            pltpu.VMEM((8, rows), F32),
                            pltpu.VMEM((rows // 2, 128), F32), pltpu.VMEM((rows // 2, 128), F32)]),
        out_shape=[jax.ShapeDtypeStruct((rows, width), BF), jax.ShapeDtypeStruct((keys, width), BF),
                   jax.ShapeDtypeStruct((keys, width), BF)],
        compiler_params=params(),
        cost_estimate=pl.CostEstimate(flops=10 * rows * npr * width * 2, bytes_accessed=2 * npr * width * 8, transcendentals=rows * npr * 12),
        name="attn_bwd",
    )(e, q, do, o, lse, ko, vo, kp, vp, cos, sin)


MESH = pl.DeviceIdType.MESH


def pick(values, lane, index):
    return jnp.sum(jnp.where(lane == index, values, 0.0), axis=1, keepdims=True)


def softmax_pair(a, b):
    top = jnp.maximum(a, b)
    ea, eb = jnp.exp(a - top), jnp.exp(b - top)
    total = ea + eb
    return ea / total, eb / total


def gate_kernel(x_ref, o_ref, w_ref, gain_ref, wcat_ref, prev_ref, routes_ref, x2_ref, h2_ref, aux_ref, ext_ref, *, experts):
    x2 = x_ref[...].astype(F32) + dot(o_ref[...], w_ref[...])
    x2_ref[...] = x2
    h2 = (x2 * rms_scale(x2) * gain_ref[...]).astype(BF)
    h2_ref[...] = h2
    logits = dot(h2, wcat_ref[...]) + prev_ref[...]
    lane = lane_iota()
    gates = softmax_pair(*[pick(logits, lane, routes_ref[:, k:k + 1]) for k in range(2)])
    aux = logits
    for k in range(2):
        aux = jnp.where(lane == experts + k, gates[k], aux)
    at = experts + 2
    for c in range(2):
        alpha = softmax_pair(*[pick(logits, lane, experts + 2 * c + k) for k in range(2)])
        for k in range(2):
            aux = jnp.where(lane == at + 2 * c + k, alpha[k], aux)
    aux_ref[...] = aux
    for k in range(2):
        parts, left = [], gates[k]
        for _ in range(3):
            part = left.astype(BF)
            parts.append(part.astype(F32))
            left = left - parts[-1]
        spread = jnp.where(lane == 0, parts[0], jnp.where(lane == 1, parts[1], jnp.where(lane == 2, parts[2], 0.0)))
        ext_ref[:, k * 128:(k + 1) * 128] = spread.astype(BF)


def gates(x, o, w_out, gain, wcat, prev, routes, experts, tile=256):
    rows, width = x.shape
    block = pl.BlockSpec((tile, width), lambda i: (i, 0))
    thin = pl.BlockSpec((tile, 128), lambda i: (i, 0))
    return pl.pallas_call(
        functools.partial(gate_kernel, experts=experts),
        grid=(rows // tile,),
        in_specs=[block, block, whole(w_out.shape), whole(gain.shape), whole(wcat.shape), thin,
                  pl.BlockSpec((tile, 2), lambda i: (i, 0))],
        out_specs=[block, block, thin, pl.BlockSpec((tile, 256), lambda i: (i, 0))],
        out_shape=[jax.ShapeDtypeStruct((rows, width), F32), jax.ShapeDtypeStruct((rows, width), BF),
                   jax.ShapeDtypeStruct((rows, 128), F32), jax.ShapeDtypeStruct((rows, 256), BF)],
        compiler_params=params(),
        cost_estimate=pl.CostEstimate(flops=2 * rows * width * width, bytes_accessed=12 * rows * width, transcendentals=0),
        name="gates",
    )(x, o, w_out, gain, wcat, prev, routes)


def dispatch_kernel(slot_ref, rows_ref, out_ref, *, capacity):
    ids = pl.program_id(0) * capacity + lax.broadcasted_iota(jnp.int32, (capacity, 1), 0)
    hot = [jnp.where(ids == slot_ref[k:k + 1, :], 1.0, 0.0).astype(BF) for k in range(2)]
    out_ref[0] = dot(hot[0] + hot[1], rows_ref[...]).astype(BF)


def dispatch(slots, rows, destinations, capacity):
    count, width = rows.shape
    return pl.pallas_call(
        functools.partial(dispatch_kernel, capacity=capacity),
        grid=(destinations,),
        in_specs=[whole(slots.shape), whole(rows.shape)],
        out_specs=pl.BlockSpec((1, capacity, width), lambda i: (i, 0, 0)),
        out_shape=jax.ShapeDtypeStruct((destinations, capacity, width), BF),
        compiler_params=params(),
        cost_estimate=pl.CostEstimate(flops=2 * destinations * capacity * count * width, bytes_accessed=4 * count * width,
                                      transcendentals=0),
        name="dispatch_grads",
    )(slots, rows)


def expert_kernel(slot_ref, h2_ref, ext_ref, g_ref, wg_hbm, wu_hbm, wd_hbm, made_hbm, back_hbm, grad_hbm,
                  wg_ref, wu_ref, wd_ref, a_ref, s_ref, b_ref, d_ref, at_ref, dt_ref, hid_ref, dg_ref, du_ref, macc_ref,
                  bacc_ref, out_ref, send_sem, recv_sem, local_sem, out_sem, *, capacity, tile, grad_tile):
    dp, ex = lax.axis_index("dp"), lax.axis_index("expert")
    j, c, x = dp % 2, ex % 2, ex // 2
    width = h2_ref.shape[1]
    ff = wg_ref.shape[1]
    loads = [pltpu.make_async_copy(src.at[j], dst, local_sem.at[n])
             for n, (src, dst) in enumerate(((wg_hbm, wg_ref), (wu_hbm, wu_ref), (wd_hbm, wd_ref)))]
    for copy in loads:
        copy.start()

    def flip(bit, by):
        return bit + by * (1 - 2 * bit)

    def peer(r):
        return dp + (r // 2 % 2) * (1 - 2 * j), flip(x, r // 4) * 2 + flip(c, r % 2)

    def place(r):
        return flip(j, r // 2 % 2) * 4 + flip(x, r // 4) * 2 + flip(c, r % 2)

    barrier = pltpu.get_barrier_semaphore()
    for r in range(1, 8):
        pl.semaphore_signal(barrier, inc=1, device_id=peer(r), device_id_type=MESH)
    pl.semaphore_wait(barrier, 7)

    def send(src, dst, kind, r):
        n = kind * 8 + r
        copy = pltpu.make_async_remote_copy(src_ref=src, dst_ref=dst, send_sem=send_sem.at[n], recv_sem=recv_sem.at[n],
                                            device_id=peer(r), device_id_type=MESH)
        copy.start()
        return copy

    rows = {}
    for r in (4, 5, 6, 7, 2, 3, 1, 0):
        ids = place(r) * capacity + lax.broadcasted_iota(jnp.int32, (capacity, 1), 0)
        hot = [jnp.where(ids == slot_ref[k:k + 1, :], 1.0, 0.0).astype(BF) for k in range(2)]
        into = s_ref if r else a_ref
        into[r, :, :width] = dot(hot[0] + hot[1], h2_ref[...]).astype(BF)
        into[r, :, width:] = (dot(hot[0], ext_ref[:, :128]) + dot(hot[1], ext_ref[:, 128:])).astype(BF)
        if r:
            rows[r] = send(s_ref.at[r], a_ref.at[r], 0, r)

    for copy in loads:
        copy.wait()
    returned, kept = [], []
    mine = pl.ds(pl.multiple_of(place(0) * capacity, 16), capacity)
    two = 2 * capacity
    for n, first in enumerate((0, 4, 6, 2)):
        for r in (first, first + 1):
            if r:
                rows[r].wait_recv()
            got = a_ref[r]
            half = pl.ds((r - first) * capacity, capacity)
            gate = jnp.sum(got[:, width:].astype(F32), axis=1, keepdims=True)
            g = g_ref[pl.ds(pl.multiple_of(place(r) * capacity, 16), capacity), :].astype(F32)
            d_ref[half, :] = (g * gate).astype(BF)
        span = pl.ds(n * two, two)
        a = a_ref[first:first + 2, :, :width].reshape(two, width)
        at_ref[:, span] = a.T
        dt_ref[:, span] = d_ref[...].T
        macc_ref[...] = jnp.zeros_like(macc_ref)
        bacc_ref[...] = jnp.zeros_like(bacc_ref)

        @pl.loop(0, ff // tile)
        def _(i):
            cols = pl.ds(pl.multiple_of(i * tile, tile), tile)
            a = a_ref[first:first + 2, :, :width].reshape(two, width)
            gate, up = dot(a, wg_ref[:, cols]), dot(a, wu_ref[:, cols])
            dh = dot(d_ref[...], wd_ref[cols, :], NT)
            sig = jax.nn.sigmoid(gate)
            act = gate * sig
            hidden = (act * up).astype(BF)
            du = (dh * act).astype(BF)
            dg = (dh * up * sig * (1.0 + gate * (1.0 - sig))).astype(BF)
            hid_ref[span, cols] = hidden
            du_ref[span, cols] = du
            dg_ref[span, cols] = dg
            macc_ref[...] += dot(hidden, wd_ref[cols, :])
            bacc_ref[...] += dot(dg, wg_ref[:, cols], NT) + dot(du, wu_ref[:, cols], NT)

        for r in (first, first + 1):
            half = pl.ds((r - first) * capacity, capacity)
            if r:
                rows[r].wait_send()
            s_ref[r, :, :width] = macc_ref[half, :].astype(BF)
            b_ref[r] = bacc_ref[half, :].astype(BF)
            made = s_ref.at[r, :, pl.ds(0, width)]
            if r:
                returned.append(send(made, made_hbm.at[mine], 1, r))
                returned.append(send(b_ref.at[r], back_hbm.at[mine], 2, r))
            else:
                kept += [pltpu.make_async_copy(made, made_hbm.at[mine], local_sem.at[3]),
                         pltpu.make_async_copy(b_ref.at[r], back_hbm.at[mine], local_sem.at[4])]
                for copy in kept:
                    copy.start()

    steps = ff // grad_tile

    def put(i, slot):
        cols = pl.ds(pl.multiple_of(i * grad_tile, grad_tile), grad_tile)
        return pltpu.make_async_copy(out_ref.at[slot], grad_hbm.at[:, :, cols], out_sem.at[slot])

    @pl.loop(0, steps)
    def _(i):
        slot = i % 2

        @pl.when(i >= 2)
        def _():
            put(i - 2, slot).wait()

        cols = pl.ds(pl.multiple_of(i * grad_tile, grad_tile), grad_tile)
        out_ref[slot, 0] = dot(at_ref[...], dg_ref[:, cols]).astype(BF)
        out_ref[slot, 1] = dot(at_ref[...], du_ref[:, cols]).astype(BF)
        out_ref[slot, 2] = dot(dt_ref[...], hid_ref[:, cols]).astype(BF)
        put(i, slot).start()

    for i in range(max(steps - 2, 0), steps):
        put(i, i % 2).wait()
    for copy in kept:
        copy.wait()
    for copy in returned:
        copy.wait_recv()
        copy.wait_send()


def experts_on_rows(slots, h2, ext, g, w_gate, w_up, w_down, capacity, tile=512, grad_tile=256):
    width = h2.shape[1]
    ff = w_gate.shape[2]
    total = 8 * capacity
    vm = pltpu.VMEM
    vmem, hbm = pl.BlockSpec(memory_space=pltpu.VMEM), pl.BlockSpec(memory_space=pl.ANY)
    return pl.pallas_call(
        functools.partial(expert_kernel, capacity=capacity, tile=tile, grad_tile=grad_tile),
        in_specs=[vmem] * 4 + [hbm] * 3,
        out_specs=[hbm] * 3,
        out_shape=[jax.ShapeDtypeStruct((total, width), BF), jax.ShapeDtypeStruct((total, width), BF),
                   jax.ShapeDtypeStruct((3, width, ff), BF)],
        scratch_shapes=[
            vm((width, ff), BF), vm((width, ff), BF), vm((ff, width), BF),
            vm((8, capacity, width + 128), BF), vm((8, capacity, width + 128), BF), vm((8, capacity, width), BF),
            vm((2 * capacity, width), BF), vm((width, total), BF), vm((width, total), BF),
            vm((total, ff), BF), vm((total, ff), BF), vm((total, ff), BF),
            vm((2 * capacity, width), F32), vm((2 * capacity, width), F32), vm((2, 3, width, grad_tile), BF),
            pltpu.SemaphoreType.DMA((24,)), pltpu.SemaphoreType.DMA((24,)), pltpu.SemaphoreType.DMA((5,)),
            pltpu.SemaphoreType.DMA((2,)),
        ],
        compiler_params=pltpu.CompilerParams(vmem_limit_bytes=62 << 20, collective_id=1, has_side_effects=True),
        cost_estimate=pl.CostEstimate(flops=18 * total * width * ff, bytes_accessed=12 * width * ff + 8 * total * width,
                                      transcendentals=total * ff),
        name="experts_on_rows",
    )(slots, h2, ext, g, w_gate, w_up, w_down)


def combine_kernel(made_ref, back_ref, slot_ref, routes_ref, aux_ref, x2_ref, h2_ref, g_ref, gain_ref, wcat_ref, v_ref, w_ref,
                   mixed_ref, prev_ref, dx2_ref, da_ref, do_ref, cat_ref, sums_ref, *, experts):
    step = pl.program_id(0)
    lane = lane_iota()
    aux = aux_ref[...]
    h2 = h2_ref[...].astype(F32)
    g = g_ref[...].astype(F32)
    x2 = x2_ref[...]
    r2 = rms_scale(x2)
    slot_total = made_ref.shape[0]
    slot_ids = lane_iota(slot_total)
    hot = [jnp.where(slot_ids == slot_ref[:, k:k + 1], 1.0, 0.0).astype(BF) for k in range(2)]
    gate = [pick(aux, lane, experts + k) for k in range(2)]
    alpha = [[pick(aux, lane, experts + 2 + 2 * c + k) for k in range(2)] for c in range(2)]
    route = [routes_ref[:, k:k + 1] for k in range(2)]
    one = lambda cond: jnp.where(cond, 1.0, 0.0)
    copy = [one(route[k] == FFN_EXP + 1) for k in range(2)]
    const = [[one(route[k] == FFN_EXP + 2 + c) for c in range(2)] for k in range(2)]
    dgate = []
    x3 = x2
    for k in range(2):
        on_h2 = copy[k] + const[k][0] * alpha[0][0] + const[k][1] * alpha[1][0]
        branch = dot(hot[k], made_ref[...]) + on_h2 * h2
        for c in range(2):
            branch = branch + (const[k][c] * alpha[c][1]) * v_ref[c:c + 1, :]
        x3 = x3 + gate[k] * branch
        dgate.append(jnp.sum(g * branch, axis=1, keepdims=True))
    mixed_ref[...] = x3.astype(BF)
    mean = gate[0] * dgate[0] + gate[1] * dgate[1]
    dl = [gate[k] * (dgate[k] - mean) for k in range(2)]
    grads = jnp.where(lane == route[0], dl[0], 0.0) + jnp.where(lane == route[1], dl[1], 0.0)
    prev_ref[...] = grads[:, :experts]
    weight = [gate[0] * const[0][c] + gate[1] * const[1][c] for c in range(2)]
    g_h2 = jnp.sum(g * h2, axis=1, keepdims=True)
    sums = []
    on_g = copy[0] * gate[0] + copy[1] * gate[1]
    for c in range(2):
        da0 = weight[c] * g_h2
        da1 = weight[c] * jnp.sum(g * v_ref[c:c + 1, :], axis=1, keepdims=True)
        mid = alpha[c][0] * da0 + alpha[c][1] * da1
        grads = jnp.where(lane == experts + 2 * c, alpha[c][0] * (da0 - mid), grads)
        grads = jnp.where(lane == experts + 2 * c + 1, alpha[c][1] * (da1 - mid), grads)
        on_g = on_g + alpha[c][0] * weight[c]
        sums.append(jnp.sum((alpha[c][1] * weight[c]) * g, axis=0, keepdims=True))
    low = grads.astype(BF)
    cat = dot(low.T, h2_ref[...])
    dh2 = dot(low, wcat_ref[...], NT) + on_g * g + dot(hot[0] + hot[1], back_ref[...])
    sums.append(jnp.sum(dh2 * x2 * r2, axis=0, keepdims=True))
    u = dh2 * gain_ref[...]
    dx2 = g + r2 * (u - x2 * (r2 * r2) * jnp.mean(u * x2, axis=-1, keepdims=True))
    dx2_ref[...] = dx2
    da = dx2.astype(BF)
    da_ref[...] = da
    do_ref[...] = dot(da, w_ref[...], NT).astype(BF)
    parts = jnp.concatenate(sums + [jnp.zeros((8 - len(sums), g.shape[1]), F32)], axis=0)

    @pl.when(step == 0)
    def _():
        cat_ref[...] = cat
        sums_ref[...] = parts

    @pl.when(step > 0)
    def _():
        cat_ref[...] += cat
        sums_ref[...] += parts


def combine(made, back, slots, routes, aux, x2, h2, g, gain, wcat, const_v, w_out, experts, tile=256):
    rows, width = x2.shape
    block = pl.BlockSpec((tile, width), lambda i: (i, 0))
    thin = pl.BlockSpec((tile, 128), lambda i: (i, 0))
    two = pl.BlockSpec((tile, 2), lambda i: (i, 0))
    sds = jax.ShapeDtypeStruct
    return pl.pallas_call(
        functools.partial(combine_kernel, experts=experts),
        grid=(rows // tile,),
        in_specs=[whole(made.shape), whole(back.shape), two, two, thin, block, block, block, whole(gain.shape),
                  whole(wcat.shape), whole(const_v.shape), whole(w_out.shape)],
        out_specs=[block, pl.BlockSpec((tile, experts), lambda i: (i, 0)), block, block, block, whole((128, width)),
                   whole((8, width))],
        out_shape=[sds((rows, width), BF), sds((rows, experts), F32), sds((rows, width), F32), sds((rows, width), BF),
                   sds((rows, width), BF), sds((128, width), F32), sds((8, width), F32)],
        compiler_params=params(),
        cost_estimate=pl.CostEstimate(flops=8 * rows * width * made.shape[0], bytes_accessed=30 * rows * width,
                                      transcendentals=0),
        name="combine",
    )(made, back, slots, routes, aux, x2, h2, g, gain, wcat, const_v, w_out)


def prompt_back_kernel(dk_ref, dv_ref, wk_ref, wv_ref, x_ref, out_ref, sum_ref):
    dh = dot(dk_ref[...], wk_ref[...], NT) + dot(dv_ref[...], wv_ref[...], NT)
    out_ref[...] = dh.astype(BF)
    x = x_ref[...].astype(F32)
    part = jnp.sum(dh * (x * rms_scale(x)), axis=0, keepdims=True)
    step = pl.program_id(0)

    @pl.when(step == 0)
    def _():
        sum_ref[...] = part

    @pl.when(step > 0)
    def _():
        sum_ref[...] += part


def prompt_back(dk, dv, w_key, w_value, x, tile=256):
    rows, width = x.shape
    block = pl.BlockSpec((tile, width), lambda i: (i, 0))
    return pl.pallas_call(
        prompt_back_kernel,
        grid=(rows // tile,),
        in_specs=[block, block, whole(w_key.shape), whole(w_value.shape), block],
        out_specs=[block, whole((1, width))],
        out_shape=[jax.ShapeDtypeStruct((rows, width), BF), jax.ShapeDtypeStruct((1, width), F32)],
        compiler_params=params(),
        cost_estimate=pl.CostEstimate(flops=4 * rows * width * width, bytes_accessed=8 * rows * width, transcendentals=0),
        name="prompt_back",
    )(dk, dv, w_key, w_value, x)


def own_back_kernel(dq_ref, dk_ref, dv_ref, wq_ref, wk_ref, wv_ref, x_ref, out_ref, sum_ref):
    step = pl.program_id(0)
    x = x_ref[...].astype(F32)
    xr = x * rms_scale(x)

    @pl.when(step == 0)
    def _():
        sum_ref[...] = jnp.zeros_like(sum_ref)

    def put(dh):
        out_ref[...] = dh
        sum_ref[...] += jnp.sum(dh * xr, axis=0, keepdims=True)

    @pl.when(step < pl.num_programs(0) // 2)
    def _():
        put(dot(dq_ref[...], wq_ref[...], NT))

    @pl.when(step >= pl.num_programs(0) // 2)
    def _():
        put(dot(dq_ref[...], wq_ref[...], NT) + dot(dk_ref[...], wk_ref[...], NT) + dot(dv_ref[...], wv_ref[...], NT))


def own_back(dq, dk, dv, w_query, w_key, w_value, x, tile=256):
    rows, width = x.shape
    block = pl.BlockSpec((tile, width), lambda i: (i, 0))
    half = rows // 2 // tile
    first = (dk.shape[0] - rows // 2) // tile
    key = pl.BlockSpec((tile, width), lambda i: (first + jnp.maximum(i - half, 0), 0))
    return pl.pallas_call(
        own_back_kernel,
        grid=(rows // tile,),
        in_specs=[block, key, key] + [whole(w_key.shape)] * 3 + [block],
        out_specs=[block, whole((1, width))],
        out_shape=[jax.ShapeDtypeStruct((rows, width), F32), jax.ShapeDtypeStruct((1, width), F32)],
        compiler_params=params(),
        cost_estimate=pl.CostEstimate(flops=4 * rows * width * width, bytes_accessed=8 * rows * width, transcendentals=0),
        name="own_back",
    )(dq, dk, dv, w_query, w_key, w_value, x)


def weight_back_kernel(hp_ref, ho_ref, o_ref, da_ref, dq_ref, dk_ref, dv_ref, out_ref, acc_ref, *, prompt_steps, own_steps):
    step = pl.program_id(0)
    half = own_steps // 2

    @pl.when(step == 0)
    def _():
        acc_ref[...] = jnp.zeros_like(acc_ref)

    @pl.when(step < prompt_steps)
    def _():
        ht = hp_ref[...].T
        acc_ref[1] += dot(ht, dk_ref[...])
        acc_ref[2] += dot(ht, dv_ref[...])

    @pl.when(step >= prompt_steps)
    def _():
        ht = ho_ref[...].T
        acc_ref[0] += dot(ht, dq_ref[...])
        acc_ref[3] += dot(o_ref[...].T, da_ref[...])

        @pl.when(step >= prompt_steps + half)
        def _():
            acc_ref[1] += dot(ht, dk_ref[...])
            acc_ref[2] += dot(ht, dv_ref[...])

    @pl.when(step == pl.num_programs(0) - 1)
    def _():
        width = acc_ref.shape[1]
        for n in range(4):
            out_ref[n * width:(n + 1) * width, :] = acc_ref[n].astype(BF)
        if out_ref.shape[0] > 4 * width:
            out_ref[4 * width:, :] = jnp.zeros((out_ref.shape[0] - 4 * width, width), BF)


def weight_back(hp, ho, o, da, dq, dk, dv, out_rows, tile=256):
    rows, width = ho.shape
    ps, os_ = hp.shape[0] // tile, rows // tile
    half = os_ // 2
    prompt = pl.BlockSpec((tile, width), lambda i: (jnp.minimum(i, ps - 1), 0))
    own = pl.BlockSpec((tile, width), lambda i: (jnp.maximum(i - ps, 0), 0))
    key = pl.BlockSpec((tile, width), lambda i: (jnp.where(i < ps + half, jnp.minimum(i, ps - 1), i - half), 0))
    return pl.pallas_call(
        functools.partial(weight_back_kernel, prompt_steps=ps, own_steps=os_),
        grid=(ps + os_,),
        in_specs=[prompt, own, own, own, own, key, key],
        out_specs=whole((out_rows, width)),
        out_shape=jax.ShapeDtypeStruct((out_rows, width), BF),
        scratch_shapes=[pltpu.VMEM((4, width, width), F32)],
        compiler_params=params(),
        cost_estimate=pl.CostEstimate(flops=16 * rows * width * width, bytes_accessed=14 * rows * width, transcendentals=0),
        name="weight_back",
    )(hp, ho, o, da, dq, dk, dv)


def token_back_kernel(own_ref, got_ref, x_ref, dx2_ref, gain_ref, out_ref):
    x = x_ref[...].astype(F32)
    r1 = rms_scale(x)

    def put(dh):
        u = dh * gain_ref[...]
        out_ref[...] = dx2_ref[...] + r1 * (u - x * (r1 * r1) * jnp.mean(u * x, axis=-1, keepdims=True))

    step = pl.program_id(0)

    @pl.when(step < pl.num_programs(0) // 2)
    def _():
        put(own_ref[...] + got_ref[...])

    @pl.when(step >= pl.num_programs(0) // 2)
    def _():
        put(own_ref[...])


def token_back(own, got, x, dx2, gain, tile=256):
    rows, width = x.shape
    block = pl.BlockSpec((tile, width), lambda i: (i, 0))
    half = rows // 2 // tile
    return pl.pallas_call(
        token_back_kernel,
        grid=(rows // tile,),
        in_specs=[block, pl.BlockSpec((tile, width), lambda i: (jnp.minimum(i, half - 1), 0)), block, block,
                  whole(gain.shape)],
        out_specs=block,
        out_shape=jax.ShapeDtypeStruct((rows, width), F32),
        compiler_params=params(),
        cost_estimate=pl.CostEstimate(flops=10 * rows * width, bytes_accessed=14 * rows * width, transcendentals=0),
        name="token_back",
    )(own, got, x, dx2, gain)


def padded_rows(rows, rest):
    unit = 8 * rest * 16
    return -(-rows // unit) * unit


def sum_kernel(g_ref, small_ref, dh_ref, out_ref, small_out_ref, got_ref, half_ref, r0_ref, t1_ref, r1_ref, t2_ref, r2_ref,
               r3_ref, sm_ref, rs_ref, rd0_ref, td_ref, rd1_ref, send_sem, recv_sem, *, rest, chunks):
    dp, ex = lax.axis_index("dp"), lax.axis_index("expert")
    c, x, y, z = ex % 2, ex // 2, dp % 2, dp // 2
    mate = (dp, x * 2 + 1 - c)
    across = (dp, (1 - x) * 2 + c)
    beside = (z * 2 + 1 - y, ex)
    ahead = [((z + d) % rest * 2 + y, ex) for d in range(1, rest)]

    barrier = pltpu.get_barrier_semaphore()
    for peer in [mate, across, beside] + ahead:
        pl.semaphore_signal(barrier, inc=1, device_id=peer, device_id_type=MESH)
    pl.semaphore_wait(barrier, 2 + rest)

    started = []

    def send(src, dst, peer):
        n = len(started)
        copy = pltpu.make_async_remote_copy(src_ref=src, dst_ref=dst, send_sem=send_sem.at[n], recv_sem=recv_sem.at[n],
                                            device_id=peer, device_id_type=MESH)
        copy.start()
        started.append(copy)
        return copy

    rows, width = g_ref.shape
    half = rows // 2
    size = half // chunks
    lanes = width // 2
    q1, q2, q3 = size // 2, size // 4, size // 4 // rest
    part = [pl.ds(0, lanes), pl.ds(lanes, lanes)]
    first, second = [across, beside], [beside, across]
    bit1, bit2 = [x, y], [y, x]

    def ds(at, n):
        return pl.ds(pl.multiple_of(at, 16), n)

    def at1(k, p, bit):
        return k * size + bit * q1

    def spot2(k, p, bit):
        return k * size + bit1[p] * q1 + bit * q2

    def stage0(k):
        return [send(g_ref.at[ds((1 - c) * half + k * size, size)], r0_ref.at[ds(k * size, size)], mate)]

    def stage1(k):
        sl = pl.ds(k * size, size)
        half_ref[sl] = (g_ref[ds(c * half + k * size, size)].astype(F32) + r0_ref[sl].astype(F32)).astype(BF)
        return [send(half_ref.at[ds(at1(k, p, 1 - bit1[p]), q1), part[p]], r1_ref.at[p, pl.ds(k * q1, q1)], first[p])
                for p in range(2)]

    def stage2(k):
        out = []
        for p in range(2):
            sl = pl.ds(k * q1, q1)
            t1_ref[p, sl] = (half_ref[ds(at1(k, p, bit1[p]), q1), part[p]].astype(F32) + r1_ref[p, sl].astype(F32)).astype(BF)
            out.append(send(t1_ref.at[p, ds(k * q1 + (1 - bit2[p]) * q2, q2)], r2_ref.at[p, pl.ds(k * q2, q2)], second[p]))
        return out

    def stage3(k):
        out = []
        for p in range(2):
            sl = pl.ds(k * q2, q2)
            t2_ref[p, sl] = (t1_ref[p, ds(k * q1 + bit2[p] * q2, q2)].astype(F32) + r2_ref[p, sl].astype(F32)).astype(BF)
            for d in range(1, rest):
                to = (z + d) % rest
                out.append(send(t2_ref.at[p, ds(k * q2 + to * q3, q3)], r3_ref.at[p, d - 1, pl.ds(k * q3, q3)], ahead[d - 1]))
        return out

    def stage4(k):
        out = []
        for p in range(2):
            total = t2_ref[p, ds(k * q2 + z * q3, q3)].astype(F32)
            for d in range(1, rest):
                total = total + r3_ref[p, d - 1, pl.ds(k * q3, q3)].astype(F32)
            mine = ds(c * half + spot2(k, p, bit2[p]) + z * q3, q3)
            out_ref[mine, part[p]] = total.astype(BF)
            for d in range(1, rest):
                out.append(send(out_ref.at[mine, part[p]], out_ref.at[mine, part[p]], ahead[d - 1]))
        return out

    def stage5(k):
        out = []
        for p in range(2):
            mine = ds(c * half + spot2(k, p, bit2[p]), q2)
            out.append(send(out_ref.at[mine, part[p]], out_ref.at[mine, part[p]], second[p]))
        return out

    def stage6(k):
        out = []
        for p in range(2):
            mine = ds(c * half + at1(k, p, bit1[p]), q1)
            out.append(send(out_ref.at[mine, part[p]], out_ref.at[mine, part[p]], first[p]))
        return out

    def stage7(k):
        mine = ds(c * half + k * size, size)
        return [send(out_ref.at[mine], out_ref.at[mine], mate)]

    block = got_ref.shape[0]

    def dh_rows(xx, cc):
        return ds((xx * 2 + cc) * block, block)

    def dh0():
        return [send(dh_ref.at[dh_rows(w, 1 - c)], rd0_ref.at[w], mate) for w in range(2)]

    def dh1():
        td_ref[...] = (dh_ref[dh_rows(1 - x, c)].astype(F32) + rd0_ref[1 - x].astype(F32)).astype(BF)
        return [send(td_ref, rd1_ref, across)]

    def dh2():
        got_ref[...] = dh_ref[dh_rows(x, c)].astype(F32) + rd0_ref[x].astype(F32) + rd1_ref[...].astype(F32)
        return []

    def small_pair(n, peer):
        def run():
            if n:
                sm_ref[n] = sm_ref[n - 1] + rs_ref[n - 1]
            else:
                sm_ref[0] = small_ref[...]
            return [send(sm_ref.at[n], rs_ref.at[n], peer)]
        return run

    def small_rest():
        sm_ref[3] = sm_ref[2] + rs_ref[2]
        return [send(sm_ref.at[3], rs_ref.at[2 + d], ahead[d - 1]) for d in range(1, rest)]

    def small_end():
        total = sm_ref[3]
        for d in range(1, rest):
            total = total + rs_ref[2 + d]
        small_out_ref[...] = total
        return []

    lines = [[functools.partial(f, k) for f in (stage0, stage1, stage2, stage3, stage4, stage5, stage6, stage7)]
             for k in range(chunks)]
    lines.insert(1, [dh0, dh1, dh2])
    lines.append([small_pair(0, mate), small_pair(1, across), small_pair(2, beside), small_rest, small_end])
    waiting = [[] for _ in lines]
    for t in range(max(n + len(line) for n, line in enumerate(lines)) + 1):
        for n, line in enumerate(lines):
            s = t - n
            if 0 <= s <= len(line):
                for copy in waiting[n]:
                    copy.wait_recv()
                waiting[n] = line[s]() if s < len(line) else []
    for copy in started:
        copy.wait_send()


def device_sums(g, small, dh, rest, block, chunks):
    rows, width = g.shape
    half, lanes = rows // 2, width // 2
    copies = chunks * (1 + 2 + 2 + 2 * (rest - 1) * 2 + 2 + 2 + 1) + 3 + 3 + rest - 1
    vm = pltpu.VMEM
    vmem = pl.BlockSpec(memory_space=pltpu.VMEM)
    return pl.pallas_call(
        functools.partial(sum_kernel, rest=rest, chunks=chunks),
        in_specs=[vmem] * 3,
        out_specs=[vmem] * 3,
        out_shape=[jax.ShapeDtypeStruct(g.shape, BF), jax.ShapeDtypeStruct(small.shape, F32),
                   jax.ShapeDtypeStruct((block, width), F32)],
        scratch_shapes=[
            vm((half, width), BF), vm((half, width), BF), vm((2, half // 2, lanes), BF), vm((2, half // 2, lanes), BF),
            vm((2, half // 4, lanes), BF), vm((2, half // 4, lanes), BF), vm((2, rest - 1, half // 4 // rest, lanes), BF),
            vm((4,) + small.shape, F32), vm((2 + rest,) + small.shape, F32), vm((2, block, width), BF), vm((block, width), BF),
            vm((block, width), BF), pltpu.SemaphoreType.DMA((copies,)), pltpu.SemaphoreType.DMA((copies,)),
        ],
        compiler_params=params(collective_id=0, has_side_effects=True),
        cost_estimate=pl.CostEstimate(flops=4 * rows * width, bytes_accessed=8 * rows * width, transcendentals=0),
        name="device_sums",
    )(g, small, dh)


def slot_table(routes_t, priority, groups, capacity):
    ids = jnp.arange(FFN_EXP, dtype=jnp.int32)
    picked = routes_t[:, None, :] == ids[None, :, None]
    assigned = jnp.any(picked, axis=0).astype(BF)
    earlier = (priority[:, None] < priority[None, :]).astype(BF)
    rank_table = jnp.dot(assigned, earlier, preferred_element_type=F32)
    rank = jnp.sum(jnp.where(picked, rank_table[None], 0.0), axis=1).astype(jnp.int32)
    place = (routes_t % groups) * (FFN_EXP // groups) + routes_t // groups
    return jnp.where((routes_t < FFN_EXP) & (rank < capacity), place * capacity + rank, -1)


def local(
    tokens, prev_logits, routes, priority, norm_attn, w_query, w_key, w_value, w_out, norm_ffn, router, const_w, const_v,
    w_gate, w_up, w_down, cotangent,
):
    rows, width = tokens.shape
    experts = prev_logits.shape[1]
    dp = lax.axis_size("dp")
    expert_devices = lax.axis_size("expert")
    pair = w_gate.shape[0]
    capacity = 9 * rows * routes.shape[1] // (8 * experts)
    prompt_dev = PROMPT // expert_devices
    ff = w_gate.shape[2]
    e = lax.axis_index("expert").astype(jnp.int32).reshape(1)
    j = (lax.axis_index("dp") % pair).astype(jnp.int32).reshape(1)
    members = pair * expert_devices
    everyone = ("dp", "expert")
    exchange = [list(range(p * members, (p + 1) * members)) for p in range(dp // pair)]
    alike = [list(range(q, dp, pair)) for q in range(pair)]
    pairs = [list(range(p * pair, (p + 1) * pair)) for p in range(dp // pair)]

    def swap(x):
        return lax.all_to_all(x, everyone, split_axis=0, concat_axis=0, axis_index_groups=exchange, tiled=True)

    cos, sin = (jnp.asarray(t) for t in angle_tables())
    gain1, gain2 = norm_attn[None, :], norm_ffn[None, :]

    prompt_x = lax.all_gather(tokens[:prompt_dev], "expert", axis=0, tiled=True)
    slots_t = slot_table(routes.T, priority, pair, capacity)
    slots = slots_t.T
    grads_out = dispatch(slots_t, cotangent, members, capacity)
    tokens, grads_out = lax.optimization_barrier((tokens, grads_out))
    grads_in = swap(grads_out).reshape(-1, width)
    h_own, q, k_own, v_own = project(e, tokens, gain1, (w_query, w_key, w_value), cos, sin, True)
    h_prompt, k_prompt, v_prompt = project(e, prompt_x, gain1, (w_key, w_value), cos, sin, False)
    o, lse = attn_fwd(e, q, k_own, v_own, k_prompt, v_prompt)

    wcat = jnp.concatenate(
        [router, const_w.transpose(1, 0, 2).reshape(width, -1), jnp.zeros((width, 128 - experts - 4), BF)], axis=1
    )
    prev = jnp.pad(prev_logits, ((0, 0), (0, 128 - experts)))
    x2, h2, aux, ext = gates(tokens, o, w_out, gain2, wcat, prev, routes, experts)
    made, drow, ffn_sum = experts_on_rows(slots_t, h2, ext, grads_in, w_gate, w_up, w_down, capacity)
    ffn_sum = lax.psum_scatter(ffn_sum, "dp", scatter_dimension=2, axis_index_groups=alike, tiled=True)

    mixed, grad_prev, dx2, da, do, cat, sums = combine(
        made, drow, slots, routes, aux, x2, h2, cotangent, gain2, wcat, const_v, w_out, experts
    )
    dq, dk, dv = attn_bwd(e, q, do, o, lse, k_own, v_own, k_prompt, v_prompt, cos, sin)
    dh_prompt, sum_p = prompt_back(dk, dv, w_key, w_value, prompt_x)
    dh_own, sum_o = own_back(dq, dk, dv, w_query, w_key, w_value, tokens)
    rest = dp // 2
    out_rows = padded_rows(4 * width, rest)
    chunks = max(n for n in (1, 2, 3) if out_rows // 2 % (n * 4 * rest * 16) == 0)
    grad_w = weight_back(h_prompt, h_own, o, da, dq, dk, dv, out_rows)
    n = experts
    small = jnp.concatenate([cat[:n + 4], sums[:3], sum_p + sum_o, jnp.zeros((4, width), F32)], axis=0)
    grad_w, small, got = device_sums(grad_w, small, dh_prompt, rest, prompt_dev, chunks)
    grad_w = grad_w.astype(F32)
    grad_tokens = token_back(dh_own, got, tokens, dx2, gain1)

    ffn_sum = ffn_sum.reshape(3, width, pair, -1).transpose(2, 0, 1, 3)
    ffn_sum = lax.all_to_all(ffn_sum, "dp", split_axis=0, concat_axis=0, axis_index_groups=pairs, tiled=True)
    ffn_sum = ffn_sum.astype(F32)
    return (
        mixed,
        grad_tokens,
        grad_prev,
        small[n + 7],
        grad_w[:width],
        grad_w[width:2 * width],
        grad_w[2 * width:3 * width],
        grad_w[3 * width:4 * width],
        small[n + 6],
        small[:n].T,
        small[n:n + 4].reshape(2, 2, width).transpose(0, 2, 1),
        small[n + 4:n + 6],
        ffn_sum[:, 0],
        ffn_sum[:, 1],
        ffn_sum[:, 2].transpose(0, 2, 1),
    )


def solution(mesh):
    block = P(("dp", "expert"), None)
    in_specs = (block, block, block, P(("dp", "expert"))) + (P(),) * 9 + (P("expert", None, None),) * 3 + (block,)
    out_specs = (block, block, block) + (P(),) * 9 + (
        P("expert", None, "dp"), P("expert", None, "dp"), P("expert", "dp", None),
    )
    return jax.shard_map(local, mesh=mesh, in_specs=in_specs, out_specs=out_specs, check_vma=False)
```

```python
import functools

import jax
import jax.numpy as jnp
import numpy as np
from jax import lax
from jax.experimental import pallas as pl
from jax.experimental.pallas import tpu as pltpu
from jax.sharding import PartitionSpec as P

HEADS = 12
FFN_EXP = 8
PROMPT = 2048
NCONT = 8
CONT = 256

epsilon = 1e-06
LOG2E = 1.4426950408889634
F32 = jnp.float32
BF = jnp.bfloat16
NN = (((1,), (0,)), ((), ()))
NT = (((1,), (1,)), ((), ()))
VMEM_LIMIT = 56 << 20


def dot(a, b, dims=NN):
    return lax.dot_general(a, b, dims, preferred_element_type=F32)


def params(**kw):
    return pltpu.CompilerParams(vmem_limit_bytes=VMEM_LIMIT, **kw)


def whole(shape):
    return pl.BlockSpec(shape, lambda *_: (0,) * len(shape))


def rms_scale(x):
    return lax.rsqrt(jnp.mean(x * x, axis=-1, keepdims=True) + epsilon)


def angle_tables():
    positions = np.arange(PROMPT + CONT, dtype=np.float32)
    frequency = np.exp(
        np.float32(-np.log(10000.0)) * np.arange(32, dtype=np.float32) * np.float32(2.0) / np.float32(64)
    ).astype(np.float32)
    angle = (positions[:, None] * frequency[None, :]).astype(np.float64)
    cosine = np.cos(angle).astype(np.float32)
    sine = np.sin(angle).astype(np.float32)
    return (
        np.concatenate([cosine] * 4, axis=1),
        np.concatenate([-sine, sine, -sine, sine], axis=1),
    )


def lane_iota(width=128):
    return lax.broadcasted_iota(jnp.int32, (1, width), 1)


def swap_halves(x):
    return jnp.where(lane_iota() % 64 < 32, pltpu.roll(x, 96, 1), pltpu.roll(x, 32, 1))


def project_kernel(e_ref, x_ref, gain_ref, *refs, count):
    weights, (cos_ref, sin_ref), (h_ref, *outs) = refs[:count], refs[count:count + 2], refs[count + 2:]
    x = x_ref[...].astype(F32)
    h = (x * rms_scale(x) * gain_ref[...]).astype(BF)
    h_ref[...] = h
    cosine, sine = cos_ref[...], sin_ref[...]
    for n, (w_ref, out_ref) in enumerate(zip(weights, outs)):
        full = dot(h, w_ref[...])
        if n == count - 1:
            out_ref[...] = full.astype(BF)
            continue
        for i in range(full.shape[1] // 128):
            part = full[:, i * 128:(i + 1) * 128]
            out_ref[:, i * 128:(i + 1) * 128] = (part * cosine + swap_halves(part) * sine).astype(BF)


def project(e, x, gain, weights, cos, sin, own, tile=256):
    rows, width = x.shape
    block = pl.BlockSpec((tile, width), lambda i, *_: (i, 0))
    half = rows // 2 // tile

    def position(i, e_ref):
        if not own:
            return (i, 0)
        return (jnp.where(i < half, e_ref[0] * half + i, PROMPT // tile), 0)

    table = pl.BlockSpec((tile, 128), position)
    return pl.pallas_call(
        functools.partial(project_kernel, count=len(weights)),
        grid_spec=pltpu.PrefetchScalarGridSpec(
            num_scalar_prefetch=1,
            grid=(rows // tile,),
            in_specs=[block, whole((1, width))] + [whole(weights[0].shape)] * len(weights) + [table, table],
            out_specs=[block] * (len(weights) + 1),
        ),
        out_shape=[jax.ShapeDtypeStruct((rows, width), BF)] * (len(weights) + 1),
        compiler_params=params(),
        cost_estimate=pl.CostEstimate(
            flops=2 * rows * width * width * len(weights), bytes_accessed=2 * rows * width * 6, transcendentals=0
        ),
        name="project_own" if own else "project_prompt",
    )(e, x, gain, *weights, cos, sin)


def attn_fwd_kernel(e_ref, q_ref, ko_ref, vo_ref, kp_ref, vp_ref, o_ref, lse_ref, vt_ref, qm_ref, m_ref, acc_ref, *, chunk, tile, scale):
    e = e_ref[0]
    rows = q_ref.shape[0]
    half = rows // 2
    npr = kp_ref.shape[0]
    nchunk = npr // chunk
    lane = lax.broadcasted_iota(jnp.int32, (1, 128), 1)
    low = lane < 64
    c = scale * LOG2E
    zero = jnp.zeros((), BF)
    q = q_ref[...]
    qm_ref[0] = jnp.where(low, q, zero)
    qm_ref[1] = jnp.where(low, zero, q)
    ones = jnp.ones((16, npr + rows), BF)
    for r, n, ref in ((0, npr, vp_ref), (npr, rows, vo_ref)):
        vt = ref[...].T
        vt_ref[0, :64, r:r + n] = vt[:64]
        vt_ref[1, :64, r:r + n] = vt[64:]
    vt_ref[0, 64:, :] = ones
    vt_ref[1, 64:, :] = ones
    tri = lax.broadcasted_iota(jnp.int32, (tile, tile), 0) <= lax.broadcasted_iota(jnp.int32, (tile, tile), 1)

    def first(q0, qn, k, vts):
        for h in range(2):
            s = dot(k, qm_ref[h, q0:q0 + qn, :], NT)
            s = s * c
            s = jnp.where(tri, s, -1e30)
            mx = jnp.max(s, axis=0, keepdims=True)
            p = jnp.exp2(s - mx).astype(BF)
            m_ref[h, 0:1, q0:q0 + qn] = mx
            acc_ref[h, :, q0:q0 + qn] = dot(vts[h], p)

    def step(blocks, k, vts):
        ss = [[dot(k, qm_ref[h, q0:q0 + qn, :], NT) for h in range(2)] for q0, qn in blocks]
        for (q0, qn), sb in zip(blocks, ss):
            for h in range(2):
                s = sb[h] * c
                mx = jnp.max(s, axis=0, keepdims=True)
                m = m_ref[h, 0:1, q0:q0 + qn]
                mn = jnp.maximum(m, mx)
                p = jnp.exp2(s - mn).astype(BF)
                m_ref[h, 0:1, q0:q0 + qn] = mn
                acc_ref[h, :, q0:q0 + qn] = acc_ref[h, :, q0:q0 + qn] * jnp.exp2(m - mn) + dot(vts[h], p)

    for j in range(rows // tile):
        r0 = j * tile
        first(r0, tile, ko_ref[r0:r0 + tile, :], [vt_ref[h, :, npr + r0:npr + r0 + tile] for h in range(2)])
    for j in range(1, half // tile):
        for i in range(j):
            r0 = i * tile
            step([(j * tile, tile)], ko_ref[r0:r0 + tile, :], [vt_ref[h, :, npr + r0:npr + r0 + tile] for h in range(2)])

    def body(ci, blocks):
        r0 = pl.multiple_of(ci * chunk, chunk)
        step(blocks, kp_ref[pl.ds(r0, chunk), :], [vt_ref[h, :, pl.ds(r0, chunk)] for h in range(2)])

    ne = e * half // chunk

    @pl.loop(0, ne)
    def _(ci):
        body(ci, [(0, half), (half, half)])

    @pl.loop(ne, nchunk)
    def _(ci):
        body(ci, [(half, half)])

    outs = []
    for h in range(2):
        l = acc_ref[h, 64:65, :]
        outs.append(acc_ref[h, :64, :] / l)
        lse_ref[0, h:h + 1, :] = m_ref[h, 0:1, :] + jnp.log2(l)
    o_ref[...] = jnp.concatenate(outs, axis=0).T.astype(BF)


def attn_fwd(e, q, ko, vo, kp, vp, *, chunk=512, tile=256):
    rows, width = q.shape
    npr = kp.shape[0]
    pairs = width // 128
    own = pl.BlockSpec((rows, 128), lambda i, *_: (0, i))
    pr = pl.BlockSpec((npr, 128), lambda i, *_: (0, i))
    return pl.pallas_call(
        functools.partial(attn_fwd_kernel, chunk=chunk, tile=tile, scale=0.125),
        grid_spec=pltpu.PrefetchScalarGridSpec(
            num_scalar_prefetch=1, grid=(pairs,),
            in_specs=[own, own, own, pr, pr],
            out_specs=[own, pl.BlockSpec((1, 2, rows), lambda i, *_: (i, 0, 0))],
            scratch_shapes=[pltpu.VMEM((2, 80, npr + rows), BF), pltpu.VMEM((2, rows, 128), BF),
            pltpu.VMEM((2, 8, rows), F32), pltpu.VMEM((2, 80, rows), F32)]),
        out_shape=[jax.ShapeDtypeStruct((rows, width), BF), jax.ShapeDtypeStruct((pairs, 2, rows), F32)],
        compiler_params=params(),
        cost_estimate=pl.CostEstimate(flops=4 * rows * npr * width * 2, bytes_accessed=2 * npr * width * 4, transcendentals=rows * npr * 12),
        name="attn_fwd",
    )(e, q, ko, vo, kp, vp)


def attn_bwd_kernel(e_ref, q_ref, do_ref, o_ref, lse_ref, ko_ref, vo_ref, kp_ref, vp_ref, cos_ref, sin_ref,
               dq_ref, dk_ref, dv_ref,
               kt_ref, dqt_ref, qm_ref, dom_ref, dl_ref, dks_ref, dvs_ref, *, tile, scale):
    e = e_ref[0]
    rows = q_ref.shape[0]
    half = rows // 2
    chunk = half
    npr = kp_ref.shape[0]
    nchunk = npr // chunk
    cont = cos_ref.shape[0] - npr
    lane = lax.broadcasted_iota(jnp.int32, (1, 128), 1)
    low = lane < 64
    c = scale * LOG2E
    zero = jnp.zeros((), BF)
    q = q_ref[...]
    do = do_ref[...]
    qm_ref[0] = jnp.where(low, q, zero)
    qm_ref[1] = jnp.where(low, zero, q)
    dom_ref[0] = jnp.where(low, do, zero)
    dom_ref[1] = jnp.where(low, zero, do)
    prod = (do.astype(F32) * o_ref[...].astype(F32)).T
    dl_ref[0:1, :] = jnp.sum(prod[:64], axis=0, keepdims=True)
    dl_ref[1:2, :] = jnp.sum(prod[64:], axis=0, keepdims=True)
    kt_ref[:, :npr] = kp_ref[...].T
    kt_ref[:, npr:] = ko_ref[...].T
    tri = lax.broadcasted_iota(jnp.int32, (tile, tile), 0) <= lax.broadcasted_iota(jnp.int32, (tile, tile), 1)

    def unrope(x, pos, n):
        first = (lane % 64) < 32
        sw = jnp.where(first, pltpu.roll(x, 96, 1), pltpu.roll(x, 32, 1))
        return x * cos_ref[pl.ds(pos, n), :] - sw * sin_ref[pl.ds(pos, n), :]

    def block(k, v, kt, q0, qn, mask):
        dk = dv = None
        dqs = []
        qs = [qm_ref[h, q0:q0 + qn, :] for h in range(2)]
        dos = [dom_ref[h, q0:q0 + qn, :] for h in range(2)]
        sts = [dot(k, qs[h], NT) for h in range(2)]
        dps = [dot(v, dos[h], NT) for h in range(2)]
        for h in range(2):
            p = jnp.exp2(sts[h] * c - lse_ref[0, h:h + 1, q0:q0 + qn])
            if mask is not None:
                p = jnp.where(mask, p, 0.0)
            ds = (p * (dps[h] - dl_ref[h:h + 1, q0:q0 + qn])).astype(BF)
            dvh = dot(p.astype(BF), dos[h])
            dkh = dot(ds, qs[h])
            dk, dv = (dkh, dvh) if dk is None else (dk + dkh, dv + dvh)
            dqs.append(dot(kt[h * 64:(h + 1) * 64], ds))
        return dk, dv, jnp.concatenate(dqs, axis=0)

    nt = rows // tile
    for i in range(nt):
        r0 = i * tile
        k = ko_ref[r0:r0 + tile, :]
        v = vo_ref[r0:r0 + tile, :]
        kt = kt_ref[:, npr + r0:npr + r0 + tile]
        prompt = r0 < half
        dk = dv = None
        for j in (range(i, nt // 2) if prompt else [i]):
            a, b, dq = block(k, v, kt, j * tile, tile, tri if i == j else None)
            dk, dv = (a, b) if dk is None else (dk + a, dv + b)
            sl = slice(j * tile, (j + 1) * tile)
            if i == 0 or not prompt:
                dqt_ref[:, sl] = dq
            else:
                dqt_ref[:, sl] += dq
        if prompt:
            dks_ref[r0:r0 + tile, :] = dk
            dvs_ref[r0:r0 + tile, :] = dv
        else:
            o0 = npr + r0 - half
            dk_ref[o0:o0 + tile, :] = (unrope(dk, npr, tile) * scale).astype(BF)
            dv_ref[o0:o0 + tile, :] = dv.astype(BF)

    def chunk_step(ci, kind):
        r0 = pl.multiple_of(ci * chunk, chunk)
        k = kp_ref[pl.ds(r0, chunk), :]
        v = vp_ref[pl.ds(r0, chunk), :]
        kt = kt_ref[:, pl.ds(r0, chunk)]
        dk, dv, dq = block(k, v, kt, half, half, None)
        dqt_ref[:, half:] += dq
        if kind == 0:
            a, b, dq = block(k, v, kt, 0, half, None)
            dk, dv = dk + a, dv + b
            dqt_ref[:, :half] += dq
        elif kind == 1:
            dk, dv = dk + dks_ref[...], dv + dvs_ref[...]
        dk_ref[pl.ds(r0, chunk), :] = (unrope(dk, r0, chunk) * scale).astype(BF)
        dv_ref[pl.ds(r0, chunk), :] = dv.astype(BF)

    @pl.loop(0, e)
    def _(ci):
        chunk_step(ci, 0)

    chunk_step(e, 1)

    @pl.loop(e + 1, nchunk)
    def _(ci):
        chunk_step(ci, 2)

    dq = dqt_ref[...].T
    base = pl.multiple_of(e * half, half)
    dq_ref[:half, :] = (unrope(dq[:half], base, half) * scale).astype(BF)
    for r in range(half, rows, cont):
        dq_ref[r:r + cont, :] = (unrope(dq[r:r + cont], npr, cont) * scale).astype(BF)


def attn_bwd(e, q, do, o, lse, ko, vo, kp, vp, cos, sin, *, tile=256):
    rows, width = q.shape
    npr = kp.shape[0]
    keys = npr + rows // 2
    pairs = width // 128
    own = pl.BlockSpec((rows, 128), lambda i, *_: (0, i))
    pr = pl.BlockSpec((npr, 128), lambda i, *_: (0, i))
    al = pl.BlockSpec((keys, 128), lambda i, *_: (0, i))
    tab = pl.BlockSpec(cos.shape, lambda i, *_: (0, 0))
    return pl.pallas_call(
        functools.partial(attn_bwd_kernel, tile=tile, scale=0.125),
        grid_spec=pltpu.PrefetchScalarGridSpec(
            num_scalar_prefetch=1, grid=(pairs,),
            in_specs=[own, own, own, pl.BlockSpec((1, 2, rows), lambda i, *_: (i, 0, 0)), own, own, pr, pr, tab, tab],
            out_specs=[own, al, al],
            scratch_shapes=[pltpu.VMEM((128, npr + rows), BF), pltpu.VMEM((128, rows), F32),
                            pltpu.VMEM((2, rows, 128), BF), pltpu.VMEM((2, rows, 128), BF),
                            pltpu.VMEM((8, rows), F32),
                            pltpu.VMEM((rows // 2, 128), F32), pltpu.VMEM((rows // 2, 128), F32)]),
        out_shape=[jax.ShapeDtypeStruct((rows, width), BF), jax.ShapeDtypeStruct((keys, width), BF),
                   jax.ShapeDtypeStruct((keys, width), BF)],
        compiler_params=params(),
        cost_estimate=pl.CostEstimate(flops=10 * rows * npr * width * 2, bytes_accessed=2 * npr * width * 8, transcendentals=rows * npr * 12),
        name="attn_bwd",
    )(e, q, do, o, lse, ko, vo, kp, vp, cos, sin)


MESH = pl.DeviceIdType.MESH


def pick(values, lane, index):
    return jnp.sum(jnp.where(lane == index, values, 0.0), axis=1, keepdims=True)


def softmax_pair(a, b):
    top = jnp.maximum(a, b)
    ea, eb = jnp.exp(a - top), jnp.exp(b - top)
    total = ea + eb
    return ea / total, eb / total


def spread(column):
    lane = lane_iota()
    parts, left = jnp.zeros((1, 128), F32), column
    for n in range(3):
        part = left.astype(BF).astype(F32)
        parts = jnp.where(lane == n, part, parts)
        left = left - part
    return parts.astype(BF)


def gate_kernel(x_ref, o_ref, w_ref, gain_ref, wcat_ref, prev_ref, routes_ref, x2_ref, h2_ref, aux_ref, ext_ref, *, experts):
    x2 = x_ref[...].astype(F32) + dot(o_ref[...], w_ref[...])
    x2_ref[...] = x2
    h2 = (x2 * rms_scale(x2) * gain_ref[...]).astype(BF)
    h2_ref[...] = h2
    logits = dot(h2, wcat_ref[...]) + prev_ref[...]
    lane = lane_iota()
    gates = softmax_pair(*[pick(logits, lane, routes_ref[:, k:k + 1]) for k in range(2)])
    aux = logits
    for k in range(2):
        aux = jnp.where(lane == experts + k, gates[k], aux)
    at = experts + 2
    for c in range(2):
        alpha = softmax_pair(*[pick(logits, lane, experts + 2 * c + k) for k in range(2)])
        for k in range(2):
            aux = jnp.where(lane == at + 2 * c + k, alpha[k], aux)
    aux_ref[...] = aux
    for k in range(2):
        ext_ref[:, k * 128:(k + 1) * 128] = spread(gates[k])


def gates(x, o, w_out, gain, wcat, prev, routes, experts, tile=256):
    rows, width = x.shape
    block = pl.BlockSpec((tile, width), lambda i: (i, 0))
    thin = pl.BlockSpec((tile, 128), lambda i: (i, 0))
    return pl.pallas_call(
        functools.partial(gate_kernel, experts=experts),
        grid=(rows // tile,),
        in_specs=[block, block, whole(w_out.shape), whole(gain.shape), whole(wcat.shape), thin,
                  pl.BlockSpec((tile, 2), lambda i: (i, 0))],
        out_specs=[block, block, thin, pl.BlockSpec((tile, 256), lambda i: (i, 0))],
        out_shape=[jax.ShapeDtypeStruct((rows, width), F32), jax.ShapeDtypeStruct((rows, width), BF),
                   jax.ShapeDtypeStruct((rows, 128), F32), jax.ShapeDtypeStruct((rows, 256), BF)],
        compiler_params=params(),
        cost_estimate=pl.CostEstimate(flops=2 * rows * width * width, bytes_accessed=12 * rows * width, transcendentals=0),
        name="gates",
    )(x, o, w_out, gain, wcat, prev, routes)


def dispatch_kernel(slot_ref, rows_ref, out_ref, *, capacity):
    ids = pl.program_id(0) * capacity + lax.broadcasted_iota(jnp.int32, (capacity, 1), 0)
    hot = [jnp.where(ids == slot_ref[k:k + 1, :], 1.0, 0.0).astype(BF) for k in range(2)]
    out_ref[0] = dot(hot[0] + hot[1], rows_ref[...]).astype(BF)


def dispatch(slots, rows, destinations, capacity):
    count, width = rows.shape
    return pl.pallas_call(
        functools.partial(dispatch_kernel, capacity=capacity),
        grid=(destinations,),
        in_specs=[whole(slots.shape), whole(rows.shape)],
        out_specs=pl.BlockSpec((1, capacity, width), lambda i: (i, 0, 0)),
        out_shape=jax.ShapeDtypeStruct((destinations, capacity, width), BF),
        compiler_params=params(),
        cost_estimate=pl.CostEstimate(flops=2 * destinations * capacity * count * width, bytes_accessed=4 * count * width,
                                      transcendentals=0),
        name="dispatch_grads",
    )(slots, rows)


def expert_kernel(slot_ref, h2_ref, ext_ref, g_ref, wg_hbm, wu_hbm, wd_hbm, made_ref, back_hbm, grad_hbm,
                  wg_ref, wu_ref, wd_ref, a_ref, s_ref, d_ref, at_ref, dt_ref, hid_ref, dg_ref, du_ref, macc_ref,
                  bacc_ref, out_ref, send_sem, recv_sem, local_sem, out_sem, *, capacity, tile, grad_tile):
    dp, ex = lax.axis_index("dp"), lax.axis_index("expert")
    j, c, x = dp % 2, ex % 2, ex // 2
    width = h2_ref.shape[1]
    ff = wg_ref.shape[1]
    loads = [pltpu.make_async_copy(src.at[j], dst, local_sem.at[n])
             for n, (src, dst) in enumerate(((wg_hbm, wg_ref), (wu_hbm, wu_ref), (wd_hbm, wd_ref)))]
    for copy in loads:
        copy.start()

    def flip(bit, by):
        return bit + by * (1 - 2 * bit)

    def peer(r):
        return dp + (r // 2 % 2) * (1 - 2 * j), flip(x, r // 4) * 2 + flip(c, r % 2)

    def place(r):
        return flip(j, r // 2 % 2) * 4 + flip(x, r // 4) * 2 + flip(c, r % 2)

    barrier = pltpu.get_barrier_semaphore()
    for r in range(1, 8):
        pl.semaphore_signal(barrier, inc=1, device_id=peer(r), device_id_type=MESH)
    pl.semaphore_wait(barrier, 7)

    def send(src, dst, kind, r):
        n = kind * 8 + r
        copy = pltpu.make_async_remote_copy(src_ref=src, dst_ref=dst, send_sem=send_sem.at[n], recv_sem=recv_sem.at[n],
                                            device_id=peer(r), device_id_type=MESH)
        copy.start()
        return copy

    rows = {}
    for r in (4, 5, 6, 7, 2, 3, 1, 0):
        ids = place(r) * capacity + lax.broadcasted_iota(jnp.int32, (capacity, 1), 0)
        hot = [jnp.where(ids == slot_ref[k:k + 1, :], 1.0, 0.0).astype(BF) for k in range(2)]
        into = s_ref if r else a_ref
        into[r, :, :width] = dot(hot[0] + hot[1], h2_ref[...]).astype(BF)
        into[r, :, width:] = (dot(hot[0], ext_ref[:, :128]) + dot(hot[1], ext_ref[:, 128:])).astype(BF)
        if r:
            rows[r] = send(s_ref.at[r], a_ref.at[r], 0, r)

    for copy in loads:
        copy.wait()
    returned = []
    mine = pl.ds(pl.multiple_of(place(0) * capacity, 16), capacity)
    two = 2 * capacity
    for n, first in enumerate((0, 4, 6, 2)):
        for r in (first, first + 1):
            if r:
                rows[r].wait_recv()
            got = a_ref[r]
            half = pl.ds((r - first) * capacity, capacity)
            gate = jnp.sum(got[:, width:].astype(F32), axis=1, keepdims=True)
            g = g_ref[pl.ds(pl.multiple_of(place(r) * capacity, 16), capacity), :].astype(F32)
            d_ref[half, :] = (g * gate).astype(BF)
        span = pl.ds(n * two, two)
        a = a_ref[first:first + 2, :, :width].reshape(two, width)
        at_ref[:, span] = a.T
        dt_ref[:, span] = d_ref[...].T
        macc_ref[...] = jnp.zeros_like(macc_ref)
        bacc_ref[...] = jnp.zeros_like(bacc_ref)

        @pl.loop(0, ff // tile)
        def _(i):
            cols = pl.ds(pl.multiple_of(i * tile, tile), tile)
            a = a_ref[first:first + 2, :, :width].reshape(two, width)
            gate, up = dot(a, wg_ref[:, cols]), dot(a, wu_ref[:, cols])
            dh = dot(d_ref[...], wd_ref[cols, :], NT)
            sig = jax.nn.sigmoid(gate)
            act = gate * sig
            hidden = (act * up).astype(BF)
            du = (dh * act).astype(BF)
            dg = (dh * up * sig * (1.0 + gate * (1.0 - sig))).astype(BF)
            hid_ref[span, cols] = hidden
            du_ref[span, cols] = du
            dg_ref[span, cols] = dg
            macc_ref[...] += dot(hidden, wd_ref[cols, :])
            bacc_ref[...] += dot(dg, wg_ref[:, cols], NT) + dot(du, wu_ref[:, cols], NT)

        for r in (first, first + 1):
            half = pl.ds((r - first) * capacity, capacity)
            if r:
                rows[r].wait_send()
            theirs = pl.ds(pl.multiple_of(place(r) * capacity, 16), capacity)
            made = macc_ref[half, :].astype(BF)
            made_ref[theirs, :] = made
            s_ref[r, :, :width] = bacc_ref[half, :].astype(BF)
            s_ref[r, :, width:] = spread(jnp.sum(g_ref[theirs, :].astype(F32) * made.astype(F32), axis=1, keepdims=True))
            if r:
                returned.append(send(s_ref.at[r], back_hbm.at[mine], 1, r))
            else:
                kept = pltpu.make_async_copy(s_ref.at[0], back_hbm.at[mine], local_sem.at[3])
                kept.start()

    steps = ff // grad_tile

    def put(i, slot):
        cols = pl.ds(pl.multiple_of(i * grad_tile, grad_tile), grad_tile)
        return pltpu.make_async_copy(out_ref.at[slot], grad_hbm.at[:, :, cols], out_sem.at[slot])

    @pl.loop(0, steps)
    def _(i):
        slot = i % 2

        @pl.when(i >= 2)
        def _():
            put(i - 2, slot).wait()

        cols = pl.ds(pl.multiple_of(i * grad_tile, grad_tile), grad_tile)
        out_ref[slot, 0] = dot(at_ref[...], dg_ref[:, cols]).astype(BF)
        out_ref[slot, 1] = dot(at_ref[...], du_ref[:, cols]).astype(BF)
        out_ref[slot, 2] = dot(dt_ref[...], hid_ref[:, cols]).astype(BF)
        put(i, slot).start()

    for i in range(max(steps - 2, 0), steps):
        put(i, i % 2).wait()
    kept.wait()
    for copy in returned:
        copy.wait_recv()
        copy.wait_send()


def experts_on_rows(slots, h2, ext, g, w_gate, w_up, w_down, capacity, tile=512, grad_tile=256):
    width = h2.shape[1]
    ff = w_gate.shape[2]
    total = 8 * capacity
    vm = pltpu.VMEM
    vmem, hbm = pl.BlockSpec(memory_space=pltpu.VMEM), pl.BlockSpec(memory_space=pl.ANY)
    return pl.pallas_call(
        functools.partial(expert_kernel, capacity=capacity, tile=tile, grad_tile=grad_tile),
        in_specs=[vmem] * 4 + [hbm] * 3,
        out_specs=[vmem, hbm, hbm],
        out_shape=[jax.ShapeDtypeStruct((total, width), BF), jax.ShapeDtypeStruct((total, width + 128), BF),
                   jax.ShapeDtypeStruct((3, width, ff), BF)],
        scratch_shapes=[
            vm((width, ff), BF), vm((width, ff), BF), vm((ff, width), BF),
            vm((8, capacity, width + 128), BF), vm((8, capacity, width + 128), BF),
            vm((2 * capacity, width), BF), vm((width, total), BF), vm((width, total), BF),
            vm((total, ff), BF), vm((total, ff), BF), vm((total, ff), BF),
            vm((2 * capacity, width), F32), vm((2 * capacity, width), F32), vm((2, 3, width, grad_tile), BF),
            pltpu.SemaphoreType.DMA((16,)), pltpu.SemaphoreType.DMA((16,)), pltpu.SemaphoreType.DMA((4,)),
            pltpu.SemaphoreType.DMA((2,)),
        ],
        compiler_params=pltpu.CompilerParams(vmem_limit_bytes=62 << 20, collective_id=1, has_side_effects=True),
        cost_estimate=pl.CostEstimate(flops=18 * total * width * ff, bytes_accessed=12 * width * ff + 8 * total * width,
                                      transcendentals=total * ff),
        name="experts_on_rows",
    )(slots, h2, ext, g, w_gate, w_up, w_down)


def one(cond):
    return jnp.where(cond, 1.0, 0.0)


def pick_parts(aux, routes, experts):
    lane = lane_iota()
    gate = [pick(aux, lane, experts + k) for k in range(2)]
    alpha = [[pick(aux, lane, experts + 2 + 2 * c + k) for k in range(2)] for c in range(2)]
    copy = [one(routes[k] == FFN_EXP + 1) for k in range(2)]
    const = [[one(routes[k] == FFN_EXP + 2 + c) for c in range(2)] for k in range(2)]
    on_h2 = [copy[k] + const[k][0] * alpha[0][0] + const[k][1] * alpha[1][0] for k in range(2)]
    return gate, alpha, copy, const, on_h2


def one_hot(slots, total):
    return jnp.where(lane_iota(total) == slots, 1.0, 0.0).astype(BF)


def combine_kernel(back_ref, slot_ref, routes_ref, aux_ref, x2_ref, h2_ref, g_ref, gain_ref, wcat_ref, v_ref, w_ref,
                   prev_ref, dx2_ref, da_ref, do_ref, cat_ref, sums_ref, *, experts):
    step = pl.program_id(0)
    lane = lane_iota()
    h2 = h2_ref[...].astype(F32)
    g = g_ref[...].astype(F32)
    x2 = x2_ref[...]
    width = x2.shape[1]
    r2 = rms_scale(x2)
    route = [routes_ref[:, k:k + 1] for k in range(2)]
    gate, alpha, copy, const, on_h2 = pick_parts(aux_ref[...], route, experts)
    hot = [one_hot(slot_ref[:, k:k + 1], back_ref.shape[0]) for k in range(2)]
    g_h2 = jnp.sum(g * h2, axis=1, keepdims=True)
    g_v = [jnp.sum(g * v_ref[c:c + 1, :], axis=1, keepdims=True) for c in range(2)]
    dgate = []
    for k in range(2):
        at_expert = jnp.sum(dot(hot[k], back_ref[:, width:]), axis=1, keepdims=True)
        dgate.append(at_expert + on_h2[k] * g_h2 + const[k][0] * alpha[0][1] * g_v[0] + const[k][1] * alpha[1][1] * g_v[1])
    mean = gate[0] * dgate[0] + gate[1] * dgate[1]
    dl = [gate[k] * (dgate[k] - mean) for k in range(2)]
    grads = jnp.where(lane == route[0], dl[0], 0.0) + jnp.where(lane == route[1], dl[1], 0.0)
    prev_ref[...] = grads[:, :experts]
    weight = [gate[0] * const[0][c] + gate[1] * const[1][c] for c in range(2)]
    sums = []
    on_g = copy[0] * gate[0] + copy[1] * gate[1]
    for c in range(2):
        da0 = weight[c] * g_h2
        da1 = weight[c] * g_v[c]
        mid = alpha[c][0] * da0 + alpha[c][1] * da1
        grads = jnp.where(lane == experts + 2 * c, alpha[c][0] * (da0 - mid), grads)
        grads = jnp.where(lane == experts + 2 * c + 1, alpha[c][1] * (da1 - mid), grads)
        on_g = on_g + alpha[c][0] * weight[c]
        sums.append(jnp.sum((alpha[c][1] * weight[c]) * g, axis=0, keepdims=True))
    low = grads.astype(BF)
    cat = dot(low.T, h2_ref[...])
    dh2 = dot(low, wcat_ref[...], NT) + on_g * g + dot(hot[0] + hot[1], back_ref[:, :width])
    sums.append(jnp.sum(dh2 * x2 * r2, axis=0, keepdims=True))
    u = dh2 * gain_ref[...]
    dx2 = g + r2 * (u - x2 * (r2 * r2) * jnp.mean(u * x2, axis=-1, keepdims=True))
    dx2_ref[...] = dx2
    da = dx2.astype(BF)
    da_ref[...] = da
    do_ref[...] = dot(da, w_ref[...], NT).astype(BF)
    parts = jnp.concatenate(sums + [jnp.zeros((8 - len(sums), width), F32)], axis=0)

    @pl.when(step == 0)
    def _():
        cat_ref[...] = cat
        sums_ref[...] = parts

    @pl.when(step > 0)
    def _():
        cat_ref[...] += cat
        sums_ref[...] += parts


def combine(back, slots, routes, aux, x2, h2, g, gain, wcat, const_v, w_out, experts, tile=256):
    rows, width = x2.shape
    block = pl.BlockSpec((tile, width), lambda i: (i, 0))
    thin = pl.BlockSpec((tile, 128), lambda i: (i, 0))
    two = pl.BlockSpec((tile, 2), lambda i: (i, 0))
    sds = jax.ShapeDtypeStruct
    return pl.pallas_call(
        functools.partial(combine_kernel, experts=experts),
        grid=(rows // tile,),
        in_specs=[whole(back.shape), two, two, thin, block, block, block, whole(gain.shape), whole(wcat.shape),
                  whole(const_v.shape), whole(w_out.shape)],
        out_specs=[pl.BlockSpec((tile, experts), lambda i: (i, 0)), block, block, block, whole((128, width)),
                   whole((8, width))],
        out_shape=[sds((rows, experts), F32), sds((rows, width), F32), sds((rows, width), BF),
                   sds((rows, width), BF), sds((128, width), F32), sds((8, width), F32)],
        compiler_params=params(),
        cost_estimate=pl.CostEstimate(flops=4 * rows * width * back.shape[0], bytes_accessed=26 * rows * width,
                                      transcendentals=0),
        name="combine",
    )(back, slots, routes, aux, x2, h2, g, gain, wcat, const_v, w_out)


def mix_kernel(made_ref, slot_ref, routes_ref, aux_ref, x2_ref, h2_ref, v_ref, out_ref, *, experts):
    route = [routes_ref[:, k:k + 1] for k in range(2)]
    gate, alpha, _, const, on_h2 = pick_parts(aux_ref[...], route, experts)
    out = x2_ref[...] + (gate[0] * on_h2[0] + gate[1] * on_h2[1]) * h2_ref[...].astype(F32)
    for c in range(2):
        out = out + ((gate[0] * const[0][c] + gate[1] * const[1][c]) * alpha[c][1]) * v_ref[c:c + 1, :]
    for k in range(2):
        out = out + gate[k] * dot(one_hot(slot_ref[:, k:k + 1], made_ref.shape[0]), made_ref[...])
    out_ref[...] = out.astype(BF)


def mix(made, slots, routes, aux, x2, h2, const_v, experts, tile=256):
    rows, width = x2.shape
    block = pl.BlockSpec((tile, width), lambda i: (i, 0))
    two = pl.BlockSpec((tile, 2), lambda i: (i, 0))
    return pl.pallas_call(
        functools.partial(mix_kernel, experts=experts),
        grid=(rows // tile,),
        in_specs=[whole(made.shape), two, two, pl.BlockSpec((tile, 128), lambda i: (i, 0)), block, block, whole(const_v.shape)],
        out_specs=block,
        out_shape=jax.ShapeDtypeStruct((rows, width), BF),
        compiler_params=params(),
        cost_estimate=pl.CostEstimate(flops=4 * rows * width * made.shape[0], bytes_accessed=12 * rows * width,
                                      transcendentals=0),
        name="mix",
    )(made, slots, routes, aux, x2, h2, const_v)


def prompt_back_kernel(dk_ref, dv_ref, wk_ref, wv_ref, x_ref, out_ref, sum_ref):
    dh = dot(dk_ref[...], wk_ref[...], NT) + dot(dv_ref[...], wv_ref[...], NT)
    out_ref[...] = dh.astype(BF)
    x = x_ref[...].astype(F32)
    part = jnp.sum(dh * (x * rms_scale(x)), axis=0, keepdims=True)
    step = pl.program_id(0)

    @pl.when(step == 0)
    def _():
        sum_ref[...] = part

    @pl.when(step > 0)
    def _():
        sum_ref[...] += part


def prompt_back(dk, dv, w_key, w_value, x, tile=256):
    rows, width = x.shape
    block = pl.BlockSpec((tile, width), lambda i: (i, 0))
    return pl.pallas_call(
        prompt_back_kernel,
        grid=(rows // tile,),
        in_specs=[block, block, whole(w_key.shape), whole(w_value.shape), block],
        out_specs=[block, whole((1, width))],
        out_shape=[jax.ShapeDtypeStruct((rows, width), BF), jax.ShapeDtypeStruct((1, width), F32)],
        compiler_params=params(),
        cost_estimate=pl.CostEstimate(flops=4 * rows * width * width, bytes_accessed=8 * rows * width, transcendentals=0),
        name="prompt_back",
    )(dk, dv, w_key, w_value, x)


def own_back_kernel(dq_ref, dk_ref, dv_ref, wq_ref, wk_ref, wv_ref, x_ref, out_ref, sum_ref):
    step = pl.program_id(0)
    x = x_ref[...].astype(F32)
    xr = x * rms_scale(x)

    @pl.when(step == 0)
    def _():
        sum_ref[...] = jnp.zeros_like(sum_ref)

    def put(dh):
        out_ref[...] = dh
        sum_ref[...] += jnp.sum(dh * xr, axis=0, keepdims=True)

    @pl.when(step < pl.num_programs(0) // 2)
    def _():
        put(dot(dq_ref[...], wq_ref[...], NT))

    @pl.when(step >= pl.num_programs(0) // 2)
    def _():
        put(dot(dq_ref[...], wq_ref[...], NT) + dot(dk_ref[...], wk_ref[...], NT) + dot(dv_ref[...], wv_ref[...], NT))


def own_back(dq, dk, dv, w_query, w_key, w_value, x, tile=256):
    rows, width = x.shape
    block = pl.BlockSpec((tile, width), lambda i: (i, 0))
    half = rows // 2 // tile
    first = (dk.shape[0] - rows // 2) // tile
    key = pl.BlockSpec((tile, width), lambda i: (first + jnp.maximum(i - half, 0), 0))
    return pl.pallas_call(
        own_back_kernel,
        grid=(rows // tile,),
        in_specs=[block, key, key] + [whole(w_key.shape)] * 3 + [block],
        out_specs=[block, whole((1, width))],
        out_shape=[jax.ShapeDtypeStruct((rows, width), F32), jax.ShapeDtypeStruct((1, width), F32)],
        compiler_params=params(),
        cost_estimate=pl.CostEstimate(flops=4 * rows * width * width, bytes_accessed=8 * rows * width, transcendentals=0),
        name="own_back",
    )(dq, dk, dv, w_query, w_key, w_value, x)


def weight_back_kernel(hp_ref, ho_ref, o_ref, da_ref, dq_ref, dk_ref, dv_ref, out_ref, acc_ref, *, prompt_steps, own_steps):
    step = pl.program_id(0)
    half = own_steps // 2

    @pl.when(step == 0)
    def _():
        acc_ref[...] = jnp.zeros_like(acc_ref)

    @pl.when(step < prompt_steps)
    def _():
        ht = hp_ref[...].T
        acc_ref[1] += dot(ht, dk_ref[...])
        acc_ref[2] += dot(ht, dv_ref[...])

    @pl.when(step >= prompt_steps)
    def _():
        ht = ho_ref[...].T
        acc_ref[0] += dot(ht, dq_ref[...])
        acc_ref[3] += dot(o_ref[...].T, da_ref[...])

        @pl.when(step >= prompt_steps + half)
        def _():
            acc_ref[1] += dot(ht, dk_ref[...])
            acc_ref[2] += dot(ht, dv_ref[...])

    @pl.when(step == pl.num_programs(0) - 1)
    def _():
        width = acc_ref.shape[1]
        for n in range(4):
            out_ref[n * width:(n + 1) * width, :] = acc_ref[n].astype(BF)
        if out_ref.shape[0] > 4 * width:
            out_ref[4 * width:, :] = jnp.zeros((out_ref.shape[0] - 4 * width, width), BF)


def weight_back(hp, ho, o, da, dq, dk, dv, out_rows, tile=256):
    rows, width = ho.shape
    ps, os_ = hp.shape[0] // tile, rows // tile
    half = os_ // 2
    prompt = pl.BlockSpec((tile, width), lambda i: (jnp.minimum(i, ps - 1), 0))
    own = pl.BlockSpec((tile, width), lambda i: (jnp.maximum(i - ps, 0), 0))
    key = pl.BlockSpec((tile, width), lambda i: (jnp.where(i < ps + half, jnp.minimum(i, ps - 1), i - half), 0))
    return pl.pallas_call(
        functools.partial(weight_back_kernel, prompt_steps=ps, own_steps=os_),
        grid=(ps + os_,),
        in_specs=[prompt, own, own, own, own, key, key],
        out_specs=whole((out_rows, width)),
        out_shape=jax.ShapeDtypeStruct((out_rows, width), BF),
        scratch_shapes=[pltpu.VMEM((4, width, width), F32)],
        compiler_params=params(),
        cost_estimate=pl.CostEstimate(flops=16 * rows * width * width, bytes_accessed=14 * rows * width, transcendentals=0),
        name="weight_back",
    )(hp, ho, o, da, dq, dk, dv)


def token_back_kernel(own_ref, got_ref, x_ref, dx2_ref, gain_ref, out_ref):
    x = x_ref[...].astype(F32)
    r1 = rms_scale(x)

    def put(dh):
        u = dh * gain_ref[...]
        out_ref[...] = dx2_ref[...] + r1 * (u - x * (r1 * r1) * jnp.mean(u * x, axis=-1, keepdims=True))

    step = pl.program_id(0)

    @pl.when(step < pl.num_programs(0) // 2)
    def _():
        put(own_ref[...] + got_ref[...])

    @pl.when(step >= pl.num_programs(0) // 2)
    def _():
        put(own_ref[...])


def token_back(own, got, x, dx2, gain, tile=256):
    rows, width = x.shape
    block = pl.BlockSpec((tile, width), lambda i: (i, 0))
    half = rows // 2 // tile
    return pl.pallas_call(
        token_back_kernel,
        grid=(rows // tile,),
        in_specs=[block, pl.BlockSpec((tile, width), lambda i: (jnp.minimum(i, half - 1), 0)), block, block,
                  whole(gain.shape)],
        out_specs=block,
        out_shape=jax.ShapeDtypeStruct((rows, width), F32),
        compiler_params=params(),
        cost_estimate=pl.CostEstimate(flops=10 * rows * width, bytes_accessed=14 * rows * width, transcendentals=0),
        name="token_back",
    )(own, got, x, dx2, gain)


def padded_rows(rows, rest):
    unit = 8 * rest * 16
    return -(-rows // unit) * unit


def sum_kernel(g_ref, small_ref, dh_ref, out_ref, small_out_ref, got_ref, half_ref, r0_ref, t1_ref, r1_ref, t2_ref, r2_ref,
               r3_ref, sm_ref, rs_ref, rd0_ref, td_ref, rd1_ref, send_sem, recv_sem, *, rest, chunks):
    dp, ex = lax.axis_index("dp"), lax.axis_index("expert")
    c, x, y, z = ex % 2, ex // 2, dp % 2, dp // 2
    mate = (dp, x * 2 + 1 - c)
    across = (dp, (1 - x) * 2 + c)
    beside = (z * 2 + 1 - y, ex)
    ahead = [((z + d) % rest * 2 + y, ex) for d in range(1, rest)]

    barrier = pltpu.get_barrier_semaphore()
    for peer in [mate, across, beside] + ahead:
        pl.semaphore_signal(barrier, inc=1, device_id=peer, device_id_type=MESH)
    pl.semaphore_wait(barrier, 2 + rest)

    started = []

    def send(src, dst, peer):
        n = len(started)
        copy = pltpu.make_async_remote_copy(src_ref=src, dst_ref=dst, send_sem=send_sem.at[n], recv_sem=recv_sem.at[n],
                                            device_id=peer, device_id_type=MESH)
        copy.start()
        started.append(copy)
        return copy

    rows, width = g_ref.shape
    half = rows // 2
    size = half // chunks
    lanes = width // 2
    q1, q2, q3 = size // 2, size // 4, size // 4 // rest
    part = [pl.ds(0, lanes), pl.ds(lanes, lanes)]
    first, second = [across, beside], [beside, across]
    bit1, bit2 = [x, y], [y, x]

    def ds(at, n):
        return pl.ds(pl.multiple_of(at, 16), n)

    def at1(k, p, bit):
        return k * size + bit * q1

    def spot2(k, p, bit):
        return k * size + bit1[p] * q1 + bit * q2

    def stage0(k):
        return [send(g_ref.at[ds((1 - c) * half + k * size, size)], r0_ref.at[ds(k * size, size)], mate)]

    def stage1(k):
        sl = pl.ds(k * size, size)
        half_ref[sl] = (g_ref[ds(c * half + k * size, size)].astype(F32) + r0_ref[sl].astype(F32)).astype(BF)
        return [send(half_ref.at[ds(at1(k, p, 1 - bit1[p]), q1), part[p]], r1_ref.at[p, pl.ds(k * q1, q1)], first[p])
                for p in range(2)]

    def stage2(k):
        out = []
        for p in range(2):
            sl = pl.ds(k * q1, q1)
            t1_ref[p, sl] = (half_ref[ds(at1(k, p, bit1[p]), q1), part[p]].astype(F32) + r1_ref[p, sl].astype(F32)).astype(BF)
            out.append(send(t1_ref.at[p, ds(k * q1 + (1 - bit2[p]) * q2, q2)], r2_ref.at[p, pl.ds(k * q2, q2)], second[p]))
        return out

    def stage3(k):
        out = []
        for p in range(2):
            sl = pl.ds(k * q2, q2)
            t2_ref[p, sl] = (t1_ref[p, ds(k * q1 + bit2[p] * q2, q2)].astype(F32) + r2_ref[p, sl].astype(F32)).astype(BF)
            for d in range(1, rest):
                to = (z + d) % rest
                out.append(send(t2_ref.at[p, ds(k * q2 + to * q3, q3)], r3_ref.at[p, d - 1, pl.ds(k * q3, q3)], ahead[d - 1]))
        return out

    def stage4(k):
        out = []
        for p in range(2):
            total = t2_ref[p, ds(k * q2 + z * q3, q3)].astype(F32)
            for d in range(1, rest):
                total = total + r3_ref[p, d - 1, pl.ds(k * q3, q3)].astype(F32)
            mine = ds(c * half + spot2(k, p, bit2[p]) + z * q3, q3)
            out_ref[mine, part[p]] = total.astype(BF)
            for d in range(1, rest):
                out.append(send(out_ref.at[mine, part[p]], out_ref.at[mine, part[p]], ahead[d - 1]))
        return out

    def stage5(k):
        out = []
        for p in range(2):
            mine = ds(c * half + spot2(k, p, bit2[p]), q2)
            out.append(send(out_ref.at[mine, part[p]], out_ref.at[mine, part[p]], second[p]))
        return out

    def stage6(k):
        out = []
        for p in range(2):
            mine = ds(c * half + at1(k, p, bit1[p]), q1)
            out.append(send(out_ref.at[mine, part[p]], out_ref.at[mine, part[p]], first[p]))
        return out

    def stage7(k):
        mine = ds(c * half + k * size, size)
        return [send(out_ref.at[mine], out_ref.at[mine], mate)]

    block = got_ref.shape[0]

    def dh_rows(xx, cc):
        return ds((xx * 2 + cc) * block, block)

    def dh0():
        return [send(dh_ref.at[dh_rows(w, 1 - c)], rd0_ref.at[w], mate) for w in range(2)]

    def dh1():
        td_ref[...] = (dh_ref[dh_rows(1 - x, c)].astype(F32) + rd0_ref[1 - x].astype(F32)).astype(BF)
        return [send(td_ref, rd1_ref, across)]

    def dh2():
        got_ref[...] = dh_ref[dh_rows(x, c)].astype(F32) + rd0_ref[x].astype(F32) + rd1_ref[...].astype(F32)
        return []

    def small_pair(n, peer):
        def run():
            if n:
                sm_ref[n] = sm_ref[n - 1] + rs_ref[n - 1]
            else:
                sm_ref[0] = small_ref[...]
            return [send(sm_ref.at[n], rs_ref.at[n], peer)]
        return run

    def small_rest():
        sm_ref[3] = sm_ref[2] + rs_ref[2]
        return [send(sm_ref.at[3], rs_ref.at[2 + d], ahead[d - 1]) for d in range(1, rest)]

    def small_end():
        total = sm_ref[3]
        for d in range(1, rest):
            total = total + rs_ref[2 + d]
        small_out_ref[...] = total
        return []

    lines = [[functools.partial(f, k) for f in (stage0, stage1, stage2, stage3, stage4, stage5, stage6, stage7)]
             for k in range(chunks)]
    lines.insert(1, [dh0, dh1, dh2])
    lines.append([small_pair(0, mate), small_pair(1, across), small_pair(2, beside), small_rest, small_end])
    waiting = [[] for _ in lines]
    for t in range(max(n + len(line) for n, line in enumerate(lines)) + 1):
        for n, line in enumerate(lines):
            s = t - n
            if 0 <= s <= len(line):
                for copy in waiting[n]:
                    copy.wait_recv()
                waiting[n] = line[s]() if s < len(line) else []
    for copy in started:
        copy.wait_send()


def device_sums(g, small, dh, rest, block, chunks):
    rows, width = g.shape
    half, lanes = rows // 2, width // 2
    copies = chunks * (1 + 2 + 2 + 2 * (rest - 1) * 2 + 2 + 2 + 1) + 3 + 3 + rest - 1
    vm = pltpu.VMEM
    vmem = pl.BlockSpec(memory_space=pltpu.VMEM)
    return pl.pallas_call(
        functools.partial(sum_kernel, rest=rest, chunks=chunks),
        in_specs=[vmem] * 3,
        out_specs=[vmem] * 3,
        out_shape=[jax.ShapeDtypeStruct(g.shape, BF), jax.ShapeDtypeStruct(small.shape, F32),
                   jax.ShapeDtypeStruct((block, width), F32)],
        scratch_shapes=[
            vm((half, width), BF), vm((half, width), BF), vm((2, half // 2, lanes), BF), vm((2, half // 2, lanes), BF),
            vm((2, half // 4, lanes), BF), vm((2, half // 4, lanes), BF), vm((2, rest - 1, half // 4 // rest, lanes), BF),
            vm((4,) + small.shape, F32), vm((2 + rest,) + small.shape, F32), vm((2, block, width), BF), vm((block, width), BF),
            vm((block, width), BF), pltpu.SemaphoreType.DMA((copies,)), pltpu.SemaphoreType.DMA((copies,)),
        ],
        compiler_params=params(collective_id=0, has_side_effects=True),
        cost_estimate=pl.CostEstimate(flops=4 * rows * width, bytes_accessed=8 * rows * width, transcendentals=0),
        name="device_sums",
    )(g, small, dh)


def slot_table(routes_t, priority, groups, capacity):
    ids = jnp.arange(FFN_EXP, dtype=jnp.int32)
    picked = routes_t[:, None, :] == ids[None, :, None]
    assigned = jnp.any(picked, axis=0).astype(BF)
    earlier = (priority[:, None] < priority[None, :]).astype(BF)
    rank_table = jnp.dot(assigned, earlier, preferred_element_type=F32)
    rank = jnp.sum(jnp.where(picked, rank_table[None], 0.0), axis=1).astype(jnp.int32)
    place = (routes_t % groups) * (FFN_EXP // groups) + routes_t // groups
    return jnp.where((routes_t < FFN_EXP) & (rank < capacity), place * capacity + rank, -1)


def local(
    tokens, prev_logits, routes, priority, norm_attn, w_query, w_key, w_value, w_out, norm_ffn, router, const_w, const_v,
    w_gate, w_up, w_down, cotangent,
):
    rows, width = tokens.shape
    experts = prev_logits.shape[1]
    dp = lax.axis_size("dp")
    expert_devices = lax.axis_size("expert")
    pair = w_gate.shape[0]
    capacity = 9 * rows * routes.shape[1] // (8 * experts)
    prompt_dev = PROMPT // expert_devices
    ff = w_gate.shape[2]
    e = lax.axis_index("expert").astype(jnp.int32).reshape(1)
    j = (lax.axis_index("dp") % pair).astype(jnp.int32).reshape(1)
    members = pair * expert_devices
    everyone = ("dp", "expert")
    exchange = [list(range(p * members, (p + 1) * members)) for p in range(dp // pair)]
    alike = [list(range(q, dp, pair)) for q in range(pair)]
    pairs = [list(range(p * pair, (p + 1) * pair)) for p in range(dp // pair)]

    def swap(x):
        return lax.all_to_all(x, everyone, split_axis=0, concat_axis=0, axis_index_groups=exchange, tiled=True)

    cos, sin = (jnp.asarray(t) for t in angle_tables())
    gain1, gain2 = norm_attn[None, :], norm_ffn[None, :]

    prompt_x = lax.all_gather(tokens[:prompt_dev], "expert", axis=0, tiled=True)
    slots_t = slot_table(routes.T, priority, pair, capacity)
    slots = slots_t.T
    grads_out = dispatch(slots_t, cotangent, members, capacity)
    tokens, grads_out = lax.optimization_barrier((tokens, grads_out))
    grads_in = swap(grads_out).reshape(-1, width)
    h_own, q, k_own, v_own = project(e, tokens, gain1, (w_query, w_key, w_value), cos, sin, True)
    h_prompt, k_prompt, v_prompt = project(e, prompt_x, gain1, (w_key, w_value), cos, sin, False)
    o, lse = attn_fwd(e, q, k_own, v_own, k_prompt, v_prompt)

    wcat = jnp.concatenate(
        [router, const_w.transpose(1, 0, 2).reshape(width, -1), jnp.zeros((width, 128 - experts - 4), BF)], axis=1
    )
    prev = jnp.pad(prev_logits, ((0, 0), (0, 128 - experts)))
    x2, h2, aux, ext = gates(tokens, o, w_out, gain2, wcat, prev, routes, experts)
    made, back, ffn_sum = experts_on_rows(slots_t, h2, ext, grads_in, w_gate, w_up, w_down, capacity)
    ffn_sum = lax.psum_scatter(ffn_sum, "dp", scatter_dimension=2, axis_index_groups=alike, tiled=True)
    made = swap(made.reshape(members, capacity, width)).reshape(-1, width)
    grad_prev, dx2, da, do, cat, sums = combine(
        back, slots, routes, aux, x2, h2, cotangent, gain2, wcat, const_v, w_out, experts
    )
    dq, dk, dv = attn_bwd(e, q, do, o, lse, k_own, v_own, k_prompt, v_prompt, cos, sin)
    dh_prompt, sum_p = prompt_back(dk, dv, w_key, w_value, prompt_x)
    dh_own, sum_o = own_back(dq, dk, dv, w_query, w_key, w_value, tokens)
    rest = dp // 2
    out_rows = padded_rows(4 * width, rest)
    chunks = max(n for n in (1, 2, 3) if out_rows // 2 % (n * 4 * rest * 16) == 0)
    grad_w = weight_back(h_prompt, h_own, o, da, dq, dk, dv, out_rows)
    n = experts
    small = jnp.concatenate([cat[:n + 4], sums[:3], sum_p + sum_o, jnp.zeros((4, width), F32)], axis=0)
    grad_w, small, got = device_sums(grad_w, small, dh_prompt, rest, prompt_dev, chunks)
    grad_w = grad_w.astype(F32)
    grad_tokens = token_back(dh_own, got, tokens, dx2, gain1)

    mixed = mix(made, slots, routes, aux, x2, h2, const_v, experts)
    ffn_sum = ffn_sum.reshape(3, width, pair, -1).transpose(2, 0, 1, 3)
    ffn_sum = lax.all_to_all(ffn_sum, "dp", split_axis=0, concat_axis=0, axis_index_groups=pairs, tiled=True)
    ffn_sum = ffn_sum.astype(F32)
    return (
        mixed,
        grad_tokens,
        grad_prev,
        small[n + 7],
        grad_w[:width],
        grad_w[width:2 * width],
        grad_w[2 * width:3 * width],
        grad_w[3 * width:4 * width],
        small[n + 6],
        small[:n].T,
        small[n:n + 4].reshape(2, 2, width).transpose(0, 2, 1),
        small[n + 4:n + 6],
        ffn_sum[:, 0],
        ffn_sum[:, 1],
        ffn_sum[:, 2].transpose(0, 2, 1),
    )


def solution(mesh):
    block = P(("dp", "expert"), None)
    in_specs = (block, block, block, P(("dp", "expert"))) + (P(),) * 9 + (P("expert", None, None),) * 3 + (block,)
    out_specs = (block, block, block) + (P(),) * 9 + (
        P("expert", None, "dp"), P("expert", None, "dp"), P("expert", "dp", None),
    )
    return jax.shard_map(local, mesh=mesh, in_specs=in_specs, out_specs=out_specs, check_vma=False)
```

```python
import functools

import jax
import jax.numpy as jnp
import numpy as np
from jax import lax
from jax.experimental import pallas as pl
from jax.experimental.pallas import tpu as pltpu
from jax.sharding import PartitionSpec as P

HEADS = 12
FFN_EXP = 8
PROMPT = 2048
NCONT = 8
CONT = 256

epsilon = 1e-06
LOG2E = 1.4426950408889634
F32 = jnp.float32
BF = jnp.bfloat16
NN = (((1,), (0,)), ((), ()))
NT = (((1,), (1,)), ((), ()))
VMEM_LIMIT = 56 << 20


def dot(a, b, dims=NN):
    return lax.dot_general(a, b, dims, preferred_element_type=F32)


def params(**kw):
    return pltpu.CompilerParams(vmem_limit_bytes=VMEM_LIMIT, **kw)


def whole(shape):
    return pl.BlockSpec(shape, lambda *_: (0,) * len(shape))


def rms_scale(x):
    return lax.rsqrt(jnp.mean(x * x, axis=-1, keepdims=True) + epsilon)


def angle_tables():
    positions = np.arange(PROMPT + CONT, dtype=np.float32)
    frequency = np.exp(
        np.float32(-np.log(10000.0)) * np.arange(32, dtype=np.float32) * np.float32(2.0) / np.float32(64)
    ).astype(np.float32)
    angle = (positions[:, None] * frequency[None, :]).astype(np.float64)
    cosine = np.cos(angle).astype(np.float32)
    sine = np.sin(angle).astype(np.float32)
    return (
        np.concatenate([cosine] * 4, axis=1),
        np.concatenate([-sine, sine, -sine, sine], axis=1),
    )


def lane_iota(width=128):
    return lax.broadcasted_iota(jnp.int32, (1, width), 1)


def swap_halves(x):
    return jnp.where(lane_iota() % 64 < 32, pltpu.roll(x, 96, 1), pltpu.roll(x, 32, 1))


def project_kernel(e_ref, x_ref, gain_ref, *refs, count):
    weights, (cos_ref, sin_ref), (h_ref, *outs) = refs[:count], refs[count:count + 2], refs[count + 2:]
    x = x_ref[...].astype(F32)
    h = (x * rms_scale(x) * gain_ref[...]).astype(BF)
    h_ref[...] = h
    cosine, sine = cos_ref[...], sin_ref[...]
    for n, (w_ref, out_ref) in enumerate(zip(weights, outs)):
        full = dot(h, w_ref[...])
        if n == count - 1:
            out_ref[...] = full.astype(BF)
            continue
        for i in range(full.shape[1] // 128):
            part = full[:, i * 128:(i + 1) * 128]
            out_ref[:, i * 128:(i + 1) * 128] = (part * cosine + swap_halves(part) * sine).astype(BF)


def project(e, x, gain, weights, cos, sin, own, tile=256):
    rows, width = x.shape
    block = pl.BlockSpec((tile, width), lambda i, *_: (i, 0))
    half = rows // 2 // tile

    def position(i, e_ref):
        if not own:
            return (i, 0)
        return (jnp.where(i < half, e_ref[0] * half + i, PROMPT // tile), 0)

    table = pl.BlockSpec((tile, 128), position)
    return pl.pallas_call(
        functools.partial(project_kernel, count=len(weights)),
        grid_spec=pltpu.PrefetchScalarGridSpec(
            num_scalar_prefetch=1,
            grid=(rows // tile,),
            in_specs=[block, whole((1, width))] + [whole(weights[0].shape)] * len(weights) + [table, table],
            out_specs=[block] * (len(weights) + 1),
        ),
        out_shape=[jax.ShapeDtypeStruct((rows, width), BF)] * (len(weights) + 1),
        compiler_params=params(),
        cost_estimate=pl.CostEstimate(
            flops=2 * rows * width * width * len(weights), bytes_accessed=2 * rows * width * 6, transcendentals=0
        ),
        name="project_own" if own else "project_prompt",
    )(e, x, gain, *weights, cos, sin)


def attn_fwd_kernel(e_ref, q_ref, ko_ref, vo_ref, kp_ref, vp_ref, o_ref, lse_ref, vt_ref, qm_ref, m_ref, acc_ref, *, chunk, tile, scale):
    e = e_ref[0]
    rows = q_ref.shape[0]
    half = rows // 2
    npr = kp_ref.shape[0]
    nchunk = npr // chunk
    lane = lax.broadcasted_iota(jnp.int32, (1, 128), 1)
    low = lane < 64
    c = scale * LOG2E
    zero = jnp.zeros((), BF)
    q = q_ref[...]
    qm_ref[0] = jnp.where(low, q, zero)
    qm_ref[1] = jnp.where(low, zero, q)
    ones = jnp.ones((16, npr + rows), BF)
    for r, n, ref in ((0, npr, vp_ref), (npr, rows, vo_ref)):
        vt = ref[...].T
        vt_ref[0, :64, r:r + n] = vt[:64]
        vt_ref[1, :64, r:r + n] = vt[64:]
    vt_ref[0, 64:, :] = ones
    vt_ref[1, 64:, :] = ones
    tri = lax.broadcasted_iota(jnp.int32, (tile, tile), 0) <= lax.broadcasted_iota(jnp.int32, (tile, tile), 1)

    def first(q0, qn, k, vts):
        for h in range(2):
            s = dot(k, qm_ref[h, q0:q0 + qn, :], NT)
            s = s * c
            s = jnp.where(tri, s, -1e30)
            mx = jnp.max(s, axis=0, keepdims=True)
            p = jnp.exp2(s - mx).astype(BF)
            m_ref[h, 0:1, q0:q0 + qn] = mx
            acc_ref[h, :, q0:q0 + qn] = dot(vts[h], p)

    def step(blocks, k, vts):
        ss = [[dot(k, qm_ref[h, q0:q0 + qn, :], NT) for h in range(2)] for q0, qn in blocks]
        for (q0, qn), sb in zip(blocks, ss):
            for h in range(2):
                s = sb[h] * c
                mx = jnp.max(s, axis=0, keepdims=True)
                m = m_ref[h, 0:1, q0:q0 + qn]
                mn = jnp.maximum(m, mx)
                p = jnp.exp2(s - mn).astype(BF)
                m_ref[h, 0:1, q0:q0 + qn] = mn
                acc_ref[h, :, q0:q0 + qn] = acc_ref[h, :, q0:q0 + qn] * jnp.exp2(m - mn) + dot(vts[h], p)

    for j in range(rows // tile):
        r0 = j * tile
        first(r0, tile, ko_ref[r0:r0 + tile, :], [vt_ref[h, :, npr + r0:npr + r0 + tile] for h in range(2)])
    for j in range(1, half // tile):
        for i in range(j):
            r0 = i * tile
            step([(j * tile, tile)], ko_ref[r0:r0 + tile, :], [vt_ref[h, :, npr + r0:npr + r0 + tile] for h in range(2)])

    def body(ci, blocks):
        r0 = pl.multiple_of(ci * chunk, chunk)
        step(blocks, kp_ref[pl.ds(r0, chunk), :], [vt_ref[h, :, pl.ds(r0, chunk)] for h in range(2)])

    ne = e * half // chunk

    @pl.loop(0, ne)
    def _(ci):
        body(ci, [(0, half), (half, half)])

    @pl.loop(ne, nchunk)
    def _(ci):
        body(ci, [(half, half)])

    outs = []
    for h in range(2):
        l = acc_ref[h, 64:65, :]
        outs.append(acc_ref[h, :64, :] / l)
        lse_ref[0, h:h + 1, :] = m_ref[h, 0:1, :] + jnp.log2(l)
    o_ref[...] = jnp.concatenate(outs, axis=0).T.astype(BF)


def attn_fwd(e, q, ko, vo, kp, vp, *, chunk=512, tile=256):
    rows, width = q.shape
    npr = kp.shape[0]
    pairs = width // 128
    own = pl.BlockSpec((rows, 128), lambda i, *_: (0, i))
    pr = pl.BlockSpec((npr, 128), lambda i, *_: (0, i))
    return pl.pallas_call(
        functools.partial(attn_fwd_kernel, chunk=chunk, tile=tile, scale=0.125),
        grid_spec=pltpu.PrefetchScalarGridSpec(
            num_scalar_prefetch=1, grid=(pairs,),
            in_specs=[own, own, own, pr, pr],
            out_specs=[own, pl.BlockSpec((1, 2, rows), lambda i, *_: (i, 0, 0))],
            scratch_shapes=[pltpu.VMEM((2, 80, npr + rows), BF), pltpu.VMEM((2, rows, 128), BF),
            pltpu.VMEM((2, 8, rows), F32), pltpu.VMEM((2, 80, rows), F32)]),
        out_shape=[jax.ShapeDtypeStruct((rows, width), BF), jax.ShapeDtypeStruct((pairs, 2, rows), F32)],
        compiler_params=params(),
        cost_estimate=pl.CostEstimate(flops=4 * rows * npr * width * 2, bytes_accessed=2 * npr * width * 4, transcendentals=rows * npr * 12),
        name="attn_fwd",
    )(e, q, ko, vo, kp, vp)


def attn_bwd_kernel(e_ref, q_ref, do_ref, o_ref, lse_ref, ko_ref, vo_ref, kp_ref, vp_ref, cos_ref, sin_ref,
               dq_ref, dk_ref, dv_ref,
               kt_ref, dqt_ref, qm_ref, dom_ref, dl_ref, dks_ref, dvs_ref, *, tile, scale):
    e = e_ref[0]
    rows = q_ref.shape[0]
    half = rows // 2
    chunk = half
    npr = kp_ref.shape[0]
    nchunk = npr // chunk
    cont = cos_ref.shape[0] - npr
    lane = lax.broadcasted_iota(jnp.int32, (1, 128), 1)
    low = lane < 64
    c = scale * LOG2E
    zero = jnp.zeros((), BF)
    q = q_ref[...]
    do = do_ref[...]
    qm_ref[0] = jnp.where(low, q, zero)
    qm_ref[1] = jnp.where(low, zero, q)
    dom_ref[0] = jnp.where(low, do, zero)
    dom_ref[1] = jnp.where(low, zero, do)
    prod = (do.astype(F32) * o_ref[...].astype(F32)).T
    dl_ref[0:1, :] = jnp.sum(prod[:64], axis=0, keepdims=True)
    dl_ref[1:2, :] = jnp.sum(prod[64:], axis=0, keepdims=True)
    kt_ref[:, :npr] = kp_ref[...].T
    kt_ref[:, npr:] = ko_ref[...].T
    tri = lax.broadcasted_iota(jnp.int32, (tile, tile), 0) <= lax.broadcasted_iota(jnp.int32, (tile, tile), 1)

    def unrope(x, pos, n):
        first = (lane % 64) < 32
        sw = jnp.where(first, pltpu.roll(x, 96, 1), pltpu.roll(x, 32, 1))
        return x * cos_ref[pl.ds(pos, n), :] - sw * sin_ref[pl.ds(pos, n), :]

    def block(k, v, kt, q0, qn, mask):
        dk = dv = None
        dqs = []
        qs = [qm_ref[h, q0:q0 + qn, :] for h in range(2)]
        dos = [dom_ref[h, q0:q0 + qn, :] for h in range(2)]
        sts = [dot(k, qs[h], NT) for h in range(2)]
        dps = [dot(v, dos[h], NT) for h in range(2)]
        for h in range(2):
            p = jnp.exp2(sts[h] * c - lse_ref[0, h:h + 1, q0:q0 + qn])
            if mask is not None:
                p = jnp.where(mask, p, 0.0)
            ds = (p * (dps[h] - dl_ref[h:h + 1, q0:q0 + qn])).astype(BF)
            dvh = dot(p.astype(BF), dos[h])
            dkh = dot(ds, qs[h])
            dk, dv = (dkh, dvh) if dk is None else (dk + dkh, dv + dvh)
            dqs.append(dot(kt[h * 64:(h + 1) * 64], ds))
        return dk, dv, jnp.concatenate(dqs, axis=0)

    nt = rows // tile
    for i in range(nt):
        r0 = i * tile
        k = ko_ref[r0:r0 + tile, :]
        v = vo_ref[r0:r0 + tile, :]
        kt = kt_ref[:, npr + r0:npr + r0 + tile]
        prompt = r0 < half
        dk = dv = None
        for j in (range(i, nt // 2) if prompt else [i]):
            a, b, dq = block(k, v, kt, j * tile, tile, tri if i == j else None)
            dk, dv = (a, b) if dk is None else (dk + a, dv + b)
            sl = slice(j * tile, (j + 1) * tile)
            if i == 0 or not prompt:
                dqt_ref[:, sl] = dq
            else:
                dqt_ref[:, sl] += dq
        if prompt:
            dks_ref[r0:r0 + tile, :] = dk
            dvs_ref[r0:r0 + tile, :] = dv
        else:
            o0 = npr + r0 - half
            dk_ref[o0:o0 + tile, :] = (unrope(dk, npr, tile) * scale).astype(BF)
            dv_ref[o0:o0 + tile, :] = dv.astype(BF)

    def chunk_step(ci, kind):
        r0 = pl.multiple_of(ci * chunk, chunk)
        k = kp_ref[pl.ds(r0, chunk), :]
        v = vp_ref[pl.ds(r0, chunk), :]
        kt = kt_ref[:, pl.ds(r0, chunk)]
        dk, dv, dq = block(k, v, kt, half, half, None)
        dqt_ref[:, half:] += dq
        if kind == 0:
            a, b, dq = block(k, v, kt, 0, half, None)
            dk, dv = dk + a, dv + b
            dqt_ref[:, :half] += dq
        elif kind == 1:
            dk, dv = dk + dks_ref[...], dv + dvs_ref[...]
        dk_ref[pl.ds(r0, chunk), :] = (unrope(dk, r0, chunk) * scale).astype(BF)
        dv_ref[pl.ds(r0, chunk), :] = dv.astype(BF)

    @pl.loop(0, e)
    def _(ci):
        chunk_step(ci, 0)

    chunk_step(e, 1)

    @pl.loop(e + 1, nchunk)
    def _(ci):
        chunk_step(ci, 2)

    dq = dqt_ref[...].T
    base = pl.multiple_of(e * half, half)
    dq_ref[:half, :] = (unrope(dq[:half], base, half) * scale).astype(BF)
    for r in range(half, rows, cont):
        dq_ref[r:r + cont, :] = (unrope(dq[r:r + cont], npr, cont) * scale).astype(BF)


def attn_bwd(e, q, do, o, lse, ko, vo, kp, vp, cos, sin, *, tile=256):
    rows, width = q.shape
    npr = kp.shape[0]
    keys = npr + rows // 2
    pairs = width // 128
    own = pl.BlockSpec((rows, 128), lambda i, *_: (0, i))
    pr = pl.BlockSpec((npr, 128), lambda i, *_: (0, i))
    al = pl.BlockSpec((keys, 128), lambda i, *_: (0, i))
    tab = pl.BlockSpec(cos.shape, lambda i, *_: (0, 0))
    return pl.pallas_call(
        functools.partial(attn_bwd_kernel, tile=tile, scale=0.125),
        grid_spec=pltpu.PrefetchScalarGridSpec(
            num_scalar_prefetch=1, grid=(pairs,),
            in_specs=[own, own, own, pl.BlockSpec((1, 2, rows), lambda i, *_: (i, 0, 0)), own, own, pr, pr, tab, tab],
            out_specs=[own, al, al],
            scratch_shapes=[pltpu.VMEM((128, npr + rows), BF), pltpu.VMEM((128, rows), F32),
                            pltpu.VMEM((2, rows, 128), BF), pltpu.VMEM((2, rows, 128), BF),
                            pltpu.VMEM((8, rows), F32),
                            pltpu.VMEM((rows // 2, 128), F32), pltpu.VMEM((rows // 2, 128), F32)]),
        out_shape=[jax.ShapeDtypeStruct((rows, width), BF), jax.ShapeDtypeStruct((keys, width), BF),
                   jax.ShapeDtypeStruct((keys, width), BF)],
        compiler_params=params(),
        cost_estimate=pl.CostEstimate(flops=10 * rows * npr * width * 2, bytes_accessed=2 * npr * width * 8, transcendentals=rows * npr * 12),
        name="attn_bwd",
    )(e, q, do, o, lse, ko, vo, kp, vp, cos, sin)


MESH = pl.DeviceIdType.MESH


def pick(values, lane, index):
    return jnp.sum(jnp.where(lane == index, values, 0.0), axis=1, keepdims=True)


def softmax_pair(a, b):
    top = jnp.maximum(a, b)
    ea, eb = jnp.exp(a - top), jnp.exp(b - top)
    total = ea + eb
    return ea / total, eb / total


def spread(column):
    lane = lane_iota()
    parts, left = jnp.zeros((1, 128), F32), column
    for n in range(3):
        part = left.astype(BF).astype(F32)
        parts = jnp.where(lane == n, part, parts)
        left = left - part
    return parts.astype(BF)


def gate_kernel(x_ref, o_ref, w_ref, gain_ref, wcat_ref, prev_ref, routes_ref, x2_ref, h2_ref, aux_ref, ext_ref, *, experts):
    x2 = x_ref[...].astype(F32) + dot(o_ref[...], w_ref[...])
    x2_ref[...] = x2
    h2 = (x2 * rms_scale(x2) * gain_ref[...]).astype(BF)
    h2_ref[...] = h2
    logits = dot(h2, wcat_ref[...]) + prev_ref[...]
    lane = lane_iota()
    gates = softmax_pair(*[pick(logits, lane, routes_ref[:, k:k + 1]) for k in range(2)])
    aux = logits
    for k in range(2):
        aux = jnp.where(lane == experts + k, gates[k], aux)
    at = experts + 2
    for c in range(2):
        alpha = softmax_pair(*[pick(logits, lane, experts + 2 * c + k) for k in range(2)])
        for k in range(2):
            aux = jnp.where(lane == at + 2 * c + k, alpha[k], aux)
    aux_ref[...] = aux
    for k in range(2):
        ext_ref[:, k * 128:(k + 1) * 128] = spread(gates[k])


def gates(x, o, w_out, gain, wcat, prev, routes, experts, tile=256):
    rows, width = x.shape
    block = pl.BlockSpec((tile, width), lambda i: (i, 0))
    thin = pl.BlockSpec((tile, 128), lambda i: (i, 0))
    return pl.pallas_call(
        functools.partial(gate_kernel, experts=experts),
        grid=(rows // tile,),
        in_specs=[block, block, whole(w_out.shape), whole(gain.shape), whole(wcat.shape), thin,
                  pl.BlockSpec((tile, 2), lambda i: (i, 0))],
        out_specs=[block, block, thin, pl.BlockSpec((tile, 256), lambda i: (i, 0))],
        out_shape=[jax.ShapeDtypeStruct((rows, width), F32), jax.ShapeDtypeStruct((rows, width), BF),
                   jax.ShapeDtypeStruct((rows, 128), F32), jax.ShapeDtypeStruct((rows, 256), BF)],
        compiler_params=params(),
        cost_estimate=pl.CostEstimate(flops=2 * rows * width * width, bytes_accessed=12 * rows * width, transcendentals=0),
        name="gates",
    )(x, o, w_out, gain, wcat, prev, routes)


def dispatch_kernel(slot_ref, rows_ref, out_ref, *, capacity):
    ids = pl.program_id(0) * capacity + lax.broadcasted_iota(jnp.int32, (capacity, 1), 0)
    hot = [jnp.where(ids == slot_ref[k:k + 1, :], 1.0, 0.0).astype(BF) for k in range(2)]
    out_ref[0] = dot(hot[0] + hot[1], rows_ref[...]).astype(BF)


def dispatch(slots, rows, destinations, capacity):
    count, width = rows.shape
    return pl.pallas_call(
        functools.partial(dispatch_kernel, capacity=capacity),
        grid=(destinations,),
        in_specs=[whole(slots.shape), whole(rows.shape)],
        out_specs=pl.BlockSpec((1, capacity, width), lambda i: (i, 0, 0)),
        out_shape=jax.ShapeDtypeStruct((destinations, capacity, width), BF),
        compiler_params=params(),
        cost_estimate=pl.CostEstimate(flops=2 * destinations * capacity * count * width, bytes_accessed=4 * count * width,
                                      transcendentals=0),
        name="dispatch_grads",
    )(slots, rows)


def expert_kernel(slot_ref, h2_ref, ext_ref, g_ref, wg_hbm, wu_hbm, wd_hbm, made_ref, back_hbm, grad_hbm,
                  wg_ref, wu_ref, wd_ref, a_ref, s_ref, d_ref, at_ref, dt_ref, hid_ref, dg_ref, du_ref, macc_ref,
                  bacc_ref, out_ref, send_sem, recv_sem, local_sem, out_sem, *, capacity, tile, grad_tile):
    dp, ex = lax.axis_index("dp"), lax.axis_index("expert")
    j, c, x = dp % 2, ex % 2, ex // 2
    width = h2_ref.shape[1]
    ff = wg_ref.shape[1]
    loads = [pltpu.make_async_copy(src.at[j], dst, local_sem.at[n])
             for n, (src, dst) in enumerate(((wg_hbm, wg_ref), (wu_hbm, wu_ref), (wd_hbm, wd_ref)))]
    for copy in loads:
        copy.start()

    def flip(bit, by):
        return bit + by * (1 - 2 * bit)

    def peer(r):
        return dp + (r // 2 % 2) * (1 - 2 * j), flip(x, r // 4) * 2 + flip(c, r % 2)

    def place(r):
        return flip(j, r // 2 % 2) * 4 + flip(x, r // 4) * 2 + flip(c, r % 2)

    barrier = pltpu.get_barrier_semaphore()
    for r in range(1, 8):
        pl.semaphore_signal(barrier, inc=1, device_id=peer(r), device_id_type=MESH)
    pl.semaphore_wait(barrier, 7)

    def send(src, dst, kind, r):
        n = kind * 8 + r
        copy = pltpu.make_async_remote_copy(src_ref=src, dst_ref=dst, send_sem=send_sem.at[n], recv_sem=recv_sem.at[n],
                                            device_id=peer(r), device_id_type=MESH)
        copy.start()
        return copy

    rows = {}
    for r in (4, 5, 6, 7, 2, 3, 1, 0):
        ids = place(r) * capacity + lax.broadcasted_iota(jnp.int32, (capacity, 1), 0)
        hot = [jnp.where(ids == slot_ref[k:k + 1, :], 1.0, 0.0).astype(BF) for k in range(2)]
        into = s_ref if r else a_ref
        into[r, :, :width] = dot(hot[0] + hot[1], h2_ref[...]).astype(BF)
        into[r, :, width:] = (dot(hot[0], ext_ref[:, :128]) + dot(hot[1], ext_ref[:, 128:])).astype(BF)
        if r:
            rows[r] = send(s_ref.at[r], a_ref.at[r], 0, r)

    for copy in loads:
        copy.wait()
    returned = []
    mine = pl.ds(pl.multiple_of(place(0) * capacity, 16), capacity)
    two = 2 * capacity
    for n, first in enumerate((0, 4, 6, 2)):
        for r in (first, first + 1):
            if r:
                rows[r].wait_recv()
            got = a_ref[r]
            half = pl.ds((r - first) * capacity, capacity)
            gate = jnp.sum(got[:, width:].astype(F32), axis=1, keepdims=True)
            g = g_ref[pl.ds(pl.multiple_of(place(r) * capacity, 16), capacity), :].astype(F32)
            d_ref[half, :] = (g * gate).astype(BF)
        span = pl.ds(n * two, two)
        a = a_ref[first:first + 2, :, :width].reshape(two, width)
        at_ref[:, span] = a.T
        dt_ref[:, span] = d_ref[...].T
        macc_ref[...] = jnp.zeros_like(macc_ref)
        bacc_ref[...] = jnp.zeros_like(bacc_ref)

        @pl.loop(0, ff // tile)
        def _(i):
            cols = pl.ds(pl.multiple_of(i * tile, tile), tile)
            a = a_ref[first:first + 2, :, :width].reshape(two, width)
            gate, up = dot(a, wg_ref[:, cols]), dot(a, wu_ref[:, cols])
            dh = dot(d_ref[...], wd_ref[cols, :], NT)
            sig = jax.nn.sigmoid(gate)
            act = gate * sig
            hidden = (act * up).astype(BF)
            du = (dh * act).astype(BF)
            dg = (dh * up * sig * (1.0 + gate * (1.0 - sig))).astype(BF)
            hid_ref[span, cols] = hidden
            du_ref[span, cols] = du
            dg_ref[span, cols] = dg
            macc_ref[...] += dot(hidden, wd_ref[cols, :])
            bacc_ref[...] += dot(dg, wg_ref[:, cols], NT) + dot(du, wu_ref[:, cols], NT)

        for r in (first, first + 1):
            half = pl.ds((r - first) * capacity, capacity)
            if r:
                rows[r].wait_send()
            theirs = pl.ds(pl.multiple_of(place(r) * capacity, 16), capacity)
            made = macc_ref[half, :].astype(BF)
            made_ref[theirs, :] = made
            s_ref[r, :, :width] = bacc_ref[half, :].astype(BF)
            s_ref[r, :, width:] = spread(jnp.sum(g_ref[theirs, :].astype(F32) * made.astype(F32), axis=1, keepdims=True))
            if r:
                returned.append(send(s_ref.at[r], back_hbm.at[mine], 1, r))
            else:
                kept = pltpu.make_async_copy(s_ref.at[0], back_hbm.at[mine], local_sem.at[3])
                kept.start()

    steps = ff // grad_tile

    def put(i, slot):
        cols = pl.ds(pl.multiple_of(i * grad_tile, grad_tile), grad_tile)
        return pltpu.make_async_copy(out_ref.at[slot], grad_hbm.at[:, :, cols], out_sem.at[slot])

    @pl.loop(0, steps)
    def _(i):
        slot = i % 2

        @pl.when(i >= 2)
        def _():
            put(i - 2, slot).wait()

        cols = pl.ds(pl.multiple_of(i * grad_tile, grad_tile), grad_tile)
        out_ref[slot, 0] = dot(at_ref[...], dg_ref[:, cols]).astype(BF)
        out_ref[slot, 1] = dot(at_ref[...], du_ref[:, cols]).astype(BF)
        out_ref[slot, 2] = dot(dt_ref[...], hid_ref[:, cols]).astype(BF)
        put(i, slot).start()

    for i in range(max(steps - 2, 0), steps):
        put(i, i % 2).wait()
    kept.wait()
    for copy in returned:
        copy.wait_recv()
        copy.wait_send()


def experts_on_rows(slots, h2, ext, g, w_gate, w_up, w_down, capacity, tile=512, grad_tile=256):
    width = h2.shape[1]
    ff = w_gate.shape[2]
    total = 8 * capacity
    vm = pltpu.VMEM
    vmem, hbm = pl.BlockSpec(memory_space=pltpu.VMEM), pl.BlockSpec(memory_space=pl.ANY)
    return pl.pallas_call(
        functools.partial(expert_kernel, capacity=capacity, tile=tile, grad_tile=grad_tile),
        in_specs=[vmem] * 4 + [hbm] * 3,
        out_specs=[vmem, hbm, hbm],
        out_shape=[jax.ShapeDtypeStruct((total, width), BF), jax.ShapeDtypeStruct((total, width + 128), BF),
                   jax.ShapeDtypeStruct((3, width, ff), BF)],
        scratch_shapes=[
            vm((width, ff), BF), vm((width, ff), BF), vm((ff, width), BF),
            vm((8, capacity, width + 128), BF), vm((8, capacity, width + 128), BF),
            vm((2 * capacity, width), BF), vm((width, total), BF), vm((width, total), BF),
            vm((total, ff), BF), vm((total, ff), BF), vm((total, ff), BF),
            vm((2 * capacity, width), F32), vm((2 * capacity, width), F32), vm((2, 3, width, grad_tile), BF),
            pltpu.SemaphoreType.DMA((16,)), pltpu.SemaphoreType.DMA((16,)), pltpu.SemaphoreType.DMA((4,)),
            pltpu.SemaphoreType.DMA((2,)),
        ],
        compiler_params=pltpu.CompilerParams(vmem_limit_bytes=62 << 20, collective_id=1, has_side_effects=True),
        cost_estimate=pl.CostEstimate(flops=18 * total * width * ff, bytes_accessed=12 * width * ff + 8 * total * width,
                                      transcendentals=total * ff),
        name="experts_on_rows",
    )(slots, h2, ext, g, w_gate, w_up, w_down)


def one(cond):
    return jnp.where(cond, 1.0, 0.0)


def pick_parts(aux, routes, experts):
    lane = lane_iota()
    gate = [pick(aux, lane, experts + k) for k in range(2)]
    alpha = [[pick(aux, lane, experts + 2 + 2 * c + k) for k in range(2)] for c in range(2)]
    copy = [one(routes[k] == FFN_EXP + 1) for k in range(2)]
    const = [[one(routes[k] == FFN_EXP + 2 + c) for c in range(2)] for k in range(2)]
    on_h2 = [copy[k] + const[k][0] * alpha[0][0] + const[k][1] * alpha[1][0] for k in range(2)]
    return gate, alpha, copy, const, on_h2


def one_hot(slots, total):
    return jnp.where(lane_iota(total) == slots, 1.0, 0.0).astype(BF)


def combine_kernel(back_ref, slot_ref, routes_ref, aux_ref, x2_ref, h2_ref, g_ref, gain_ref, wcat_ref, v_ref, w_ref,
                   prev_ref, dx2_ref, da_ref, do_ref, cat_ref, sums_ref, *, experts):
    step = pl.program_id(0)
    lane = lane_iota()
    h2 = h2_ref[...].astype(F32)
    g = g_ref[...].astype(F32)
    x2 = x2_ref[...]
    width = x2.shape[1]
    r2 = rms_scale(x2)
    route = [routes_ref[:, k:k + 1] for k in range(2)]
    gate, alpha, copy, const, on_h2 = pick_parts(aux_ref[...], route, experts)
    hot = [one_hot(slot_ref[:, k:k + 1], back_ref.shape[0]) for k in range(2)]
    g_h2 = jnp.sum(g * h2, axis=1, keepdims=True)
    g_v = [jnp.sum(g * v_ref[c:c + 1, :], axis=1, keepdims=True) for c in range(2)]
    dgate = []
    for k in range(2):
        at_expert = jnp.sum(dot(hot[k], back_ref[:, width:]), axis=1, keepdims=True)
        dgate.append(at_expert + on_h2[k] * g_h2 + const[k][0] * alpha[0][1] * g_v[0] + const[k][1] * alpha[1][1] * g_v[1])
    mean = gate[0] * dgate[0] + gate[1] * dgate[1]
    dl = [gate[k] * (dgate[k] - mean) for k in range(2)]
    grads = jnp.where(lane == route[0], dl[0], 0.0) + jnp.where(lane == route[1], dl[1], 0.0)
    prev_ref[...] = grads[:, :experts]
    weight = [gate[0] * const[0][c] + gate[1] * const[1][c] for c in range(2)]
    sums = []
    on_g = copy[0] * gate[0] + copy[1] * gate[1]
    for c in range(2):
        da0 = weight[c] * g_h2
        da1 = weight[c] * g_v[c]
        mid = alpha[c][0] * da0 + alpha[c][1] * da1
        grads = jnp.where(lane == experts + 2 * c, alpha[c][0] * (da0 - mid), grads)
        grads = jnp.where(lane == experts + 2 * c + 1, alpha[c][1] * (da1 - mid), grads)
        on_g = on_g + alpha[c][0] * weight[c]
        sums.append(jnp.sum((alpha[c][1] * weight[c]) * g, axis=0, keepdims=True))
    low = grads.astype(BF)
    cat = dot(low.T, h2_ref[...])
    dh2 = dot(low, wcat_ref[...], NT) + on_g * g + dot(hot[0] + hot[1], back_ref[:, :width])
    sums.append(jnp.sum(dh2 * x2 * r2, axis=0, keepdims=True))
    u = dh2 * gain_ref[...]
    dx2 = g + r2 * (u - x2 * (r2 * r2) * jnp.mean(u * x2, axis=-1, keepdims=True))
    dx2_ref[...] = dx2
    da = dx2.astype(BF)
    da_ref[...] = da
    do_ref[...] = dot(da, w_ref[...], NT).astype(BF)
    parts = jnp.concatenate(sums + [jnp.zeros((8 - len(sums), width), F32)], axis=0)

    @pl.when(step == 0)
    def _():
        cat_ref[...] = cat
        sums_ref[...] = parts

    @pl.when(step > 0)
    def _():
        cat_ref[...] += cat
        sums_ref[...] += parts


def combine(back, slots, routes, aux, x2, h2, g, gain, wcat, const_v, w_out, experts, tile=256):
    rows, width = x2.shape
    block = pl.BlockSpec((tile, width), lambda i: (i, 0))
    thin = pl.BlockSpec((tile, 128), lambda i: (i, 0))
    two = pl.BlockSpec((tile, 2), lambda i: (i, 0))
    sds = jax.ShapeDtypeStruct
    return pl.pallas_call(
        functools.partial(combine_kernel, experts=experts),
        grid=(rows // tile,),
        in_specs=[whole(back.shape), two, two, thin, block, block, block, whole(gain.shape), whole(wcat.shape),
                  whole(const_v.shape), whole(w_out.shape)],
        out_specs=[pl.BlockSpec((tile, experts), lambda i: (i, 0)), block, block, block, whole((128, width)),
                   whole((8, width))],
        out_shape=[sds((rows, experts), F32), sds((rows, width), F32), sds((rows, width), BF),
                   sds((rows, width), BF), sds((128, width), F32), sds((8, width), F32)],
        compiler_params=params(),
        cost_estimate=pl.CostEstimate(flops=4 * rows * width * back.shape[0], bytes_accessed=26 * rows * width,
                                      transcendentals=0),
        name="combine",
    )(back, slots, routes, aux, x2, h2, g, gain, wcat, const_v, w_out)


def mix_kernel(made_ref, slot_ref, routes_ref, aux_ref, x2_ref, h2_ref, v_ref, out_ref, *, experts):
    route = [routes_ref[:, k:k + 1] for k in range(2)]
    gate, alpha, _, const, on_h2 = pick_parts(aux_ref[...], route, experts)
    out = x2_ref[...] + (gate[0] * on_h2[0] + gate[1] * on_h2[1]) * h2_ref[...].astype(F32)
    for c in range(2):
        out = out + ((gate[0] * const[0][c] + gate[1] * const[1][c]) * alpha[c][1]) * v_ref[c:c + 1, :]
    for k in range(2):
        out = out + gate[k] * dot(one_hot(slot_ref[:, k:k + 1], made_ref.shape[0]), made_ref[...])
    out_ref[...] = out.astype(BF)


def mix(made, slots, routes, aux, x2, h2, const_v, experts, tile=256):
    rows, width = x2.shape
    block = pl.BlockSpec((tile, width), lambda i: (i, 0))
    two = pl.BlockSpec((tile, 2), lambda i: (i, 0))
    return pl.pallas_call(
        functools.partial(mix_kernel, experts=experts),
        grid=(rows // tile,),
        in_specs=[whole(made.shape), two, two, pl.BlockSpec((tile, 128), lambda i: (i, 0)), block, block, whole(const_v.shape)],
        out_specs=block,
        out_shape=jax.ShapeDtypeStruct((rows, width), BF),
        compiler_params=params(),
        cost_estimate=pl.CostEstimate(flops=4 * rows * width * made.shape[0], bytes_accessed=12 * rows * width,
                                      transcendentals=0),
        name="mix",
    )(made, slots, routes, aux, x2, h2, const_v)


def padded_rows(rows, rest):
    unit = 8 * rest * 16
    return -(-rows // unit) * unit


def finale_kernel(small_ref, gain_ref, *refs, rest, chunks, norm_row, tile):
    hbm, refs = refs[:12], refs[12:]
    out_ref, small_out_ref, token_hbm = refs[:3]
    local, refs = refs[3:15], refs[15:]
    (turned_ref, g_ref, norm_ref, dh_ref, r0_ref, sm_ref, rs_ref, rd0_ref, td_ref, rd1_ref, tok_ref,
     load_sem, tok_sem, send_sem, recv_sem) = refs[:15]
    r1_ref, r2_ref, r3_ref = (refs[15 + 2 * n:17 + 2 * n] for n in range(3))
    ho_ref, dq_ref, o_ref, da_ref, wq_ref, dk_ref, wk_ref, dv_ref, wv_ref, hp_ref, x_ref, dx2_ref = local[:12]

    loads = [pltpu.make_async_copy(src, dst, load_sem.at[n]) for n, (src, dst) in enumerate(zip(hbm, local))]
    for copy in loads:
        copy.start()

    dp, ex = lax.axis_index("dp"), lax.axis_index("expert")
    c, x, y, z = ex % 2, ex // 2, dp % 2, dp // 2
    mate = (dp, x * 2 + 1 - c)
    across = (dp, (1 - x) * 2 + c)
    beside = (z * 2 + 1 - y, ex)
    ahead = [((z + d) % rest * 2 + y, ex) for d in range(1, rest)]
    barrier = pltpu.get_barrier_semaphore()
    for peer in [mate, across, beside] + ahead:
        pl.semaphore_signal(barrier, inc=1, device_id=peer, device_id_type=MESH)
    pl.semaphore_wait(barrier, 2 + rest)

    started = []

    def send(src, dst, peer):
        n = len(started)
        copy = pltpu.make_async_remote_copy(src_ref=src, dst_ref=dst, send_sem=send_sem.at[n], recv_sem=recv_sem.at[n],
                                            device_id=peer, device_id_type=MESH)
        copy.start()
        started.append(copy)
        return copy

    rows, width = g_ref.shape
    own = ho_ref.shape[0]
    prompt = hp_ref.shape[0]
    half = rows // 2
    size = half // chunks
    q1, q2, q3 = size // 2, size // 4, size // 4 // rest
    cut = width // 3
    part = [pl.ds(0, cut), pl.ds(cut, width - cut)]
    first, second = [across, beside], [beside, across]
    bit1, bit2 = [x, y], [y, x]

    def ds(at, n):
        return pl.ds(pl.multiple_of(at, 16), n)

    def at1(k, p, bit):
        return k * size + bit * q1

    def spot2(k, p, bit):
        return k * size + bit1[p] * q1 + bit * q2

    def stage0(k):
        return [send(g_ref.at[ds((1 - c) * half + k * size, size)], r0_ref.at[ds(k * size, size)], mate)]

    def stage1(k):
        sl = pl.ds(k * size, size)
        r0_ref[sl] = (g_ref[ds(c * half + k * size, size)].astype(F32) + r0_ref[sl].astype(F32)).astype(BF)
        return [send(r0_ref.at[ds(at1(k, p, 1 - bit1[p]), q1), part[p]], r1_ref[p].at[pl.ds(k * q1, q1)], first[p])
                for p in range(2)]

    def stage2(k):
        out = []
        for p in range(2):
            sl = pl.ds(k * q1, q1)
            r1_ref[p][sl] = (r0_ref[ds(at1(k, p, bit1[p]), q1), part[p]].astype(F32) + r1_ref[p][sl].astype(F32)).astype(BF)
            out.append(send(r1_ref[p].at[ds(k * q1 + (1 - bit2[p]) * q2, q2)], r2_ref[p].at[pl.ds(k * q2, q2)], second[p]))
        return out

    def stage3(k):
        out = []
        for p in range(2):
            sl = pl.ds(k * q2, q2)
            r2_ref[p][sl] = (r1_ref[p][ds(k * q1 + bit2[p] * q2, q2)].astype(F32) + r2_ref[p][sl].astype(F32)).astype(BF)
            for d in range(1, rest):
                to = (z + d) % rest
                out.append(send(r2_ref[p].at[ds(k * q2 + to * q3, q3)], r3_ref[p].at[d - 1, pl.ds(k * q3, q3)], ahead[d - 1]))
        return out

    def stage4(k):
        out = []
        for p in range(2):
            total = r2_ref[p][ds(k * q2 + z * q3, q3)].astype(F32)
            for d in range(1, rest):
                total = total + r3_ref[p][d - 1, pl.ds(k * q3, q3)].astype(F32)
            mine = ds(c * half + spot2(k, p, bit2[p]) + z * q3, q3)
            out_ref[mine, part[p]] = total.astype(BF)
            for d in range(1, rest):
                out.append(send(out_ref.at[mine, part[p]], out_ref.at[mine, part[p]], ahead[d - 1]))
        return out

    def stage5(k):
        out = []
        for p in range(2):
            mine = ds(c * half + spot2(k, p, bit2[p]), q2)
            out.append(send(out_ref.at[mine, part[p]], out_ref.at[mine, part[p]], second[p]))
        return out

    def stage6(k):
        out = []
        for p in range(2):
            mine = ds(c * half + at1(k, p, bit1[p]), q1)
            out.append(send(out_ref.at[mine, part[p]], out_ref.at[mine, part[p]], first[p]))
        return out

    def stage7(k):
        mine = ds(c * half + k * size, size)
        return [send(out_ref.at[mine], out_ref.at[mine], mate)]

    stages = (stage0, stage1, stage2, stage3, stage4, stage5, stage6, stage7)
    waiting = {}

    def wait(line):
        for copy in waiting.pop(line, []):
            copy.wait_recv()

    def step(k, s):
        wait(k)
        waiting[k] = stages[s](k) if s < len(stages) else []

    block = own // 2

    def dh_rows(xx, cc):
        return ds((xx * 2 + cc) * block, block)

    def prompt_rows(cc):
        @pl.loop(0, 2 * (block // tile))
        def _(i):
            at = ds((i // (block // tile) * 2 + cc) * block + i % (block // tile) * tile, tile)
            dh_ref[at] = (dot(dk_ref[at], wk_ref[...], NT) + dot(dv_ref[at], wv_ref[...], NT)).astype(BF)

    small_peers = [mate, across, beside]

    def small_step(n):
        wait("small")
        if n < 4:
            sm_ref[n] = small_ref[...] if n == 0 else sm_ref[n - 1] + rs_ref[n - 1]
            if n == 0:
                at = lax.broadcasted_iota(jnp.int32, (small_ref.shape[0], 1), 0)
                norm = jnp.sum(norm_ref[...].T, axis=0, keepdims=True) / gain_ref[...]
                sm_ref[0] = jnp.where(at == norm_row, norm, small_ref[...])
        if n < 3:
            waiting["small"] = [send(sm_ref.at[n], rs_ref.at[n], small_peers[n])]
        elif n == 3:
            waiting["small"] = [send(sm_ref.at[3], rs_ref.at[2 + d], ahead[d - 1]) for d in range(1, rest)]
        else:
            total = sm_ref[3]
            for d in range(1, rest):
                total = total + rs_ref[2 + d]
            small_out_ref[...] = total

    strip = width // 3

    def gradient(b, terms, first_row, w_ref):
        mine = slice(b * strip, (b + 1) * strip)
        got = sum(dot(turned_ref[mine, at:at + count], rhs_ref[...]) for at, count, rhs_ref in terms)
        g_ref[first_row + b * strip:first_row + (b + 1) * strip, :] = got.astype(BF)
        if w_ref is not None:
            share = got * w_ref[mine, :].astype(F32)
            norm_ref[mine, :] += sum(share[:, n:n + 128] for n in range(0, width, 128))

    def put_tokens(i, dh, copies):
        at = pl.ds(i * tile, tile)
        xf = x_ref[at].astype(F32)
        r1 = rms_scale(xf)
        u = dh * gain_ref[...]
        slot = i % 2
        tok_ref[slot] = dx2_ref[at] + r1 * (u - xf * (r1 * r1) * jnp.mean(u * xf, axis=-1, keepdims=True))
        copy = pltpu.make_async_copy(tok_ref.at[slot], token_hbm.at[at], tok_sem.at[slot])
        copy.start()
        copies.append(copy)

    if rows > 4 * width:
        g_ref[4 * width:, :] = jnp.zeros((rows - 4 * width, width), BF)
    norm_ref[...] = jnp.zeros_like(norm_ref)
    tokens = []

    def own_tokens(i):
        at = pl.ds(i * tile, tile)
        dh = dot(dq_ref[at], wq_ref[...], NT)
        if i * tile >= block:
            kv = pl.ds(prompt + i * tile - block, tile)
            dh = dh + dot(dk_ref[kv], wk_ref[...], NT) + dot(dv_ref[kv], wv_ref[...], NT)
        else:
            inner = ds((x * 2 + c) * block + i * tile, tile)
            dh = dh + dh_ref[inner].astype(F32) + rd0_ref[x, at].astype(F32) + rd1_ref[at].astype(F32)
        if len(tokens) >= 2:
            tokens[-2].wait()
        put_tokens(i, dh, tokens)

    hops = (4.5, 6.0, 5.0, 6.5, 6.5, 5.0, 6.0, 4.5)
    due = []

    def begin(now, k):
        step(k, 0)
        due.append([now + hops[0], k, 1])

    def ready(now):
        for entry in sorted(due, key=lambda entry: (entry[0], str(entry[1]))):
            if entry[0] <= now:
                _, k, s = entry
                due.remove(entry)
                if k == "small":
                    small_step(s)
                    last = 4
                else:
                    step(k, s)
                    last = len(stages)
                if s < last:
                    due.append([max(now, entry[0]) + (hops[s] if k != "small" else 5.0), k, s + 1])

    def wait_loads(*numbers):
        for n in numbers:
            loads[n].wait()

    def first_turn():
        wait_loads(0, 1, 2, 3, 4)
        turned_ref[:, :own] = ho_ref[...].T
        turned_ref[:, own:2 * own] = o_ref[...].T

    def second_turn():
        wait_loads(5, 6, 7, 8, 9)
        turned_ref[:, :prompt] = hp_ref[...].T
        turned_ref[:, prompt:] = ho_ref[block:].T

    def first_grads(b):
        gradient(b, [(0, own, dq_ref)], 0, wq_ref)
        gradient(b, [(own, own, da_ref)], 2 * width, None)

    def second_grads(b):
        gradient(b, [(0, prompt + block, dk_ref)], width, wk_ref)
        gradient(b, [(0, prompt + block, dv_ref)], 3 * width, wv_ref)

    def mates():
        prompt_rows(1 - c)
        waiting["dh"] = [send(dh_ref.at[dh_rows(w, 1 - c)], rd0_ref.at[w], mate) for w in range(2)]

    def over():
        wait("dh")
        td_ref[...] = (dh_ref[dh_rows(1 - x, c)].astype(F32) + rd0_ref[1 - x].astype(F32)).astype(BF)
        waiting["dh"] = [send(td_ref, rd1_ref, across)]

    def prompt_tokens(i):
        wait("dh")
        own_tokens(i)

    blocks = own // tile
    tasks = [(4.0, first_turn)] + [(2.0, functools.partial(first_grads, b)) for b in range(3)] + [(3.0, second_turn)]
    tasks += [(4.0, functools.partial(second_grads, b)) for b in range(3)]
    tasks += [(4.0, mates), (4.0, lambda: prompt_rows(c)), (0.5, over)]
    tasks += [(2.0, lambda: wait_loads(10, 11))] + [(2.0, functools.partial(own_tokens, i)) for i in range(blocks // 2, blocks)]
    after = {1: [0], 2: [1], 3: [2], 5: [3], 6: [4], 7: [5]} if chunks == 6 else {7: list(range(chunks))}
    now = 0.0
    for n, (length, task) in enumerate(tasks):
        task()
        now += length
        for k in after.get(n, []):
            begin(now, k)
        if n == 7:
            small_step(0)
            due.append([now + 5.0, "small", 1])
        ready(now)
    late = list(range(blocks // 2))
    while due or late:
        now = max(now, min(entry[0] for entry in due)) if due else now
        ready(now)
        if late and (now > 52.0 or not due):
            prompt_tokens(late.pop(0))
            now += 2.0
    for copy in tokens[-2:]:
        copy.wait()
    for copy in started:
        copy.wait_send()


def finale(small, gain, arrays, rest, norm_row, out_rows, tile=256):
    own, width = arrays[0].shape
    prompt = arrays[9].shape[0]
    block = own // 2
    half = out_rows // 2
    chunks = 6 if half == 6 * 4 * rest * 16 else 1
    lanes = (width // 3, width - width // 3)
    copies = chunks * (1 + 2 + 2 + 2 * (rest - 1) * 2 + 2 + 2 + 1) + 3 + 3 + rest - 1
    vm, dma = pltpu.VMEM, pltpu.SemaphoreType.DMA
    vmem, hbm = pl.BlockSpec(memory_space=pltpu.VMEM), pl.BlockSpec(memory_space=pl.ANY)
    return pl.pallas_call(
        functools.partial(finale_kernel, rest=rest, chunks=chunks, norm_row=norm_row, tile=tile),
        in_specs=[vmem] * 2 + [hbm] * len(arrays),
        out_specs=[vmem, vmem, hbm],
        out_shape=[jax.ShapeDtypeStruct((out_rows, width), BF), jax.ShapeDtypeStruct(small.shape, F32),
                   jax.ShapeDtypeStruct((own, width), F32)],
        scratch_shapes=[vm(a.shape, a.dtype) for a in arrays] + [
            vm((width, prompt + block), BF), vm((out_rows, width), BF), vm((width, 128), F32), vm((prompt, width), BF),
            vm((half, width), BF), vm((4,) + small.shape, F32), vm((2 + rest,) + small.shape, F32),
            vm((2, block, width), BF), vm((block, width), BF), vm((block, width), BF), vm((2, tile, width), F32),
            dma((len(arrays),)), dma((2,)), dma((copies,)), dma((copies,)),
        ] + [vm((half // n, k), BF) for n in (2, 4) for k in lanes]
        + [vm((rest - 1, half // 4 // rest, k), BF) for k in lanes],
        compiler_params=pltpu.CompilerParams(vmem_limit_bytes=62 << 20, collective_id=0, has_side_effects=True),
        cost_estimate=pl.CostEstimate(flops=30 * own * width * width, bytes_accessed=8 * out_rows * width, transcendentals=0),
        name="finale",
    )(small, gain, *arrays)


def slot_table(routes_t, priority, groups, capacity):
    ids = jnp.arange(FFN_EXP, dtype=jnp.int32)
    picked = routes_t[:, None, :] == ids[None, :, None]
    assigned = jnp.any(picked, axis=0).astype(BF)
    earlier = (priority[:, None] < priority[None, :]).astype(BF)
    rank_table = jnp.dot(assigned, earlier, preferred_element_type=F32)
    rank = jnp.sum(jnp.where(picked, rank_table[None], 0.0), axis=1).astype(jnp.int32)
    place = (routes_t % groups) * (FFN_EXP // groups) + routes_t // groups
    return jnp.where((routes_t < FFN_EXP) & (rank < capacity), place * capacity + rank, -1)


def local(
    tokens, prev_logits, routes, priority, norm_attn, w_query, w_key, w_value, w_out, norm_ffn, router, const_w, const_v,
    w_gate, w_up, w_down, cotangent,
):
    rows, width = tokens.shape
    experts = prev_logits.shape[1]
    dp = lax.axis_size("dp")
    expert_devices = lax.axis_size("expert")
    pair = w_gate.shape[0]
    capacity = 9 * rows * routes.shape[1] // (8 * experts)
    prompt_dev = PROMPT // expert_devices
    ff = w_gate.shape[2]
    e = lax.axis_index("expert").astype(jnp.int32).reshape(1)
    j = (lax.axis_index("dp") % pair).astype(jnp.int32).reshape(1)
    members = pair * expert_devices
    everyone = ("dp", "expert")
    exchange = [list(range(p * members, (p + 1) * members)) for p in range(dp // pair)]
    alike = [list(range(q, dp, pair)) for q in range(pair)]
    pairs = [list(range(p * pair, (p + 1) * pair)) for p in range(dp // pair)]

    def swap(x):
        return lax.all_to_all(x, everyone, split_axis=0, concat_axis=0, axis_index_groups=exchange, tiled=True)

    cos, sin = (jnp.asarray(t) for t in angle_tables())
    gain1, gain2 = norm_attn[None, :], norm_ffn[None, :]

    prompt_x = lax.all_gather(tokens[:prompt_dev], "expert", axis=0, tiled=True)
    slots_t = slot_table(routes.T, priority, pair, capacity)
    slots = slots_t.T
    grads_out = dispatch(slots_t, cotangent, members, capacity)
    h_own, q, k_own, v_own = project(e, tokens, gain1, (w_query, w_key, w_value), cos, sin, True)
    prompt_x, grads_out, h_own = lax.optimization_barrier((prompt_x, grads_out, h_own))
    grads_in = swap(grads_out).reshape(-1, width)
    h_prompt, k_prompt, v_prompt = project(e, prompt_x, gain1, (w_key, w_value), cos, sin, False)
    o, lse = attn_fwd(e, q, k_own, v_own, k_prompt, v_prompt)

    wcat = jnp.concatenate(
        [router, const_w.transpose(1, 0, 2).reshape(width, -1), jnp.zeros((width, 128 - experts - 4), BF)], axis=1
    )
    prev = jnp.pad(prev_logits, ((0, 0), (0, 128 - experts)))
    x2, h2, aux, ext = gates(tokens, o, w_out, gain2, wcat, prev, routes, experts)
    made, back, ffn_sum = experts_on_rows(slots_t, h2, ext, grads_in, w_gate, w_up, w_down, capacity)
    ffn_sum = lax.psum_scatter(ffn_sum, "dp", scatter_dimension=2, axis_index_groups=alike, tiled=True)
    made = swap(made.reshape(members, capacity, width)).reshape(-1, width)
    grad_prev, dx2, da, do, cat, sums = combine(
        back, slots, routes, aux, x2, h2, cotangent, gain2, wcat, const_v, w_out, experts
    )
    dq, dk, dv = attn_bwd(e, q, do, o, lse, k_own, v_own, k_prompt, v_prompt, cos, sin)
    rest = dp // 2
    n = experts
    small = jnp.concatenate([cat[:n + 4], sums[:3], jnp.zeros((5, width), F32)], axis=0)
    grad_w, small, grad_tokens = finale(
        small, gain1, (h_own, dq, o, da, w_query, dk, w_key, dv, w_value, h_prompt, tokens, dx2), rest, n + 7,
        padded_rows(4 * width, rest),
    )
    grad_w = grad_w.astype(F32)
    mixed = mix(made, slots, routes, aux, x2, h2, const_v, experts)
    ffn_sum = ffn_sum.reshape(3, width, pair, -1).transpose(2, 0, 1, 3)
    ffn_sum = lax.all_to_all(ffn_sum, "dp", split_axis=0, concat_axis=0, axis_index_groups=pairs, tiled=True)
    ffn_sum = ffn_sum.astype(F32)
    return (
        mixed,
        grad_tokens,
        grad_prev,
        small[n + 7],
        grad_w[:width],
        grad_w[width:2 * width],
        grad_w[3 * width:4 * width],
        grad_w[2 * width:3 * width],
        small[n + 6],
        small[:n].T,
        small[n:n + 4].reshape(2, 2, width).transpose(0, 2, 1),
        small[n + 4:n + 6],
        ffn_sum[:, 0],
        ffn_sum[:, 1],
        ffn_sum[:, 2].transpose(0, 2, 1),
    )


def solution(mesh):
    block = P(("dp", "expert"), None)
    in_specs = (block, block, block, P(("dp", "expert"))) + (P(),) * 9 + (P("expert", None, None),) * 3 + (block,)
    out_specs = (block, block, block) + (P(),) * 9 + (
        P("expert", None, "dp"), P("expert", None, "dp"), P("expert", "dp", None),
    )
    return jax.shard_map(local, mesh=mesh, in_specs=in_specs, out_specs=out_specs, check_vma=False)
```

```python
import functools

import jax
import jax.numpy as jnp
import numpy as np
from jax import lax
from jax.experimental import pallas as pl
from jax.experimental.pallas import tpu as pltpu
from jax.sharding import PartitionSpec as P

HEADS = 12
FFN_EXP = 8
PROMPT = 2048
NCONT = 8
CONT = 256

epsilon = 1e-06
LOG2E = 1.4426950408889634
F32 = jnp.float32
BF = jnp.bfloat16
NN = (((1,), (0,)), ((), ()))
NT = (((1,), (1,)), ((), ()))
VMEM_LIMIT = 56 << 20


def dot(a, b, dims=NN):
    return lax.dot_general(a, b, dims, preferred_element_type=F32)


def params(**kw):
    return pltpu.CompilerParams(vmem_limit_bytes=VMEM_LIMIT, **kw)


def whole(shape):
    return pl.BlockSpec(shape, lambda *_: (0,) * len(shape))


def rms_scale(x):
    return lax.rsqrt(jnp.mean(x * x, axis=-1, keepdims=True) + epsilon)


def angle_tables():
    fine = 64
    frequency = np.exp(-np.log(10000.0) * np.arange(32) * 2.0 / 64)
    frequency = np.tile(frequency.astype(np.float32).astype(np.float64), 4)
    near = np.arange(fine)[:, None] * frequency
    far = (np.arange((PROMPT + CONT) // fine) * fine)[:, None] * frequency
    near_cos, near_sin, far_cos, far_sin = (
        jnp.asarray(table.astype(np.float32)) for table in (np.cos(near), np.sin(near), np.cos(far), np.sin(far))
    )
    near_cos, near_sin, far_cos, far_sin = near_cos[None], near_sin[None], far_cos[:, None], far_sin[:, None]
    sign = jnp.where(jnp.arange(128) % 64 < 32, -1.0, 1.0)
    cosine = far_cos * near_cos - far_sin * near_sin
    sine = (far_sin * near_cos + far_cos * near_sin) * sign
    return cosine.reshape(-1, 128), sine.reshape(-1, 128)


def lane_iota(width=128):
    return lax.broadcasted_iota(jnp.int32, (1, width), 1)


def swap_halves(x):
    return jnp.where(lane_iota() % 64 < 32, pltpu.roll(x, 96, 1), pltpu.roll(x, 32, 1))


def project_kernel(e_ref, x_ref, gain_ref, *refs, count):
    weights, (cos_ref, sin_ref), (h_ref, *outs) = refs[:count], refs[count:count + 2], refs[count + 2:]
    x = x_ref[...].astype(F32)
    h = (x * rms_scale(x) * gain_ref[...]).astype(BF)
    h_ref[...] = h
    cosine, sine = cos_ref[...], sin_ref[...]
    for n, (w_ref, out_ref) in enumerate(zip(weights, outs)):
        full = dot(h, w_ref[...])
        if n == count - 1:
            out_ref[...] = full.astype(BF)
            continue
        for i in range(full.shape[1] // 128):
            part = full[:, i * 128:(i + 1) * 128]
            out_ref[:, i * 128:(i + 1) * 128] = (part * cosine + swap_halves(part) * sine).astype(BF)


def project(e, x, gain, weights, cos, sin, own, tile=256):
    rows, width = x.shape
    block = pl.BlockSpec((tile, width), lambda i, *_: (i, 0))
    half = rows // 2 // tile

    def position(i, e_ref):
        if not own:
            return (i, 0)
        return (jnp.where(i < half, e_ref[0] * half + i, PROMPT // tile), 0)

    table = pl.BlockSpec((tile, 128), position)
    return pl.pallas_call(
        functools.partial(project_kernel, count=len(weights)),
        grid_spec=pltpu.PrefetchScalarGridSpec(
            num_scalar_prefetch=1,
            grid=(rows // tile,),
            in_specs=[block, whole((1, width))] + [whole(weights[0].shape)] * len(weights) + [table, table],
            out_specs=[block] * (len(weights) + 1),
        ),
        out_shape=[jax.ShapeDtypeStruct((rows, width), BF)] * (len(weights) + 1),
        compiler_params=params(),
        cost_estimate=pl.CostEstimate(
            flops=2 * rows * width * width * len(weights), bytes_accessed=2 * rows * width * 6, transcendentals=0
        ),
        name="project_own" if own else "project_prompt",
    )(e, x, gain, *weights, cos, sin)


def attn_fwd_kernel(e_ref, q_ref, ko_ref, vo_ref, kp_ref, vp_ref, o_ref, lse_ref, vt_ref, qm_ref, m_ref, acc_ref, *, chunk, tile, scale):
    e = e_ref[0]
    rows = q_ref.shape[0]
    half = rows // 2
    npr = kp_ref.shape[0]
    nchunk = npr // chunk
    lane = lax.broadcasted_iota(jnp.int32, (1, 128), 1)
    low = lane < 64
    c = scale * LOG2E
    zero = jnp.zeros((), BF)
    q = q_ref[...]
    qm_ref[0] = jnp.where(low, q, zero)
    qm_ref[1] = jnp.where(low, zero, q)
    ones = jnp.ones((16, npr + rows), BF)
    for r, n, ref in ((0, npr, vp_ref), (npr, rows, vo_ref)):
        vt = ref[...].T
        vt_ref[0, :64, r:r + n] = vt[:64]
        vt_ref[1, :64, r:r + n] = vt[64:]
    vt_ref[0, 64:, :] = ones
    vt_ref[1, 64:, :] = ones
    tri = lax.broadcasted_iota(jnp.int32, (tile, tile), 0) <= lax.broadcasted_iota(jnp.int32, (tile, tile), 1)

    def first(q0, qn, k, vts):
        for h in range(2):
            s = dot(k, qm_ref[h, q0:q0 + qn, :], NT)
            s = s * c
            s = jnp.where(tri, s, -1e30)
            mx = jnp.max(s, axis=0, keepdims=True)
            p = jnp.exp2(s - mx).astype(BF)
            m_ref[h, 0:1, q0:q0 + qn] = mx
            acc_ref[h, :, q0:q0 + qn] = dot(vts[h], p)

    def step(blocks, k, vts):
        ss = [[dot(k, qm_ref[h, q0:q0 + qn, :], NT) for h in range(2)] for q0, qn in blocks]
        for (q0, qn), sb in zip(blocks, ss):
            for h in range(2):
                s = sb[h] * c
                mx = jnp.max(s, axis=0, keepdims=True)
                m = m_ref[h, 0:1, q0:q0 + qn]
                mn = jnp.maximum(m, mx)
                p = jnp.exp2(s - mn).astype(BF)
                m_ref[h, 0:1, q0:q0 + qn] = mn
                acc_ref[h, :, q0:q0 + qn] = acc_ref[h, :, q0:q0 + qn] * jnp.exp2(m - mn) + dot(vts[h], p)

    for j in range(rows // tile):
        r0 = j * tile
        first(r0, tile, ko_ref[r0:r0 + tile, :], [vt_ref[h, :, npr + r0:npr + r0 + tile] for h in range(2)])
    for j in range(1, half // tile):
        for i in range(j):
            r0 = i * tile
            step([(j * tile, tile)], ko_ref[r0:r0 + tile, :], [vt_ref[h, :, npr + r0:npr + r0 + tile] for h in range(2)])

    def body(ci, blocks):
        r0 = pl.multiple_of(ci * chunk, chunk)
        step(blocks, kp_ref[pl.ds(r0, chunk), :], [vt_ref[h, :, pl.ds(r0, chunk)] for h in range(2)])

    ne = e * half // chunk

    @pl.loop(0, ne)
    def _(ci):
        body(ci, [(0, half), (half, half)])

    @pl.loop(ne, nchunk)
    def _(ci):
        body(ci, [(half, half)])

    outs = []
    for h in range(2):
        l = acc_ref[h, 64:65, :]
        outs.append(acc_ref[h, :64, :] / l)
        lse_ref[0, h:h + 1, :] = m_ref[h, 0:1, :] + jnp.log2(l)
    o_ref[...] = jnp.concatenate(outs, axis=0).T.astype(BF)


def attn_fwd(e, q, ko, vo, kp, vp, *, chunk=512, tile=256):
    rows, width = q.shape
    npr = kp.shape[0]
    pairs = width // 128
    own = pl.BlockSpec((rows, 128), lambda i, *_: (0, i))
    pr = pl.BlockSpec((npr, 128), lambda i, *_: (0, i))
    return pl.pallas_call(
        functools.partial(attn_fwd_kernel, chunk=chunk, tile=tile, scale=0.125),
        grid_spec=pltpu.PrefetchScalarGridSpec(
            num_scalar_prefetch=1, grid=(pairs,),
            in_specs=[own, own, own, pr, pr],
            out_specs=[own, pl.BlockSpec((1, 2, rows), lambda i, *_: (i, 0, 0))],
            scratch_shapes=[pltpu.VMEM((2, 80, npr + rows), BF), pltpu.VMEM((2, rows, 128), BF),
            pltpu.VMEM((2, 8, rows), F32), pltpu.VMEM((2, 80, rows), F32)]),
        out_shape=[jax.ShapeDtypeStruct((rows, width), BF), jax.ShapeDtypeStruct((pairs, 2, rows), F32)],
        compiler_params=params(),
        cost_estimate=pl.CostEstimate(flops=4 * rows * npr * width * 2, bytes_accessed=2 * npr * width * 4, transcendentals=rows * npr * 12),
        name="attn_fwd",
    )(e, q, ko, vo, kp, vp)


def attn_bwd_kernel(e_ref, q_ref, do_ref, o_ref, lse_ref, ko_ref, vo_ref, kp_ref, vp_ref, cos_ref, sin_ref,
               dq_ref, dk_ref, dv_ref,
               kt_ref, dqt_ref, qm_ref, dom_ref, dl_ref, dks_ref, dvs_ref, *, tile, scale):
    e = e_ref[0]
    rows = q_ref.shape[0]
    half = rows // 2
    chunk = half
    npr = kp_ref.shape[0]
    nchunk = npr // chunk
    cont = cos_ref.shape[0] - npr
    lane = lax.broadcasted_iota(jnp.int32, (1, 128), 1)
    low = lane < 64
    c = scale * LOG2E
    zero = jnp.zeros((), BF)
    q = q_ref[...]
    do = do_ref[...]
    qm_ref[0] = jnp.where(low, q, zero)
    qm_ref[1] = jnp.where(low, zero, q)
    dom_ref[0] = jnp.where(low, do, zero)
    dom_ref[1] = jnp.where(low, zero, do)
    prod = (do.astype(F32) * o_ref[...].astype(F32)).T
    dl_ref[0:1, :] = jnp.sum(prod[:64], axis=0, keepdims=True)
    dl_ref[1:2, :] = jnp.sum(prod[64:], axis=0, keepdims=True)
    kt_ref[:, :npr] = kp_ref[...].T
    kt_ref[:, npr:] = ko_ref[...].T
    tri = lax.broadcasted_iota(jnp.int32, (tile, tile), 0) <= lax.broadcasted_iota(jnp.int32, (tile, tile), 1)

    def unrope(x, pos, n):
        first = (lane % 64) < 32
        sw = jnp.where(first, pltpu.roll(x, 96, 1), pltpu.roll(x, 32, 1))
        return x * cos_ref[pl.ds(pos, n), :] - sw * sin_ref[pl.ds(pos, n), :]

    def block(k, v, kt, q0, qn, mask):
        dk = dv = None
        dqs = []
        qs = [qm_ref[h, q0:q0 + qn, :] for h in range(2)]
        dos = [dom_ref[h, q0:q0 + qn, :] for h in range(2)]
        sts = [dot(k, qs[h], NT) for h in range(2)]
        dps = [dot(v, dos[h], NT) for h in range(2)]
        for h in range(2):
            p = jnp.exp2(sts[h] * c - lse_ref[0, h:h + 1, q0:q0 + qn])
            if mask is not None:
                p = jnp.where(mask, p, 0.0)
            ds = (p * (dps[h] - dl_ref[h:h + 1, q0:q0 + qn])).astype(BF)
            dvh = dot(p.astype(BF), dos[h])
            dkh = dot(ds, qs[h])
            dk, dv = (dkh, dvh) if dk is None else (dk + dkh, dv + dvh)
            dqs.append(dot(kt[h * 64:(h + 1) * 64], ds))
        return dk, dv, jnp.concatenate(dqs, axis=0)

    nt = rows // tile
    for i in range(nt):
        r0 = i * tile
        k = ko_ref[r0:r0 + tile, :]
        v = vo_ref[r0:r0 + tile, :]
        kt = kt_ref[:, npr + r0:npr + r0 + tile]
        prompt = r0 < half
        dk = dv = None
        for j in (range(i, nt // 2) if prompt else [i]):
            a, b, dq = block(k, v, kt, j * tile, tile, tri if i == j else None)
            dk, dv = (a, b) if dk is None else (dk + a, dv + b)
            sl = slice(j * tile, (j + 1) * tile)
            if i == 0 or not prompt:
                dqt_ref[:, sl] = dq
            else:
                dqt_ref[:, sl] += dq
        if prompt:
            dks_ref[r0:r0 + tile, :] = dk
            dvs_ref[r0:r0 + tile, :] = dv
        else:
            o0 = npr + r0 - half
            dk_ref[o0:o0 + tile, :] = (unrope(dk, npr, tile) * scale).astype(BF)
            dv_ref[o0:o0 + tile, :] = dv.astype(BF)

    def chunk_step(ci, kind):
        r0 = pl.multiple_of(ci * chunk, chunk)
        k = kp_ref[pl.ds(r0, chunk), :]
        v = vp_ref[pl.ds(r0, chunk), :]
        kt = kt_ref[:, pl.ds(r0, chunk)]
        dk, dv, dq = block(k, v, kt, half, half, None)
        dqt_ref[:, half:] += dq
        if kind == 0:
            a, b, dq = block(k, v, kt, 0, half, None)
            dk, dv = dk + a, dv + b
            dqt_ref[:, :half] += dq
        elif kind == 1:
            dk, dv = dk + dks_ref[...], dv + dvs_ref[...]
        dk_ref[pl.ds(r0, chunk), :] = (unrope(dk, r0, chunk) * scale).astype(BF)
        dv_ref[pl.ds(r0, chunk), :] = dv.astype(BF)

    @pl.loop(0, e)
    def _(ci):
        chunk_step(ci, 0)

    chunk_step(e, 1)

    @pl.loop(e + 1, nchunk)
    def _(ci):
        chunk_step(ci, 2)

    dq = dqt_ref[...].T
    base = pl.multiple_of(e * half, half)
    dq_ref[:half, :] = (unrope(dq[:half], base, half) * scale).astype(BF)
    for r in range(half, rows, cont):
        dq_ref[r:r + cont, :] = (unrope(dq[r:r + cont], npr, cont) * scale).astype(BF)


def attn_bwd(e, q, do, o, lse, ko, vo, kp, vp, cos, sin, *, tile=256):
    rows, width = q.shape
    npr = kp.shape[0]
    keys = npr + rows // 2
    pairs = width // 128
    own = pl.BlockSpec((rows, 128), lambda i, *_: (0, i))
    pr = pl.BlockSpec((npr, 128), lambda i, *_: (0, i))
    al = pl.BlockSpec((keys, 128), lambda i, *_: (0, i))
    tab = pl.BlockSpec(cos.shape, lambda i, *_: (0, 0))
    return pl.pallas_call(
        functools.partial(attn_bwd_kernel, tile=tile, scale=0.125),
        grid_spec=pltpu.PrefetchScalarGridSpec(
            num_scalar_prefetch=1, grid=(pairs,),
            in_specs=[own, own, own, pl.BlockSpec((1, 2, rows), lambda i, *_: (i, 0, 0)), own, own, pr, pr, tab, tab],
            out_specs=[own, al, al],
            scratch_shapes=[pltpu.VMEM((128, npr + rows), BF), pltpu.VMEM((128, rows), F32),
                            pltpu.VMEM((2, rows, 128), BF), pltpu.VMEM((2, rows, 128), BF),
                            pltpu.VMEM((8, rows), F32),
                            pltpu.VMEM((rows // 2, 128), F32), pltpu.VMEM((rows // 2, 128), F32)]),
        out_shape=[jax.ShapeDtypeStruct((rows, width), BF), jax.ShapeDtypeStruct((keys, width), BF),
                   jax.ShapeDtypeStruct((keys, width), BF)],
        compiler_params=params(),
        cost_estimate=pl.CostEstimate(flops=10 * rows * npr * width * 2, bytes_accessed=2 * npr * width * 8, transcendentals=rows * npr * 12),
        name="attn_bwd",
    )(e, q, do, o, lse, ko, vo, kp, vp, cos, sin)


MESH = pl.DeviceIdType.MESH


def pick(values, lane, index):
    return jnp.sum(jnp.where(lane == index, values, 0.0), axis=1, keepdims=True)


def softmax_pair(a, b):
    top = jnp.maximum(a, b)
    ea, eb = jnp.exp(a - top), jnp.exp(b - top)
    total = ea + eb
    return ea / total, eb / total


def spread(column):
    lane = lane_iota()
    parts, left = jnp.zeros((1, 128), F32), column
    for n in range(3):
        part = left.astype(BF).astype(F32)
        parts = jnp.where(lane == n, part, parts)
        left = left - part
    return parts.astype(BF)


def gate_kernel(x_ref, o_ref, w_ref, gain_ref, wcat_ref, prev_ref, routes_ref, x2_ref, h2_ref, aux_ref, ext_ref, *, experts):
    x2 = x_ref[...].astype(F32) + dot(o_ref[...], w_ref[...])
    x2_ref[...] = x2
    h2 = (x2 * rms_scale(x2) * gain_ref[...]).astype(BF)
    h2_ref[...] = h2
    logits = dot(h2, wcat_ref[...]) + prev_ref[...]
    lane = lane_iota()
    gates = softmax_pair(*[pick(logits, lane, routes_ref[:, k:k + 1]) for k in range(2)])
    aux = logits
    for k in range(2):
        aux = jnp.where(lane == experts + k, gates[k], aux)
    at = experts + 2
    for c in range(2):
        alpha = softmax_pair(*[pick(logits, lane, experts + 2 * c + k) for k in range(2)])
        for k in range(2):
            aux = jnp.where(lane == at + 2 * c + k, alpha[k], aux)
    aux_ref[...] = aux
    for k in range(2):
        ext_ref[:, k * 128:(k + 1) * 128] = spread(gates[k])


def gates(x, o, w_out, gain, wcat, prev, routes, experts, tile=256):
    rows, width = x.shape
    block = pl.BlockSpec((tile, width), lambda i: (i, 0))
    thin = pl.BlockSpec((tile, 128), lambda i: (i, 0))
    return pl.pallas_call(
        functools.partial(gate_kernel, experts=experts),
        grid=(rows // tile,),
        in_specs=[block, block, whole(w_out.shape), whole(gain.shape), whole(wcat.shape), thin,
                  pl.BlockSpec((tile, 2), lambda i: (i, 0))],
        out_specs=[block, block, thin, pl.BlockSpec((tile, 256), lambda i: (i, 0))],
        out_shape=[jax.ShapeDtypeStruct((rows, width), F32), jax.ShapeDtypeStruct((rows, width), BF),
                   jax.ShapeDtypeStruct((rows, 128), F32), jax.ShapeDtypeStruct((rows, 256), BF)],
        compiler_params=params(),
        cost_estimate=pl.CostEstimate(flops=2 * rows * width * width, bytes_accessed=12 * rows * width, transcendentals=0),
        name="gates",
    )(x, o, w_out, gain, wcat, prev, routes)


def dispatch_kernel(slot_ref, rows_ref, out_ref, *, capacity):
    ids = pl.program_id(0) * capacity + lax.broadcasted_iota(jnp.int32, (capacity, 1), 0)
    hot = [jnp.where(ids == slot_ref[k:k + 1, :], 1.0, 0.0).astype(BF) for k in range(2)]
    out_ref[0] = dot(hot[0] + hot[1], rows_ref[...]).astype(BF)


def dispatch(slots, rows, destinations, capacity):
    count, width = rows.shape
    return pl.pallas_call(
        functools.partial(dispatch_kernel, capacity=capacity),
        grid=(destinations,),
        in_specs=[whole(slots.shape), whole(rows.shape)],
        out_specs=pl.BlockSpec((1, capacity, width), lambda i: (i, 0, 0)),
        out_shape=jax.ShapeDtypeStruct((destinations, capacity, width), BF),
        compiler_params=params(),
        cost_estimate=pl.CostEstimate(flops=2 * destinations * capacity * count * width, bytes_accessed=4 * count * width,
                                      transcendentals=0),
        name="dispatch_grads",
    )(slots, rows)


def expert_kernel(slot_ref, h2_ref, ext_ref, g_ref, wg_hbm, wu_hbm, wd_hbm, made_ref, back_hbm, grad_hbm,
                  wg_ref, wu_ref, wd_ref, a_ref, s_ref, d_ref, at_ref, dt_ref, hid_ref, dg_ref, du_ref, macc_ref,
                  bacc_ref, out_ref, send_sem, recv_sem, local_sem, out_sem, *, capacity, tile, grad_tile):
    dp, ex = lax.axis_index("dp"), lax.axis_index("expert")
    j, c, x = dp % 2, ex % 2, ex // 2
    width = h2_ref.shape[1]
    ff = wg_ref.shape[1]
    loads = [pltpu.make_async_copy(src.at[j], dst, local_sem.at[n])
             for n, (src, dst) in enumerate(((wg_hbm, wg_ref), (wu_hbm, wu_ref), (wd_hbm, wd_ref)))]
    for copy in loads:
        copy.start()

    def flip(bit, by):
        return bit + by * (1 - 2 * bit)

    def peer(r):
        return dp + (r // 2 % 2) * (1 - 2 * j), flip(x, r // 4) * 2 + flip(c, r % 2)

    def place(r):
        return flip(j, r // 2 % 2) * 4 + flip(x, r // 4) * 2 + flip(c, r % 2)

    barrier = pltpu.get_barrier_semaphore()
    for r in range(1, 8):
        pl.semaphore_signal(barrier, inc=1, device_id=peer(r), device_id_type=MESH)
    pl.semaphore_wait(barrier, 7)

    def send(src, dst, kind, r):
        n = kind * 8 + r
        copy = pltpu.make_async_remote_copy(src_ref=src, dst_ref=dst, send_sem=send_sem.at[n], recv_sem=recv_sem.at[n],
                                            device_id=peer(r), device_id_type=MESH)
        copy.start()
        return copy

    rows = {}
    for r in (4, 5, 2, 3, 6, 7, 1, 0):
        ids = place(r) * capacity + lax.broadcasted_iota(jnp.int32, (capacity, 1), 0)
        hot = [jnp.where(ids == slot_ref[k:k + 1, :], 1.0, 0.0).astype(BF) for k in range(2)]
        into = s_ref if r else a_ref
        into[r, :, :width] = dot(hot[0] + hot[1], h2_ref[...]).astype(BF)
        into[r, :, width:] = (dot(hot[0], ext_ref[:, :128]) + dot(hot[1], ext_ref[:, 128:])).astype(BF)
        if r:
            rows[r] = send(s_ref.at[r], a_ref.at[r], 0, r)

    for copy in loads:
        copy.wait()
    returned = []
    mine = pl.ds(pl.multiple_of(place(0) * capacity, 16), capacity)
    two = 2 * capacity
    for n, first in enumerate((0, 4, 2, 6)):
        for r in (first, first + 1):
            if r:
                rows[r].wait_recv()
            got = a_ref[r]
            half = pl.ds((r - first) * capacity, capacity)
            gate = jnp.sum(got[:, width:].astype(F32), axis=1, keepdims=True)
            g = g_ref[pl.ds(pl.multiple_of(place(r) * capacity, 16), capacity), :].astype(F32)
            d_ref[half, :] = (g * gate).astype(BF)
        span = pl.ds(n * two, two)
        a = a_ref[first:first + 2, :, :width].reshape(two, width)
        at_ref[:, span] = a.T
        dt_ref[:, span] = d_ref[...].T
        macc_ref[...] = jnp.zeros_like(macc_ref)
        bacc_ref[...] = jnp.zeros_like(bacc_ref)

        @pl.loop(0, ff // tile)
        def _(i):
            cols = pl.ds(pl.multiple_of(i * tile, tile), tile)
            a = a_ref[first:first + 2, :, :width].reshape(two, width)
            gate, up = dot(a, wg_ref[:, cols]), dot(a, wu_ref[:, cols])
            dh = dot(d_ref[...], wd_ref[cols, :], NT)
            sig = jax.nn.sigmoid(gate)
            act = gate * sig
            hidden = (act * up).astype(BF)
            du = (dh * act).astype(BF)
            dg = (dh * up * sig * (1.0 + gate * (1.0 - sig))).astype(BF)
            hid_ref[span, cols] = hidden
            du_ref[span, cols] = du
            dg_ref[span, cols] = dg
            macc_ref[...] += dot(hidden, wd_ref[cols, :])
            bacc_ref[...] += dot(dg, wg_ref[:, cols], NT) + dot(du, wu_ref[:, cols], NT)

        for r in (first, first + 1):
            half = pl.ds((r - first) * capacity, capacity)
            if r:
                rows[r].wait_send()
            theirs = pl.ds(pl.multiple_of(place(r) * capacity, 16), capacity)
            made = macc_ref[half, :].astype(BF)
            made_ref[theirs, :] = made
            s_ref[r, :, :width] = bacc_ref[half, :].astype(BF)
            s_ref[r, :, width:] = spread(jnp.sum(g_ref[theirs, :].astype(F32) * made.astype(F32), axis=1, keepdims=True))
            if r:
                returned.append(send(s_ref.at[r], back_hbm.at[mine], 1, r))
            else:
                kept = pltpu.make_async_copy(s_ref.at[0], back_hbm.at[mine], local_sem.at[3])
                kept.start()

    steps = ff // grad_tile

    def put(i, slot):
        cols = pl.ds(pl.multiple_of(i * grad_tile, grad_tile), grad_tile)
        return pltpu.make_async_copy(out_ref.at[slot], grad_hbm.at[:, :, cols], out_sem.at[slot])

    @pl.loop(0, steps)
    def _(i):
        slot = i % 2

        @pl.when(i >= 2)
        def _():
            put(i - 2, slot).wait()

        cols = pl.ds(pl.multiple_of(i * grad_tile, grad_tile), grad_tile)
        out_ref[slot, 0] = dot(at_ref[...], dg_ref[:, cols]).astype(BF)
        out_ref[slot, 1] = dot(at_ref[...], du_ref[:, cols]).astype(BF)
        out_ref[slot, 2] = dot(dt_ref[...], hid_ref[:, cols]).astype(BF)
        put(i, slot).start()

    for i in range(max(steps - 2, 0), steps):
        put(i, i % 2).wait()
    kept.wait()
    for copy in returned:
        copy.wait_recv()
        copy.wait_send()


def experts_on_rows(slots, h2, ext, g, w_gate, w_up, w_down, capacity, tile=512, grad_tile=256):
    width = h2.shape[1]
    ff = w_gate.shape[2]
    total = 8 * capacity
    vm = pltpu.VMEM
    vmem, hbm = pl.BlockSpec(memory_space=pltpu.VMEM), pl.BlockSpec(memory_space=pl.ANY)
    return pl.pallas_call(
        functools.partial(expert_kernel, capacity=capacity, tile=tile, grad_tile=grad_tile),
        in_specs=[vmem] * 4 + [hbm] * 3,
        out_specs=[vmem, hbm, hbm],
        out_shape=[jax.ShapeDtypeStruct((total, width), BF), jax.ShapeDtypeStruct((total, width + 128), BF),
                   jax.ShapeDtypeStruct((3, width, ff), BF)],
        scratch_shapes=[
            vm((width, ff), BF), vm((width, ff), BF), vm((ff, width), BF),
            vm((8, capacity, width + 128), BF), vm((8, capacity, width + 128), BF),
            vm((2 * capacity, width), BF), vm((width, total), BF), vm((width, total), BF),
            vm((total, ff), BF), vm((total, ff), BF), vm((total, ff), BF),
            vm((2 * capacity, width), F32), vm((2 * capacity, width), F32), vm((2, 3, width, grad_tile), BF),
            pltpu.SemaphoreType.DMA((16,)), pltpu.SemaphoreType.DMA((16,)), pltpu.SemaphoreType.DMA((4,)),
            pltpu.SemaphoreType.DMA((2,)),
        ],
        compiler_params=pltpu.CompilerParams(vmem_limit_bytes=62 << 20, collective_id=1, has_side_effects=True),
        cost_estimate=pl.CostEstimate(flops=18 * total * width * ff, bytes_accessed=12 * width * ff + 8 * total * width,
                                      transcendentals=total * ff),
        name="experts_on_rows",
    )(slots, h2, ext, g, w_gate, w_up, w_down)


def one(cond):
    return jnp.where(cond, 1.0, 0.0)


def pick_parts(aux, routes, experts):
    lane = lane_iota()
    gate = [pick(aux, lane, experts + k) for k in range(2)]
    alpha = [[pick(aux, lane, experts + 2 + 2 * c + k) for k in range(2)] for c in range(2)]
    copy = [one(routes[k] == FFN_EXP + 1) for k in range(2)]
    const = [[one(routes[k] == FFN_EXP + 2 + c) for c in range(2)] for k in range(2)]
    on_h2 = [copy[k] + const[k][0] * alpha[0][0] + const[k][1] * alpha[1][0] for k in range(2)]
    return gate, alpha, copy, const, on_h2


def one_hot(slots, total):
    return jnp.where(lane_iota(total) == slots, 1.0, 0.0).astype(BF)


def combine_kernel(back_ref, slot_ref, routes_ref, aux_ref, x2_ref, h2_ref, g_ref, gain_ref, wcat_ref, v_ref, w_ref,
                   prev_ref, dx2_ref, da_ref, do_ref, cat_ref, sums_ref, *, experts):
    step = pl.program_id(0)
    lane = lane_iota()
    h2 = h2_ref[...].astype(F32)
    g = g_ref[...].astype(F32)
    x2 = x2_ref[...]
    width = x2.shape[1]
    r2 = rms_scale(x2)
    route = [routes_ref[:, k:k + 1] for k in range(2)]
    gate, alpha, copy, const, on_h2 = pick_parts(aux_ref[...], route, experts)
    hot = [one_hot(slot_ref[:, k:k + 1], back_ref.shape[0]) for k in range(2)]
    g_h2 = jnp.sum(g * h2, axis=1, keepdims=True)
    g_v = [jnp.sum(g * v_ref[c:c + 1, :], axis=1, keepdims=True) for c in range(2)]
    dgate = []
    for k in range(2):
        at_expert = jnp.sum(dot(hot[k], back_ref[:, width:]), axis=1, keepdims=True)
        dgate.append(at_expert + on_h2[k] * g_h2 + const[k][0] * alpha[0][1] * g_v[0] + const[k][1] * alpha[1][1] * g_v[1])
    mean = gate[0] * dgate[0] + gate[1] * dgate[1]
    dl = [gate[k] * (dgate[k] - mean) for k in range(2)]
    grads = jnp.where(lane == route[0], dl[0], 0.0) + jnp.where(lane == route[1], dl[1], 0.0)
    prev_ref[...] = grads[:, :experts]
    weight = [gate[0] * const[0][c] + gate[1] * const[1][c] for c in range(2)]
    sums = []
    on_g = copy[0] * gate[0] + copy[1] * gate[1]
    for c in range(2):
        da0 = weight[c] * g_h2
        da1 = weight[c] * g_v[c]
        mid = alpha[c][0] * da0 + alpha[c][1] * da1
        grads = jnp.where(lane == experts + 2 * c, alpha[c][0] * (da0 - mid), grads)
        grads = jnp.where(lane == experts + 2 * c + 1, alpha[c][1] * (da1 - mid), grads)
        on_g = on_g + alpha[c][0] * weight[c]
        sums.append(jnp.sum((alpha[c][1] * weight[c]) * g, axis=0, keepdims=True))
    low = grads.astype(BF)
    cat = dot(low.T, h2_ref[...])
    dh2 = dot(low, wcat_ref[...], NT) + on_g * g + dot(hot[0] + hot[1], back_ref[:, :width])
    sums.append(jnp.sum(dh2 * x2 * r2, axis=0, keepdims=True))
    u = dh2 * gain_ref[...]
    dx2 = g + r2 * (u - x2 * (r2 * r2) * jnp.mean(u * x2, axis=-1, keepdims=True))
    dx2_ref[...] = dx2
    da = dx2.astype(BF)
    da_ref[...] = da
    do_ref[...] = dot(da, w_ref[...], NT).astype(BF)
    parts = jnp.concatenate(sums + [jnp.zeros((8 - len(sums), width), F32)], axis=0)

    @pl.when(step == 0)
    def _():
        cat_ref[...] = cat
        sums_ref[...] = parts

    @pl.when(step > 0)
    def _():
        cat_ref[...] += cat
        sums_ref[...] += parts


def combine(back, slots, routes, aux, x2, h2, g, gain, wcat, const_v, w_out, experts, tile=256):
    rows, width = x2.shape
    block = pl.BlockSpec((tile, width), lambda i: (i, 0))
    thin = pl.BlockSpec((tile, 128), lambda i: (i, 0))
    two = pl.BlockSpec((tile, 2), lambda i: (i, 0))
    sds = jax.ShapeDtypeStruct
    return pl.pallas_call(
        functools.partial(combine_kernel, experts=experts),
        grid=(rows // tile,),
        in_specs=[whole(back.shape), two, two, thin, block, block, block, whole(gain.shape), whole(wcat.shape),
                  whole(const_v.shape), whole(w_out.shape)],
        out_specs=[pl.BlockSpec((tile, experts), lambda i: (i, 0)), block, block, block, whole((128, width)),
                   whole((8, width))],
        out_shape=[sds((rows, experts), F32), sds((rows, width), F32), sds((rows, width), BF),
                   sds((rows, width), BF), sds((128, width), F32), sds((8, width), F32)],
        compiler_params=params(),
        cost_estimate=pl.CostEstimate(flops=4 * rows * width * back.shape[0], bytes_accessed=26 * rows * width,
                                      transcendentals=0),
        name="combine",
    )(back, slots, routes, aux, x2, h2, g, gain, wcat, const_v, w_out)


def padded_rows(rows, rest):
    unit = 8 * rest * 16
    return -(-rows // unit) * unit


def finale_kernel(small_ref, gain_ref, *refs, rest, chunks, norm_row, tile):
    hbm, refs = refs[:12], refs[12:]
    shard_refs, (small_out_ref, token_hbm) = refs[:2], refs[2:4]
    local, refs = refs[4:16], refs[16:]
    (turned_ref, g_ref, norm_ref, dh_ref, r0_ref, sm_ref, rs_ref, rd0_ref, td_ref, rd1_ref, tok_ref,
     load_sem, tok_sem, send_sem, recv_sem) = refs[:15]
    r1_ref, r2_ref = (refs[15 + 2 * n:17 + 2 * n] for n in range(2))
    ho_ref, dq_ref, o_ref, da_ref, wq_ref, dk_ref, wk_ref, dv_ref, wv_ref, hp_ref, x_ref, dx2_ref = local[:12]

    loads = [pltpu.make_async_copy(src, dst, load_sem.at[n]) for n, (src, dst) in enumerate(zip(hbm, local))]
    for copy in loads:
        copy.start()

    dp, ex = lax.axis_index("dp"), lax.axis_index("expert")
    c, x, y, z = ex % 2, ex // 2, dp % 2, dp // 2
    mate = (dp, x * 2 + 1 - c)
    across = (dp, (1 - x) * 2 + c)
    beside = (z * 2 + 1 - y, ex)
    ahead = [((z + d) % rest * 2 + y, ex) for d in range(1, rest)]
    barrier = pltpu.get_barrier_semaphore()
    for peer in [mate, across, beside] + ahead:
        pl.semaphore_signal(barrier, inc=1, device_id=peer, device_id_type=MESH)
    pl.semaphore_wait(barrier, 2 + rest)

    started = []

    def send(src, dst, peer):
        n = len(started)
        copy = pltpu.make_async_remote_copy(src_ref=src, dst_ref=dst, send_sem=send_sem.at[n], recv_sem=recv_sem.at[n],
                                            device_id=peer, device_id_type=MESH)
        copy.start()
        started.append(copy)
        return copy

    rows, width = g_ref.shape
    own = ho_ref.shape[0]
    prompt = hp_ref.shape[0]
    half = rows // 2
    size = half // chunks
    q1, q2 = size // 2, size // 4
    cut = width // 2
    part = [pl.ds(0, cut), pl.ds(cut, width - cut)]
    first, second = [across, beside], [beside, across]
    bit1, bit2 = [x, y], [y, x]

    def ds(at, n):
        return pl.ds(pl.multiple_of(at, 16), n)

    def at1(k, p, bit):
        return k * size + bit * q1

    def stage0(k):
        return [send(g_ref.at[ds((1 - c) * half + k * size, size)], r0_ref.at[ds(k * size, size)], mate)]

    def stage1(k):
        sl = pl.ds(k * size, size)
        r0_ref[sl] = (g_ref[ds(c * half + k * size, size)].astype(F32) + r0_ref[sl].astype(F32)).astype(BF)
        return [send(r0_ref.at[ds(at1(k, p, 1 - bit1[p]), q1), part[p]], r1_ref[p].at[pl.ds(k * q1, q1)], first[p])
                for p in range(2)]

    def stage2(k):
        out = []
        for p in range(2):
            sl = pl.ds(k * q1, q1)
            r1_ref[p][sl] = (r0_ref[ds(at1(k, p, bit1[p]), q1), part[p]].astype(F32) + r1_ref[p][sl].astype(F32)).astype(BF)
            out.append(send(r1_ref[p].at[ds(k * q1 + (1 - bit2[p]) * q2, q2)], r2_ref[p].at[pl.ds(k * q2, q2)], second[p]))
        return out

    def stage3(k):
        for p in range(2):
            sl = pl.ds(k * q2, q2)
            shard_refs[p][sl] = (r1_ref[p][ds(k * q1 + bit2[p] * q2, q2)].astype(F32) + r2_ref[p][sl].astype(F32)).astype(BF)
        return []

    stages = (stage0, stage1, stage2, stage3)
    waiting = {}

    def wait(line):
        for copy in waiting.pop(line, []):
            copy.wait_recv()

    def step(k, s):
        wait(k)
        waiting[k] = stages[s](k) if s < len(stages) else []

    block = own // 2

    def dh_rows(xx, cc):
        return ds((xx * 2 + cc) * block, block)

    def prompt_rows(cc):
        @pl.loop(0, 2 * (block // tile))
        def _(i):
            at = ds((i // (block // tile) * 2 + cc) * block + i % (block // tile) * tile, tile)
            dh_ref[at] = (dot(dk_ref[at], wk_ref[...], NT) + dot(dv_ref[at], wv_ref[...], NT)).astype(BF)

    small_peers = [mate, across, beside]

    def small_step(n):
        wait("small")
        if n < 4:
            sm_ref[n] = small_ref[...] if n == 0 else sm_ref[n - 1] + rs_ref[n - 1]
            if n == 0:
                at = lax.broadcasted_iota(jnp.int32, (small_ref.shape[0], 1), 0)
                norm = jnp.sum(norm_ref[...].T, axis=0, keepdims=True) / gain_ref[...]
                sm_ref[0] = jnp.where(at == norm_row, norm, small_ref[...])
        if n < 3:
            waiting["small"] = [send(sm_ref.at[n], rs_ref.at[n], small_peers[n])]
        elif n == 3:
            waiting["small"] = [send(sm_ref.at[3], rs_ref.at[2 + d], ahead[d - 1]) for d in range(1, rest)]
        else:
            total = sm_ref[3]
            for d in range(1, rest):
                total = total + rs_ref[2 + d]
            small_out_ref[...] = total

    strip = width // 3

    def gradient(b, terms, first_row, w_ref):
        mine = slice(b * strip, (b + 1) * strip)
        got = sum(dot(turned_ref[mine, at:at + count], rhs_ref[...]) for at, count, rhs_ref in terms)
        g_ref[first_row + b * strip:first_row + (b + 1) * strip, :] = got.astype(BF)
        if w_ref is not None:
            share = got * w_ref[mine, :].astype(F32)
            norm_ref[mine, :] += sum(share[:, n:n + 128] for n in range(0, width, 128))

    def put_tokens(i, dh, copies):
        at = pl.ds(i * tile, tile)
        xf = x_ref[at].astype(F32)
        r1 = rms_scale(xf)
        u = dh * gain_ref[...]
        slot = i % 2
        tok_ref[slot] = dx2_ref[at] + r1 * (u - xf * (r1 * r1) * jnp.mean(u * xf, axis=-1, keepdims=True))
        copy = pltpu.make_async_copy(tok_ref.at[slot], token_hbm.at[at], tok_sem.at[slot])
        copy.start()
        copies.append(copy)

    if rows > 4 * width:
        g_ref[4 * width:, :] = jnp.zeros((rows - 4 * width, width), BF)
    norm_ref[...] = jnp.zeros_like(norm_ref)
    tokens = []

    def own_tokens(i):
        at = pl.ds(i * tile, tile)
        dh = dot(dq_ref[at], wq_ref[...], NT)
        if i * tile >= block:
            kv = pl.ds(prompt + i * tile - block, tile)
            dh = dh + dot(dk_ref[kv], wk_ref[...], NT) + dot(dv_ref[kv], wv_ref[...], NT)
        else:
            inner = ds((x * 2 + c) * block + i * tile, tile)
            dh = dh + dh_ref[inner].astype(F32) + rd0_ref[x, at].astype(F32) + rd1_ref[at].astype(F32)
        if len(tokens) >= 2:
            tokens[-2].wait()
        put_tokens(i, dh, tokens)

    hops = (4.5, 6.0, 5.0)
    due = []

    def begin(now, k):
        step(k, 0)
        due.append([now + hops[0], k, 1])

    def ready(now):
        for entry in sorted(due, key=lambda entry: (entry[0], str(entry[1]))):
            if entry[0] <= now:
                _, k, s = entry
                due.remove(entry)
                if k == "small":
                    small_step(s)
                    last = 4
                else:
                    step(k, s)
                    last = len(stages) - 1
                if s < last:
                    due.append([max(now, entry[0]) + (hops[s] if k != "small" else 5.0), k, s + 1])

    def wait_loads(*numbers):
        for n in numbers:
            loads[n].wait()

    def first_turn():
        wait_loads(0, 1, 2, 3, 4)
        turned_ref[:, :own] = ho_ref[...].T
        turned_ref[:, own:2 * own] = o_ref[...].T

    def second_turn():
        wait_loads(5, 6, 7, 8, 9)
        turned_ref[:, :prompt] = hp_ref[...].T
        turned_ref[:, prompt:] = ho_ref[block:].T

    def first_grads(b):
        gradient(b, [(0, own, dq_ref)], 0, wq_ref)
        gradient(b, [(own, own, da_ref)], 2 * width, None)

    def second_grads(b):
        gradient(b, [(0, prompt + block, dk_ref)], width, wk_ref)
        gradient(b, [(0, prompt + block, dv_ref)], 3 * width, wv_ref)

    def mates():
        prompt_rows(1 - c)
        waiting["dh"] = [send(dh_ref.at[dh_rows(w, 1 - c)], rd0_ref.at[w], mate) for w in range(2)]

    def over():
        wait("dh")
        td_ref[...] = (dh_ref[dh_rows(1 - x, c)].astype(F32) + rd0_ref[1 - x].astype(F32)).astype(BF)
        waiting["dh"] = [send(td_ref, rd1_ref, across)]

    def prompt_tokens(i):
        wait("dh")
        own_tokens(i)

    blocks = own // tile
    tasks = [(4.0, first_turn)] + [(2.0, functools.partial(first_grads, b)) for b in range(3)] + [(3.0, second_turn)]
    tasks += [(4.0, functools.partial(second_grads, b)) for b in range(3)]
    tasks += [(4.0, mates), (4.0, lambda: prompt_rows(c)), (0.5, over)]
    tasks += [(2.0, lambda: wait_loads(10, 11))] + [(2.0, functools.partial(own_tokens, i)) for i in range(blocks // 2, blocks)]
    after = {1: [0], 2: [1], 3: [2], 5: [3], 6: [4], 7: [5]} if chunks == 6 else {7: list(range(chunks))}
    now = 0.0
    for n, (length, task) in enumerate(tasks):
        task()
        now += length
        for k in after.get(n, []):
            begin(now, k)
        if n == 7:
            small_step(0)
            due.append([now + 5.0, "small", 1])
        ready(now)
    late = list(range(blocks // 2))
    while due or late:
        now = max(now, min(entry[0] for entry in due)) if due else now
        ready(now)
        if late and not due:
            prompt_tokens(late.pop(0))
    for copy in tokens[-2:]:
        copy.wait()
    for copy in started:
        copy.wait_send()


def finale(small, gain, arrays, rest, norm_row, out_rows, tile=256):
    own, width = arrays[0].shape
    prompt = arrays[9].shape[0]
    block = own // 2
    half = out_rows // 2
    chunks = 6 if half == 6 * 4 * rest * 16 else 1
    lanes = (width // 2, width // 2)
    copies = chunks * (1 + 2 + 2) + 3 + 3 + rest - 1
    vm, dma = pltpu.VMEM, pltpu.SemaphoreType.DMA
    vmem, hbm = pl.BlockSpec(memory_space=pltpu.VMEM), pl.BlockSpec(memory_space=pl.ANY)
    return pl.pallas_call(
        functools.partial(finale_kernel, rest=rest, chunks=chunks, norm_row=norm_row, tile=tile),
        in_specs=[vmem] * 2 + [hbm] * len(arrays),
        out_specs=[vmem, vmem, vmem, hbm],
        out_shape=[jax.ShapeDtypeStruct((half // 4, k), BF) for k in lanes]
        + [jax.ShapeDtypeStruct(small.shape, F32), jax.ShapeDtypeStruct((own, width), F32)],
        scratch_shapes=[vm(a.shape, a.dtype) for a in arrays] + [
            vm((width, prompt + block), BF), vm((out_rows, width), BF), vm((width, 128), F32), vm((prompt, width), BF),
            vm((half, width), BF), vm((4,) + small.shape, F32), vm((2 + rest,) + small.shape, F32),
            vm((2, block, width), BF), vm((block, width), BF), vm((block, width), BF), vm((2, tile, width), F32),
            dma((len(arrays),)), dma((2,)), dma((copies,)), dma((copies,)),
        ] + [vm((half // n, k), BF) for n in (2, 4) for k in lanes],
        compiler_params=pltpu.CompilerParams(vmem_limit_bytes=62 << 20, collective_id=0, has_side_effects=True),
        cost_estimate=pl.CostEstimate(flops=30 * own * width * width, bytes_accessed=8 * out_rows * width, transcendentals=0),
        name="finale",
    )(small, gain, *arrays)


def spread_kernel(shard0_ref, shard1_ref, v_ref, *refs, rest, chunks, experts, tile):
    shards = (shard0_ref, shard1_ref)
    hbm, (out_ref, mixed_ref), refs = refs[:6], refs[6:8], refs[8:]
    local, (r3a_ref, r3b_ref, load_sem, send_sem, recv_sem) = refs[:6], refs[6:]
    r3_ref = (r3a_ref, r3b_ref)
    made_ref, slot_ref, routes_ref, aux_ref, x2_ref, h2_ref = local
    loads = [pltpu.make_async_copy(src, dst, load_sem.at[n]) for n, (src, dst) in enumerate(zip(hbm, local))]
    for copy in loads:
        copy.start()
    dp, ex = lax.axis_index("dp"), lax.axis_index("expert")
    c, x, y, z = ex % 2, ex // 2, dp % 2, dp // 2
    mate = (dp, x * 2 + 1 - c)
    across = (dp, (1 - x) * 2 + c)
    beside = (z * 2 + 1 - y, ex)
    ahead = [((z + d) % rest * 2 + y, ex) for d in range(1, rest)]
    barrier = pltpu.get_barrier_semaphore()
    for peer in [mate, across, beside] + ahead:
        pl.semaphore_signal(barrier, inc=1, device_id=peer, device_id_type=MESH)
    pl.semaphore_wait(barrier, 2 + rest)

    started = []
    rows, width = out_ref.shape
    half = rows // 2
    size = half // chunks
    q1, q2, q3 = size // 2, size // 4, size // 4 // rest
    cut = width // 2
    part = [pl.ds(0, cut), pl.ds(cut, width - cut)]
    first, second = [across, beside], [beside, across]
    bit1, bit2 = [x, y], [y, x]

    def copy_to(src, dst, peer):
        n = len(started)
        copy = pltpu.make_async_remote_copy(src_ref=src, dst_ref=dst, send_sem=send_sem.at[n], recv_sem=recv_sem.at[n],
                                            device_id=peer, device_id_type=MESH)
        copy.start()
        started.append(copy)
        return copy

    def send(at, count, lanes, peer):
        spot = out_ref.at[pl.ds(pl.multiple_of(at, 16), count), lanes]
        return copy_to(spot, spot, peer)

    def base(k, p, depth):
        at = c * half + k * size
        if depth > 0:
            at = at + bit1[p] * q1
        if depth > 1:
            at = at + bit2[p] * q2
        if depth > 2:
            at = at + z * q3
        return at

    def stage0(k):
        out = []
        for p in range(2):
            at = base(k, p, 3)
            total = shards[p][pl.ds(pl.multiple_of(k * q2 + z * q3, 16), q3)].astype(F32)
            for d in range(1, rest):
                total = total + r3_ref[p][d - 1, pl.ds(k * q3, q3)].astype(F32)
            out_ref[pl.ds(pl.multiple_of(at, 16), q3), part[p]] = total.astype(BF)
            out += [send(at, q3, part[p], peer) for peer in ahead]
        return out

    def reduce(k):
        out = []
        for p in range(2):
            for d in range(1, rest):
                to = pl.ds(pl.multiple_of(k * q2 + (z + d) % rest * q3, 16), q3)
                out.append(copy_to(shards[p].at[to], r3_ref[p].at[d - 1, pl.ds(k * q3, q3)], ahead[d - 1]))
        return out

    def stage1(k):
        return [send(base(k, p, 2), q2, part[p], second[p]) for p in range(2)]

    def stage2(k):
        return [send(base(k, p, 1), q1, part[p], first[p]) for p in range(2)]

    def stage3(k):
        return [send(base(k, 0, 0), size, pl.ds(0, width), mate)]

    def end(k):
        return []

    stages = (reduce, stage0, stage1, stage2, stage3, end)
    waiting = {k: [] for k in range(chunks)}

    def mixing(i):
        at = pl.ds(i * tile, tile)
        if i == 0:
            for copy in loads:
                copy.wait()
        route = [routes_ref[at, k:k + 1] for k in range(2)]
        gate, alpha, _, const, on_h2 = pick_parts(aux_ref[at], route, experts)
        out = x2_ref[at] + (gate[0] * on_h2[0] + gate[1] * on_h2[1]) * h2_ref[at].astype(F32)
        for n in range(2):
            out = out + ((gate[0] * const[0][n] + gate[1] * const[1][n]) * alpha[n][1]) * v_ref[n:n + 1, :]
        for k in range(2):
            out = out + gate[k] * dot(one_hot(slot_ref[at, k:k + 1], made_ref.shape[0]), made_ref[...])
        mixed_ref[at] = out.astype(BF)

    blocks = list(range(x2_ref.shape[0] // tile))
    for t in range(len(stages) + (chunks + 1) // 2 - 1):
        for k in range(chunks):
            s = t - k // 2
            if 0 <= s < len(stages):
                for copy in waiting[k]:
                    copy.wait_recv()
                waiting[k] = stages[s](k)
        if blocks:
            mixing(blocks.pop(0))
    for i in blocks:
        mixing(i)
    for copy in started:
        copy.wait_send()


def spread_sums(shards, const_v, arrays, rest, out_rows, experts, tile=256):
    rows, width = arrays[4].shape
    half = out_rows // 2
    chunks = 6 if half == 6 * 4 * rest * 16 else 1
    copies = chunks * (4 * (rest - 1) + 2 + 2 + 1)
    vm, dma = pltpu.VMEM, pltpu.SemaphoreType.DMA
    vmem, hbm = pl.BlockSpec(memory_space=pltpu.VMEM), pl.BlockSpec(memory_space=pl.ANY)
    return pl.pallas_call(
        functools.partial(spread_kernel, rest=rest, chunks=chunks, experts=experts, tile=tile),
        in_specs=[vmem] * 3 + [hbm] * len(arrays),
        out_specs=[vmem, vmem],
        out_shape=[jax.ShapeDtypeStruct((out_rows, width), BF), jax.ShapeDtypeStruct((rows, width), BF)],
        scratch_shapes=[vm(a.shape, a.dtype) for a in arrays] + [vm((rest - 1, half // 4 // rest, width // 2), BF)] * 2
        + [dma((len(arrays),)), dma((copies,)), dma((copies,))],
        compiler_params=params(collective_id=2, has_side_effects=True),
        cost_estimate=pl.CostEstimate(flops=4 * rows * width * 1536, bytes_accessed=8 * out_rows * width, transcendentals=0),
        name="spread_sums",
    )(*shards, const_v, *arrays)


def slot_table(routes_t, priority, groups, capacity):
    ids = jnp.arange(FFN_EXP, dtype=jnp.int32)
    picked = routes_t[:, None, :] == ids[None, :, None]
    assigned = jnp.any(picked, axis=0).astype(BF)
    earlier = (priority[:, None] < priority[None, :]).astype(BF)
    rank_table = jnp.dot(assigned, earlier, preferred_element_type=F32)
    rank = jnp.sum(jnp.where(picked, rank_table[None], 0.0), axis=1).astype(jnp.int32)
    place = (routes_t % groups) * (FFN_EXP // groups) + routes_t // groups
    return jnp.where((routes_t < FFN_EXP) & (rank < capacity), place * capacity + rank, -1)


def local(
    tokens, prev_logits, routes, priority, norm_attn, w_query, w_key, w_value, w_out, norm_ffn, router, const_w, const_v,
    w_gate, w_up, w_down, cotangent,
):
    rows, width = tokens.shape
    experts = prev_logits.shape[1]
    dp = lax.axis_size("dp")
    expert_devices = lax.axis_size("expert")
    pair = w_gate.shape[0]
    capacity = 9 * rows * routes.shape[1] // (8 * experts)
    prompt_dev = PROMPT // expert_devices
    ff = w_gate.shape[2]
    e = lax.axis_index("expert").astype(jnp.int32).reshape(1)
    j = (lax.axis_index("dp") % pair).astype(jnp.int32).reshape(1)
    members = pair * expert_devices
    everyone = ("dp", "expert")
    exchange = [list(range(p * members, (p + 1) * members)) for p in range(dp // pair)]
    alike = [list(range(q, dp, pair)) for q in range(pair)]
    pairs = [list(range(p * pair, (p + 1) * pair)) for p in range(dp // pair)]

    def swap(x):
        return lax.all_to_all(x, everyone, split_axis=0, concat_axis=0, axis_index_groups=exchange, tiled=True)

    cos, sin = angle_tables()
    gain1, gain2 = norm_attn[None, :], norm_ffn[None, :]

    prompt_x = lax.all_gather(tokens[:prompt_dev], "expert", axis=0, tiled=True)
    slots_t = slot_table(routes.T, priority, pair, capacity)
    slots = slots_t.T
    grads_out = dispatch(slots_t, cotangent, members, capacity)
    h_own, q, k_own, v_own = project(e, tokens, gain1, (w_query, w_key, w_value), cos, sin, True)
    prompt_x, grads_out, h_own = lax.optimization_barrier((prompt_x, grads_out, h_own))
    grads_in = swap(grads_out).reshape(-1, width)
    h_prompt, k_prompt, v_prompt = project(e, prompt_x, gain1, (w_key, w_value), cos, sin, False)
    o, lse = attn_fwd(e, q, k_own, v_own, k_prompt, v_prompt)

    wcat = jnp.concatenate(
        [router, const_w.transpose(1, 0, 2).reshape(width, -1), jnp.zeros((width, 128 - experts - 4), BF)], axis=1
    )
    prev = jnp.pad(prev_logits, ((0, 0), (0, 128 - experts)))
    x2, h2, aux, ext = gates(tokens, o, w_out, gain2, wcat, prev, routes, experts)
    made, back, ffn_sum = experts_on_rows(slots_t, h2, ext, grads_in, w_gate, w_up, w_down, capacity)
    ffn_sum = lax.psum_scatter(ffn_sum, "dp", scatter_dimension=2, axis_index_groups=alike, tiled=True)
    made = swap(made.reshape(members, capacity, width)).reshape(-1, width)
    grad_prev, dx2, da, do, cat, sums = combine(
        back, slots, routes, aux, x2, h2, cotangent, gain2, wcat, const_v, w_out, experts
    )
    dq, dk, dv = attn_bwd(e, q, do, o, lse, k_own, v_own, k_prompt, v_prompt, cos, sin)
    rest = dp // 2
    n = experts
    small = jnp.concatenate([cat[:n + 4], sums[:3], jnp.zeros((5, width), F32)], axis=0)
    out_rows = padded_rows(4 * width, rest)
    *shards, small, grad_tokens = finale(
        small, gain1, (h_own, dq, o, da, w_query, dk, w_key, dv, w_value, h_prompt, tokens, dx2), rest, n + 7, out_rows
    )
    ffn_sum = ffn_sum.reshape(3, width, pair, -1).transpose(2, 0, 1, 3)
    ffn_sum, small, shards = lax.optimization_barrier((ffn_sum, small, shards))
    ffn_sum = lax.all_to_all(ffn_sum, "dp", split_axis=0, concat_axis=0, axis_index_groups=pairs, tiled=True)
    grad_w, mixed = spread_sums(shards, const_v, (made, slots, routes, aux, x2, h2), rest, out_rows, experts)
    grad_w = grad_w.astype(F32)
    ffn_sum = ffn_sum.astype(F32)
    return (
        mixed,
        grad_tokens,
        grad_prev,
        small[n + 7],
        grad_w[:width],
        grad_w[width:2 * width],
        grad_w[3 * width:4 * width],
        grad_w[2 * width:3 * width],
        small[n + 6],
        small[:n].T,
        small[n:n + 4].reshape(2, 2, width).transpose(0, 2, 1),
        small[n + 4:n + 6],
        ffn_sum[:, 0],
        ffn_sum[:, 1],
        ffn_sum[:, 2].transpose(0, 2, 1),
    )


def solution(mesh):
    block = P(("dp", "expert"), None)
    in_specs = (block, block, block, P(("dp", "expert"))) + (P(),) * 9 + (P("expert", None, None),) * 3 + (block,)
    out_specs = (block, block, block) + (P(),) * 9 + (
        P("expert", None, "dp"), P("expert", None, "dp"), P("expert", "dp", None),
    )
    return jax.shard_map(local, mesh=mesh, in_specs=in_specs, out_specs=out_specs, check_vma=False)
```

```python
import functools

import jax
import jax.numpy as jnp
import numpy as np
from jax import lax
from jax.experimental import pallas as pl
from jax.experimental.pallas import tpu as pltpu
from jax.sharding import PartitionSpec as P

HEADS = 12
FFN_EXP = 8
PROMPT = 2048
NCONT = 8
CONT = 256

epsilon = 1e-06
LOG2E = 1.4426950408889634
F32 = jnp.float32
BF = jnp.bfloat16
NN = (((1,), (0,)), ((), ()))
NT = (((1,), (1,)), ((), ()))
VMEM_LIMIT = 56 << 20


def dot(a, b, dims=NN):
    return lax.dot_general(a, b, dims, preferred_element_type=F32)


def params(**kw):
    return pltpu.CompilerParams(vmem_limit_bytes=VMEM_LIMIT, **kw)


def whole(shape):
    return pl.BlockSpec(shape, lambda *_: (0,) * len(shape))


def rms_scale(x):
    return lax.rsqrt(jnp.mean(x * x, axis=-1, keepdims=True) + epsilon)


def angle_tables():
    fine = 64
    frequency = np.exp(-np.log(10000.0) * np.arange(32) * 2.0 / 64)
    frequency = np.tile(frequency.astype(np.float32).astype(np.float64), 4)
    near = np.arange(fine)[:, None] * frequency
    far = (np.arange((PROMPT + CONT) // fine) * fine)[:, None] * frequency
    near_cos, near_sin, far_cos, far_sin = (
        jnp.asarray(table.astype(np.float32)) for table in (np.cos(near), np.sin(near), np.cos(far), np.sin(far))
    )
    near_cos, near_sin, far_cos, far_sin = near_cos[None], near_sin[None], far_cos[:, None], far_sin[:, None]
    sign = jnp.where(jnp.arange(128) % 64 < 32, -1.0, 1.0)
    cosine = far_cos * near_cos - far_sin * near_sin
    sine = (far_sin * near_cos + far_cos * near_sin) * sign
    return cosine.reshape(-1, 128), sine.reshape(-1, 128)


def lane_iota(width=128):
    return lax.broadcasted_iota(jnp.int32, (1, width), 1)


def swap_halves(x):
    return jnp.where(lane_iota() % 64 < 32, pltpu.roll(x, 96, 1), pltpu.roll(x, 32, 1))


def project_kernel(e_ref, x_ref, gain_ref, *refs, count):
    weights, (cos_ref, sin_ref), (h_ref, *outs) = refs[:count], refs[count:count + 2], refs[count + 2:]
    x = x_ref[...].astype(F32)
    h = (x * rms_scale(x) * gain_ref[...]).astype(BF)
    h_ref[...] = h
    cosine, sine = cos_ref[...], sin_ref[...]
    for n, (w_ref, out_ref) in enumerate(zip(weights, outs)):
        full = dot(h, w_ref[...])
        if n == count - 1:
            out_ref[...] = full.astype(BF)
            continue
        for i in range(full.shape[1] // 128):
            part = full[:, i * 128:(i + 1) * 128]
            out_ref[:, i * 128:(i + 1) * 128] = (part * cosine + swap_halves(part) * sine).astype(BF)


def project(e, x, gain, weights, cos, sin, own, tile=256):
    rows, width = x.shape
    block = pl.BlockSpec((tile, width), lambda i, *_: (i, 0))
    half = rows // 2 // tile

    def position(i, e_ref):
        if not own:
            return (i, 0)
        return (jnp.where(i < half, e_ref[0] * half + i, PROMPT // tile), 0)

    table = pl.BlockSpec((tile, 128), position)
    return pl.pallas_call(
        functools.partial(project_kernel, count=len(weights)),
        grid_spec=pltpu.PrefetchScalarGridSpec(
            num_scalar_prefetch=1,
            grid=(rows // tile,),
            in_specs=[block, whole((1, width))] + [whole(weights[0].shape)] * len(weights) + [table, table],
            out_specs=[block] * (len(weights) + 1),
        ),
        out_shape=[jax.ShapeDtypeStruct((rows, width), BF)] * (len(weights) + 1),
        compiler_params=params(),
        cost_estimate=pl.CostEstimate(
            flops=2 * rows * width * width * len(weights), bytes_accessed=2 * rows * width * 6, transcendentals=0
        ),
        name="project_own" if own else "project_prompt",
    )(e, x, gain, *weights, cos, sin)


MESH = pl.DeviceIdType.MESH


def eight():
    dp, ex = lax.axis_index("dp"), lax.axis_index("expert")
    j, c, x = dp % 2, ex % 2, ex // 2

    def flip(bit, by):
        return bit + by * (1 - 2 * bit)

    def peer(r):
        return dp + (r // 2 % 2) * (1 - 2 * j), flip(x, r // 4) * 2 + flip(c, r % 2)

    def place(r):
        return flip(j, r // 2 % 2) * 4 + flip(x, r // 4) * 2 + flip(c, r % 2)

    return peer, place


def return_outputs(made_hbm, got_hbm, send_sem, recv_sem, local_sem, capacity):
    peer, place = eight()
    step = pl.program_id(0)

    def spot(r):
        return pl.ds(pl.multiple_of(place(r) * capacity, 16), capacity)

    def copies():
        return [
            pltpu.make_async_remote_copy(
                src_ref=made_hbm.at[spot(r)], dst_ref=got_hbm.at[spot(0)], send_sem=send_sem.at[r], recv_sem=recv_sem.at[r],
                device_id=peer(r), device_id_type=MESH,
            )
            for r in range(1, 8)
        ] + [pltpu.make_async_copy(made_hbm.at[spot(0)], got_hbm.at[spot(0)], local_sem.at[0])]

    barrier = pltpu.get_barrier_semaphore()

    @pl.when(step == 0)
    def _():
        for r in range(1, 8):
            pl.semaphore_signal(barrier, inc=1, device_id=peer(r), device_id_type=MESH)

    @pl.when(step == 1)
    def _():
        pl.semaphore_wait(barrier, 7)
        for copy in copies():
            copy.start()

    @pl.when(step == pl.num_programs(0) - 1)
    def _():
        for copy in copies():
            copy.wait()


def attn_fwd_kernel(e_ref, q_ref, ko_ref, vo_ref, kp_ref, vp_ref, o_ref, lse_ref, vt_ref, qm_ref, m_ref, acc_ref, *, chunk, tile, scale):
    e = e_ref[0]
    rows = q_ref.shape[0]
    half = rows // 2
    npr = kp_ref.shape[0]
    nchunk = npr // chunk
    lane = lax.broadcasted_iota(jnp.int32, (1, 128), 1)
    low = lane < 64
    c = scale * LOG2E
    zero = jnp.zeros((), BF)
    q = q_ref[...]
    qm_ref[0] = jnp.where(low, q, zero)
    qm_ref[1] = jnp.where(low, zero, q)
    ones = jnp.ones((16, npr + rows), BF)
    for r, n, ref in ((0, npr, vp_ref), (npr, rows, vo_ref)):
        vt = ref[...].T
        vt_ref[0, :64, r:r + n] = vt[:64]
        vt_ref[1, :64, r:r + n] = vt[64:]
    vt_ref[0, 64:, :] = ones
    vt_ref[1, 64:, :] = ones
    tri = lax.broadcasted_iota(jnp.int32, (tile, tile), 0) <= lax.broadcasted_iota(jnp.int32, (tile, tile), 1)

    def first(q0, qn, k, vts):
        for h in range(2):
            s = dot(k, qm_ref[h, q0:q0 + qn, :], NT)
            s = s * c
            s = jnp.where(tri, s, -1e30)
            mx = jnp.max(s, axis=0, keepdims=True)
            p = jnp.exp2(s - mx).astype(BF)
            m_ref[h, 0:1, q0:q0 + qn] = mx
            acc_ref[h, :, q0:q0 + qn] = dot(vts[h], p)

    def step(blocks, k, vts):
        ss = [[dot(k, qm_ref[h, q0:q0 + qn, :], NT) for h in range(2)] for q0, qn in blocks]
        for (q0, qn), sb in zip(blocks, ss):
            for h in range(2):
                s = sb[h] * c
                mx = jnp.max(s, axis=0, keepdims=True)
                m = m_ref[h, 0:1, q0:q0 + qn]
                mn = jnp.maximum(m, mx)
                p = jnp.exp2(s - mn).astype(BF)
                m_ref[h, 0:1, q0:q0 + qn] = mn
                acc_ref[h, :, q0:q0 + qn] = acc_ref[h, :, q0:q0 + qn] * jnp.exp2(m - mn) + dot(vts[h], p)

    for j in range(rows // tile):
        r0 = j * tile
        first(r0, tile, ko_ref[r0:r0 + tile, :], [vt_ref[h, :, npr + r0:npr + r0 + tile] for h in range(2)])
    for j in range(1, half // tile):
        for i in range(j):
            r0 = i * tile
            step([(j * tile, tile)], ko_ref[r0:r0 + tile, :], [vt_ref[h, :, npr + r0:npr + r0 + tile] for h in range(2)])

    def body(ci, blocks):
        r0 = pl.multiple_of(ci * chunk, chunk)
        step(blocks, kp_ref[pl.ds(r0, chunk), :], [vt_ref[h, :, pl.ds(r0, chunk)] for h in range(2)])

    ne = e * half // chunk

    @pl.loop(0, ne)
    def _(ci):
        body(ci, [(0, half), (half, half)])

    @pl.loop(ne, nchunk)
    def _(ci):
        body(ci, [(half, half)])

    outs = []
    for h in range(2):
        l = acc_ref[h, 64:65, :]
        outs.append(acc_ref[h, :64, :] / l)
        lse_ref[0, h:h + 1, :] = m_ref[h, 0:1, :] + jnp.log2(l)
    o_ref[...] = jnp.concatenate(outs, axis=0).T.astype(BF)


def attn_fwd(e, q, ko, vo, kp, vp, *, chunk=512, tile=256):
    rows, width = q.shape
    npr = kp.shape[0]
    pairs = width // 128
    own = pl.BlockSpec((rows, 128), lambda i, *_: (0, i))
    pr = pl.BlockSpec((npr, 128), lambda i, *_: (0, i))
    return pl.pallas_call(
        functools.partial(attn_fwd_kernel, chunk=chunk, tile=tile, scale=0.125),
        grid_spec=pltpu.PrefetchScalarGridSpec(
            num_scalar_prefetch=1, grid=(pairs,),
            in_specs=[own, own, own, pr, pr],
            out_specs=[own, pl.BlockSpec((1, 2, rows), lambda i, *_: (i, 0, 0))],
            scratch_shapes=[pltpu.VMEM((2, 80, npr + rows), BF), pltpu.VMEM((2, rows, 128), BF),
            pltpu.VMEM((2, 8, rows), F32), pltpu.VMEM((2, 80, rows), F32)]),
        out_shape=[jax.ShapeDtypeStruct((rows, width), BF), jax.ShapeDtypeStruct((pairs, 2, rows), F32)],
        compiler_params=params(),
        cost_estimate=pl.CostEstimate(flops=4 * rows * npr * width * 2, bytes_accessed=2 * npr * width * 4, transcendentals=rows * npr * 12),
        name="attn_fwd",
    )(e, q, ko, vo, kp, vp)


def attn_bwd_kernel(q_ref, do_ref, o_ref, lse_ref, ko_ref, vo_ref, kp_ref, vp_ref, cos_ref, sin_ref, made_hbm,
               dq_ref, dk_ref, dv_ref, got_hbm,
               kt_ref, dqt_ref, qm_ref, dom_ref, dl_ref, dks_ref, dvs_ref, send_sem, recv_sem, local_sem, *, tile, scale,
               capacity):
    e = lax.axis_index("expert")
    return_outputs(made_hbm, got_hbm, send_sem, recv_sem, local_sem, capacity)
    rows = q_ref.shape[0]
    half = rows // 2
    chunk = half
    npr = kp_ref.shape[0]
    nchunk = npr // chunk
    cont = cos_ref.shape[0] - npr
    lane = lax.broadcasted_iota(jnp.int32, (1, 128), 1)
    low = lane < 64
    c = scale * LOG2E
    zero = jnp.zeros((), BF)
    q = q_ref[...]
    do = do_ref[...]
    qm_ref[0] = jnp.where(low, q, zero)
    qm_ref[1] = jnp.where(low, zero, q)
    dom_ref[0] = jnp.where(low, do, zero)
    dom_ref[1] = jnp.where(low, zero, do)
    prod = (do.astype(F32) * o_ref[...].astype(F32)).T
    dl_ref[0:1, :] = jnp.sum(prod[:64], axis=0, keepdims=True)
    dl_ref[1:2, :] = jnp.sum(prod[64:], axis=0, keepdims=True)
    kt_ref[:, :npr] = kp_ref[...].T
    kt_ref[:, npr:] = ko_ref[...].T
    tri = lax.broadcasted_iota(jnp.int32, (tile, tile), 0) <= lax.broadcasted_iota(jnp.int32, (tile, tile), 1)

    def unrope(x, pos, n):
        first = (lane % 64) < 32
        sw = jnp.where(first, pltpu.roll(x, 96, 1), pltpu.roll(x, 32, 1))
        return x * cos_ref[pl.ds(pos, n), :] - sw * sin_ref[pl.ds(pos, n), :]

    def block(k, v, kt, q0, qn, mask):
        dk = dv = None
        dqs = []
        qs = [qm_ref[h, q0:q0 + qn, :] for h in range(2)]
        dos = [dom_ref[h, q0:q0 + qn, :] for h in range(2)]
        sts = [dot(k, qs[h], NT) for h in range(2)]
        dps = [dot(v, dos[h], NT) for h in range(2)]
        for h in range(2):
            p = jnp.exp2(sts[h] * c - lse_ref[0, h:h + 1, q0:q0 + qn])
            if mask is not None:
                p = jnp.where(mask, p, 0.0)
            ds = (p * (dps[h] - dl_ref[h:h + 1, q0:q0 + qn])).astype(BF)
            dvh = dot(p.astype(BF), dos[h])
            dkh = dot(ds, qs[h])
            dk, dv = (dkh, dvh) if dk is None else (dk + dkh, dv + dvh)
            dqs.append(dot(kt[h * 64:(h + 1) * 64], ds))
        return dk, dv, jnp.concatenate(dqs, axis=0)

    nt = rows // tile
    for i in range(nt):
        r0 = i * tile
        k = ko_ref[r0:r0 + tile, :]
        v = vo_ref[r0:r0 + tile, :]
        kt = kt_ref[:, npr + r0:npr + r0 + tile]
        prompt = r0 < half
        dk = dv = None
        for j in (range(i, nt // 2) if prompt else [i]):
            a, b, dq = block(k, v, kt, j * tile, tile, tri if i == j else None)
            dk, dv = (a, b) if dk is None else (dk + a, dv + b)
            sl = slice(j * tile, (j + 1) * tile)
            if i == 0 or not prompt:
                dqt_ref[:, sl] = dq
            else:
                dqt_ref[:, sl] += dq
        if prompt:
            dks_ref[r0:r0 + tile, :] = dk
            dvs_ref[r0:r0 + tile, :] = dv
        else:
            o0 = npr + r0 - half
            dk_ref[o0:o0 + tile, :] = (unrope(dk, npr, tile) * scale).astype(BF)
            dv_ref[o0:o0 + tile, :] = dv.astype(BF)

    def chunk_step(ci, kind):
        r0 = pl.multiple_of(ci * chunk, chunk)
        k = kp_ref[pl.ds(r0, chunk), :]
        v = vp_ref[pl.ds(r0, chunk), :]
        kt = kt_ref[:, pl.ds(r0, chunk)]
        dk, dv, dq = block(k, v, kt, half, half, None)
        dqt_ref[:, half:] += dq
        if kind == 0:
            a, b, dq = block(k, v, kt, 0, half, None)
            dk, dv = dk + a, dv + b
            dqt_ref[:, :half] += dq
        elif kind == 1:
            dk, dv = dk + dks_ref[...], dv + dvs_ref[...]
        dk_ref[pl.ds(r0, chunk), :] = (unrope(dk, r0, chunk) * scale).astype(BF)
        dv_ref[pl.ds(r0, chunk), :] = dv.astype(BF)

    @pl.loop(0, e)
    def _(ci):
        chunk_step(ci, 0)

    chunk_step(e, 1)

    @pl.loop(e + 1, nchunk)
    def _(ci):
        chunk_step(ci, 2)

    dq = dqt_ref[...].T
    base = pl.multiple_of(e * half, half)
    dq_ref[:half, :] = (unrope(dq[:half], base, half) * scale).astype(BF)
    for r in range(half, rows, cont):
        dq_ref[r:r + cont, :] = (unrope(dq[r:r + cont], npr, cont) * scale).astype(BF)


def attn_bwd(q, do, o, lse, ko, vo, kp, vp, cos, sin, made, capacity, *, tile=256):
    rows, width = q.shape
    npr = kp.shape[0]
    keys = npr + rows // 2
    pairs = width // 128
    own = pl.BlockSpec((rows, 128), lambda i, *_: (0, i))
    pr = pl.BlockSpec((npr, 128), lambda i, *_: (0, i))
    al = pl.BlockSpec((keys, 128), lambda i, *_: (0, i))
    hbm = pl.BlockSpec(memory_space=pl.ANY)
    tab = pl.BlockSpec(cos.shape, lambda i, *_: (0, 0))
    return pl.pallas_call(
        functools.partial(attn_bwd_kernel, tile=tile, scale=0.125, capacity=capacity),
        grid_spec=pl.GridSpec(
            grid=(pairs,),
            in_specs=[own, own, own, pl.BlockSpec((1, 2, rows), lambda i, *_: (i, 0, 0)), own, own, pr, pr, tab, tab, hbm],
            out_specs=[own, al, al, hbm],
            scratch_shapes=[pltpu.VMEM((128, npr + rows), BF), pltpu.VMEM((128, rows), F32),
                            pltpu.VMEM((2, rows, 128), BF), pltpu.VMEM((2, rows, 128), BF),
                            pltpu.VMEM((8, rows), F32),
                            pltpu.VMEM((rows // 2, 128), F32), pltpu.VMEM((rows // 2, 128), F32),
                            pltpu.SemaphoreType.DMA((8,)), pltpu.SemaphoreType.DMA((8,)), pltpu.SemaphoreType.DMA((1,))]),
        out_shape=[jax.ShapeDtypeStruct((rows, width), BF), jax.ShapeDtypeStruct((keys, width), BF),
                   jax.ShapeDtypeStruct((keys, width), BF), jax.ShapeDtypeStruct(made.shape, BF)],
        compiler_params=params(collective_id=3, has_side_effects=True),
        cost_estimate=pl.CostEstimate(flops=10 * rows * npr * width * 2, bytes_accessed=2 * npr * width * 8, transcendentals=rows * npr * 12),
        name="attn_bwd",
    )(q, do, o, lse, ko, vo, kp, vp, cos, sin, made)


def pick(values, lane, index):
    return jnp.sum(jnp.where(lane == index, values, 0.0), axis=1, keepdims=True)


def softmax_pair(a, b):
    top = jnp.maximum(a, b)
    ea, eb = jnp.exp(a - top), jnp.exp(b - top)
    total = ea + eb
    return ea / total, eb / total


def spread(column):
    lane = lane_iota()
    parts, left = jnp.zeros((1, 128), F32), column
    for n in range(3):
        part = left.astype(BF).astype(F32)
        parts = jnp.where(lane == n, part, parts)
        left = left - part
    return parts.astype(BF)


def gate_kernel(x_ref, o_ref, w_ref, gain_ref, wcat_ref, prev_ref, routes_ref, x2_ref, h2_ref, aux_ref, ext_ref, *, experts):
    x2 = x_ref[...].astype(F32) + dot(o_ref[...], w_ref[...])
    x2_ref[...] = x2
    h2 = (x2 * rms_scale(x2) * gain_ref[...]).astype(BF)
    h2_ref[...] = h2
    logits = dot(h2, wcat_ref[...]) + prev_ref[...]
    lane = lane_iota()
    gates = softmax_pair(*[pick(logits, lane, routes_ref[:, k:k + 1]) for k in range(2)])
    aux = logits
    for k in range(2):
        aux = jnp.where(lane == experts + k, gates[k], aux)
    at = experts + 2
    for c in range(2):
        alpha = softmax_pair(*[pick(logits, lane, experts + 2 * c + k) for k in range(2)])
        for k in range(2):
            aux = jnp.where(lane == at + 2 * c + k, alpha[k], aux)
    aux_ref[...] = aux
    for k in range(2):
        ext_ref[:, k * 128:(k + 1) * 128] = spread(gates[k])


def gates(x, o, w_out, gain, wcat, prev, routes, experts, tile=256):
    rows, width = x.shape
    block = pl.BlockSpec((tile, width), lambda i: (i, 0))
    thin = pl.BlockSpec((tile, 128), lambda i: (i, 0))
    return pl.pallas_call(
        functools.partial(gate_kernel, experts=experts),
        grid=(rows // tile,),
        in_specs=[block, block, whole(w_out.shape), whole(gain.shape), whole(wcat.shape), thin,
                  pl.BlockSpec((tile, 2), lambda i: (i, 0))],
        out_specs=[block, block, thin, pl.BlockSpec((tile, 256), lambda i: (i, 0))],
        out_shape=[jax.ShapeDtypeStruct((rows, width), F32), jax.ShapeDtypeStruct((rows, width), BF),
                   jax.ShapeDtypeStruct((rows, 128), F32), jax.ShapeDtypeStruct((rows, 256), BF)],
        compiler_params=params(),
        cost_estimate=pl.CostEstimate(flops=2 * rows * width * width, bytes_accessed=12 * rows * width, transcendentals=0),
        name="gates",
    )(x, o, w_out, gain, wcat, prev, routes)


def dispatch_kernel(slot_ref, rows_ref, out_ref, *, capacity):
    ids = pl.program_id(0) * capacity + lax.broadcasted_iota(jnp.int32, (capacity, 1), 0)
    hot = [jnp.where(ids == slot_ref[k:k + 1, :], 1.0, 0.0).astype(BF) for k in range(2)]
    out_ref[0] = dot(hot[0] + hot[1], rows_ref[...]).astype(BF)


def dispatch(slots, rows, destinations, capacity):
    count, width = rows.shape
    return pl.pallas_call(
        functools.partial(dispatch_kernel, capacity=capacity),
        grid=(destinations,),
        in_specs=[whole(slots.shape), whole(rows.shape)],
        out_specs=pl.BlockSpec((1, capacity, width), lambda i: (i, 0, 0)),
        out_shape=jax.ShapeDtypeStruct((destinations, capacity, width), BF),
        compiler_params=params(),
        cost_estimate=pl.CostEstimate(flops=2 * destinations * capacity * count * width, bytes_accessed=4 * count * width,
                                      transcendentals=0),
        name="dispatch_grads",
    )(slots, rows)


def expert_kernel(slot_ref, h2_ref, ext_ref, g_ref, wg_hbm, wu_hbm, wd_hbm, made_ref, back_hbm, grad_hbm,
                  wg_ref, wu_ref, wd_ref, a_ref, s_ref, d_ref, at_ref, dt_ref, hid_ref, dg_ref, du_ref, macc_ref,
                  bacc_ref, out_ref, send_sem, recv_sem, local_sem, out_sem, *, capacity, tile, grad_tile):
    dp, ex = lax.axis_index("dp"), lax.axis_index("expert")
    j, c, x = dp % 2, ex % 2, ex // 2
    width = h2_ref.shape[1]
    ff = wg_ref.shape[1]
    loads = [pltpu.make_async_copy(src.at[j], dst, local_sem.at[n])
             for n, (src, dst) in enumerate(((wg_hbm, wg_ref), (wu_hbm, wu_ref), (wd_hbm, wd_ref)))]
    for copy in loads:
        copy.start()

    def flip(bit, by):
        return bit + by * (1 - 2 * bit)

    def peer(r):
        return dp + (r // 2 % 2) * (1 - 2 * j), flip(x, r // 4) * 2 + flip(c, r % 2)

    def place(r):
        return flip(j, r // 2 % 2) * 4 + flip(x, r // 4) * 2 + flip(c, r % 2)

    barrier = pltpu.get_barrier_semaphore()
    for r in range(1, 8):
        pl.semaphore_signal(barrier, inc=1, device_id=peer(r), device_id_type=MESH)
    pl.semaphore_wait(barrier, 7)

    def send(src, dst, kind, r):
        n = kind * 8 + r
        copy = pltpu.make_async_remote_copy(src_ref=src, dst_ref=dst, send_sem=send_sem.at[n], recv_sem=recv_sem.at[n],
                                            device_id=peer(r), device_id_type=MESH)
        copy.start()
        return copy

    rows = {}
    for r in (4, 5, 2, 3, 6, 7, 1, 0):
        ids = place(r) * capacity + lax.broadcasted_iota(jnp.int32, (capacity, 1), 0)
        hot = [jnp.where(ids == slot_ref[k:k + 1, :], 1.0, 0.0).astype(BF) for k in range(2)]
        into = s_ref if r else a_ref
        into[r, :, :width] = dot(hot[0] + hot[1], h2_ref[...]).astype(BF)
        into[r, :, width:] = (dot(hot[0], ext_ref[:, :128]) + dot(hot[1], ext_ref[:, 128:])).astype(BF)
        if r:
            rows[r] = send(s_ref.at[r], a_ref.at[r], 0, r)

    for copy in loads:
        copy.wait()
    returned = []
    mine = pl.ds(pl.multiple_of(place(0) * capacity, 16), capacity)
    two = 2 * capacity
    for n, first in enumerate((0, 4, 2, 6)):
        for r in (first, first + 1):
            if r:
                rows[r].wait_recv()
            got = a_ref[r]
            half = pl.ds((r - first) * capacity, capacity)
            gate = jnp.sum(got[:, width:].astype(F32), axis=1, keepdims=True)
            g = g_ref[pl.ds(pl.multiple_of(place(r) * capacity, 16), capacity), :].astype(F32)
            d_ref[half, :] = (g * gate).astype(BF)
        span = pl.ds(n * two, two)
        a = a_ref[first:first + 2, :, :width].reshape(two, width)
        at_ref[:, span] = a.T
        dt_ref[:, span] = d_ref[...].T
        macc_ref[...] = jnp.zeros_like(macc_ref)
        bacc_ref[...] = jnp.zeros_like(bacc_ref)

        @pl.loop(0, ff // tile)
        def _(i):
            cols = pl.ds(pl.multiple_of(i * tile, tile), tile)
            a = a_ref[first:first + 2, :, :width].reshape(two, width)
            gate, up = dot(a, wg_ref[:, cols]), dot(a, wu_ref[:, cols])
            dh = dot(d_ref[...], wd_ref[cols, :], NT)
            sig = jax.nn.sigmoid(gate)
            act = gate * sig
            hidden = (act * up).astype(BF)
            du = (dh * act).astype(BF)
            dg = (dh * up * sig * (1.0 + gate * (1.0 - sig))).astype(BF)
            hid_ref[span, cols] = hidden
            du_ref[span, cols] = du
            dg_ref[span, cols] = dg
            macc_ref[...] += dot(hidden, wd_ref[cols, :])
            bacc_ref[...] += dot(dg, wg_ref[:, cols], NT) + dot(du, wu_ref[:, cols], NT)

        for r in (first, first + 1):
            half = pl.ds((r - first) * capacity, capacity)
            if r:
                rows[r].wait_send()
            theirs = pl.ds(pl.multiple_of(place(r) * capacity, 16), capacity)
            made = macc_ref[half, :].astype(BF)
            made_ref[theirs, :] = made
            s_ref[r, :, :width] = bacc_ref[half, :].astype(BF)
            s_ref[r, :, width:] = spread(jnp.sum(g_ref[theirs, :].astype(F32) * made.astype(F32), axis=1, keepdims=True))
            if r:
                returned.append(send(s_ref.at[r], back_hbm.at[mine], 1, r))
            else:
                kept = pltpu.make_async_copy(s_ref.at[0], back_hbm.at[mine], local_sem.at[3])
                kept.start()

    steps = ff // grad_tile

    def put(i, slot):
        cols = pl.ds(pl.multiple_of(i * grad_tile, grad_tile), grad_tile)
        return pltpu.make_async_copy(out_ref.at[slot], grad_hbm.at[:, :, cols], out_sem.at[slot])

    @pl.loop(0, steps)
    def _(i):
        slot = i % 2

        @pl.when(i >= 2)
        def _():
            put(i - 2, slot).wait()

        cols = pl.ds(pl.multiple_of(i * grad_tile, grad_tile), grad_tile)
        out_ref[slot, 0] = dot(at_ref[...], dg_ref[:, cols]).astype(BF)
        out_ref[slot, 1] = dot(at_ref[...], du_ref[:, cols]).astype(BF)
        out_ref[slot, 2] = dot(dt_ref[...], hid_ref[:, cols]).astype(BF)
        put(i, slot).start()

    for i in range(max(steps - 2, 0), steps):
        put(i, i % 2).wait()
    kept.wait()
    for copy in returned:
        copy.wait_recv()
        copy.wait_send()


def experts_on_rows(slots, h2, ext, g, w_gate, w_up, w_down, capacity, tile=512, grad_tile=256):
    width = h2.shape[1]
    ff = w_gate.shape[2]
    total = 8 * capacity
    vm = pltpu.VMEM
    vmem, hbm = pl.BlockSpec(memory_space=pltpu.VMEM), pl.BlockSpec(memory_space=pl.ANY)
    return pl.pallas_call(
        functools.partial(expert_kernel, capacity=capacity, tile=tile, grad_tile=grad_tile),
        in_specs=[vmem] * 4 + [hbm] * 3,
        out_specs=[vmem, hbm, hbm],
        out_shape=[jax.ShapeDtypeStruct((total, width), BF), jax.ShapeDtypeStruct((total, width + 128), BF),
                   jax.ShapeDtypeStruct((3, width, ff), BF)],
        scratch_shapes=[
            vm((width, ff), BF), vm((width, ff), BF), vm((ff, width), BF),
            vm((8, capacity, width + 128), BF), vm((8, capacity, width + 128), BF),
            vm((2 * capacity, width), BF), vm((width, total), BF), vm((width, total), BF),
            vm((total, ff), BF), vm((total, ff), BF), vm((total, ff), BF),
            vm((2 * capacity, width), F32), vm((2 * capacity, width), F32), vm((2, 3, width, grad_tile), BF),
            pltpu.SemaphoreType.DMA((16,)), pltpu.SemaphoreType.DMA((16,)), pltpu.SemaphoreType.DMA((4,)),
            pltpu.SemaphoreType.DMA((2,)),
        ],
        compiler_params=pltpu.CompilerParams(vmem_limit_bytes=62 << 20, collective_id=1, has_side_effects=True),
        cost_estimate=pl.CostEstimate(flops=18 * total * width * ff, bytes_accessed=12 * width * ff + 8 * total * width,
                                      transcendentals=total * ff),
        name="experts_on_rows",
    )(slots, h2, ext, g, w_gate, w_up, w_down)


def one(cond):
    return jnp.where(cond, 1.0, 0.0)


def pick_parts(aux, routes, experts):
    lane = lane_iota()
    gate = [pick(aux, lane, experts + k) for k in range(2)]
    alpha = [[pick(aux, lane, experts + 2 + 2 * c + k) for k in range(2)] for c in range(2)]
    copy = [one(routes[k] == FFN_EXP + 1) for k in range(2)]
    const = [[one(routes[k] == FFN_EXP + 2 + c) for c in range(2)] for k in range(2)]
    on_h2 = [copy[k] + const[k][0] * alpha[0][0] + const[k][1] * alpha[1][0] for k in range(2)]
    return gate, alpha, copy, const, on_h2


def one_hot(slots, total):
    return jnp.where(lane_iota(total) == slots, 1.0, 0.0).astype(BF)


def combine_kernel(back_ref, slot_ref, routes_ref, aux_ref, x2_ref, h2_ref, g_ref, gain_ref, wcat_ref, v_ref, w_ref,
                   prev_ref, dx2_ref, da_ref, do_ref, cat_ref, sums_ref, *, experts):
    step = pl.program_id(0)
    lane = lane_iota()
    h2 = h2_ref[...].astype(F32)
    g = g_ref[...].astype(F32)
    x2 = x2_ref[...]
    width = x2.shape[1]
    r2 = rms_scale(x2)
    route = [routes_ref[:, k:k + 1] for k in range(2)]
    gate, alpha, copy, const, on_h2 = pick_parts(aux_ref[...], route, experts)
    hot = [one_hot(slot_ref[:, k:k + 1], back_ref.shape[0]) for k in range(2)]
    g_h2 = jnp.sum(g * h2, axis=1, keepdims=True)
    g_v = [jnp.sum(g * v_ref[c:c + 1, :], axis=1, keepdims=True) for c in range(2)]
    dgate = []
    for k in range(2):
        at_expert = jnp.sum(dot(hot[k], back_ref[:, width:]), axis=1, keepdims=True)
        dgate.append(at_expert + on_h2[k] * g_h2 + const[k][0] * alpha[0][1] * g_v[0] + const[k][1] * alpha[1][1] * g_v[1])
    mean = gate[0] * dgate[0] + gate[1] * dgate[1]
    dl = [gate[k] * (dgate[k] - mean) for k in range(2)]
    grads = jnp.where(lane == route[0], dl[0], 0.0) + jnp.where(lane == route[1], dl[1], 0.0)
    prev_ref[...] = grads[:, :experts]
    weight = [gate[0] * const[0][c] + gate[1] * const[1][c] for c in range(2)]
    sums = []
    on_g = copy[0] * gate[0] + copy[1] * gate[1]
    for c in range(2):
        da0 = weight[c] * g_h2
        da1 = weight[c] * g_v[c]
        mid = alpha[c][0] * da0 + alpha[c][1] * da1
        grads = jnp.where(lane == experts + 2 * c, alpha[c][0] * (da0 - mid), grads)
        grads = jnp.where(lane == experts + 2 * c + 1, alpha[c][1] * (da1 - mid), grads)
        on_g = on_g + alpha[c][0] * weight[c]
        sums.append(jnp.sum((alpha[c][1] * weight[c]) * g, axis=0, keepdims=True))
    low = grads.astype(BF)
    cat = dot(low.T, h2_ref[...])
    dh2 = dot(low, wcat_ref[...], NT) + on_g * g + dot(hot[0] + hot[1], back_ref[:, :width])
    sums.append(jnp.sum(dh2 * x2 * r2, axis=0, keepdims=True))
    u = dh2 * gain_ref[...]
    dx2 = g + r2 * (u - x2 * (r2 * r2) * jnp.mean(u * x2, axis=-1, keepdims=True))
    dx2_ref[...] = dx2
    da = dx2.astype(BF)
    da_ref[...] = da
    do_ref[...] = dot(da, w_ref[...], NT).astype(BF)
    parts = jnp.concatenate(sums + [jnp.zeros((8 - len(sums), width), F32)], axis=0)

    @pl.when(step == 0)
    def _():
        cat_ref[...] = cat
        sums_ref[...] = parts

    @pl.when(step > 0)
    def _():
        cat_ref[...] += cat
        sums_ref[...] += parts


def combine(back, slots, routes, aux, x2, h2, g, gain, wcat, const_v, w_out, experts, tile=256):
    rows, width = x2.shape
    block = pl.BlockSpec((tile, width), lambda i: (i, 0))
    thin = pl.BlockSpec((tile, 128), lambda i: (i, 0))
    two = pl.BlockSpec((tile, 2), lambda i: (i, 0))
    sds = jax.ShapeDtypeStruct
    return pl.pallas_call(
        functools.partial(combine_kernel, experts=experts),
        grid=(rows // tile,),
        in_specs=[whole(back.shape), two, two, thin, block, block, block, whole(gain.shape), whole(wcat.shape),
                  whole(const_v.shape), whole(w_out.shape)],
        out_specs=[pl.BlockSpec((tile, experts), lambda i: (i, 0)), block, block, block, whole((128, width)),
                   whole((8, width))],
        out_shape=[sds((rows, experts), F32), sds((rows, width), F32), sds((rows, width), BF),
                   sds((rows, width), BF), sds((128, width), F32), sds((8, width), F32)],
        compiler_params=params(),
        cost_estimate=pl.CostEstimate(flops=4 * rows * width * back.shape[0], bytes_accessed=26 * rows * width,
                                      transcendentals=0),
        name="combine",
    )(back, slots, routes, aux, x2, h2, g, gain, wcat, const_v, w_out)


def padded_rows(rows, rest):
    unit = 8 * rest * 16
    return -(-rows // unit) * unit


def finale_kernel(small_ref, gain_ref, *refs, rest, chunks, norm_row, tile):
    hbm, refs = refs[:12], refs[12:]
    shard_refs, (small_out_ref, token_hbm) = refs[:2], refs[2:4]
    local, refs = refs[4:16], refs[16:]
    (turned_ref, g_ref, norm_ref, dh_ref, r0_ref, sm_ref, rs_ref, rd0_ref, td_ref, rd1_ref, tok_ref,
     load_sem, tok_sem, send_sem, recv_sem) = refs[:15]
    r1_ref, r2_ref = (refs[15 + 2 * n:17 + 2 * n] for n in range(2))
    ho_ref, dq_ref, o_ref, da_ref, wq_ref, dk_ref, wk_ref, dv_ref, wv_ref, hp_ref, x_ref, dx2_ref = local[:12]

    loads = [pltpu.make_async_copy(src, dst, load_sem.at[n]) for n, (src, dst) in enumerate(zip(hbm, local))]
    for copy in loads:
        copy.start()

    dp, ex = lax.axis_index("dp"), lax.axis_index("expert")
    c, x, y, z = ex % 2, ex // 2, dp % 2, dp // 2
    mate = (dp, x * 2 + 1 - c)
    across = (dp, (1 - x) * 2 + c)
    beside = (z * 2 + 1 - y, ex)
    ahead = [((z + d) % rest * 2 + y, ex) for d in range(1, rest)]
    barrier = pltpu.get_barrier_semaphore()
    for peer in [mate, across, beside] + ahead:
        pl.semaphore_signal(barrier, inc=1, device_id=peer, device_id_type=MESH)
    pl.semaphore_wait(barrier, 2 + rest)

    started = []

    def send(src, dst, peer):
        n = len(started)
        copy = pltpu.make_async_remote_copy(src_ref=src, dst_ref=dst, send_sem=send_sem.at[n], recv_sem=recv_sem.at[n],
                                            device_id=peer, device_id_type=MESH)
        copy.start()
        started.append(copy)
        return copy

    rows, width = g_ref.shape
    own = ho_ref.shape[0]
    prompt = hp_ref.shape[0]
    half = rows // 2
    size = half // chunks
    q1, q2 = size // 2, size // 4
    cut = width // 2
    part = [pl.ds(0, cut), pl.ds(cut, width - cut)]
    first, second = [across, beside], [beside, across]
    bit1, bit2 = [x, y], [y, x]

    def ds(at, n):
        return pl.ds(pl.multiple_of(at, 16), n)

    def at1(k, p, bit):
        return k * size + bit * q1

    def stage0(k):
        return [send(g_ref.at[ds((1 - c) * half + k * size, size)], r0_ref.at[ds(k * size, size)], mate)]

    def stage1(k):
        sl = pl.ds(k * size, size)
        r0_ref[sl] = (g_ref[ds(c * half + k * size, size)].astype(F32) + r0_ref[sl].astype(F32)).astype(BF)
        return [send(r0_ref.at[ds(at1(k, p, 1 - bit1[p]), q1), part[p]], r1_ref[p].at[pl.ds(k * q1, q1)], first[p])
                for p in range(2)]

    def stage2(k):
        out = []
        for p in range(2):
            sl = pl.ds(k * q1, q1)
            r1_ref[p][sl] = (r0_ref[ds(at1(k, p, bit1[p]), q1), part[p]].astype(F32) + r1_ref[p][sl].astype(F32)).astype(BF)
            out.append(send(r1_ref[p].at[ds(k * q1 + (1 - bit2[p]) * q2, q2)], r2_ref[p].at[pl.ds(k * q2, q2)], second[p]))
        return out

    def stage3(k):
        for p in range(2):
            sl = pl.ds(k * q2, q2)
            shard_refs[p][sl] = (r1_ref[p][ds(k * q1 + bit2[p] * q2, q2)].astype(F32) + r2_ref[p][sl].astype(F32)).astype(BF)
        return []

    stages = (stage0, stage1, stage2, stage3)
    waiting = {}

    def wait(line):
        for copy in waiting.pop(line, []):
            copy.wait_recv()

    def step(k, s):
        wait(k)
        waiting[k] = stages[s](k) if s < len(stages) else []

    block = own // 2

    def dh_rows(xx, cc):
        return ds((xx * 2 + cc) * block, block)

    def prompt_rows(cc):
        @pl.loop(0, 2 * (block // tile))
        def _(i):
            at = ds((i // (block // tile) * 2 + cc) * block + i % (block // tile) * tile, tile)
            dh_ref[at] = (dot(dk_ref[at], wk_ref[...], NT) + dot(dv_ref[at], wv_ref[...], NT)).astype(BF)

    small_peers = [mate, across, beside]

    def small_step(n):
        wait("small")
        if n < 4:
            sm_ref[n] = small_ref[...] if n == 0 else sm_ref[n - 1] + rs_ref[n - 1]
            if n == 0:
                at = lax.broadcasted_iota(jnp.int32, (small_ref.shape[0], 1), 0)
                norm = jnp.sum(norm_ref[...].T, axis=0, keepdims=True) / gain_ref[...]
                sm_ref[0] = jnp.where(at == norm_row, norm, small_ref[...])
        if n < 3:
            waiting["small"] = [send(sm_ref.at[n], rs_ref.at[n], small_peers[n])]
        elif n == 3:
            waiting["small"] = [send(sm_ref.at[3], rs_ref.at[2 + d], ahead[d - 1]) for d in range(1, rest)]
        else:
            total = sm_ref[3]
            for d in range(1, rest):
                total = total + rs_ref[2 + d]
            small_out_ref[...] = total

    strip = width // 3

    def gradient(b, terms, first_row, w_ref):
        mine = slice(b * strip, (b + 1) * strip)
        got = sum(dot(turned_ref[mine, at:at + count], rhs_ref[...]) for at, count, rhs_ref in terms)
        g_ref[first_row + b * strip:first_row + (b + 1) * strip, :] = got.astype(BF)
        if w_ref is not None:
            share = got * w_ref[mine, :].astype(F32)
            norm_ref[mine, :] += sum(share[:, n:n + 128] for n in range(0, width, 128))

    def put_tokens(i, dh, copies):
        at = pl.ds(i * tile, tile)
        xf = x_ref[at].astype(F32)
        r1 = rms_scale(xf)
        u = dh * gain_ref[...]
        slot = i % 2
        tok_ref[slot] = dx2_ref[at] + r1 * (u - xf * (r1 * r1) * jnp.mean(u * xf, axis=-1, keepdims=True))
        copy = pltpu.make_async_copy(tok_ref.at[slot], token_hbm.at[at], tok_sem.at[slot])
        copy.start()
        copies.append(copy)

    if rows > 4 * width:
        g_ref[4 * width:, :] = jnp.zeros((rows - 4 * width, width), BF)
    norm_ref[...] = jnp.zeros_like(norm_ref)
    tokens = []

    def own_tokens(i):
        at = pl.ds(i * tile, tile)
        dh = dot(dq_ref[at], wq_ref[...], NT)
        if i * tile >= block:
            kv = pl.ds(prompt + i * tile - block, tile)
            dh = dh + dot(dk_ref[kv], wk_ref[...], NT) + dot(dv_ref[kv], wv_ref[...], NT)
        else:
            inner = ds((x * 2 + c) * block + i * tile, tile)
            dh = dh + dh_ref[inner].astype(F32) + rd0_ref[x, at].astype(F32) + rd1_ref[at].astype(F32)
        if len(tokens) >= 2:
            tokens[-2].wait()
        put_tokens(i, dh, tokens)

    hops = (4.5, 6.0, 5.0)
    due = []

    def begin(now, k):
        step(k, 0)
        due.append([now + hops[0], k, 1])

    def ready(now):
        for entry in sorted(due, key=lambda entry: (entry[0], str(entry[1]))):
            if entry[0] <= now:
                _, k, s = entry
                due.remove(entry)
                if k == "small":
                    small_step(s)
                    last = 4
                else:
                    step(k, s)
                    last = len(stages) - 1
                if s < last:
                    due.append([max(now, entry[0]) + (hops[s] if k != "small" else 5.0), k, s + 1])

    def wait_loads(*numbers):
        for n in numbers:
            loads[n].wait()

    def first_turn():
        wait_loads(0, 1, 2, 3, 4)
        turned_ref[:, :own] = ho_ref[...].T
        turned_ref[:, own:2 * own] = o_ref[...].T

    def second_turn():
        wait_loads(5, 6, 7, 8, 9)
        turned_ref[:, :prompt] = hp_ref[...].T
        turned_ref[:, prompt:] = ho_ref[block:].T

    def first_grads(b):
        gradient(b, [(0, own, dq_ref)], 0, wq_ref)
        gradient(b, [(own, own, da_ref)], 2 * width, None)

    def second_grads(b):
        gradient(b, [(0, prompt + block, dk_ref)], width, wk_ref)
        gradient(b, [(0, prompt + block, dv_ref)], 3 * width, wv_ref)

    def mates():
        prompt_rows(1 - c)
        waiting["dh"] = [send(dh_ref.at[dh_rows(w, 1 - c)], rd0_ref.at[w], mate) for w in range(2)]

    def over():
        wait("dh")
        td_ref[...] = (dh_ref[dh_rows(1 - x, c)].astype(F32) + rd0_ref[1 - x].astype(F32)).astype(BF)
        waiting["dh"] = [send(td_ref, rd1_ref, across)]

    def prompt_tokens(i):
        wait("dh")
        own_tokens(i)

    blocks = own // tile
    tasks = [(4.0, first_turn)] + [(2.0, functools.partial(first_grads, b)) for b in range(3)] + [(3.0, second_turn)]
    tasks += [(4.0, functools.partial(second_grads, b)) for b in range(3)]
    tasks += [(4.0, mates), (4.0, lambda: prompt_rows(c)), (0.5, over)]
    tasks += [(2.0, lambda: wait_loads(10, 11))] + [(2.0, functools.partial(own_tokens, i)) for i in range(blocks // 2, blocks)]
    after = {1: [0], 2: [1], 3: [2], 5: [3], 6: [4], 7: [5]} if chunks == 6 else {7: list(range(chunks))}
    now = 0.0
    for n, (length, task) in enumerate(tasks):
        task()
        now += length
        for k in after.get(n, []):
            begin(now, k)
        if n == 7:
            small_step(0)
            due.append([now + 5.0, "small", 1])
        ready(now)
    late = list(range(blocks // 2))
    while due or late:
        now = max(now, min(entry[0] for entry in due)) if due else now
        ready(now)
        if late and not due:
            prompt_tokens(late.pop(0))
    for copy in tokens[-2:]:
        copy.wait()
    for copy in started:
        copy.wait_send()


def finale(small, gain, arrays, rest, norm_row, out_rows, tile=256):
    own, width = arrays[0].shape
    prompt = arrays[9].shape[0]
    block = own // 2
    half = out_rows // 2
    chunks = 6 if half == 6 * 4 * rest * 16 else 1
    lanes = (width // 2, width // 2)
    copies = chunks * (1 + 2 + 2) + 3 + 3 + rest - 1
    vm, dma = pltpu.VMEM, pltpu.SemaphoreType.DMA
    vmem, hbm = pl.BlockSpec(memory_space=pltpu.VMEM), pl.BlockSpec(memory_space=pl.ANY)
    return pl.pallas_call(
        functools.partial(finale_kernel, rest=rest, chunks=chunks, norm_row=norm_row, tile=tile),
        in_specs=[vmem] * 2 + [hbm] * len(arrays),
        out_specs=[vmem, vmem, vmem, hbm],
        out_shape=[jax.ShapeDtypeStruct((half // 4, k), BF) for k in lanes]
        + [jax.ShapeDtypeStruct(small.shape, F32), jax.ShapeDtypeStruct((own, width), F32)],
        scratch_shapes=[vm(a.shape, a.dtype) for a in arrays] + [
            vm((width, prompt + block), BF), vm((out_rows, width), BF), vm((width, 128), F32), vm((prompt, width), BF),
            vm((half, width), BF), vm((4,) + small.shape, F32), vm((2 + rest,) + small.shape, F32),
            vm((2, block, width), BF), vm((block, width), BF), vm((block, width), BF), vm((2, tile, width), F32),
            dma((len(arrays),)), dma((2,)), dma((copies,)), dma((copies,)),
        ] + [vm((half // n, k), BF) for n in (2, 4) for k in lanes],
        compiler_params=pltpu.CompilerParams(vmem_limit_bytes=62 << 20, collective_id=0, has_side_effects=True),
        cost_estimate=pl.CostEstimate(flops=30 * own * width * width, bytes_accessed=8 * out_rows * width, transcendentals=0),
        name="finale",
    )(small, gain, *arrays)


def spread_kernel(shard0_ref, shard1_ref, v_ref, *refs, rest, chunks, experts, tile):
    shards = (shard0_ref, shard1_ref)
    hbm, (out_ref, mixed_ref), refs = refs[:6], refs[6:8], refs[8:]
    local, (r3a_ref, r3b_ref, load_sem, send_sem, recv_sem) = refs[:6], refs[6:]
    r3_ref = (r3a_ref, r3b_ref)
    made_ref, slot_ref, routes_ref, aux_ref, x2_ref, h2_ref = local
    loads = [pltpu.make_async_copy(src, dst, load_sem.at[n]) for n, (src, dst) in enumerate(zip(hbm, local))]
    for copy in loads:
        copy.start()
    dp, ex = lax.axis_index("dp"), lax.axis_index("expert")
    c, x, y, z = ex % 2, ex // 2, dp % 2, dp // 2
    mate = (dp, x * 2 + 1 - c)
    across = (dp, (1 - x) * 2 + c)
    beside = (z * 2 + 1 - y, ex)
    ahead = [((z + d) % rest * 2 + y, ex) for d in range(1, rest)]
    barrier = pltpu.get_barrier_semaphore()
    for peer in [mate, across, beside] + ahead:
        pl.semaphore_signal(barrier, inc=1, device_id=peer, device_id_type=MESH)
    pl.semaphore_wait(barrier, 2 + rest)

    started = []
    rows, width = out_ref.shape
    half = rows // 2
    size = half // chunks
    q1, q2, q3 = size // 2, size // 4, size // 4 // rest
    cut = width // 2
    part = [pl.ds(0, cut), pl.ds(cut, width - cut)]
    first, second = [across, beside], [beside, across]
    bit1, bit2 = [x, y], [y, x]

    def copy_to(src, dst, peer):
        n = len(started)
        copy = pltpu.make_async_remote_copy(src_ref=src, dst_ref=dst, send_sem=send_sem.at[n], recv_sem=recv_sem.at[n],
                                            device_id=peer, device_id_type=MESH)
        copy.start()
        started.append(copy)
        return copy

    def send(at, count, lanes, peer):
        spot = out_ref.at[pl.ds(pl.multiple_of(at, 16), count), lanes]
        return copy_to(spot, spot, peer)

    def base(k, p, depth):
        at = c * half + k * size
        if depth > 0:
            at = at + bit1[p] * q1
        if depth > 1:
            at = at + bit2[p] * q2
        if depth > 2:
            at = at + z * q3
        return at

    def stage0(k):
        out = []
        for p in range(2):
            at = base(k, p, 3)
            total = shards[p][pl.ds(pl.multiple_of(k * q2 + z * q3, 16), q3)].astype(F32)
            for d in range(1, rest):
                total = total + r3_ref[p][d - 1, pl.ds(k * q3, q3)].astype(F32)
            out_ref[pl.ds(pl.multiple_of(at, 16), q3), part[p]] = total.astype(BF)
            out += [send(at, q3, part[p], peer) for peer in ahead]
        return out

    def reduce(k):
        out = []
        for p in range(2):
            for d in range(1, rest):
                to = pl.ds(pl.multiple_of(k * q2 + (z + d) % rest * q3, 16), q3)
                out.append(copy_to(shards[p].at[to], r3_ref[p].at[d - 1, pl.ds(k * q3, q3)], ahead[d - 1]))
        return out

    def stage1(k):
        return [send(base(k, p, 2), q2, part[p], second[p]) for p in range(2)]

    def stage2(k):
        return [send(base(k, p, 1), q1, part[p], first[p]) for p in range(2)]

    def stage3(k):
        return [send(base(k, 0, 0), size, pl.ds(0, width), mate)]

    def end(k):
        return []

    stages = (reduce, stage0, stage1, stage2, stage3, end)
    waiting = {k: [] for k in range(chunks)}

    def mixing(i):
        at = pl.ds(i * tile, tile)
        if i == 0:
            for copy in loads:
                copy.wait()
        route = [routes_ref[at, k:k + 1] for k in range(2)]
        gate, alpha, _, const, on_h2 = pick_parts(aux_ref[at], route, experts)
        out = x2_ref[at] + (gate[0] * on_h2[0] + gate[1] * on_h2[1]) * h2_ref[at].astype(F32)
        for n in range(2):
            out = out + ((gate[0] * const[0][n] + gate[1] * const[1][n]) * alpha[n][1]) * v_ref[n:n + 1, :]
        for k in range(2):
            out = out + gate[k] * dot(one_hot(slot_ref[at, k:k + 1], made_ref.shape[0]), made_ref[...])
        mixed_ref[at] = out.astype(BF)

    blocks = list(range(x2_ref.shape[0] // tile))
    for t in range(len(stages) + (chunks + 1) // 2 - 1):
        for k in range(chunks):
            s = t - k // 2
            if 0 <= s < len(stages):
                for copy in waiting[k]:
                    copy.wait_recv()
                waiting[k] = stages[s](k)
        if blocks:
            mixing(blocks.pop(0))
    for i in blocks:
        mixing(i)
    for copy in started:
        copy.wait_send()


def spread_sums(shards, const_v, arrays, rest, out_rows, experts, tile=256):
    rows, width = arrays[4].shape
    half = out_rows // 2
    chunks = 6 if half == 6 * 4 * rest * 16 else 1
    copies = chunks * (4 * (rest - 1) + 2 + 2 + 1)
    vm, dma = pltpu.VMEM, pltpu.SemaphoreType.DMA
    vmem, hbm = pl.BlockSpec(memory_space=pltpu.VMEM), pl.BlockSpec(memory_space=pl.ANY)
    return pl.pallas_call(
        functools.partial(spread_kernel, rest=rest, chunks=chunks, experts=experts, tile=tile),
        in_specs=[vmem] * 3 + [hbm] * len(arrays),
        out_specs=[vmem, vmem],
        out_shape=[jax.ShapeDtypeStruct((out_rows, width), BF), jax.ShapeDtypeStruct((rows, width), BF)],
        scratch_shapes=[vm(a.shape, a.dtype) for a in arrays] + [vm((rest - 1, half // 4 // rest, width // 2), BF)] * 2
        + [dma((len(arrays),)), dma((copies,)), dma((copies,))],
        compiler_params=params(collective_id=2, has_side_effects=True),
        cost_estimate=pl.CostEstimate(flops=4 * rows * width * 1536, bytes_accessed=8 * out_rows * width, transcendentals=0),
        name="spread_sums",
    )(*shards, const_v, *arrays)


def slot_table(routes_t, priority, groups, capacity):
    ids = jnp.arange(FFN_EXP, dtype=jnp.int32)
    picked = routes_t[:, None, :] == ids[None, :, None]
    assigned = jnp.any(picked, axis=0).astype(BF)
    earlier = (priority[:, None] < priority[None, :]).astype(BF)
    rank_table = jnp.dot(assigned, earlier, preferred_element_type=F32)
    rank = jnp.sum(jnp.where(picked, rank_table[None], 0.0), axis=1).astype(jnp.int32)
    place = (routes_t % groups) * (FFN_EXP // groups) + routes_t // groups
    return jnp.where((routes_t < FFN_EXP) & (rank < capacity), place * capacity + rank, -1)


def local(
    tokens, prev_logits, routes, priority, norm_attn, w_query, w_key, w_value, w_out, norm_ffn, router, const_w, const_v,
    w_gate, w_up, w_down, cotangent,
):
    rows, width = tokens.shape
    experts = prev_logits.shape[1]
    dp = lax.axis_size("dp")
    expert_devices = lax.axis_size("expert")
    pair = w_gate.shape[0]
    capacity = 9 * rows * routes.shape[1] // (8 * experts)
    prompt_dev = PROMPT // expert_devices
    ff = w_gate.shape[2]
    e = lax.axis_index("expert").astype(jnp.int32).reshape(1)
    j = (lax.axis_index("dp") % pair).astype(jnp.int32).reshape(1)
    members = pair * expert_devices
    everyone = ("dp", "expert")
    exchange = [list(range(p * members, (p + 1) * members)) for p in range(dp // pair)]
    alike = [list(range(q, dp, pair)) for q in range(pair)]
    pairs = [list(range(p * pair, (p + 1) * pair)) for p in range(dp // pair)]

    def swap(x):
        return lax.all_to_all(x, everyone, split_axis=0, concat_axis=0, axis_index_groups=exchange, tiled=True)

    cos, sin = angle_tables()
    gain1, gain2 = norm_attn[None, :], norm_ffn[None, :]

    prompt_x = lax.all_gather(tokens[:prompt_dev], "expert", axis=0, tiled=True)
    slots_t = slot_table(routes.T, priority, pair, capacity)
    slots = slots_t.T
    grads_out = dispatch(slots_t, cotangent, members, capacity)
    h_own, q, k_own, v_own = project(e, tokens, gain1, (w_query, w_key, w_value), cos, sin, True)
    prompt_x, grads_out, h_own = lax.optimization_barrier((prompt_x, grads_out, h_own))
    grads_in = swap(grads_out).reshape(-1, width)
    h_prompt, k_prompt, v_prompt = project(e, prompt_x, gain1, (w_key, w_value), cos, sin, False)
    o, lse = attn_fwd(e, q, k_own, v_own, k_prompt, v_prompt)

    wcat = jnp.concatenate(
        [router, const_w.transpose(1, 0, 2).reshape(width, -1), jnp.zeros((width, 128 - experts - 4), BF)], axis=1
    )
    prev = jnp.pad(prev_logits, ((0, 0), (0, 128 - experts)))
    x2, h2, aux, ext = gates(tokens, o, w_out, gain2, wcat, prev, routes, experts)
    made, back, ffn_sum = experts_on_rows(slots_t, h2, ext, grads_in, w_gate, w_up, w_down, capacity)
    ffn_sum = lax.psum_scatter(ffn_sum, "dp", scatter_dimension=2, axis_index_groups=alike, tiled=True)
    grad_prev, dx2, da, do, cat, sums = combine(
        back, slots, routes, aux, x2, h2, cotangent, gain2, wcat, const_v, w_out, experts
    )
    dq, dk, dv, made = attn_bwd(q, do, o, lse, k_own, v_own, k_prompt, v_prompt, cos, sin, made, capacity)
    rest = dp // 2
    n = experts
    small = jnp.concatenate([cat[:n + 4], sums[:3], jnp.zeros((5, width), F32)], axis=0)
    out_rows = padded_rows(4 * width, rest)
    *shards, small, grad_tokens = finale(
        small, gain1, (h_own, dq, o, da, w_query, dk, w_key, dv, w_value, h_prompt, tokens, dx2), rest, n + 7, out_rows
    )
    ffn_sum = ffn_sum.reshape(3, width, pair, -1).transpose(2, 0, 1, 3)
    ffn_sum, small, shards = lax.optimization_barrier((ffn_sum, small, shards))
    ffn_sum = lax.all_to_all(ffn_sum, "dp", split_axis=0, concat_axis=0, axis_index_groups=pairs, tiled=True)
    grad_w, mixed = spread_sums(shards, const_v, (made, slots, routes, aux, x2, h2), rest, out_rows, experts)
    grad_w = grad_w.astype(F32)
    ffn_sum = ffn_sum.astype(F32)
    return (
        mixed,
        grad_tokens,
        grad_prev,
        small[n + 7],
        grad_w[:width],
        grad_w[width:2 * width],
        grad_w[3 * width:4 * width],
        grad_w[2 * width:3 * width],
        small[n + 6],
        small[:n].T,
        small[n:n + 4].reshape(2, 2, width).transpose(0, 2, 1),
        small[n + 4:n + 6],
        ffn_sum[:, 0],
        ffn_sum[:, 1],
        ffn_sum[:, 2].transpose(0, 2, 1),
    )


def solution(mesh):
    block = P(("dp", "expert"), None)
    in_specs = (block, block, block, P(("dp", "expert"))) + (P(),) * 9 + (P("expert", None, None),) * 3 + (block,)
    out_specs = (block, block, block) + (P(),) * 9 + (
        P("expert", None, "dp"), P("expert", None, "dp"), P("expert", "dp", None),
    )
    return jax.shard_map(local, mesh=mesh, in_specs=in_specs, out_specs=out_specs, check_vma=False)
```

```python
import functools

import jax
import jax.numpy as jnp
import numpy as np
from jax import lax
from jax.experimental import pallas as pl
from jax.experimental.pallas import tpu as pltpu
from jax.sharding import PartitionSpec as P

HEADS = 12
FFN_EXP = 8
PROMPT = 2048
NCONT = 8
CONT = 256

epsilon = 1e-06
LOG2E = 1.4426950408889634
F32 = jnp.float32
BF = jnp.bfloat16
NN = (((1,), (0,)), ((), ()))
NT = (((1,), (1,)), ((), ()))
VMEM_LIMIT = 56 << 20


def dot(a, b, dims=NN):
    return lax.dot_general(a, b, dims, preferred_element_type=F32)


def params(**kw):
    return pltpu.CompilerParams(vmem_limit_bytes=VMEM_LIMIT, **kw)


def whole(shape):
    return pl.BlockSpec(shape, lambda *_: (0,) * len(shape))


def rms_scale(x):
    return lax.rsqrt(jnp.mean(x * x, axis=-1, keepdims=True) + epsilon)


def angle_tables():
    fine = 64
    frequency = np.exp(-np.log(10000.0) * np.arange(32) * 2.0 / 64)
    frequency = np.tile(frequency.astype(np.float32).astype(np.float64), 4)
    near = np.arange(fine)[:, None] * frequency
    far = (np.arange((PROMPT + CONT) // fine) * fine)[:, None] * frequency
    near_cos, near_sin, far_cos, far_sin = (
        jnp.asarray(table.astype(np.float32)) for table in (np.cos(near), np.sin(near), np.cos(far), np.sin(far))
    )
    near_cos, near_sin, far_cos, far_sin = near_cos[None], near_sin[None], far_cos[:, None], far_sin[:, None]
    sign = jnp.where(jnp.arange(128) % 64 < 32, -1.0, 1.0)
    cosine = far_cos * near_cos - far_sin * near_sin
    sine = (far_sin * near_cos + far_cos * near_sin) * sign
    return cosine.reshape(-1, 128), sine.reshape(-1, 128)


def lane_iota(width=128):
    return lax.broadcasted_iota(jnp.int32, (1, width), 1)


def swap_halves(x):
    return jnp.where(lane_iota() % 64 < 32, pltpu.roll(x, 96, 1), pltpu.roll(x, 32, 1))


def project_kernel(e_ref, x_ref, gain_ref, *refs, count):
    weights, (cos_ref, sin_ref), (h_ref, *outs) = refs[:count], refs[count:count + 2], refs[count + 2:]
    x = x_ref[...].astype(F32)
    h = (x * rms_scale(x) * gain_ref[...]).astype(BF)
    h_ref[...] = h
    cosine, sine = cos_ref[...], sin_ref[...]
    for n, (w_ref, out_ref) in enumerate(zip(weights, outs)):
        full = dot(h, w_ref[...])
        if n == count - 1:
            out_ref[...] = full.astype(BF)
            continue
        for i in range(full.shape[1] // 128):
            part = full[:, i * 128:(i + 1) * 128]
            out_ref[:, i * 128:(i + 1) * 128] = (part * cosine + swap_halves(part) * sine).astype(BF)


def project(e, x, gain, weights, cos, sin, own, tile=256):
    rows, width = x.shape
    block = pl.BlockSpec((tile, width), lambda i, *_: (i, 0))
    half = rows // 2 // tile

    def position(i, e_ref):
        if not own:
            return (i, 0)
        return (jnp.where(i < half, e_ref[0] * half + i, PROMPT // tile), 0)

    table = pl.BlockSpec((tile, 128), position)
    return pl.pallas_call(
        functools.partial(project_kernel, count=len(weights)),
        grid_spec=pltpu.PrefetchScalarGridSpec(
            num_scalar_prefetch=1,
            grid=(rows // tile,),
            in_specs=[block, whole((1, width))] + [whole(weights[0].shape)] * len(weights) + [table, table],
            out_specs=[block] * (len(weights) + 1),
        ),
        out_shape=[jax.ShapeDtypeStruct((rows, width), BF)] * (len(weights) + 1),
        compiler_params=params(),
        cost_estimate=pl.CostEstimate(
            flops=2 * rows * width * width * len(weights), bytes_accessed=2 * rows * width * 6, transcendentals=0
        ),
        name="project_own" if own else "project_prompt",
    )(e, x, gain, *weights, cos, sin)


MESH = pl.DeviceIdType.MESH


def eight():
    dp, ex = lax.axis_index("dp"), lax.axis_index("expert")
    j, c, x = dp % 2, ex % 2, ex // 2

    def flip(bit, by):
        return bit + by * (1 - 2 * bit)

    def peer(r):
        return dp + (r // 2 % 2) * (1 - 2 * j), flip(x, r // 4) * 2 + flip(c, r % 2)

    def place(r):
        return flip(j, r // 2 % 2) * 4 + flip(x, r // 4) * 2 + flip(c, r % 2)

    return peer, place


def exchange_rows(rows_hbm, got_hbm, send_sem, recv_sem, local_sem, capacity):
    peer, place = eight()
    step = pl.program_id(0)

    def spot(r):
        return pl.ds(pl.multiple_of(place(r) * capacity, 16), capacity)

    def copies():
        return [
            pltpu.make_async_remote_copy(
                src_ref=rows_hbm.at[spot(r)], dst_ref=got_hbm.at[spot(0)], send_sem=send_sem.at[r], recv_sem=recv_sem.at[r],
                device_id=peer(r), device_id_type=MESH,
            )
            for r in range(1, 8)
        ] + [pltpu.make_async_copy(rows_hbm.at[spot(0)], got_hbm.at[spot(0)], local_sem.at[0])]

    barrier = pltpu.get_barrier_semaphore()

    @pl.when(step == 0)
    def _():
        for r in range(1, 8):
            pl.semaphore_signal(barrier, inc=1, device_id=peer(r), device_id_type=MESH)

    @pl.when(step == 1)
    def _():
        pl.semaphore_wait(barrier, 7)
        for copy in copies():
            copy.start()

    @pl.when(step == pl.num_programs(0) - 1)
    def _():
        for copy in copies():
            copy.wait()


def attn_fwd_kernel(q_ref, ko_ref, vo_ref, kp_ref, vp_ref, rows_hbm, o_ref, lse_ref, got_hbm, vt_ref, qm_ref, m_ref, acc_ref,
                    send_sem, recv_sem, local_sem, *, chunk, tile, scale, capacity):
    e = lax.axis_index("expert")
    exchange_rows(rows_hbm, got_hbm, send_sem, recv_sem, local_sem, capacity)
    rows = q_ref.shape[0]
    half = rows // 2
    npr = kp_ref.shape[0]
    nchunk = npr // chunk
    lane = lax.broadcasted_iota(jnp.int32, (1, 128), 1)
    low = lane < 64
    c = scale * LOG2E
    zero = jnp.zeros((), BF)
    q = q_ref[...]
    qm_ref[0] = jnp.where(low, q, zero)
    qm_ref[1] = jnp.where(low, zero, q)
    ones = jnp.ones((16, npr + rows), BF)
    for r, n, ref in ((0, npr, vp_ref), (npr, rows, vo_ref)):
        vt = ref[...].T
        vt_ref[0, :64, r:r + n] = vt[:64]
        vt_ref[1, :64, r:r + n] = vt[64:]
    vt_ref[0, 64:, :] = ones
    vt_ref[1, 64:, :] = ones
    tri = lax.broadcasted_iota(jnp.int32, (tile, tile), 0) <= lax.broadcasted_iota(jnp.int32, (tile, tile), 1)

    def first(q0, qn, k, vts):
        for h in range(2):
            s = dot(k, qm_ref[h, q0:q0 + qn, :], NT)
            s = s * c
            s = jnp.where(tri, s, -1e30)
            mx = jnp.max(s, axis=0, keepdims=True)
            p = jnp.exp2(s - mx).astype(BF)
            m_ref[h, 0:1, q0:q0 + qn] = mx
            acc_ref[h, :, q0:q0 + qn] = dot(vts[h], p)

    def step(blocks, k, vts):
        ss = [[dot(k, qm_ref[h, q0:q0 + qn, :], NT) for h in range(2)] for q0, qn in blocks]
        for (q0, qn), sb in zip(blocks, ss):
            for h in range(2):
                s = sb[h] * c
                mx = jnp.max(s, axis=0, keepdims=True)
                m = m_ref[h, 0:1, q0:q0 + qn]
                mn = jnp.maximum(m, mx)
                p = jnp.exp2(s - mn).astype(BF)
                m_ref[h, 0:1, q0:q0 + qn] = mn
                acc_ref[h, :, q0:q0 + qn] = acc_ref[h, :, q0:q0 + qn] * jnp.exp2(m - mn) + dot(vts[h], p)

    for j in range(rows // tile):
        r0 = j * tile
        first(r0, tile, ko_ref[r0:r0 + tile, :], [vt_ref[h, :, npr + r0:npr + r0 + tile] for h in range(2)])
    for j in range(1, half // tile):
        for i in range(j):
            r0 = i * tile
            step([(j * tile, tile)], ko_ref[r0:r0 + tile, :], [vt_ref[h, :, npr + r0:npr + r0 + tile] for h in range(2)])

    def body(ci, blocks):
        r0 = pl.multiple_of(ci * chunk, chunk)
        step(blocks, kp_ref[pl.ds(r0, chunk), :], [vt_ref[h, :, pl.ds(r0, chunk)] for h in range(2)])

    ne = e * half // chunk

    @pl.loop(0, ne)
    def _(ci):
        body(ci, [(0, half), (half, half)])

    @pl.loop(ne, nchunk)
    def _(ci):
        body(ci, [(half, half)])

    outs = []
    for h in range(2):
        l = acc_ref[h, 64:65, :]
        outs.append(acc_ref[h, :64, :] / l)
        lse_ref[0, h:h + 1, :] = m_ref[h, 0:1, :] + jnp.log2(l)
    o_ref[...] = jnp.concatenate(outs, axis=0).T.astype(BF)


def attn_fwd(q, ko, vo, kp, vp, made, capacity, *, chunk=512, tile=256):
    rows, width = q.shape
    npr = kp.shape[0]
    pairs = width // 128
    hbm = pl.BlockSpec(memory_space=pl.ANY)
    own = pl.BlockSpec((rows, 128), lambda i, *_: (0, i))
    pr = pl.BlockSpec((npr, 128), lambda i, *_: (0, i))
    return pl.pallas_call(
        functools.partial(attn_fwd_kernel, chunk=chunk, tile=tile, scale=0.125, capacity=capacity),
        grid_spec=pl.GridSpec(
            grid=(pairs,),
            in_specs=[own, own, own, pr, pr, hbm],
            out_specs=[own, pl.BlockSpec((1, 2, rows), lambda i, *_: (i, 0, 0)), hbm],
            scratch_shapes=[pltpu.VMEM((2, 80, npr + rows), BF), pltpu.VMEM((2, rows, 128), BF),
            pltpu.VMEM((2, 8, rows), F32), pltpu.VMEM((2, 80, rows), F32),
            pltpu.SemaphoreType.DMA((8,)), pltpu.SemaphoreType.DMA((8,)), pltpu.SemaphoreType.DMA((1,))]),
        out_shape=[jax.ShapeDtypeStruct((rows, width), BF), jax.ShapeDtypeStruct((pairs, 2, rows), F32),
                   jax.ShapeDtypeStruct(made.shape, BF)],
        compiler_params=params(collective_id=4, has_side_effects=True),
        cost_estimate=pl.CostEstimate(flops=4 * rows * npr * width * 2, bytes_accessed=2 * npr * width * 4, transcendentals=rows * npr * 12),
        name="attn_fwd",
    )(q, ko, vo, kp, vp, made)


def attn_bwd_kernel(q_ref, do_ref, o_ref, lse_ref, ko_ref, vo_ref, kp_ref, vp_ref, cos_ref, sin_ref, rows_hbm,
               dq_ref, dk_ref, dv_ref, got_hbm,
               kt_ref, dqt_ref, qm_ref, dom_ref, dl_ref, dks_ref, dvs_ref, send_sem, recv_sem, local_sem, *, tile, scale,
               capacity):
    e = lax.axis_index("expert")
    exchange_rows(rows_hbm, got_hbm, send_sem, recv_sem, local_sem, capacity)
    rows = q_ref.shape[0]
    half = rows // 2
    chunk = half
    npr = kp_ref.shape[0]
    nchunk = npr // chunk
    cont = cos_ref.shape[0] - npr
    lane = lax.broadcasted_iota(jnp.int32, (1, 128), 1)
    low = lane < 64
    c = scale * LOG2E
    zero = jnp.zeros((), BF)
    q = q_ref[...]
    do = do_ref[...]
    qm_ref[0] = jnp.where(low, q, zero)
    qm_ref[1] = jnp.where(low, zero, q)
    dom_ref[0] = jnp.where(low, do, zero)
    dom_ref[1] = jnp.where(low, zero, do)
    prod = (do.astype(F32) * o_ref[...].astype(F32)).T
    dl_ref[0:1, :] = jnp.sum(prod[:64], axis=0, keepdims=True)
    dl_ref[1:2, :] = jnp.sum(prod[64:], axis=0, keepdims=True)
    kt_ref[:, :npr] = kp_ref[...].T
    kt_ref[:, npr:] = ko_ref[...].T
    tri = lax.broadcasted_iota(jnp.int32, (tile, tile), 0) <= lax.broadcasted_iota(jnp.int32, (tile, tile), 1)

    def unrope(x, pos, n):
        first = (lane % 64) < 32
        sw = jnp.where(first, pltpu.roll(x, 96, 1), pltpu.roll(x, 32, 1))
        return x * cos_ref[pl.ds(pos, n), :] - sw * sin_ref[pl.ds(pos, n), :]

    def block(k, v, kt, q0, qn, mask):
        dk = dv = None
        dqs = []
        qs = [qm_ref[h, q0:q0 + qn, :] for h in range(2)]
        dos = [dom_ref[h, q0:q0 + qn, :] for h in range(2)]
        sts = [dot(k, qs[h], NT) for h in range(2)]
        dps = [dot(v, dos[h], NT) for h in range(2)]
        for h in range(2):
            p = jnp.exp2(sts[h] * c - lse_ref[0, h:h + 1, q0:q0 + qn])
            if mask is not None:
                p = jnp.where(mask, p, 0.0)
            ds = (p * (dps[h] - dl_ref[h:h + 1, q0:q0 + qn])).astype(BF)
            dvh = dot(p.astype(BF), dos[h])
            dkh = dot(ds, qs[h])
            dk, dv = (dkh, dvh) if dk is None else (dk + dkh, dv + dvh)
            dqs.append(dot(kt[h * 64:(h + 1) * 64], ds))
        return dk, dv, jnp.concatenate(dqs, axis=0)

    nt = rows // tile
    for i in range(nt):
        r0 = i * tile
        k = ko_ref[r0:r0 + tile, :]
        v = vo_ref[r0:r0 + tile, :]
        kt = kt_ref[:, npr + r0:npr + r0 + tile]
        prompt = r0 < half
        dk = dv = None
        for j in (range(i, nt // 2) if prompt else [i]):
            a, b, dq = block(k, v, kt, j * tile, tile, tri if i == j else None)
            dk, dv = (a, b) if dk is None else (dk + a, dv + b)
            sl = slice(j * tile, (j + 1) * tile)
            if i == 0 or not prompt:
                dqt_ref[:, sl] = dq
            else:
                dqt_ref[:, sl] += dq
        if prompt:
            dks_ref[r0:r0 + tile, :] = dk
            dvs_ref[r0:r0 + tile, :] = dv
        else:
            o0 = npr + r0 - half
            dk_ref[o0:o0 + tile, :] = (unrope(dk, npr, tile) * scale).astype(BF)
            dv_ref[o0:o0 + tile, :] = dv.astype(BF)

    def chunk_step(ci, kind):
        r0 = pl.multiple_of(ci * chunk, chunk)
        k = kp_ref[pl.ds(r0, chunk), :]
        v = vp_ref[pl.ds(r0, chunk), :]
        kt = kt_ref[:, pl.ds(r0, chunk)]
        dk, dv, dq = block(k, v, kt, half, half, None)
        dqt_ref[:, half:] += dq
        if kind == 0:
            a, b, dq = block(k, v, kt, 0, half, None)
            dk, dv = dk + a, dv + b
            dqt_ref[:, :half] += dq
        elif kind == 1:
            dk, dv = dk + dks_ref[...], dv + dvs_ref[...]
        dk_ref[pl.ds(r0, chunk), :] = (unrope(dk, r0, chunk) * scale).astype(BF)
        dv_ref[pl.ds(r0, chunk), :] = dv.astype(BF)

    @pl.loop(0, e)
    def _(ci):
        chunk_step(ci, 0)

    chunk_step(e, 1)

    @pl.loop(e + 1, nchunk)
    def _(ci):
        chunk_step(ci, 2)

    dq = dqt_ref[...].T
    base = pl.multiple_of(e * half, half)
    dq_ref[:half, :] = (unrope(dq[:half], base, half) * scale).astype(BF)
    for r in range(half, rows, cont):
        dq_ref[r:r + cont, :] = (unrope(dq[r:r + cont], npr, cont) * scale).astype(BF)


def attn_bwd(q, do, o, lse, ko, vo, kp, vp, cos, sin, made, capacity, *, tile=256):
    rows, width = q.shape
    npr = kp.shape[0]
    keys = npr + rows // 2
    pairs = width // 128
    own = pl.BlockSpec((rows, 128), lambda i, *_: (0, i))
    pr = pl.BlockSpec((npr, 128), lambda i, *_: (0, i))
    al = pl.BlockSpec((keys, 128), lambda i, *_: (0, i))
    hbm = pl.BlockSpec(memory_space=pl.ANY)
    tab = pl.BlockSpec(cos.shape, lambda i, *_: (0, 0))
    return pl.pallas_call(
        functools.partial(attn_bwd_kernel, tile=tile, scale=0.125, capacity=capacity),
        grid_spec=pl.GridSpec(
            grid=(pairs,),
            in_specs=[own, own, own, pl.BlockSpec((1, 2, rows), lambda i, *_: (i, 0, 0)), own, own, pr, pr, tab, tab, hbm],
            out_specs=[own, al, al, hbm],
            scratch_shapes=[pltpu.VMEM((128, npr + rows), BF), pltpu.VMEM((128, rows), F32),
                            pltpu.VMEM((2, rows, 128), BF), pltpu.VMEM((2, rows, 128), BF),
                            pltpu.VMEM((8, rows), F32),
                            pltpu.VMEM((rows // 2, 128), F32), pltpu.VMEM((rows // 2, 128), F32),
                            pltpu.SemaphoreType.DMA((8,)), pltpu.SemaphoreType.DMA((8,)), pltpu.SemaphoreType.DMA((1,))]),
        out_shape=[jax.ShapeDtypeStruct((rows, width), BF), jax.ShapeDtypeStruct((keys, width), BF),
                   jax.ShapeDtypeStruct((keys, width), BF), jax.ShapeDtypeStruct(made.shape, BF)],
        compiler_params=params(collective_id=3, has_side_effects=True),
        cost_estimate=pl.CostEstimate(flops=10 * rows * npr * width * 2, bytes_accessed=2 * npr * width * 8, transcendentals=rows * npr * 12),
        name="attn_bwd",
    )(q, do, o, lse, ko, vo, kp, vp, cos, sin, made)


def pick(values, lane, index):
    return jnp.sum(jnp.where(lane == index, values, 0.0), axis=1, keepdims=True)


def softmax_pair(a, b):
    top = jnp.maximum(a, b)
    ea, eb = jnp.exp(a - top), jnp.exp(b - top)
    total = ea + eb
    return ea / total, eb / total


def spread(column):
    lane = lane_iota()
    parts, left = jnp.zeros((1, 128), F32), column
    for n in range(3):
        part = left.astype(BF).astype(F32)
        parts = jnp.where(lane == n, part, parts)
        left = left - part
    return parts.astype(BF)


def gate_kernel(x_ref, o_ref, w_ref, gain_ref, wcat_ref, prev_ref, routes_ref, x2_ref, h2_ref, aux_ref, ext_ref, *, experts):
    x2 = x_ref[...].astype(F32) + dot(o_ref[...], w_ref[...])
    x2_ref[...] = x2
    h2 = (x2 * rms_scale(x2) * gain_ref[...]).astype(BF)
    h2_ref[...] = h2
    logits = dot(h2, wcat_ref[...]) + prev_ref[...]
    lane = lane_iota()
    gates = softmax_pair(*[pick(logits, lane, routes_ref[:, k:k + 1]) for k in range(2)])
    aux = logits
    for k in range(2):
        aux = jnp.where(lane == experts + k, gates[k], aux)
    at = experts + 2
    for c in range(2):
        alpha = softmax_pair(*[pick(logits, lane, experts + 2 * c + k) for k in range(2)])
        for k in range(2):
            aux = jnp.where(lane == at + 2 * c + k, alpha[k], aux)
    aux_ref[...] = aux
    for k in range(2):
        ext_ref[:, k * 128:(k + 1) * 128] = spread(gates[k])


def gates(x, o, w_out, gain, wcat, prev, routes, experts, tile=256):
    rows, width = x.shape
    block = pl.BlockSpec((tile, width), lambda i: (i, 0))
    thin = pl.BlockSpec((tile, 128), lambda i: (i, 0))
    return pl.pallas_call(
        functools.partial(gate_kernel, experts=experts),
        grid=(rows // tile,),
        in_specs=[block, block, whole(w_out.shape), whole(gain.shape), whole(wcat.shape), thin,
                  pl.BlockSpec((tile, 2), lambda i: (i, 0))],
        out_specs=[block, block, thin, pl.BlockSpec((tile, 256), lambda i: (i, 0))],
        out_shape=[jax.ShapeDtypeStruct((rows, width), F32), jax.ShapeDtypeStruct((rows, width), BF),
                   jax.ShapeDtypeStruct((rows, 128), F32), jax.ShapeDtypeStruct((rows, 256), BF)],
        compiler_params=params(),
        cost_estimate=pl.CostEstimate(flops=2 * rows * width * width, bytes_accessed=12 * rows * width, transcendentals=0),
        name="gates",
    )(x, o, w_out, gain, wcat, prev, routes)


def dispatch_kernel(slot_ref, rows_ref, out_ref, *, capacity):
    ids = pl.program_id(0) * capacity + lax.broadcasted_iota(jnp.int32, (capacity, 1), 0)
    hot = [jnp.where(ids == slot_ref[k:k + 1, :], 1.0, 0.0).astype(BF) for k in range(2)]
    out_ref[0] = dot(hot[0] + hot[1], rows_ref[...]).astype(BF)


def dispatch(slots, rows, destinations, capacity):
    count, width = rows.shape
    return pl.pallas_call(
        functools.partial(dispatch_kernel, capacity=capacity),
        grid=(destinations,),
        in_specs=[whole(slots.shape), whole(rows.shape)],
        out_specs=pl.BlockSpec((1, capacity, width), lambda i: (i, 0, 0)),
        out_shape=jax.ShapeDtypeStruct((destinations, capacity, width), BF),
        compiler_params=params(),
        cost_estimate=pl.CostEstimate(flops=2 * destinations * capacity * count * width, bytes_accessed=4 * count * width,
                                      transcendentals=0),
        name="dispatch_grads",
    )(slots, rows)


def expert_kernel(slot_ref, h2_ref, ext_ref, g_ref, wg_hbm, wu_hbm, wd_hbm, made_ref, back_hbm, grad_hbm,
                  wg_ref, wu_ref, wd_ref, a_ref, s_ref, d_ref, at_ref, dt_ref, hid_ref, dg_ref, du_ref, macc_ref,
                  bacc_ref, out_ref, send_sem, recv_sem, local_sem, out_sem, *, capacity, tile, grad_tile):
    dp, ex = lax.axis_index("dp"), lax.axis_index("expert")
    j, c, x = dp % 2, ex % 2, ex // 2
    width = h2_ref.shape[1]
    ff = wg_ref.shape[1]
    loads = [pltpu.make_async_copy(src.at[j], dst, local_sem.at[n])
             for n, (src, dst) in enumerate(((wg_hbm, wg_ref), (wu_hbm, wu_ref), (wd_hbm, wd_ref)))]
    for copy in loads:
        copy.start()

    def flip(bit, by):
        return bit + by * (1 - 2 * bit)

    def peer(r):
        return dp + (r // 2 % 2) * (1 - 2 * j), flip(x, r // 4) * 2 + flip(c, r % 2)

    def place(r):
        return flip(j, r // 2 % 2) * 4 + flip(x, r // 4) * 2 + flip(c, r % 2)

    barrier = pltpu.get_barrier_semaphore()
    for r in range(1, 8):
        pl.semaphore_signal(barrier, inc=1, device_id=peer(r), device_id_type=MESH)
    pl.semaphore_wait(barrier, 7)

    def send(src, dst, kind, r):
        n = kind * 8 + r
        copy = pltpu.make_async_remote_copy(src_ref=src, dst_ref=dst, send_sem=send_sem.at[n], recv_sem=recv_sem.at[n],
                                            device_id=peer(r), device_id_type=MESH)
        copy.start()
        return copy

    rows = {}
    for r in (4, 5, 2, 3, 6, 7, 1, 0):
        ids = place(r) * capacity + lax.broadcasted_iota(jnp.int32, (capacity, 1), 0)
        hot = [jnp.where(ids == slot_ref[k:k + 1, :], 1.0, 0.0).astype(BF) for k in range(2)]
        into = s_ref if r else a_ref
        into[r, :, :width] = dot(hot[0] + hot[1], h2_ref[...]).astype(BF)
        into[r, :, width:] = (dot(hot[0], ext_ref[:, :128]) + dot(hot[1], ext_ref[:, 128:])).astype(BF)
        if r:
            rows[r] = send(s_ref.at[r], a_ref.at[r], 0, r)

    for copy in loads:
        copy.wait()
    returned = []
    mine = pl.ds(pl.multiple_of(place(0) * capacity, 16), capacity)
    two = 2 * capacity
    for n, first in enumerate((0, 4, 2, 6)):
        for r in (first, first + 1):
            if r:
                rows[r].wait_recv()
            got = a_ref[r]
            half = pl.ds((r - first) * capacity, capacity)
            gate = jnp.sum(got[:, width:].astype(F32), axis=1, keepdims=True)
            g = g_ref[pl.ds(pl.multiple_of(place(r) * capacity, 16), capacity), :].astype(F32)
            d_ref[half, :] = (g * gate).astype(BF)
        span = pl.ds(n * two, two)
        a = a_ref[first:first + 2, :, :width].reshape(two, width)
        at_ref[:, span] = a.T
        dt_ref[:, span] = d_ref[...].T
        macc_ref[...] = jnp.zeros_like(macc_ref)
        bacc_ref[...] = jnp.zeros_like(bacc_ref)

        @pl.loop(0, ff // tile)
        def _(i):
            cols = pl.ds(pl.multiple_of(i * tile, tile), tile)
            a = a_ref[first:first + 2, :, :width].reshape(two, width)
            gate, up = dot(a, wg_ref[:, cols]), dot(a, wu_ref[:, cols])
            dh = dot(d_ref[...], wd_ref[cols, :], NT)
            sig = jax.nn.sigmoid(gate)
            act = gate * sig
            hidden = (act * up).astype(BF)
            du = (dh * act).astype(BF)
            dg = (dh * up * sig * (1.0 + gate * (1.0 - sig))).astype(BF)
            hid_ref[span, cols] = hidden
            du_ref[span, cols] = du
            dg_ref[span, cols] = dg
            macc_ref[...] += dot(hidden, wd_ref[cols, :])
            bacc_ref[...] += dot(dg, wg_ref[:, cols], NT) + dot(du, wu_ref[:, cols], NT)

        for r in (first, first + 1):
            half = pl.ds((r - first) * capacity, capacity)
            if r:
                rows[r].wait_send()
            theirs = pl.ds(pl.multiple_of(place(r) * capacity, 16), capacity)
            made = macc_ref[half, :].astype(BF)
            made_ref[theirs, :] = made
            s_ref[r, :, :width] = bacc_ref[half, :].astype(BF)
            s_ref[r, :, width:] = spread(jnp.sum(g_ref[theirs, :].astype(F32) * made.astype(F32), axis=1, keepdims=True))
            if r:
                returned.append(send(s_ref.at[r], back_hbm.at[mine], 1, r))
            else:
                kept = pltpu.make_async_copy(s_ref.at[0], back_hbm.at[mine], local_sem.at[3])
                kept.start()

    steps = ff // grad_tile

    def put(i, slot):
        cols = pl.ds(pl.multiple_of(i * grad_tile, grad_tile), grad_tile)
        return pltpu.make_async_copy(out_ref.at[slot], grad_hbm.at[:, :, cols], out_sem.at[slot])

    @pl.loop(0, steps)
    def _(i):
        slot = i % 2

        @pl.when(i >= 2)
        def _():
            put(i - 2, slot).wait()

        cols = pl.ds(pl.multiple_of(i * grad_tile, grad_tile), grad_tile)
        out_ref[slot, 0] = dot(at_ref[...], dg_ref[:, cols]).astype(BF)
        out_ref[slot, 1] = dot(at_ref[...], du_ref[:, cols]).astype(BF)
        out_ref[slot, 2] = dot(dt_ref[...], hid_ref[:, cols]).astype(BF)
        put(i, slot).start()

    for i in range(max(steps - 2, 0), steps):
        put(i, i % 2).wait()
    kept.wait()
    for copy in returned:
        copy.wait_recv()
        copy.wait_send()


def experts_on_rows(slots, h2, ext, g, w_gate, w_up, w_down, capacity, tile=512, grad_tile=256):
    width = h2.shape[1]
    ff = w_gate.shape[2]
    total = 8 * capacity
    vm = pltpu.VMEM
    vmem, hbm = pl.BlockSpec(memory_space=pltpu.VMEM), pl.BlockSpec(memory_space=pl.ANY)
    return pl.pallas_call(
        functools.partial(expert_kernel, capacity=capacity, tile=tile, grad_tile=grad_tile),
        in_specs=[vmem] * 4 + [hbm] * 3,
        out_specs=[vmem, hbm, hbm],
        out_shape=[jax.ShapeDtypeStruct((total, width), BF), jax.ShapeDtypeStruct((total, width + 128), BF),
                   jax.ShapeDtypeStruct((3, width, ff), BF)],
        scratch_shapes=[
            vm((width, ff), BF), vm((width, ff), BF), vm((ff, width), BF),
            vm((8, capacity, width + 128), BF), vm((8, capacity, width + 128), BF),
            vm((2 * capacity, width), BF), vm((width, total), BF), vm((width, total), BF),
            vm((total, ff), BF), vm((total, ff), BF), vm((total, ff), BF),
            vm((2 * capacity, width), F32), vm((2 * capacity, width), F32), vm((2, 3, width, grad_tile), BF),
            pltpu.SemaphoreType.DMA((16,)), pltpu.SemaphoreType.DMA((16,)), pltpu.SemaphoreType.DMA((4,)),
            pltpu.SemaphoreType.DMA((2,)),
        ],
        compiler_params=pltpu.CompilerParams(vmem_limit_bytes=62 << 20, collective_id=1, has_side_effects=True),
        cost_estimate=pl.CostEstimate(flops=18 * total * width * ff, bytes_accessed=12 * width * ff + 8 * total * width,
                                      transcendentals=total * ff),
        name="experts_on_rows",
    )(slots, h2, ext, g, w_gate, w_up, w_down)


def one(cond):
    return jnp.where(cond, 1.0, 0.0)


def pick_parts(aux, routes, experts):
    lane = lane_iota()
    gate = [pick(aux, lane, experts + k) for k in range(2)]
    alpha = [[pick(aux, lane, experts + 2 + 2 * c + k) for k in range(2)] for c in range(2)]
    copy = [one(routes[k] == FFN_EXP + 1) for k in range(2)]
    const = [[one(routes[k] == FFN_EXP + 2 + c) for c in range(2)] for k in range(2)]
    on_h2 = [copy[k] + const[k][0] * alpha[0][0] + const[k][1] * alpha[1][0] for k in range(2)]
    return gate, alpha, copy, const, on_h2


def one_hot(slots, total):
    return jnp.where(lane_iota(total) == slots, 1.0, 0.0).astype(BF)


def combine_kernel(back_ref, slot_ref, routes_ref, aux_ref, x2_ref, h2_ref, g_ref, gain_ref, wcat_ref, v_ref, w_ref,
                   prev_ref, dx2_ref, da_ref, do_ref, cat_ref, sums_ref, *, experts):
    step = pl.program_id(0)
    lane = lane_iota()
    h2 = h2_ref[...].astype(F32)
    g = g_ref[...].astype(F32)
    x2 = x2_ref[...]
    width = x2.shape[1]
    r2 = rms_scale(x2)
    route = [routes_ref[:, k:k + 1] for k in range(2)]
    gate, alpha, copy, const, on_h2 = pick_parts(aux_ref[...], route, experts)
    hot = [one_hot(slot_ref[:, k:k + 1], back_ref.shape[0]) for k in range(2)]
    g_h2 = jnp.sum(g * h2, axis=1, keepdims=True)
    g_v = [jnp.sum(g * v_ref[c:c + 1, :], axis=1, keepdims=True) for c in range(2)]
    dgate = []
    for k in range(2):
        at_expert = jnp.sum(dot(hot[k], back_ref[:, width:]), axis=1, keepdims=True)
        dgate.append(at_expert + on_h2[k] * g_h2 + const[k][0] * alpha[0][1] * g_v[0] + const[k][1] * alpha[1][1] * g_v[1])
    mean = gate[0] * dgate[0] + gate[1] * dgate[1]
    dl = [gate[k] * (dgate[k] - mean) for k in range(2)]
    grads = jnp.where(lane == route[0], dl[0], 0.0) + jnp.where(lane == route[1], dl[1], 0.0)
    prev_ref[...] = grads[:, :experts]
    weight = [gate[0] * const[0][c] + gate[1] * const[1][c] for c in range(2)]
    sums = []
    on_g = copy[0] * gate[0] + copy[1] * gate[1]
    for c in range(2):
        da0 = weight[c] * g_h2
        da1 = weight[c] * g_v[c]
        mid = alpha[c][0] * da0 + alpha[c][1] * da1
        grads = jnp.where(lane == experts + 2 * c, alpha[c][0] * (da0 - mid), grads)
        grads = jnp.where(lane == experts + 2 * c + 1, alpha[c][1] * (da1 - mid), grads)
        on_g = on_g + alpha[c][0] * weight[c]
        sums.append(jnp.sum((alpha[c][1] * weight[c]) * g, axis=0, keepdims=True))
    low = grads.astype(BF)
    cat = dot(low.T, h2_ref[...])
    dh2 = dot(low, wcat_ref[...], NT) + on_g * g + dot(hot[0] + hot[1], back_ref[:, :width])
    sums.append(jnp.sum(dh2 * x2 * r2, axis=0, keepdims=True))
    u = dh2 * gain_ref[...]
    dx2 = g + r2 * (u - x2 * (r2 * r2) * jnp.mean(u * x2, axis=-1, keepdims=True))
    dx2_ref[...] = dx2
    da = dx2.astype(BF)
    da_ref[...] = da
    do_ref[...] = dot(da, w_ref[...], NT).astype(BF)
    parts = jnp.concatenate(sums + [jnp.zeros((8 - len(sums), width), F32)], axis=0)

    @pl.when(step == 0)
    def _():
        cat_ref[...] = cat
        sums_ref[...] = parts

    @pl.when(step > 0)
    def _():
        cat_ref[...] += cat
        sums_ref[...] += parts


def combine(back, slots, routes, aux, x2, h2, g, gain, wcat, const_v, w_out, experts, tile=256):
    rows, width = x2.shape
    block = pl.BlockSpec((tile, width), lambda i: (i, 0))
    thin = pl.BlockSpec((tile, 128), lambda i: (i, 0))
    two = pl.BlockSpec((tile, 2), lambda i: (i, 0))
    sds = jax.ShapeDtypeStruct
    return pl.pallas_call(
        functools.partial(combine_kernel, experts=experts),
        grid=(rows // tile,),
        in_specs=[whole(back.shape), two, two, thin, block, block, block, whole(gain.shape), whole(wcat.shape),
                  whole(const_v.shape), whole(w_out.shape)],
        out_specs=[pl.BlockSpec((tile, experts), lambda i: (i, 0)), block, block, block, whole((128, width)),
                   whole((8, width))],
        out_shape=[sds((rows, experts), F32), sds((rows, width), F32), sds((rows, width), BF),
                   sds((rows, width), BF), sds((128, width), F32), sds((8, width), F32)],
        compiler_params=params(),
        cost_estimate=pl.CostEstimate(flops=4 * rows * width * back.shape[0], bytes_accessed=26 * rows * width,
                                      transcendentals=0),
        name="combine",
    )(back, slots, routes, aux, x2, h2, g, gain, wcat, const_v, w_out)


def padded_rows(rows, rest):
    unit = 8 * rest * 16
    return -(-rows // unit) * unit


def finale_kernel(small_ref, gain_ref, *refs, rest, chunks, norm_row, tile):
    hbm, refs = refs[:12], refs[12:]
    shard_refs, (small_out_ref, token_hbm) = refs[:2], refs[2:4]
    local, refs = refs[4:16], refs[16:]
    (turned_ref, g_ref, norm_ref, dh_ref, r0_ref, sm_ref, rs_ref, rd0_ref, td_ref, rd1_ref, tok_ref,
     load_sem, tok_sem, send_sem, recv_sem) = refs[:15]
    r1_ref, r2_ref = (refs[15 + 2 * n:17 + 2 * n] for n in range(2))
    ho_ref, dq_ref, o_ref, da_ref, wq_ref, dk_ref, wk_ref, dv_ref, wv_ref, hp_ref, x_ref, dx2_ref = local[:12]

    loads = [pltpu.make_async_copy(src, dst, load_sem.at[n]) for n, (src, dst) in enumerate(zip(hbm, local))]
    for copy in loads:
        copy.start()

    dp, ex = lax.axis_index("dp"), lax.axis_index("expert")
    c, x, y, z = ex % 2, ex // 2, dp % 2, dp // 2
    mate = (dp, x * 2 + 1 - c)
    across = (dp, (1 - x) * 2 + c)
    beside = (z * 2 + 1 - y, ex)
    ahead = [((z + d) % rest * 2 + y, ex) for d in range(1, rest)]
    barrier = pltpu.get_barrier_semaphore()
    for peer in [mate, across, beside] + ahead:
        pl.semaphore_signal(barrier, inc=1, device_id=peer, device_id_type=MESH)
    pl.semaphore_wait(barrier, 2 + rest)

    started = []

    def send(src, dst, peer):
        n = len(started)
        copy = pltpu.make_async_remote_copy(src_ref=src, dst_ref=dst, send_sem=send_sem.at[n], recv_sem=recv_sem.at[n],
                                            device_id=peer, device_id_type=MESH)
        copy.start()
        started.append(copy)
        return copy

    rows, width = g_ref.shape
    own = ho_ref.shape[0]
    prompt = hp_ref.shape[0]
    half = rows // 2
    size = half // chunks
    q1, q2 = size // 2, size // 4
    cut = width // 2
    part = [pl.ds(0, cut), pl.ds(cut, width - cut)]
    first, second = [across, beside], [beside, across]
    bit1, bit2 = [x, y], [y, x]

    def ds(at, n):
        return pl.ds(pl.multiple_of(at, 16), n)

    def at1(k, p, bit):
        return k * size + bit * q1

    def stage0(k):
        return [send(g_ref.at[ds((1 - c) * half + k * size, size)], r0_ref.at[ds(k * size, size)], mate)]

    def stage1(k):
        sl = pl.ds(k * size, size)
        r0_ref[sl] = (g_ref[ds(c * half + k * size, size)].astype(F32) + r0_ref[sl].astype(F32)).astype(BF)
        return [send(r0_ref.at[ds(at1(k, p, 1 - bit1[p]), q1), part[p]], r1_ref[p].at[pl.ds(k * q1, q1)], first[p])
                for p in range(2)]

    def stage2(k):
        out = []
        for p in range(2):
            sl = pl.ds(k * q1, q1)
            r1_ref[p][sl] = (r0_ref[ds(at1(k, p, bit1[p]), q1), part[p]].astype(F32) + r1_ref[p][sl].astype(F32)).astype(BF)
            out.append(send(r1_ref[p].at[ds(k * q1 + (1 - bit2[p]) * q2, q2)], r2_ref[p].at[pl.ds(k * q2, q2)], second[p]))
        return out

    def stage3(k):
        for p in range(2):
            sl = pl.ds(k * q2, q2)
            shard_refs[p][sl] = (r1_ref[p][ds(k * q1 + bit2[p] * q2, q2)].astype(F32) + r2_ref[p][sl].astype(F32)).astype(BF)
        return []

    stages = (stage0, stage1, stage2, stage3)
    waiting = {}

    def wait(line):
        for copy in waiting.pop(line, []):
            copy.wait_recv()

    def step(k, s):
        wait(k)
        waiting[k] = stages[s](k) if s < len(stages) else []

    block = own // 2

    def dh_rows(xx, cc):
        return ds((xx * 2 + cc) * block, block)

    def prompt_rows(cc):
        @pl.loop(0, 2 * (block // tile))
        def _(i):
            at = ds((i // (block // tile) * 2 + cc) * block + i % (block // tile) * tile, tile)
            dh_ref[at] = (dot(dk_ref[at], wk_ref[...], NT) + dot(dv_ref[at], wv_ref[...], NT)).astype(BF)

    small_peers = [mate, across, beside]

    def small_step(n):
        wait("small")
        if n < 4:
            sm_ref[n] = small_ref[...] if n == 0 else sm_ref[n - 1] + rs_ref[n - 1]
            if n == 0:
                at = lax.broadcasted_iota(jnp.int32, (small_ref.shape[0], 1), 0)
                norm = jnp.sum(norm_ref[...].T, axis=0, keepdims=True) / gain_ref[...]
                sm_ref[0] = jnp.where(at == norm_row, norm, small_ref[...])
        if n < 3:
            waiting["small"] = [send(sm_ref.at[n], rs_ref.at[n], small_peers[n])]
        elif n == 3:
            waiting["small"] = [send(sm_ref.at[3], rs_ref.at[2 + d], ahead[d - 1]) for d in range(1, rest)]
        else:
            total = sm_ref[3]
            for d in range(1, rest):
                total = total + rs_ref[2 + d]
            small_out_ref[...] = total

    strip = width // 3

    def gradient(b, terms, first_row, w_ref):
        mine = slice(b * strip, (b + 1) * strip)
        got = sum(dot(turned_ref[mine, at:at + count], rhs_ref[...]) for at, count, rhs_ref in terms)
        g_ref[first_row + b * strip:first_row + (b + 1) * strip, :] = got.astype(BF)
        if w_ref is not None:
            share = got * w_ref[mine, :].astype(F32)
            norm_ref[mine, :] += sum(share[:, n:n + 128] for n in range(0, width, 128))

    def put_tokens(i, dh, copies):
        at = pl.ds(i * tile, tile)
        xf = x_ref[at].astype(F32)
        r1 = rms_scale(xf)
        u = dh * gain_ref[...]
        slot = i % 2
        tok_ref[slot] = dx2_ref[at] + r1 * (u - xf * (r1 * r1) * jnp.mean(u * xf, axis=-1, keepdims=True))
        copy = pltpu.make_async_copy(tok_ref.at[slot], token_hbm.at[at], tok_sem.at[slot])
        copy.start()
        copies.append(copy)

    if rows > 4 * width:
        g_ref[4 * width:, :] = jnp.zeros((rows - 4 * width, width), BF)
    norm_ref[...] = jnp.zeros_like(norm_ref)
    tokens = []

    def own_tokens(i):
        at = pl.ds(i * tile, tile)
        dh = dot(dq_ref[at], wq_ref[...], NT)
        if i * tile >= block:
            kv = pl.ds(prompt + i * tile - block, tile)
            dh = dh + dot(dk_ref[kv], wk_ref[...], NT) + dot(dv_ref[kv], wv_ref[...], NT)
        else:
            inner = ds((x * 2 + c) * block + i * tile, tile)
            dh = dh + dh_ref[inner].astype(F32) + rd0_ref[x, at].astype(F32) + rd1_ref[at].astype(F32)
        if len(tokens) >= 2:
            tokens[-2].wait()
        put_tokens(i, dh, tokens)

    hops = (4.5, 6.0, 5.0)
    due = []

    def begin(now, k):
        step(k, 0)
        due.append([now + hops[0], k, 1])

    def ready(now):
        for entry in sorted(due, key=lambda entry: (entry[0], str(entry[1]))):
            if entry[0] <= now:
                _, k, s = entry
                due.remove(entry)
                if k == "small":
                    small_step(s)
                    last = 4
                else:
                    step(k, s)
                    last = len(stages) - 1
                if s < last:
                    due.append([max(now, entry[0]) + (hops[s] if k != "small" else 5.0), k, s + 1])

    def wait_loads(*numbers):
        for n in numbers:
            loads[n].wait()

    def first_turn():
        wait_loads(0, 1, 2, 3, 4)
        turned_ref[:, :own] = ho_ref[...].T
        turned_ref[:, own:2 * own] = o_ref[...].T

    def second_turn():
        wait_loads(5, 6, 7, 8, 9)
        turned_ref[:, :prompt] = hp_ref[...].T
        turned_ref[:, prompt:] = ho_ref[block:].T

    def first_grads(b):
        gradient(b, [(0, own, dq_ref)], 0, wq_ref)
        gradient(b, [(own, own, da_ref)], 2 * width, None)

    def second_grads(b):
        gradient(b, [(0, prompt + block, dk_ref)], width, wk_ref)
        gradient(b, [(0, prompt + block, dv_ref)], 3 * width, wv_ref)

    def mates():
        prompt_rows(1 - c)
        waiting["dh"] = [send(dh_ref.at[dh_rows(w, 1 - c)], rd0_ref.at[w], mate) for w in range(2)]

    def over():
        wait("dh")
        td_ref[...] = (dh_ref[dh_rows(1 - x, c)].astype(F32) + rd0_ref[1 - x].astype(F32)).astype(BF)
        waiting["dh"] = [send(td_ref, rd1_ref, across)]

    def prompt_tokens(i):
        wait("dh")
        own_tokens(i)

    blocks = own // tile
    tasks = [(4.0, first_turn)] + [(2.0, functools.partial(first_grads, b)) for b in range(3)] + [(3.0, second_turn)]
    tasks += [(4.0, functools.partial(second_grads, b)) for b in range(3)]
    tasks += [(4.0, mates), (4.0, lambda: prompt_rows(c)), (0.5, over)]
    tasks += [(2.0, lambda: wait_loads(10, 11))] + [(2.0, functools.partial(own_tokens, i)) for i in range(blocks // 2, blocks)]
    after = {1: [0], 2: [1], 3: [2], 5: [3], 6: [4], 7: [5]} if chunks == 6 else {7: list(range(chunks))}
    now = 0.0
    for n, (length, task) in enumerate(tasks):
        task()
        now += length
        for k in after.get(n, []):
            begin(now, k)
        if n == 7:
            small_step(0)
            due.append([now + 5.0, "small", 1])
        ready(now)
    late = list(range(blocks // 2))
    while due or late:
        now = max(now, min(entry[0] for entry in due)) if due else now
        ready(now)
        if late and not due:
            prompt_tokens(late.pop(0))
    for copy in tokens[-2:]:
        copy.wait()
    for copy in started:
        copy.wait_send()


def finale(small, gain, arrays, rest, norm_row, out_rows, tile=256):
    own, width = arrays[0].shape
    prompt = arrays[9].shape[0]
    block = own // 2
    half = out_rows // 2
    chunks = 6 if half == 6 * 4 * rest * 16 else 1
    lanes = (width // 2, width // 2)
    copies = chunks * (1 + 2 + 2) + 3 + 3 + rest - 1
    vm, dma = pltpu.VMEM, pltpu.SemaphoreType.DMA
    vmem, hbm = pl.BlockSpec(memory_space=pltpu.VMEM), pl.BlockSpec(memory_space=pl.ANY)
    return pl.pallas_call(
        functools.partial(finale_kernel, rest=rest, chunks=chunks, norm_row=norm_row, tile=tile),
        in_specs=[vmem] * 2 + [hbm] * len(arrays),
        out_specs=[vmem, vmem, vmem, hbm],
        out_shape=[jax.ShapeDtypeStruct((half // 4, k), BF) for k in lanes]
        + [jax.ShapeDtypeStruct(small.shape, F32), jax.ShapeDtypeStruct((own, width), F32)],
        scratch_shapes=[vm(a.shape, a.dtype) for a in arrays] + [
            vm((width, prompt + block), BF), vm((out_rows, width), BF), vm((width, 128), F32), vm((prompt, width), BF),
            vm((half, width), BF), vm((4,) + small.shape, F32), vm((2 + rest,) + small.shape, F32),
            vm((2, block, width), BF), vm((block, width), BF), vm((block, width), BF), vm((2, tile, width), F32),
            dma((len(arrays),)), dma((2,)), dma((copies,)), dma((copies,)),
        ] + [vm((half // n, k), BF) for n in (2, 4) for k in lanes],
        compiler_params=pltpu.CompilerParams(vmem_limit_bytes=62 << 20, collective_id=0, has_side_effects=True),
        cost_estimate=pl.CostEstimate(flops=30 * own * width * width, bytes_accessed=8 * out_rows * width, transcendentals=0),
        name="finale",
    )(small, gain, *arrays)


def spread_kernel(shard0_ref, shard1_ref, v_ref, *refs, rest, chunks, experts, tile):
    shards = (shard0_ref, shard1_ref)
    hbm, (out_ref, mixed_ref), refs = refs[:6], refs[6:8], refs[8:]
    local, (r3a_ref, r3b_ref, load_sem, send_sem, recv_sem) = refs[:6], refs[6:]
    r3_ref = (r3a_ref, r3b_ref)
    made_ref, slot_ref, routes_ref, aux_ref, x2_ref, h2_ref = local
    loads = [pltpu.make_async_copy(src, dst, load_sem.at[n]) for n, (src, dst) in enumerate(zip(hbm, local))]
    for copy in loads:
        copy.start()
    dp, ex = lax.axis_index("dp"), lax.axis_index("expert")
    c, x, y, z = ex % 2, ex // 2, dp % 2, dp // 2
    mate = (dp, x * 2 + 1 - c)
    across = (dp, (1 - x) * 2 + c)
    beside = (z * 2 + 1 - y, ex)
    ahead = [((z + d) % rest * 2 + y, ex) for d in range(1, rest)]
    barrier = pltpu.get_barrier_semaphore()
    for peer in [mate, across, beside] + ahead:
        pl.semaphore_signal(barrier, inc=1, device_id=peer, device_id_type=MESH)
    pl.semaphore_wait(barrier, 2 + rest)

    started = []
    rows, width = out_ref.shape
    half = rows // 2
    size = half // chunks
    q1, q2, q3 = size // 2, size // 4, size // 4 // rest
    cut = width // 2
    part = [pl.ds(0, cut), pl.ds(cut, width - cut)]
    first, second = [across, beside], [beside, across]
    bit1, bit2 = [x, y], [y, x]

    def copy_to(src, dst, peer):
        n = len(started)
        copy = pltpu.make_async_remote_copy(src_ref=src, dst_ref=dst, send_sem=send_sem.at[n], recv_sem=recv_sem.at[n],
                                            device_id=peer, device_id_type=MESH)
        copy.start()
        started.append(copy)
        return copy

    def send(at, count, lanes, peer):
        spot = out_ref.at[pl.ds(pl.multiple_of(at, 16), count), lanes]
        return copy_to(spot, spot, peer)

    def base(k, p, depth):
        at = c * half + k * size
        if depth > 0:
            at = at + bit1[p] * q1
        if depth > 1:
            at = at + bit2[p] * q2
        if depth > 2:
            at = at + z * q3
        return at

    def stage0(k):
        out = []
        for p in range(2):
            at = base(k, p, 3)
            total = shards[p][pl.ds(pl.multiple_of(k * q2 + z * q3, 16), q3)].astype(F32)
            for d in range(1, rest):
                total = total + r3_ref[p][d - 1, pl.ds(k * q3, q3)].astype(F32)
            out_ref[pl.ds(pl.multiple_of(at, 16), q3), part[p]] = total.astype(BF)
            out += [send(at, q3, part[p], peer) for peer in ahead]
        return out

    def reduce(k):
        out = []
        for p in range(2):
            for d in range(1, rest):
                to = pl.ds(pl.multiple_of(k * q2 + (z + d) % rest * q3, 16), q3)
                out.append(copy_to(shards[p].at[to], r3_ref[p].at[d - 1, pl.ds(k * q3, q3)], ahead[d - 1]))
        return out

    def stage1(k):
        return [send(base(k, p, 2), q2, part[p], second[p]) for p in range(2)]

    def stage2(k):
        return [send(base(k, p, 1), q1, part[p], first[p]) for p in range(2)]

    def stage3(k):
        return [send(base(k, 0, 0), size, pl.ds(0, width), mate)]

    def end(k):
        return []

    stages = (reduce, stage0, stage1, stage2, stage3, end)
    waiting = {k: [] for k in range(chunks)}

    def mixing(i):
        at = pl.ds(i * tile, tile)
        if i == 0:
            for copy in loads:
                copy.wait()
        route = [routes_ref[at, k:k + 1] for k in range(2)]
        gate, alpha, _, const, on_h2 = pick_parts(aux_ref[at], route, experts)
        out = x2_ref[at] + (gate[0] * on_h2[0] + gate[1] * on_h2[1]) * h2_ref[at].astype(F32)
        for n in range(2):
            out = out + ((gate[0] * const[0][n] + gate[1] * const[1][n]) * alpha[n][1]) * v_ref[n:n + 1, :]
        for k in range(2):
            out = out + gate[k] * dot(one_hot(slot_ref[at, k:k + 1], made_ref.shape[0]), made_ref[...])
        mixed_ref[at] = out.astype(BF)

    blocks = list(range(x2_ref.shape[0] // tile))
    for t in range(len(stages) + (chunks + 1) // 2 - 1):
        for k in range(chunks):
            s = t - k // 2
            if 0 <= s < len(stages):
                for copy in waiting[k]:
                    copy.wait_recv()
                waiting[k] = stages[s](k)
        if blocks:
            mixing(blocks.pop(0))
    for i in blocks:
        mixing(i)
    for copy in started:
        copy.wait_send()


def spread_sums(shards, const_v, arrays, rest, out_rows, experts, tile=256):
    rows, width = arrays[4].shape
    half = out_rows // 2
    chunks = 6 if half == 6 * 4 * rest * 16 else 1
    copies = chunks * (4 * (rest - 1) + 2 + 2 + 1)
    vm, dma = pltpu.VMEM, pltpu.SemaphoreType.DMA
    vmem, hbm = pl.BlockSpec(memory_space=pltpu.VMEM), pl.BlockSpec(memory_space=pl.ANY)
    return pl.pallas_call(
        functools.partial(spread_kernel, rest=rest, chunks=chunks, experts=experts, tile=tile),
        in_specs=[vmem] * 3 + [hbm] * len(arrays),
        out_specs=[vmem, vmem],
        out_shape=[jax.ShapeDtypeStruct((out_rows, width), BF), jax.ShapeDtypeStruct((rows, width), BF)],
        scratch_shapes=[vm(a.shape, a.dtype) for a in arrays] + [vm((rest - 1, half // 4 // rest, width // 2), BF)] * 2
        + [dma((len(arrays),)), dma((copies,)), dma((copies,))],
        compiler_params=params(collective_id=2, has_side_effects=True),
        cost_estimate=pl.CostEstimate(flops=4 * rows * width * 1536, bytes_accessed=8 * out_rows * width, transcendentals=0),
        name="spread_sums",
    )(*shards, const_v, *arrays)


def slot_table(routes_t, priority, groups, capacity):
    ids = jnp.arange(FFN_EXP, dtype=jnp.int32)
    picked = routes_t[:, None, :] == ids[None, :, None]
    assigned = jnp.any(picked, axis=0).astype(BF)
    earlier = (priority[:, None] < priority[None, :]).astype(BF)
    rank_table = jnp.dot(assigned, earlier, preferred_element_type=F32)
    rank = jnp.sum(jnp.where(picked, rank_table[None], 0.0), axis=1).astype(jnp.int32)
    place = (routes_t % groups) * (FFN_EXP // groups) + routes_t // groups
    return jnp.where((routes_t < FFN_EXP) & (rank < capacity), place * capacity + rank, -1)


def local(
    tokens, prev_logits, routes, priority, norm_attn, w_query, w_key, w_value, w_out, norm_ffn, router, const_w, const_v,
    w_gate, w_up, w_down, cotangent,
):
    rows, width = tokens.shape
    experts = prev_logits.shape[1]
    dp = lax.axis_size("dp")
    expert_devices = lax.axis_size("expert")
    pair = w_gate.shape[0]
    capacity = 9 * rows * routes.shape[1] // (8 * experts)
    prompt_dev = PROMPT // expert_devices
    ff = w_gate.shape[2]
    e = lax.axis_index("expert").astype(jnp.int32).reshape(1)
    j = (lax.axis_index("dp") % pair).astype(jnp.int32).reshape(1)
    members = pair * expert_devices
    alike = [list(range(q, dp, pair)) for q in range(pair)]
    pairs = [list(range(p * pair, (p + 1) * pair)) for p in range(dp // pair)]

    cos, sin = angle_tables()
    gain1, gain2 = norm_attn[None, :], norm_ffn[None, :]

    prompt_x = lax.all_gather(tokens[:prompt_dev], "expert", axis=0, tiled=True)
    slots_t = slot_table(routes.T, priority, pair, capacity)
    slots = slots_t.T
    grads_out = dispatch(slots_t, cotangent, members, capacity)
    h_own, q, k_own, v_own = project(e, tokens, gain1, (w_query, w_key, w_value), cos, sin, True)
    prompt_x, grads_out, h_own = lax.optimization_barrier((prompt_x, grads_out, h_own))
    h_prompt, k_prompt, v_prompt = project(e, prompt_x, gain1, (w_key, w_value), cos, sin, False)
    o, lse, grads_in = attn_fwd(q, k_own, v_own, k_prompt, v_prompt, grads_out.reshape(-1, width), capacity)

    wcat = jnp.concatenate(
        [router, const_w.transpose(1, 0, 2).reshape(width, -1), jnp.zeros((width, 128 - experts - 4), BF)], axis=1
    )
    prev = jnp.pad(prev_logits, ((0, 0), (0, 128 - experts)))
    x2, h2, aux, ext = gates(tokens, o, w_out, gain2, wcat, prev, routes, experts)
    made, back, ffn_sum = experts_on_rows(slots_t, h2, ext, grads_in, w_gate, w_up, w_down, capacity)
    ffn_sum = lax.psum_scatter(ffn_sum, "dp", scatter_dimension=2, axis_index_groups=alike, tiled=True)
    grad_prev, dx2, da, do, cat, sums = combine(
        back, slots, routes, aux, x2, h2, cotangent, gain2, wcat, const_v, w_out, experts
    )
    dq, dk, dv, made = attn_bwd(q, do, o, lse, k_own, v_own, k_prompt, v_prompt, cos, sin, made, capacity)
    rest = dp // 2
    n = experts
    small = jnp.concatenate([cat[:n + 4], sums[:3], jnp.zeros((5, width), F32)], axis=0)
    out_rows = padded_rows(4 * width, rest)
    *shards, small, grad_tokens = finale(
        small, gain1, (h_own, dq, o, da, w_query, dk, w_key, dv, w_value, h_prompt, tokens, dx2), rest, n + 7, out_rows
    )
    ffn_sum = ffn_sum.reshape(3, width, pair, -1).transpose(2, 0, 1, 3)
    ffn_sum, small, shards = lax.optimization_barrier((ffn_sum, small, shards))
    ffn_sum = lax.all_to_all(ffn_sum, "dp", split_axis=0, concat_axis=0, axis_index_groups=pairs, tiled=True)
    grad_w, mixed = spread_sums(shards, const_v, (made, slots, routes, aux, x2, h2), rest, out_rows, experts)
    grad_w = grad_w.astype(F32)
    ffn_sum = ffn_sum.astype(F32)
    return (
        mixed,
        grad_tokens,
        grad_prev,
        small[n + 7],
        grad_w[:width],
        grad_w[width:2 * width],
        grad_w[3 * width:4 * width],
        grad_w[2 * width:3 * width],
        small[n + 6],
        small[:n].T,
        small[n:n + 4].reshape(2, 2, width).transpose(0, 2, 1),
        small[n + 4:n + 6],
        ffn_sum[:, 0],
        ffn_sum[:, 1],
        ffn_sum[:, 2].transpose(0, 2, 1),
    )


def solution(mesh):
    block = P(("dp", "expert"), None)
    in_specs = (block, block, block, P(("dp", "expert"))) + (P(),) * 9 + (P("expert", None, None),) * 3 + (block,)
    out_specs = (block, block, block) + (P(),) * 9 + (
        P("expert", None, "dp"), P("expert", None, "dp"), P("expert", "dp", None),
    )
    return jax.shard_map(local, mesh=mesh, in_specs=in_specs, out_specs=out_specs, check_vma=False)
```
